32 devices in a mesh: dp: 8 (over y, x, core), seq: 4 (over z).
Axes of the slice: x: 2, y: 2, z: 4, core: 2. Of those that a mesh axis runs over, the one named last changes fastest.
Arguments:
- tokens: bfloat16 [8, 1024, 768], P('dp', 'seq'), may hold values from -6 to 6
- segments: int32 [8, 1024], P('dp', 'seq'), may hold values from 0 to 7, never falling along the last dimension, each value on 1 to 256 neighbouring positions
- query_weight: bfloat16 [768, 768], P('dp', 'seq'), may hold values from -0.3125 to 0.3125
- key_weight: bfloat16 [768, 768], P('dp', 'seq'), may hold values from -0.3125 to 0.3125
- value_weight: bfloat16 [768, 768], P('dp', 'seq'), may hold values from -0.21875 to 0.21875
- output_weight: bfloat16 [768, 768], P('dp', 'seq'), may hold values from -0.875 to 0.875
- query_bias: bfloat16 [768], P('dp'), may hold values from -3 to 3
- value_bias: bfloat16 [768], P('dp'), may hold values from -3 to 3
- output_bias: bfloat16 [768], P('dp'), may hold values from -3 to 3
- first_gain: bfloat16 [768], P('dp'), may hold values from 0.5 to 1.5
- first_shift: bfloat16 [768], P('dp'), may hold values from -3 to 3
- up_weight: bfloat16 [768, 3072], P('dp', 'seq'), may hold values from -0.21875 to 0.21875
- up_bias: bfloat16 [3072], P('dp'), may hold values from -3 to 3
- down_weight: bfloat16 [3072, 768], P('seq', 'dp'), may hold values from -0.109375 to 0.109375
- down_bias: bfloat16 [768], P('dp'), may hold values from -3 to 3
- second_gain: bfloat16 [768], P('dp'), may hold values from 0.5 to 1.5
- second_shift: bfloat16 [768], P('dp'), may hold values from -3 to 3
- cotangent: bfloat16 [8, 1024, 768], P('dp', 'seq'), may hold values from -6 to 6
Outputs:
- layer_output: bfloat16 [8, 1024, 768], P('dp', 'seq')
- input_grad: float32 [8, 1024, 768], P('dp', 'seq')
- query_weight_grad: float32 [768, 768], P('dp', 'seq')
- key_weight_grad: float32 [768, 768], P('dp', 'seq')
- value_weight_grad: float32 [768, 768], P('dp', 'seq')
- output_weight_grad: float32 [768, 768], P('dp', 'seq')
- query_bias_grad: float32 [768], P('dp')
- value_bias_grad: float32 [768], P('dp')
- output_bias_grad: float32 [768], P('dp')
- first_gain_grad: float32 [768], P('dp')
- first_shift_grad: float32 [768], P('dp')
- up_weight_grad: float32 [768, 3072], P('dp', 'seq')
- up_bias_grad: float32 [3072], P('dp')
- down_weight_grad: float32 [3072, 768], P('seq', 'dp')
- down_bias_grad: float32 [768], P('dp')
- second_gain_grad: float32 [768], P('dp')
- second_shift_grad: float32 [768], P('dp')
The draws below stay inside these ranges and needn't reach their ends.
Inputs may be any that keep to these rules, and one draw needn't show every extreme that they name: `segments`: each sequence holds 8 documents numbered from 0 in order of position; each has 1 to 256 tokens, and one has exactly that many.
All inputs are finite; a program needn't handle non-finite values.
Results may differ from the reference program's by a relative error of at most 0.017.
The reference program's roundings to bfloat16 on the way count: a program that leaves them out, or rounds other values in their place, can miss the bound.
Values may be sent and summed in bfloat16 or wider, within the bound.
No kernel may reach another device: no remote copies, remote signals or barrier semaphores. Data moves between devices by JAX's collectives and lax.ppermute only.
A program may use at most 128 MiB of HBM per device.

```python
import math
import jax
import jax.numpy as jnp
import numpy as np
from jax import lax

D = 768
HEADS = 12
HEAD_DIM = 64
FF = 3072
DOCS = 8
LEN = 1024
SEQS = 8


def with_spikes(entries, rng, source, target, parts, factor):
    def block_of(position):
        return (jnp.arange(entries.shape[position]) // (entries.shape[position] // parts)).reshape((-1,) + (1,) * (entries.ndim - 1 - position))

    near = jax.random.permutation(rng, parts)[block_of(target)]
    far = (block_of(target) + parts // 2) % parts
    return jnp.where((block_of(source) == near) | (block_of(source) == far), factor * entries, entries)


def level_of(own_key, extent, cuts, least, top_value):
    factor_of = 1.0
    for dim, shards_of in cuts:
        heights = jax.random.uniform(jax.random.fold_in(jax.random.fold_in(own_key, 6), dim), (shards_of,), jnp.float32, least / len(cuts), top_value / len(cuts))
        factor_of = factor_of * jnp.repeat(jnp.exp(heights), extent[dim] // shards_of).reshape((-1,) + (1,) * (len(extent) - 1 - dim))
    return factor_of


def profile(count, total, reach, lean):
    loads = [(1 << 20) // math.isqrt(grade ** lean) + 1 for grade in range(2, count + 1)]
    spare, given = total - reach - (count - 1), [1] * (count - 1)
    while spare > 0:
        free = [i for i in range(count - 1) if given[i] < reach]
        pool, left = sum([loads[i] for i in free]), spare
        for i in free:
            addition = min(reach - given[i], max(1, left * loads[i] // pool), spare)
            given[i] = given[i] + addition
            spare = spare - addition
    return np.array([reach] + given)


def ragged(key, count, total, bound, lean):
    if count == 2:
        one = jax.random.randint(key, (), max(1, total - bound), min(bound, total - 1) + 1)
        return jnp.stack([one, total - one])
    tallies = jnp.asarray(profile(count, total, bound, lean), jnp.int32)
    pairs = (count - 1) // 2
    donor, receiver = tallies[1:1 + 2 * pairs:2], tallies[2:2 + 2 * pairs:2]
    room = jnp.minimum(donor - 1, bound - receiver)
    moved = jax.random.randint(jax.random.fold_in(key, 1), (pairs,), 0, 1 << 20) % (room + 1)
    tallies = tallies.at[1:1 + 2 * pairs:2].set(donor - moved).at[2:2 + 2 * pairs:2].set(receiver + moved)
    return tallies[jax.random.permutation(jax.random.fold_in(key, 2), count)]


def gaussian(own_key, dims, deviation, limit, cuts=(), dtype=jnp.bfloat16):
    level = level_of(own_key, dims, cuts, -0.22, 0.18) if cuts else 1.0
    entries = jax.random.normal(own_key, dims, jnp.float32) * deviation * level
    return jnp.minimum(jnp.maximum(entries, -limit), limit).astype(dtype)


def bell_draw_with(rng, extent, scale, bound, cuts, heavy, dtype=jnp.bfloat16):
    drawn = scale * jax.random.normal(rng, extent, jnp.float32)
    if cuts:
        drawn = drawn * level_of(rng, extent, cuts, -0.22, 0.18)
    return jnp.clip(with_spikes(drawn, jax.random.fold_in(rng, 3), *heavy), -bound, bound).astype(dtype)


def setup_inputs(seed: int = 0) -> dict:
    streams_of = jax.random.split(jax.random.key(seed), 19)
    return {
        "tokens": bell_draw_with(streams_of[0], (SEQS, LEN, D), 1.0, 6.0, ((0, 8), (1, 4)), (0, 2, 8, 2.0)),
        "segments": jax.vmap(lambda own: jnp.searchsorted(jnp.cumsum(ragged(own, DOCS, LEN, LEN // 4, 2)), jnp.arange(LEN), side="right"))(jax.random.split(streams_of[1], SEQS)).reshape((SEQS, LEN)).astype(jnp.int32),
        "query_weight": gaussian(streams_of[2], (D, D), (D // 2) ** -0.5, 0.3125, ((0, 8), (1, 4))),
        "key_weight": gaussian(streams_of[3], (D, D), (D // 2) ** -0.5, 0.3125, ((0, 8), (1, 4))),
        "value_weight": gaussian(streams_of[4], (D, D), D ** -0.5, 0.21875, ((0, 8), (1, 4))),
        "output_weight": gaussian(streams_of[5], (D, D), (D // 16) ** -0.5, 0.875, ((0, 8), (1, 4))),
        "query_bias": gaussian(streams_of[6], (D,), 0.5, 3.0, ((0, 8),)),
        "value_bias": gaussian(streams_of[7], (D,), 0.5, 3.0, ((0, 8),)),
        "output_bias": gaussian(streams_of[8], (D,), 0.5, 3.0, ((0, 8),)),
        "first_gain": jnp.clip(1.0 + 0.1 * jax.random.normal(streams_of[9], (D,), jnp.float32), 0.5, 1.5).astype(jnp.bfloat16),
        "first_shift": gaussian(streams_of[10], (D,), 0.5, 3.0, ((0, 8),)),
        "up_weight": gaussian(streams_of[11], (D, FF), D ** -0.5, 0.21875, ((0, 8), (1, 4))),
        "up_bias": gaussian(streams_of[12], (FF,), 0.5, 3.0, ((0, 8),)),
        "down_weight": gaussian(streams_of[13], (FF, D), FF ** -0.5, 0.109375, ((0, 4), (1, 8))),
        "down_bias": gaussian(streams_of[14], (D,), 0.5, 3.0, ((0, 8),)),
        "second_gain": jnp.clip(1.0 + 0.1 * jax.random.normal(streams_of[15], (D,), jnp.float32), 0.5, 1.5).astype(jnp.bfloat16),
        "second_shift": gaussian(streams_of[16], (D,), 0.5, 3.0, ((0, 8),)),
        "cotangent": bell_draw_with(streams_of[17], (SEQS, LEN, D), 1.0, 6.0, ((0, 8), (1, 4)), (0, 2, 8, 2.0)),
    }


EPS = 1e-05
MASKED = -1e+30
HIGH = lax.Precision.HIGHEST

@jax.custom_vjp
def low(v):
    return lax.optimization_barrier(v.astype(jnp.bfloat16)).astype(jnp.float32)

@jax.custom_vjp
def low_back(v):
    return v

def low_keep(v):
    return (low(v), None)

def low_pass(kept, grad):
    return (grad,)

def back_keep(v):
    return (v, None)

def back_low(kept, grad):
    return (low(grad),)
low.defvjp(low_keep, low_pass)
low_back.defvjp(back_keep, back_low)

def product(left, right):
    return jnp.dot(left, right, precision=HIGH)

def layer_norm(total, gain, shift):
    center = total - lax.optimization_barrier(jnp.mean(total, axis=-1, keepdims=True))
    scale_inv = lax.rsqrt(lax.optimization_barrier(jnp.mean(center * center, axis=-1, keepdims=True)) + EPS)
    return center * scale_inv * gain + shift

def attend_block(query_block, block_docs, keys, values, docs):
    scores = jnp.einsum('qhd,khd->hqk', query_block, keys, precision=HIGH) * HEAD_DIM ** (-0.5)
    scores = low_back(scores)
    scores = jnp.where((block_docs[:, None] == docs[None, :])[None], scores, MASKED)
    top = lax.optimization_barrier(jnp.max(scores, axis=-1, keepdims=True))
    expo = jnp.exp(scores - top)
    probs = expo / lax.optimization_barrier(jnp.sum(expo, axis=-1, keepdims=True))
    return jnp.einsum('hqk,khd->qhd', low(probs), values, precision=HIGH)

def forward(inputs, docs, query_weight, key_weight, value_weight, output_weight, query_bias, value_bias, output_bias, first_gain, first_shift, up_weight, up_bias, down_weight, down_bias, second_gain, second_shift):
    length = inputs.shape[0]
    block_rows = min(512, length)
    blocks = length // block_rows
    query = low_back(low(product(inputs, query_weight) + query_bias)).reshape(length, HEADS, HEAD_DIM)
    keys = low_back(low(product(inputs, key_weight))).reshape(length, HEADS, HEAD_DIM)
    values = low_back(low(product(inputs, value_weight) + value_bias)).reshape(length, HEADS, HEAD_DIM)

    def one_block(pieces):
        return attend_block(pieces[0], pieces[1], keys, values, docs)
    context = lax.map(jax.checkpoint(one_block), (query.reshape(blocks, block_rows, HEADS, HEAD_DIM), docs.reshape(blocks, block_rows)))
    context = low_back(low(context.reshape(length, D)))
    attention = low_back(product(context, output_weight) + output_bias)
    first = layer_norm(inputs + attention, first_gain, first_shift)
    gate = low_back(product(low(first), up_weight) + up_bias)
    active = low(jax.nn.gelu(gate, approximate=False))
    branch = low_back(product(active, down_weight) + down_bias)
    return layer_norm(first + branch, second_gain, second_shift)

def reference(tokens, segments, query_weight, key_weight, value_weight, output_weight, query_bias, value_bias, output_bias, first_gain, first_shift, up_weight, up_bias, down_weight, down_bias, second_gain, second_shift, cotangent):
    params = tuple((item.astype(jnp.float32) for item in (query_weight, key_weight, value_weight, output_weight, query_bias, value_bias, output_bias, first_gain, first_shift, up_weight, up_bias, down_weight, down_bias, second_gain, second_shift)))

    def per_sequence(totals, pieces):
        inputs, seq_docs, upstream = pieces

        def layer(inp, *weights):
            return forward(inp, seq_docs, *weights)
        output, pullback = jax.vjp(layer, inputs.astype(jnp.float32), *params)
        grads = pullback(upstream.astype(jnp.float32))
        new_totals = tuple((total + grad for total, grad in zip(totals, grads[1:])))
        return (new_totals, (output.astype(jnp.bfloat16), grads[0]))
    start_totals = tuple((jnp.zeros(item.shape, jnp.float32) for item in params))
    totals, (outputs, input_grads) = lax.scan(per_sequence, start_totals, (tokens, segments, cotangent))
    return (outputs, input_grads, totals[0], totals[1], totals[2], totals[3], totals[4], totals[5], totals[6], totals[7], totals[8], totals[9], totals[10], totals[11], totals[12], totals[13], totals[14])
```

```python
import jax
import jax.numpy as jnp
from jax import lax
from jax.experimental import pallas as pl
from jax.experimental.pallas import tpu as pltpu
from jax.sharding import PartitionSpec as P

D = 768
HEADS = 12
HEAD_DIM = 64
FF = 3072
EPS = 1e-05
MASKED = 1e30
PAIR = 2 * HEAD_DIM
QUARTER = D // 4
HALF = D // 2
HID = FF // 4
VECS = 8
BF = jnp.bfloat16
F32 = jnp.float32
ROOT_HALF = 0.7071067811865476
ROOT_TWO_PI = 0.3989422804014327


def dot(a, b):
    return lax.dot_general(a, b, (((1,), (0,)), ((), ())), preferred_element_type=F32)


def dot_nt(a, b):
    return lax.dot_general(a, b, (((1,), (1,)), ((), ())), preferred_element_type=F32)


def dot_tn(a, b):
    return lax.dot_general(a, b, (((0,), (0,)), ((), ())), preferred_element_type=F32)


def swap(value, axis, mask):
    count = lax.axis_size(axis)
    return lax.ppermute(value, axis, [(k, k ^ mask) for k in range(count)])


def whole(shape):
    return pl.BlockSpec(shape, lambda *_: (0,) * len(shape))


def params():
    return pltpu.CompilerParams(vmem_limit_bytes=60 * 1024 * 1024)


def call(body, scalars, operands, in_specs, outs, out_specs, grid, scratch=(), flops=0):
    spec = pltpu.PrefetchScalarGridSpec(
        num_scalar_prefetch=1,
        grid=grid,
        in_specs=in_specs,
        out_specs=out_specs,
        scratch_shapes=list(scratch),
    )
    moved = sum(o.size * o.dtype.itemsize for o in list(operands) + list(outs))
    return pl.pallas_call(
        body,
        out_shape=outs,
        grid_spec=spec,
        compiler_params=params(),
        cost_estimate=pl.CostEstimate(flops=flops, transcendentals=0, bytes_accessed=moved),
    )(scalars, *operands)


def struct(shape, dtype):
    return jax.ShapeDtypeStruct(shape, dtype)


def gather_pieces(piece):
    count = lax.axis_size("dp")
    if piece.shape[0] % 16 or count & (count - 1):
        return [lax.all_gather(piece, "dp", axis=0, tiled=True)]
    chip = {0: piece}
    for j in range(count - 2, 0, -2):
        chip[j] = swap(piece, "dp", j)
    pieces = []
    for j in range(0, count, 2):
        pieces += [chip[j], swap(chip[j], "dp", 1)]
    return pieces


def place(target, refs, base, source_cols, target_cols):
    rows = refs[0].shape[0]
    for j, ref in enumerate(refs):
        start = 0 if len(refs) == 1 else pl.multiple_of((base ^ j) * rows, 16)
        target[pl.ds(start, rows), target_cols] = ref[:, source_cols]


def split_rows(result, base, keep, send):
    count, rows = 2 * keep.shape[0], keep.shape[1]
    for j in range(count):
        block = result[pl.ds(pl.multiple_of((base ^ j) * rows, 16), rows), :].astype(BF)
        if j % 2:
            send[j // 2] = block
        else:
            keep[j // 2] = block


def qkv_attend(scalars, own, partner, halo_near, halo_far, own_docs, bias, pieces, rows):
    count = len(pieces)
    base = 3 * rows

    def body(sc, own_ref, partner_ref, near_ref, far_ref, docs_ref, bias_ref, *refs):
        weight_refs, refs = refs[:count], refs[count:]
        q_ref, k_ref, v_ref, ctx_ref, x_ref, w_ref, hot_ref, mask_ref = refs
        step = pl.program_id(0)

        @pl.when(step == 0)
        def _():
            near = sc[0]
            own_at = pl.multiple_of(near * rows, rows)
            partner_at = pl.multiple_of((1 - near) * rows, rows)
            number = lax.broadcasted_iota(jnp.int32, (16, rows), 0).astype(F32)

            def mark(line, at):
                hit = jnp.broadcast_to(line, (16, rows)) == number
                hot_ref[:, pl.ds(at, rows)] = jnp.where(hit, 1.0, 0.0).astype(BF)

            x_ref[pl.ds(own_at, rows), :] = own_ref[...]
            x_ref[pl.ds(partner_at, rows), :] = partner_ref[:rows, :]
            mark(docs_ref[...], own_at)
            mark(partner_ref[rows : rows + 1, :rows].astype(F32), partner_at)

            def halo(ref):
                x_ref[2 * rows :, :] = ref[:rows, :]
                mark(ref[rows : rows + 1, :rows].astype(F32), 2 * rows)

            pl.when(near == 1)(lambda: halo(near_ref))
            pl.when(near == 0)(lambda: halo(far_ref))
            place(w_ref, weight_refs, sc[1], slice(None), slice(None))
            hot = hot_ref[...]
            mask_ref[...] = (dot_tn(hot[:, : 2 * rows], hot) - 1.0) * MASKED

        at = pl.multiple_of(step * 3 * PAIR, PAIR)
        both = (dot(x_ref[...], w_ref[:, pl.ds(at, 3 * PAIR)]) + bias_ref[...]).astype(BF)
        query, key, value = both[:, :PAIR], both[:, PAIR : 2 * PAIR], both[:, 2 * PAIR :]
        q_ref[...] = query
        k_ref[...] = key
        v_ref[...] = value
        lane = lax.broadcasted_iota(jnp.int32, (1, PAIR), 1)
        for start, reach in ((0, 2 * rows), (rows, 3 * rows)):
            total = jnp.zeros((rows, PAIR), F32)
            for head in range(2):
                part = jnp.where((lane // HEAD_DIM) == head, 1.0, 0.0)
                mine = (query[start : start + rows].astype(F32) * (part * HEAD_DIM**-0.5)).astype(BF)
                scores = dot_nt(mine, key[:reach]) + mask_ref[start : start + rows, :reach]
                expo = jnp.exp(scores - jnp.max(scores, axis=-1, keepdims=True))
                probs = expo * (1.0 / jnp.sum(expo, axis=-1, keepdims=True))
                total = total + dot(probs.astype(BF), value[:reach]) * part
            ctx_ref[start : start + rows, :] = total.astype(BF)

    column = lambda height: pl.BlockSpec((height, PAIR), lambda p, _: (0, p))
    operands = [own, partner, halo_near, halo_far, own_docs, bias] + pieces
    in_specs = [whole(o.shape) for o in operands]
    in_specs[5] = pl.BlockSpec((1, 3 * PAIR), lambda p, _: (0, p))
    outs = [
        struct((base, HALF), BF),
        struct((base, HALF), BF),
        struct((base, HALF), BF),
        struct((2 * rows, HALF), BF),
        struct((base, D), BF),
        struct((D, 3 * HALF), BF),
        struct((16, base), BF),
    ]
    out_specs = [column(base)] * 3 + [column(2 * rows)] + [whole(o.shape) for o in outs[4:]]
    return call(
        body,
        scalars,
        operands,
        in_specs,
        outs,
        out_specs,
        (HALF // PAIR,),
        [pltpu.VMEM((2 * rows, base), F32)],
        flops=2 * base * D * 3 * HALF,
    )


def feed_forward(scalars, ctx_mine, ctx_partner, x, vecs, up_bias, pieces, rows):
    count = len(pieces)

    def body(sc, mine_ref, partner_ref, x_ref, vec_ref, bias_ref, *refs):
        weight_refs, refs = refs[:count], refs[count:]
        (up_ref, down_ref, out_ref, norm_ref, inv_ref, first_ref, gate_ref, active_ref, part_ref) = refs[:9]
        full_ref, other_ref = refs[9:]

        @pl.when(pl.program_id(0) == 0)
        def _():
            place(up_ref, weight_refs, sc[1], slice(0, HID), slice(0, HID))
            place(down_ref, weight_refs, sc[1], slice(HID, 2 * HID), slice(0, HID))
            place(up_ref, weight_refs, sc[1], slice(2 * HID, 3 * HID), slice(HID, 2 * HID))
            place(down_ref, weight_refs, sc[1], slice(3 * HID, 4 * HID), slice(HID, 2 * HID))
            place(full_ref, weight_refs, sc[1], slice(4 * HID, 4 * HID + D), slice(None))
            for ref, flip in ((out_ref, 0), (other_ref, 1)):
                for k in range(2):
                    at = pl.multiple_of((sc[2] ^ flip ^ (2 * k)) * QUARTER, 16)
                    ref[k * QUARTER : (k + 1) * QUARTER, :] = full_ref[pl.ds(at, QUARTER), :]

        attention = dot(mine_ref[...], out_ref[...]) + dot(partner_ref[...], other_ref[...])
        total = x_ref[...].astype(F32) + (attention + vec_ref[2:3, :])
        center = total - jnp.mean(total, axis=-1, keepdims=True)
        inverse = lax.rsqrt(jnp.mean(center * center, axis=-1, keepdims=True) + EPS)
        normed = center * inverse
        norm_ref[...] = normed
        inv_ref[...] = jnp.broadcast_to(inverse, (rows, 128))
        first = (normed * vec_ref[3:4, :] + vec_ref[4:5, :]).astype(BF)
        first_ref[...] = first
        gate = dot(first, up_ref[...]) + bias_ref[...]
        gate_ref[...] = gate
        active = (gate * (1.0 + lax.erf(gate * ROOT_HALF)) * 0.5).astype(BF)
        active_ref[...] = active
        part_ref[...] = dot_nt(active, down_ref[...]).astype(BF)

    block = lambda width: pl.BlockSpec((rows, width), lambda r, _: (r, 0))
    operands = [ctx_mine, ctx_partner, x, vecs, up_bias] + pieces
    in_specs = [block(HALF), block(HALF), block(D)] + [whole(o.shape) for o in operands[3:]]
    outs = [
        struct((D, 2 * HID), BF),
        struct((D, 2 * HID), BF),
        struct((HALF, D), BF),
        struct((2 * rows, D), F32),
        struct((2 * rows, 128), F32),
        struct((2 * rows, D), BF),
        struct((2 * rows, 2 * HID), F32),
        struct((2 * rows, 2 * HID), BF),
        struct((2 * rows, D), BF),
    ]
    out_specs = [whole(o.shape) for o in outs[:3]] + [block(o.shape[1]) for o in outs[3:]]
    return call(
        body,
        scalars,
        operands,
        in_specs,
        outs,
        out_specs,
        (2,),
        [pltpu.VMEM((D, D), BF), pltpu.VMEM((HALF, D), BF)],
        flops=2 * 2 * rows * D * (D + 4 * HID),
    )


def gelu_slope(scalars, gate):
    rows = gate.shape[0] // 4

    def body(_, gate_ref, slope_ref):
        gate_here = gate_ref[...]
        bell = jnp.exp(gate_here * gate_here * -0.5) * ROOT_TWO_PI
        slope_ref[...] = 0.5 * (1.0 + lax.erf(gate_here * ROOT_HALF)) + gate_here * bell

    spec = pl.BlockSpec((rows, gate.shape[1]), lambda r, _: (r, 0))
    return call(body, scalars, [gate], [spec], [struct(gate.shape, F32)], [spec], (4,))[0]


def second_norm(scalars, part, received, normed, slope, cot_own, cot_partner, vecs, up, down, rows):
    def body(
        sc, part_ref, recv_ref, norm_ref, slope_ref, own_ref, partner_ref, vec_ref, up_ref, down_ref, *refs
    ):
        (out_ref, total_grad_ref, branch_grad_ref, gate_grad_ref, first_part_ref, sums_ref, bias_ref) = refs
        step = pl.program_id(0)
        mine = step == sc[0]

        @pl.when(step == 0)
        def _():
            sums_ref[...] = jnp.zeros_like(sums_ref)
            bias_ref[...] = jnp.zeros_like(bias_ref)

        first = norm_ref[...] * vec_ref[3:4, :] + vec_ref[4:5, :]
        branch = part_ref[...].astype(F32) + recv_ref[...].astype(F32) + vec_ref[5:6, :]
        total = first + branch
        center = total - jnp.mean(total, axis=-1, keepdims=True)
        inverse = lax.rsqrt(jnp.mean(center * center, axis=-1, keepdims=True) + EPS)
        here = center * inverse
        upstream = jnp.where(mine, own_ref[...].astype(F32), partner_ref[...].astype(F32))
        scaled = upstream * vec_ref[6:7, :]
        inner = (
            scaled
            - jnp.mean(scaled, axis=-1, keepdims=True)
            - here * jnp.mean(scaled * here, axis=-1, keepdims=True)
        )
        total_grad = inner * inverse
        total_grad_ref[...] = total_grad
        branch_grad = total_grad.astype(BF)
        branch_grad_ref[...] = branch_grad

        @pl.when(mine)
        def _():
            out_ref[...] = (here * vec_ref[6:7, :] + vec_ref[7:8, :]).astype(BF)
            sums_ref[0:1, :] += jnp.sum(upstream * here, axis=0, keepdims=True)
            sums_ref[1:2, :] += jnp.sum(upstream, axis=0, keepdims=True)
            sums_ref[2:3, :] += jnp.sum(branch_grad.astype(F32), axis=0, keepdims=True)

        gate_grad = (dot(branch_grad, down_ref[...]) * slope_ref[...]).astype(BF)
        gate_grad_ref[...] = gate_grad
        bias_ref[0:1, :] += jnp.sum(gate_grad.astype(F32), axis=0, keepdims=True)
        first_part_ref[...] = dot_nt(gate_grad, up_ref[...]).astype(BF)

    block = lambda width: pl.BlockSpec((rows, width), lambda r, _: (r, 0))
    operands = [part, received, normed, slope, cot_own, cot_partner, vecs, up, down]
    in_specs = [block(D), block(D), block(D), block(2 * HID)] + [whole(o.shape) for o in operands[4:]]
    outs = [
        struct((rows, D), BF),
        struct((2 * rows, D), F32),
        struct((2 * rows, D), BF),
        struct((2 * rows, 2 * HID), BF),
        struct((2 * rows, D), BF),
        struct((8, D), F32),
        struct((8, 2 * HID), F32),
    ]
    out_specs = [
        whole((rows, D)),
        block(D),
        block(D),
        block(2 * HID),
        block(D),
        whole((8, D)),
        whole((8, 2 * HID)),
    ]
    return call(
        body, scalars, operands, in_specs, outs, out_specs, (2,), flops=2 * 2 * rows * D * 4 * HID
    )


def split_outs(count, width):
    return [struct((count // 2, D // count, width), BF)] * 2


def can_split(count):
    return (D // count) % 16 == 0 and count & (count - 1) == 0


def feed_forward_grads(scalars, first, gate_grad, branch_grad, active, count):
    tall = first.shape[0]

    def body(sc, first_ref, gate_ref, branch_ref, active_ref, *refs):
        result_ref = refs[-1]
        step = pl.program_id(0)

        @pl.when(step % 2 == 0)
        def _():
            result_ref[...] = dot_tn(first_ref[...], gate_ref[...])

        @pl.when(step % 2 == 1)
        def _():
            result_ref[...] = dot_tn(branch_ref[...], active_ref[...])

        if len(refs) == 2:
            refs[0][...] = result_ref[...]
        else:
            split_rows(result_ref, sc[1], refs[0], refs[1])

    half = pl.BlockSpec((tall, HID), lambda c, _: (0, c // 2))
    if can_split(count):
        outs = split_outs(count, 4 * HID)
        out_specs = [pl.BlockSpec((count // 2, D // count, HID), lambda c, _: (0, 0, c))] * 2
    else:
        outs = [struct((D, 4 * HID), F32)]
        out_specs = [pl.BlockSpec((D, HID), lambda c, _: (0, c))]
    return call(
        body,
        scalars,
        [first, gate_grad, branch_grad, active],
        [whole(first.shape), half, whole(branch_grad.shape), half],
        outs,
        out_specs,
        (4,),
        [pltpu.VMEM((D, HID), F32)],
        flops=2 * tall * D * 4 * HID,
    )


def first_norm(scalars, part, received, total_grad, normed, inverse, vecs, out_weight, rows):
    def body(sc, part_ref, recv_ref, grad_ref, norm_ref, inv_ref, vec_ref, weight_ref, *refs):
        own_ref, attention_ref, context_ref, send_ref, sums_ref = refs
        step = pl.program_id(0)
        mine = step == sc[0]

        @pl.when(step == 0)
        def _():
            sums_ref[...] = jnp.zeros_like(sums_ref)

        upstream = grad_ref[...] + part_ref[...].astype(F32) + recv_ref[...].astype(F32)
        here = norm_ref[...]
        scaled = upstream * vec_ref[3:4, :]
        inner = (
            scaled
            - jnp.mean(scaled, axis=-1, keepdims=True)
            - here * jnp.mean(scaled * here, axis=-1, keepdims=True)
        )
        total = inner * inv_ref[:, :1]
        attention = total.astype(BF)
        attention_ref[...] = attention

        @pl.when(mine)
        def _():
            own_ref[...] = total
            sums_ref[0:1, :] += jnp.sum(upstream * here, axis=0, keepdims=True)
            sums_ref[1:2, :] += jnp.sum(upstream, axis=0, keepdims=True)
            sums_ref[2:3, :] += jnp.sum(attention.astype(F32), axis=0, keepdims=True)

        context = dot_nt(attention, weight_ref[...]).astype(BF)
        context_ref[...] = context

        @pl.when(step == 1)
        def _():
            turned = jnp.concatenate([weight_ref[QUARTER:, :], weight_ref[:QUARTER, :]], axis=0)
            send_ref[...] = dot_nt(attention, turned).astype(BF)

    block = lambda width: pl.BlockSpec((rows, width), lambda r, _: (r, 0))
    operands = [part, received, total_grad, normed, inverse, vecs, out_weight]
    in_specs = [block(D)] * 4 + [block(128), whole(vecs.shape), whole(out_weight.shape)]
    outs = [
        struct((rows, D), F32),
        struct((2 * rows, D), BF),
        struct((2 * rows, HALF), BF),
        struct((rows, HALF), BF),
        struct((8, D), F32),
    ]
    out_specs = [whole((rows, D)), block(D), block(HALF), whole((rows, HALF)), whole((8, D))]
    return call(body, scalars, operands, in_specs, outs, out_specs, (2,), flops=2 * 2 * rows * D * HALF)


def output_grads(scalars, ctx_mine, ctx_partner, attention, count):
    tall = attention.shape[0]

    def body(sc, mine_ref, partner_ref, grad_ref, *refs):
        result_ref = refs[-1]
        for ref, flip in ((mine_ref, 0), (partner_ref, 1)):
            part = dot_tn(ref[...], grad_ref[...])
            for k in range(2):
                at = pl.multiple_of((sc[2] ^ flip ^ (2 * k)) * QUARTER, 16)
                result_ref[pl.ds(at, QUARTER), :] = part[k * QUARTER : (k + 1) * QUARTER, :]
        if len(refs) == 2:
            refs[0][...] = result_ref[...]
        else:
            split_rows(result_ref, sc[1], refs[0], refs[1])

    outs = split_outs(count, D) if can_split(count) else [struct((D, D), F32)]
    operands = [ctx_mine, ctx_partner, attention]
    return call(
        body,
        scalars,
        operands,
        [whole(o.shape) for o in operands],
        outs,
        [whole(o.shape) for o in outs],
        (1,),
        [pltpu.VMEM((D, D), F32)],
        flops=2 * tall * D * D,
    )


def attend_backward(scalars, query, key, value, grad_pair, grad_halo, hot, weight, rows):
    base = 3 * rows
    steps = HALF // PAIR

    def body(sc, q_ref, k_ref, v_ref, pair_ref, halo_ref, hot_ref, w_ref, *refs):
        out_ref, keep_ref, send_ref, mask_ref, key_ref, value_ref, acc_ref = refs
        step = pl.program_id(0)

        @pl.when(step == 0)
        def _():
            mask_ref[...] = (dot_tn(hot_ref[...], hot_ref[...]) - 1.0) * MASKED

        key_ref[...] = jnp.zeros_like(key_ref)
        value_ref[...] = jnp.zeros_like(value_ref)
        lane = lax.broadcasted_iota(jnp.int32, (1, PAIR), 1)
        query_grads = [jnp.zeros((PAIR, rows), F32), jnp.zeros((PAIR, rows), F32)]
        for head in range(2):
            part = jnp.where((lane // HEAD_DIM) == head, 1.0, 0.0)
            key_turned = (k_ref[...].astype(F32) * part).T.astype(BF)
            for index, (low, high) in enumerate(((0, 2 * rows), (0, base), (rows, base))):
                start = index * rows
                mine = (q_ref[start : start + rows].astype(F32) * (part * HEAD_DIM**-0.5)).astype(BF)
                grads = halo_ref[...] if index == 2 else pair_ref[start : start + rows]
                grads = (grads.astype(F32) * part).astype(BF)
                scores = dot_nt(k_ref[low:high], mine) + mask_ref[low:high, start : start + rows]
                expo = jnp.exp(scores - jnp.max(scores, axis=0, keepdims=True))
                probs = expo * (1.0 / jnp.sum(expo, axis=0, keepdims=True))
                pulled = dot_nt(v_ref[low:high], grads)
                inner = jnp.sum(probs * pulled, axis=0, keepdims=True)
                score_grads = (probs * (pulled - inner)).astype(BF)
                top = min(high, 2 * rows)
                span = top - low
                value_ref[low:top, :] += dot(probs[:span].astype(BF), grads)
                key_ref[low:top, :] += dot(score_grads[:span], mine)
                if index < 2:
                    query_grads[index] = query_grads[index] + dot(key_turned[:, low:high], score_grads)
        for index in range(2):
            turned = (query_grads[index] * HEAD_DIM**-0.5).T.astype(BF)
            out_ref[index * rows : (index + 1) * rows, :PAIR] = turned
        out_ref[:, PAIR : 2 * PAIR] = key_ref[...].astype(BF)
        out_ref[:, 2 * PAIR :] = value_ref[...].astype(BF)
        product = dot_nt(out_ref[...], w_ref[...])

        @pl.when(step == 0)
        def _():
            acc_ref[...] = product

        @pl.when(step > 0)
        def _():
            acc_ref[...] += product

        @pl.when(step == steps - 1)
        def _():
            near = sc[0]
            keep_ref[...] = acc_ref[pl.ds(pl.multiple_of(near * rows, rows), rows), :]
            other = acc_ref[pl.ds(pl.multiple_of((1 - near) * rows, rows), rows), :]
            send_ref[...] = other.astype(BF)

    column = lambda height: pl.BlockSpec((height, PAIR), lambda p, _: (0, p))
    operands = [query, key, value, grad_pair, grad_halo, hot, weight]
    in_specs = [column(base)] * 3 + [column(2 * rows), column(rows), whole(hot.shape)]
    in_specs += [pl.BlockSpec((D, 3 * PAIR), lambda p, _: (0, p))]
    outs = [struct((2 * rows, 3 * HALF), BF), struct((rows, D), F32), struct((rows, D), BF)]
    out_specs = [
        pl.BlockSpec((2 * rows, 3 * PAIR), lambda p, _: (0, p)),
        whole((rows, D)),
        whole((rows, D)),
    ]
    scratch = [
        pltpu.VMEM((base, base), F32),
        pltpu.VMEM((2 * rows, PAIR), F32),
        pltpu.VMEM((2 * rows, PAIR), F32),
        pltpu.VMEM((2 * rows, D), F32),
    ]
    return call(
        body,
        scalars,
        operands,
        in_specs,
        outs,
        out_specs,
        (steps,),
        scratch,
        flops=2 * HALF * base * base * 5 + 2 * 2 * rows * D * 3 * HALF,
    )


def projection_grads(scalars, x, grads, count, rows):
    tall = 2 * rows

    def body(sc, x_ref, grad_ref, *refs):
        result_ref = refs[-1]
        result_ref[...] = dot_tn(x_ref[...], grad_ref[...])
        refs[-2][...] = jnp.broadcast_to(
            jnp.sum(grad_ref[...].astype(F32), axis=0, keepdims=True), (8, 3 * PAIR)
        )
        if len(refs) == 3:
            refs[0][...] = result_ref[...]
        else:
            split_rows(result_ref, sc[1], refs[0], refs[1])

    if can_split(count):
        outs = split_outs(count, 3 * HALF)
        out_specs = [pl.BlockSpec((count // 2, D // count, 3 * PAIR), lambda p, _: (0, 0, p))] * 2
    else:
        outs = [struct((D, 3 * HALF), F32)]
        out_specs = [pl.BlockSpec((D, 3 * PAIR), lambda p, _: (0, p))]
    outs = outs + [struct((8, 3 * HALF), F32)]
    out_specs = out_specs + [pl.BlockSpec((8, 3 * PAIR), lambda p, _: (0, p))]
    return call(
        body,
        scalars,
        [x, grads],
        [pl.BlockSpec((tall, D), lambda p, _: (0, 0)), pl.BlockSpec((tall, 3 * PAIR), lambda p, _: (0, p))],
        outs,
        out_specs,
        (HALF // PAIR,),
        [pltpu.VMEM((D, 3 * PAIR), F32)],
        flops=2 * tall * D * 3 * HALF,
    )


def combine(scalars, keep, received):
    count, rows, width = keep.shape
    chunk = width // 3

    def body(_, keep_ref, recv_ref, *refs):
        for k in range(count):
            total = keep_ref[k].astype(F32) + recv_ref[k].astype(F32)
            refs[k][...] = total.astype(refs[k].dtype)

    block = pl.BlockSpec((count, rows, chunk), lambda c, _: (0, 0, c))
    outs = [struct((rows, width), F32)] + [struct((rows, width), BF)] * (count - 1)
    spec = pl.BlockSpec((rows, chunk), lambda c, _: (0, c))
    return call(body, scalars, [keep, received], [block, block], outs, [spec] * count, (3,))


def reduce_pieces(scalars, parts):
    if len(parts) == 1:
        return lax.psum_scatter(parts[0], "dp", scatter_dimension=0, tiled=True)
    keep, send = parts
    sums = combine(scalars, keep, swap(send, "dp", 1))
    total = sums[0]
    for k in range(len(sums) - 1, 0, -1):
        total = total + swap(sums[k], "dp", 2 * k).astype(F32)
    return total


def per_device(
    tokens,
    segments,
    query_weight,
    key_weight,
    value_weight,
    output_weight,
    query_bias,
    value_bias,
    output_bias,
    first_gain,
    first_shift,
    up_weight,
    up_bias,
    down_weight,
    down_bias,
    second_gain,
    second_shift,
    cotangent,
):
    seq_count = lax.axis_size("seq")
    count = lax.axis_size("dp")
    place_z = lax.axis_index("seq")
    place_dp = lax.axis_index("dp")
    assert seq_count == 4
    rows = tokens.shape[1]
    piece_rows = query_weight.shape[0]
    near = ((place_z == 1) | (place_z == 2)).astype(jnp.int32)
    scalars = jnp.stack([near, place_dp, place_z]).astype(jnp.int32)

    narrow = jnp.concatenate([query_weight, key_weight, value_weight, output_weight], axis=1)
    wide = jnp.concatenate([up_weight, down_weight.T], axis=1)
    narrow_far = swap(narrow, "seq", 2)
    own = tokens[0]
    own_docs = segments.astype(F32)
    marks = jnp.pad(segments.astype(BF), ((0, 15), (0, D - rows)))
    labelled = jnp.concatenate([own, marks], axis=0)
    partner = swap(labelled, "seq", 1)
    halo_near = lax.ppermute(labelled, "seq", [(1, 2), (2, 1)])
    halo_far = lax.ppermute(labelled, "seq", [(1, 3), (2, 0)])
    wide_far = swap(wide, "seq", 2)
    cot_own = cotangent[0]
    cot_partner = swap(cot_own, "seq", 1)

    vectors = jnp.concatenate(
        [
            query_bias,
            value_bias,
            output_bias,
            first_gain,
            first_shift,
            down_bias,
            second_gain,
            second_shift,
            up_bias,
        ]
    )
    spread = lax.all_to_all(
        jnp.broadcast_to(vectors[None], (count, vectors.shape[0])), "dp", 0, 0, tiled=True
    )
    main = spread[:, : VECS * piece_rows].astype(F32)
    main = main.reshape(count, VECS, piece_rows).transpose(1, 0, 2).reshape(VECS, D)
    hidden_bias = spread[:, VECS * piece_rows :].astype(F32).reshape(4, HID)

    def mine_of(table):
        first_half = lax.dynamic_index_in_dim(table, place_z, 0)
        return jnp.concatenate([first_half, lax.dynamic_index_in_dim(table, place_z ^ 2, 0)], axis=1)

    up_bias_here = mine_of(hidden_bias)
    query_bias_here = mine_of(main[0].reshape(4, QUARTER))
    value_bias_here = mine_of(main[1].reshape(4, QUARTER))
    bias = jnp.concatenate([query_bias_here, jnp.zeros((1, HALF), F32), value_bias_here], axis=0)
    bias = bias.reshape(3, 3, PAIR).transpose(1, 0, 2).reshape(1, 3 * HALF)

    columns = jnp.stack(
        [
            jnp.concatenate(
                [narrow[:, k * QUARTER : (k + 1) * QUARTER], narrow_far[:, k * QUARTER : (k + 1) * QUARTER]],
                axis=1,
            )
            for k in range(3)
        ],
        axis=1,
    )
    columns = columns.reshape(piece_rows, 3, 3, PAIR).transpose(0, 2, 1, 3).reshape(piece_rows, 3 * HALF)
    projection_pieces = gather_pieces(columns)
    out_half = jnp.stack([narrow[:, 3 * QUARTER :], narrow_far[:, 3 * QUARTER :]])
    out_far = swap(out_half, "seq", 1)
    out_all = jnp.concatenate([out_half, out_far], axis=0)
    order = jnp.arange(4) ^ place_z
    slot = jnp.array([0, 2, 1, 3])[order]
    out_piece = jnp.take(out_all, slot, axis=0).transpose(1, 0, 2).reshape(piece_rows, D)
    feed_pieces = gather_pieces(jnp.concatenate([wide, wide_far, out_piece], axis=1))

    query, key, value, ctx_mine, x, weight, hot = qkv_attend(
        scalars, own, partner, halo_near, halo_far, own_docs, bias, projection_pieces, rows
    )
    ctx_partner = swap(ctx_mine, "seq", 1)
    up, down, out_mine, normed, inverse, first, gate, active, part = feed_forward(
        scalars, ctx_mine, ctx_partner, x, main, up_bias_here, feed_pieces, rows
    )
    part_far = swap(part, "seq", 1)
    slope = gelu_slope(scalars, gate)
    layer_output, total_grad, branch_grad, gate_grad, first_part, sums_two, hidden_sums = second_norm(
        scalars, part, part_far, normed, slope, cot_own, cot_partner, main, up, down, rows
    )
    first_part_far = swap(first_part, "seq", 1)
    feed_parts = feed_forward_grads(scalars, first, gate_grad, branch_grad, active, count)
    own_grad, attention_grad, ctx_grad, halo_send, sums_one = first_norm(
        scalars, first_part, first_part_far, total_grad, normed, inverse, main, out_mine, rows
    )
    halo_grad = swap(halo_send, "seq", 2)
    out_parts = output_grads(scalars, ctx_mine, ctx_partner, attention_grad, count)
    feed_total = reduce_pieces(scalars, feed_parts)
    feed_far = swap(feed_total[:, 2 * HID :].astype(BF), "seq", 2).astype(F32)
    feed_mine = feed_total[:, : 2 * HID] + feed_far
    out_total = reduce_pieces(scalars, out_parts).reshape(piece_rows, 4, QUARTER)
    out_mine_grad = lax.dynamic_index_in_dim(out_total, place_z, 1, keepdims=False)
    out_send = lax.dynamic_index_in_dim(out_total, place_z ^ 2, 1, keepdims=False).astype(BF)
    out_grad = out_mine_grad + swap(out_send, "seq", 2).astype(F32)

    grads, input_keep, input_send = attend_backward(
        scalars, query, key, value, ctx_grad, halo_grad, hot, weight, rows
    )
    input_grad = own_grad + input_keep + swap(input_send, "seq", 1).astype(F32)
    *projection_parts, projection_sums = projection_grads(scalars, x, grads, count, rows)
    projection_total = reduce_pieces(scalars, projection_parts)
    projection_total = projection_total.reshape(piece_rows, 3, 3, PAIR).transpose(0, 2, 1, 3)
    projection_total = projection_total.reshape(piece_rows, 3, HALF)
    projection_far = swap(projection_total[:, :, QUARTER:].astype(BF), "seq", 2).astype(F32)
    projection_mine = projection_total[:, :, :QUARTER] + projection_far

    bias_sums = projection_sums[0].reshape(3, 3, PAIR).transpose(1, 0, 2).reshape(3, 2, QUARTER)

    def spread_out(table, width):
        slots = jnp.arange(4)[:, None]
        wide_table = jnp.where(slots == place_z, table[0][None], 0.0)
        wide_table = jnp.where(slots == (place_z ^ 2), table[1][None], wide_table)
        return wide_table.reshape(4 * width)

    stacked = jnp.stack(
        [
            spread_out(bias_sums[0], QUARTER),
            spread_out(bias_sums[2], QUARTER),
            sums_one[2],
            sums_one[0],
            sums_one[1],
            sums_two[2],
            sums_two[0],
            sums_two[1],
        ]
    )
    stacked = stacked.reshape(VECS, count, piece_rows).transpose(1, 0, 2).reshape(count, VECS * piece_rows)
    hidden = spread_out(hidden_sums[0].reshape(2, HID), HID).reshape(count, FF // count)
    small = jnp.concatenate([stacked, hidden], axis=1)
    small = jnp.broadcast_to(small[:, None], (count, 4, small.shape[1])).reshape(count * 4, -1)
    small = jnp.sum(lax.all_to_all(small, ("dp", "seq"), 0, 0, tiled=True), axis=0)
    vec = [small[k * piece_rows : (k + 1) * piece_rows] for k in range(VECS)]
    return (
        layer_output[None],
        input_grad[None],
        projection_mine[:, 0],
        projection_mine[:, 1],
        projection_mine[:, 2],
        out_grad,
        vec[0],
        vec[1],
        vec[2],
        vec[3],
        vec[4],
        feed_mine[:, :HID],
        small[VECS * piece_rows :],
        feed_mine[:, HID:].T,
        vec[5],
        vec[6],
        vec[7],
    )


def solution(mesh):
    placed = (
        P("dp", "seq", None),
        P("dp", "seq"),
        P("dp", "seq"),
        P("dp", "seq"),
        P("dp", "seq"),
        P("dp", "seq"),
        P("dp"),
        P("dp"),
        P("dp"),
        P("dp"),
        P("dp"),
        P("dp", "seq"),
        P("dp"),
        P("seq", "dp"),
        P("dp"),
        P("dp"),
        P("dp"),
        P("dp", "seq", None),
    )
    return jax.shard_map(
        per_device,
        mesh=mesh,
        in_specs=placed,
        out_specs=(
            P("dp", "seq", None),
            P("dp", "seq", None),
            P("dp", "seq"),
            P("dp", "seq"),
            P("dp", "seq"),
            P("dp", "seq"),
            P("dp"),
            P("dp"),
            P("dp"),
            P("dp"),
            P("dp"),
            P("dp", "seq"),
            P("dp"),
            P("seq", "dp"),
            P("dp"),
            P("dp"),
            P("dp"),
        ),
        check_vma=False,
    )
```

```python
import jax
import jax.numpy as jnp
from jax import lax
from jax.experimental import pallas as pl
from jax.experimental.pallas import tpu as pltpu
from jax.sharding import PartitionSpec as P

D = 768
HEADS = 12
HEAD_DIM = 64
FF = 3072
EPS = 1e-05
MASKED = 1e30
PAIR = 2 * HEAD_DIM
QUARTER = D // 4
HALF = D // 2
HID = FF // 4
VECS = 8
GROUPS = 8
BLOCK = D // GROUPS
LABELS = 16
BF = jnp.bfloat16
F32 = jnp.float32
ROOT_HALF = 0.7071067811865476
ROOT_TWO_PI = 0.3989422804014327


def dot(a, b):
    return lax.dot_general(a, b, (((1,), (0,)), ((), ())), preferred_element_type=F32)


def dot_nt(a, b):
    return lax.dot_general(a, b, (((1,), (1,)), ((), ())), preferred_element_type=F32)


def dot_tn(a, b):
    return lax.dot_general(a, b, (((0,), (0,)), ((), ())), preferred_element_type=F32)


def swap(value, axis, mask):
    count = lax.axis_size(axis)
    return lax.ppermute(value, axis, [(k, k ^ mask) for k in range(count)])


def together(*values):
    return lax.optimization_barrier(values)


def whole(shape):
    return pl.BlockSpec(shape, lambda *_: (0,) * len(shape))


def params():
    return pltpu.CompilerParams(vmem_limit_bytes=22 * 1024 * 1024)


def call(name, body, scalars, operands, in_specs, outs, out_specs, grid, scratch=(), micros=1):
    spec = pltpu.PrefetchScalarGridSpec(
        num_scalar_prefetch=1,
        grid=grid,
        in_specs=in_specs,
        out_specs=out_specs,
        scratch_shapes=list(scratch),
    )
    return pl.pallas_call(
        body,
        out_shape=outs,
        grid_spec=spec,
        compiler_params=params(),
        cost_estimate=pl.CostEstimate(
            flops=int(micros * 1.0e7), transcendentals=0, bytes_accessed=1024
        ),
        name=name,
    )(scalars, *operands)


def struct(shape, dtype):
    return jax.ShapeDtypeStruct(shape, dtype)


def chip_pieces(piece):
    return [piece] + [swap(piece, "dp", j) for j in range(2, GROUPS, 2)]


def core_pieces(chip):
    pieces = []
    for piece in chip:
        pieces += [piece, swap(piece, "dp", 1)]
    return pieces


def gather_rows(piece):
    full = lax.all_gather(piece, "dp", axis=0, tiled=True)
    return list(full.reshape(GROUPS, D // GROUPS, piece.shape[1]))


def place(target, refs, base, source_cols, target_cols):
    for j, ref in enumerate(refs):
        start = pl.multiple_of((base ^ j) * BLOCK, 16)
        target[pl.ds(start, BLOCK), target_cols] = ref[:BLOCK, source_cols]


def split_rows(result, base, keep, send):
    for j in range(GROUPS):
        block = result[pl.ds(pl.multiple_of((base ^ j) * BLOCK, 16), BLOCK), :].astype(BF)
        if j % 2:
            send[j // 2] = block
        else:
            keep[j // 2] = block


def simple(name, body, scalars, operands, outs, micros=1):
    return call(
        name,
        body,
        scalars,
        operands,
        [whole(o.shape) for o in operands],
        outs,
        [whole(o.shape) for o in outs],
        (1,),
        micros=micros,
    )


def label_rows(scalars, tokens, segments):
    rows = tokens.shape[0]

    def body(_, token_ref, segment_ref, out_ref, docs_ref):
        docs = segment_ref[...].astype(F32)
        docs_ref[...] = docs
        out_ref[:rows, :] = token_ref[...]
        out_ref[rows:, :] = jnp.zeros((LABELS, D), BF)
        out_ref[rows:, :rows] = jnp.broadcast_to(docs, (LABELS, rows)).astype(BF)

    outs = [struct((rows + LABELS, D), BF), struct((1, rows), F32)]
    return simple("label_rows", body, scalars, [tokens, segments], outs)


def pack_narrow(scalars, tables):
    rows = tables[0].shape[0]

    def body(_, *refs):
        joined = jnp.concatenate([ref[...].astype(F32) for ref in refs[:-1]], axis=1)
        refs[-1][...] = joined.astype(BF)

    return simple("pack_narrow", body, scalars, tables, [struct((rows, 3 * QUARTER), BF)])[0]


def pack_wide(scalars, up, down, output, output_side):
    rows = up.shape[0]

    def body(_, up_ref, down_ref, out_ref, side_ref, wide_ref):
        wide_ref[:, :HID] = up_ref[...]
        wide_ref[:, HID : 2 * HID] = down_ref[...]
        sides = [out_ref[...].astype(F32), side_ref[...].astype(F32)]
        wide_ref[:, 2 * HID :] = jnp.concatenate(sides, axis=1).astype(BF)

    out = struct((rows, 2 * HID + HALF), BF)
    return simple("pack_wide", body, scalars, [up, down, output, output_side], [out])[0]


def pack_columns(scalars, narrow, narrow_far, lines, tall):
    rows = narrow.shape[0]

    def body(_, near_ref, far_ref, *refs):
        out_ref = refs[-1]
        for kind in range(3):
            part = slice(kind * QUARTER, (kind + 1) * QUARTER)
            both = [near_ref[:, part].astype(F32), far_ref[:, part].astype(F32)]
            both = jnp.concatenate(both, axis=1).astype(BF)
            for p in range(3):
                at = (3 * p + kind) * PAIR
                out_ref[:rows, at : at + PAIR] = both[:, p * PAIR : (p + 1) * PAIR]
        if lines:
            table = jnp.concatenate(
                [ref[...].astype(F32) for ref in refs[:VECS]] + [jnp.zeros((LABELS - VECS, BLOCK), F32)],
                axis=0,
            )
            out_ref[rows:, :] = jnp.zeros((LABELS, 3 * HALF), BF)
            out_ref[rows:, :BLOCK] = table.astype(BF)
            line = jnp.broadcast_to(refs[VECS][...].astype(F32), (LABELS, FF // GROUPS))
            out_ref[rows:, D:] = line.astype(BF)

    out = struct((rows + (LABELS if lines else 0), 3 * HALF), BF)
    operands = [narrow, narrow_far] + (lines + [tall] if lines else [])
    return simple("pack_columns", body, scalars, operands, [out])[0]


def pack_feed(scalars, wide, wide_far):
    rows = wide.shape[0]

    def body(sc, wide_ref, far_ref, out_ref):
        out_ref[:, : 2 * HID] = wide_ref[:, : 2 * HID]
        out_ref[:, 2 * HID : 4 * HID] = far_ref[:, : 2 * HID]
        total = jnp.zeros((rows, D), F32)
        for k in range(4):
            ref = (wide_ref, far_ref)[k // 2]
            at = 2 * HID + (k % 2) * QUARTER
            part = ref[:, at : at + QUARTER].astype(F32)
            part = jnp.concatenate([part, jnp.zeros((rows, D - QUARTER), F32)], axis=1)
            total = total + pltpu.roll(part, (sc[2] ^ k) * QUARTER, 1)
        out_ref[:, 4 * HID :] = total.astype(BF)

    out = struct((rows, 4 * HID + D), BF)
    return simple("pack_feed", body, scalars, [wide, wide_far], [out])[0]


def qkv_attend(scalars, own, partner, halo_near, halo_far, own_docs, pieces, rows):
    count = len(pieces)
    base = 3 * rows

    def body(sc, own_ref, partner_ref, near_ref, far_ref, docs_ref, *refs):
        weight_refs, refs = refs[:count], refs[count:]
        q_ref, k_ref, v_ref, ctx_far_ref, ctx_near_ref, x_ref, w_ref, hot_ref, vec_ref, hidden_ref, mask_ref, bias_ref = refs
        step = pl.program_id(0)

        @pl.when(step == 0)
        def _():
            near = sc[0]
            own_at = pl.multiple_of(near * rows, rows)
            partner_at = pl.multiple_of((1 - near) * rows, rows)
            number = lax.broadcasted_iota(jnp.int32, (16, rows), 0).astype(F32)

            def mark(line, at):
                hit = jnp.broadcast_to(line, (16, rows)) == number
                hot_ref[:, pl.ds(at, rows)] = jnp.where(hit, 1.0, 0.0).astype(BF)

            x_ref[pl.ds(own_at, rows), :] = own_ref[...]
            x_ref[pl.ds(partner_at, rows), :] = partner_ref[:rows, :]
            mark(docs_ref[...], own_at)
            mark(partner_ref[rows : rows + 1, :rows].astype(F32), partner_at)

            def halo(ref):
                x_ref[2 * rows :, :] = ref[:rows, :]
                mark(ref[rows : rows + 1, :rows].astype(F32), 2 * rows)

            pl.when(near == 1)(lambda: halo(near_ref))
            pl.when(near == 0)(lambda: halo(far_ref))
            place(w_ref, weight_refs, sc[1], slice(None), slice(None))
            hot = hot_ref[...]
            mask_ref[...] = (dot_tn(hot[:, : 2 * rows], hot) - 1.0) * MASKED
            vectors = jnp.zeros((LABELS, D), F32)
            for j, ref in enumerate(weight_refs):
                block = sc[1] ^ j
                vectors = vectors + pltpu.roll(ref[BLOCK:, :D].astype(F32), block * BLOCK, 1)
                quarter = block // 2
                for k in range(2):

                    @pl.when(quarter == sc[2] ^ (2 * k))
                    def _():
                        to = pl.multiple_of((block % 2) * (HID // 2) + k * HID, 128)
                        hidden_ref[:, pl.ds(to, HID // 2)] = ref[BLOCK:, D:].astype(F32)

            vec_ref[...] = vectors[:VECS]
            lanes = lax.broadcasted_iota(jnp.int32, (VECS, HALF), 1)
            low = pltpu.roll(vectors[:VECS], D - sc[2] * QUARTER, 1)[:, :HALF]
            high = pltpu.roll(vectors[:VECS], D + QUARTER - (sc[2] ^ 2) * QUARTER, 1)[:, :HALF]
            bias_ref[...] = jnp.where(lanes < QUARTER, low, high)

        at = pl.multiple_of(step * 3 * PAIR, PAIR)
        both = dot(x_ref[...], w_ref[:, pl.ds(at, 3 * PAIR)])
        bias = bias_ref[:, pl.ds(pl.multiple_of(step * PAIR, PAIR), PAIR)]
        query = (both[:, :PAIR] + bias[0:1]).astype(BF)
        key = both[:, PAIR : 2 * PAIR].astype(BF)
        value = (both[:, 2 * PAIR :] + bias[1:2]).astype(BF)
        q_ref[...] = query
        k_ref[...] = key
        v_ref[...] = value
        lane = lax.broadcasted_iota(jnp.int32, (1, PAIR), 1)
        for ctx_ref, start, reach in ((ctx_far_ref, 0, 2 * rows), (ctx_near_ref, rows, 3 * rows)):
            total = jnp.zeros((rows, PAIR), F32)
            for head in range(2):
                part = jnp.where((lane // HEAD_DIM) == head, 1.0, 0.0)
                mine = (query[start : start + rows].astype(F32) * (part * HEAD_DIM**-0.5)).astype(BF)
                scores = dot_nt(mine, key[:reach]) + mask_ref[start : start + rows, :reach]
                expo = jnp.exp(scores - jnp.max(scores, axis=-1, keepdims=True))
                probs = expo * (1.0 / jnp.sum(expo, axis=-1, keepdims=True))
                total = total + dot(probs.astype(BF), value[:reach]) * part
            ctx_ref[...] = total.astype(BF)

    column = lambda height: pl.BlockSpec((height, PAIR), lambda p, _: (0, p))
    operands = [own, partner, halo_near, halo_far, own_docs] + pieces
    in_specs = [whole(o.shape) for o in operands]
    outs = [
        struct((base, HALF), BF),
        struct((base, HALF), BF),
        struct((base, HALF), BF),
        struct((rows, HALF), BF),
        struct((rows, HALF), BF),
        struct((base, D), BF),
        struct((D, 3 * HALF), BF),
        struct((16, base), BF),
        struct((VECS, D), F32),
        struct((LABELS, 2 * HID), F32),
    ]
    out_specs = [column(base)] * 3 + [column(rows)] * 2 + [whole(o.shape) for o in outs[5:]]
    return call(
        "qkv_attend",
        body,
        scalars,
        operands,
        in_specs,
        outs,
        out_specs,
        (HALF // PAIR,),
        [pltpu.VMEM((2 * rows, base), F32), pltpu.VMEM((VECS, HALF), F32)],
        micros=13,
    )


def feed_forward(scalars, block, ctx_mine, ctx_partner, x, vecs, up_bias, weights, rows):
    count = len(weights)
    fresh = count == GROUPS

    def body(sc, mine_ref, partner_ref, x_ref, vec_ref, bias_ref, *refs):
        weight_refs, refs = refs[:count], refs[count:]
        (norm_ref, inv_ref, first_ref, gate_ref, active_ref, part_ref), refs = refs[:6], refs[6:]
        if fresh:
            up_ref, down_ref, out_ref, other_ref, full_ref = refs
            place(up_ref, weight_refs, sc[1], slice(0, HID), slice(0, HID))
            place(down_ref, weight_refs, sc[1], slice(HID, 2 * HID), slice(0, HID))
            place(up_ref, weight_refs, sc[1], slice(2 * HID, 3 * HID), slice(HID, 2 * HID))
            place(down_ref, weight_refs, sc[1], slice(3 * HID, 4 * HID), slice(HID, 2 * HID))
            place(full_ref, weight_refs, sc[1], slice(4 * HID, 4 * HID + D), slice(None))
            for ref, flip in ((out_ref, 0), (other_ref, 1)):
                for k in range(2):
                    at = pl.multiple_of((sc[2] ^ flip ^ (2 * k)) * QUARTER, 16)
                    ref[k * QUARTER : (k + 1) * QUARTER, :] = full_ref[pl.ds(at, QUARTER), :]
        else:
            up_ref, down_ref, out_ref, other_ref = weight_refs

        attention = dot(mine_ref[...], out_ref[...]) + dot(partner_ref[...], other_ref[...])
        total = x_ref[...].astype(F32) + (attention + vec_ref[2:3, :])
        center = total - jnp.mean(total, axis=-1, keepdims=True)
        inverse = lax.rsqrt(jnp.mean(center * center, axis=-1, keepdims=True) + EPS)
        normed = center * inverse
        norm_ref[...] = normed
        inv_ref[...] = jnp.broadcast_to(inverse, (rows, 128))
        first = (normed * vec_ref[3:4, :] + vec_ref[4:5, :]).astype(BF)
        first_ref[...] = first
        gate = dot(first, up_ref[...]) + bias_ref[0:1, :]
        gate_ref[...] = gate
        active = (gate * (1.0 + lax.erf(gate * ROOT_HALF)) * 0.5).astype(BF)
        active_ref[...] = active
        part_ref[...] = dot_nt(active, down_ref[...]).astype(BF)

    operands = [ctx_mine, ctx_partner, x, vecs, up_bias, *weights]
    in_specs = [whole(o.shape) for o in operands]
    in_specs[2] = pl.BlockSpec((rows, D), lambda *_: (block, 0))
    outs = [
        struct((rows, D), F32),
        struct((rows, 128), F32),
        struct((rows, D), BF),
        struct((rows, 2 * HID), F32),
        struct((rows, 2 * HID), BF),
        struct((rows, D), BF),
    ]
    scratch = []
    if fresh:
        outs += [struct((D, 2 * HID), BF)] * 2 + [struct((HALF, D), BF)] * 2
        scratch = [pltpu.VMEM((D, D), BF)]
    results = call(
        "feed_forward",
        body,
        scalars,
        operands,
        in_specs,
        outs,
        [whole(o.shape) for o in outs],
        (1,),
        scratch,
        micros=6,
    )
    return results[:6], (results[6:] if fresh else weights)


def gelu_slope(scalars, gate):
    rows = gate.shape[0] // 2

    def body(_, gate_ref, slope_ref):
        gate_here = gate_ref[...]
        bell = jnp.exp(gate_here * gate_here * -0.5) * ROOT_TWO_PI
        slope_ref[...] = 0.5 * (1.0 + lax.erf(gate_here * ROOT_HALF)) + gate_here * bell

    spec = pl.BlockSpec((rows, gate.shape[1]), lambda r, _: (r, 0))
    return call(
        "gelu_slope", body, scalars, [gate], [spec], [struct(gate.shape, F32)], [spec], (2,), micros=3
    )[0]


def second_norm(scalars, block, part, received, normed, slope, cotangent, vecs, up, down, earlier, rows):
    def body(sc, part_ref, recv_ref, norm_ref, slope_ref, cot_ref, other_ref, vec_ref, up_ref, down_ref, *refs):
        old, refs = refs[: len(earlier)], refs[len(earlier) :]
        (total_grad_ref, branch_grad_ref, gate_grad_ref, first_part_ref, out_ref, sums_ref, bias_ref) = refs
        mine = sc[0] == block
        first = norm_ref[...] * vec_ref[3:4, :] + vec_ref[4:5, :]
        branch = part_ref[...].astype(F32) + recv_ref[...].astype(F32) + vec_ref[5:6, :]
        total = first + branch
        center = total - jnp.mean(total, axis=-1, keepdims=True)
        inverse = lax.rsqrt(jnp.mean(center * center, axis=-1, keepdims=True) + EPS)
        here = center * inverse
        upstream = jnp.where(mine, cot_ref[...].astype(F32), other_ref[...].astype(F32))
        scaled = upstream * vec_ref[6:7, :]
        inner = (
            scaled
            - jnp.mean(scaled, axis=-1, keepdims=True)
            - here * jnp.mean(scaled * here, axis=-1, keepdims=True)
        )
        total_grad = inner * inverse
        total_grad_ref[...] = total_grad
        branch_grad = total_grad.astype(BF)
        branch_grad_ref[...] = branch_grad
        gate_grad = (dot(branch_grad, down_ref[...]) * slope_ref[...]).astype(BF)
        gate_grad_ref[...] = gate_grad
        hidden = jnp.broadcast_to(jnp.sum(gate_grad.astype(F32), axis=0, keepdims=True), (8, 2 * HID))
        bias_ref[...] = hidden + old[2][...] if old else hidden
        first_part_ref[...] = dot_nt(gate_grad, up_ref[...]).astype(BF)

        @pl.when(mine)
        def _():
            out_ref[...] = (here * vec_ref[6:7, :] + vec_ref[7:8, :]).astype(BF)
            sums_ref[...] = jnp.zeros_like(sums_ref)
            sums_ref[0:1, :] = jnp.sum(upstream * here, axis=0, keepdims=True)
            sums_ref[1:2, :] = jnp.sum(upstream, axis=0, keepdims=True)
            sums_ref[2:3, :] = jnp.sum(branch_grad.astype(F32), axis=0, keepdims=True)

        if old:

            @pl.when(jnp.logical_not(mine))
            def _():
                out_ref[...] = old[0][...]
                sums_ref[...] = old[1][...]

        else:

            @pl.when(jnp.logical_not(mine))
            def _():
                out_ref[...] = jnp.zeros_like(out_ref)
                sums_ref[...] = jnp.zeros_like(sums_ref)

    operands = [part, received, normed, slope, *cotangent, vecs, up, down, *earlier]
    outs = [
        struct((rows, D), F32),
        struct((rows, D), BF),
        struct((rows, 2 * HID), BF),
        struct((rows, D), BF),
        struct((rows, D), BF),
        struct((8, D), F32),
        struct((8, 2 * HID), F32),
    ]
    results = call(
        "second_norm",
        body,
        scalars,
        operands,
        [whole(o.shape) for o in operands],
        outs,
        [whole(o.shape) for o in outs],
        (1,),
        micros=5,
    )
    return results[:4], results[4:]


def split_outs(width):
    return [struct((GROUPS // 2, BLOCK, width), BF)] * 2


def feed_forward_grads(scalars, blocks, rows):
    def body(sc, *refs):
        keep_ref, send_ref, result_ref = refs[-3:]
        step = pl.program_id(0)

        @pl.when(step % 2 == 0)
        def _():
            result_ref[...] = dot_tn(refs[0][...], refs[1][...]) + dot_tn(refs[4][...], refs[5][...])

        @pl.when(step % 2 == 1)
        def _():
            result_ref[...] = dot_tn(refs[2][...], refs[3][...]) + dot_tn(refs[6][...], refs[7][...])

        split_rows(result_ref, sc[1], keep_ref, send_ref)

    half = pl.BlockSpec((rows, HID), lambda c, _: (0, c // 2))
    outs = split_outs(4 * HID)
    out_specs = [pl.BlockSpec((GROUPS // 2, BLOCK, HID), lambda c, _: (0, 0, c))] * 2
    return call(
        "feed_forward_grads",
        body,
        scalars,
        [value for block in blocks for value in block],
        [whole((rows, D)), half] * 4,
        outs,
        out_specs,
        (4,),
        [pltpu.VMEM((D, HID), F32)],
        micros=8,
    )


def first_norm(scalars, block, part, received, total_grad, normed, inverse, vecs, out_weight, earlier, rows):
    def body(sc, part_ref, recv_ref, grad_ref, norm_ref, inv_ref, vec_ref, weight_ref, *refs):
        old, refs = refs[: len(earlier)], refs[len(earlier) :]
        attention_ref, context_ref, own_ref, sums_ref = refs[:4]
        mine = sc[0] == block
        upstream = grad_ref[...] + part_ref[...].astype(F32) + recv_ref[...].astype(F32)
        here = norm_ref[...]
        scaled = upstream * vec_ref[3:4, :]
        inner = (
            scaled
            - jnp.mean(scaled, axis=-1, keepdims=True)
            - here * jnp.mean(scaled * here, axis=-1, keepdims=True)
        )
        total = inner * inv_ref[:, :1]
        attention = total.astype(BF)
        attention_ref[...] = attention
        context_ref[...] = dot_nt(attention, weight_ref[...]).astype(BF)
        if block == 1:
            turned = jnp.concatenate([weight_ref[QUARTER:, :], weight_ref[:QUARTER, :]], axis=0)
            refs[4][...] = dot_nt(attention, turned).astype(BF)

        @pl.when(mine)
        def _():
            own_ref[...] = total
            sums_ref[...] = jnp.zeros_like(sums_ref)
            sums_ref[0:1, :] = jnp.sum(upstream * here, axis=0, keepdims=True)
            sums_ref[1:2, :] = jnp.sum(upstream, axis=0, keepdims=True)
            sums_ref[2:3, :] = jnp.sum(attention.astype(F32), axis=0, keepdims=True)

        @pl.when(jnp.logical_not(mine))
        def _():
            own_ref[...] = old[0][...] if old else jnp.zeros_like(own_ref)
            sums_ref[...] = old[1][...] if old else jnp.zeros_like(sums_ref)

    operands = [part, received, total_grad, normed, inverse, vecs, out_weight, *earlier]
    outs = [
        struct((rows, D), BF),
        struct((rows, HALF), BF),
        struct((rows, D), F32),
        struct((8, D), F32),
        struct((rows, HALF), BF),
    ][: 5 if block == 1 else 4]
    return call(
        "first_norm",
        body,
        scalars,
        operands,
        [whole(o.shape) for o in operands],
        outs,
        [whole(o.shape) for o in outs],
        (1,),
        micros=3,
    )


def halves(value):
    high = value.astype(BF).astype(F32)
    return jnp.concatenate([high, value - high], axis=1).astype(BF)


def whole_of(table):
    return table[:, :128].astype(F32) + table[:, 128:].astype(F32)


def output_grads(scalars, blocks, small, small_side):
    def body(sc, *refs):
        small_ref, side_ref, keep_ref, send_ref, result_ref = refs[-5:]
        for side in range(2):
            part = dot_tn(refs[side][...], refs[2][...]) + dot_tn(refs[3 + side][...], refs[5][...])
            for k in range(2):
                at = pl.multiple_of((sc[2] ^ side ^ (2 * k)) * QUARTER, 16)
                result_ref[pl.ds(at, QUARTER), :] = part[k * QUARTER : (k + 1) * QUARTER, :]
        for j in range(GROUPS):
            target = (keep_ref, send_ref)[j % 2]
            block = sc[1] ^ j
            rows = pl.ds(pl.multiple_of(block * BLOCK, 16), BLOCK)
            target[j // 2, :BLOCK] = result_ref[rows, :].astype(BF)
            target[j // 2, BLOCK:] = jnp.zeros((LABELS, D), BF)
            target[j // 2, BLOCK:, :256] = halves(small_ref[block] + side_ref[block])

    outs = [struct((GROUPS // 2, BLOCK + LABELS, D), BF)] * 2
    operands = [value for block in blocks for value in block] + [small, small_side]
    return call(
        "output_grads",
        body,
        scalars,
        operands,
        [whole(o.shape) for o in operands],
        outs,
        [whole(o.shape) for o in outs],
        (1,),
        [pltpu.VMEM((D, D), F32)],
        micros=4,
    )


def attend_backward(scalars, query, key, value, grad_blocks, hot, weight, rows):
    base = 3 * rows
    steps = HALF // PAIR

    def body(sc, q_ref, k_ref, v_ref, far_ref, near_ref, halo_ref, hot_ref, w_ref, *refs):
        out_ref, keep_ref, send_ref, sums_ref, mask_ref, key_ref, value_ref, acc_ref = refs
        step = pl.program_id(0)

        @pl.when(step == 0)
        def _():
            mask_ref[...] = (dot_tn(hot_ref[...], hot_ref[...]) - 1.0) * MASKED

        key_ref[...] = jnp.zeros_like(key_ref)
        value_ref[...] = jnp.zeros_like(value_ref)
        lane = lax.broadcasted_iota(jnp.int32, (1, PAIR), 1)
        query_grads = [jnp.zeros((PAIR, rows), F32), jnp.zeros((PAIR, rows), F32)]
        for head in range(2):
            part = jnp.where((lane // HEAD_DIM) == head, 1.0, 0.0)
            key_turned = (k_ref[...].astype(F32) * part).T.astype(BF)
            for index, (low, high) in enumerate(((0, 2 * rows), (0, base), (rows, base))):
                start = index * rows
                mine = (q_ref[start : start + rows].astype(F32) * (part * HEAD_DIM**-0.5)).astype(BF)
                grads = (far_ref, near_ref, halo_ref)[index][...]
                grads = (grads.astype(F32) * part).astype(BF)
                scores = dot_nt(k_ref[low:high], mine) + mask_ref[low:high, start : start + rows]
                expo = jnp.exp(scores - jnp.max(scores, axis=0, keepdims=True))
                probs = expo * (1.0 / jnp.sum(expo, axis=0, keepdims=True))
                pulled = dot_nt(v_ref[low:high], grads)
                inner = jnp.sum(probs * pulled, axis=0, keepdims=True)
                score_grads = (probs * (pulled - inner)).astype(BF)
                top = min(high, 2 * rows)
                span = top - low
                value_ref[low:top, :] += dot(probs[:span].astype(BF), grads)
                key_ref[low:top, :] += dot(score_grads[:span], mine)
                if index < 2:
                    query_grads[index] = query_grads[index] + dot(key_turned[:, low:high], score_grads)
        for index in range(2):
            turned = (query_grads[index] * HEAD_DIM**-0.5).T.astype(BF)
            out_ref[index * rows : (index + 1) * rows, :PAIR] = turned
        out_ref[:, PAIR : 2 * PAIR] = key_ref[...].astype(BF)
        out_ref[:, 2 * PAIR :] = value_ref[...].astype(BF)
        sums = jnp.sum(out_ref[...].astype(F32), axis=0, keepdims=True)
        sums_ref[...] = jnp.broadcast_to(sums, (8, 3 * PAIR))
        product = dot_nt(out_ref[...], w_ref[...])

        @pl.when(step == 0)
        def _():
            acc_ref[...] = product

        @pl.when(step > 0)
        def _():
            acc_ref[...] += product

        @pl.when(step == steps - 1)
        def _():
            near = sc[0]
            keep_ref[...] = acc_ref[pl.ds(pl.multiple_of(near * rows, rows), rows), :]
            other = acc_ref[pl.ds(pl.multiple_of((1 - near) * rows, rows), rows), :]
            send_ref[...] = other.astype(BF)

    column = lambda height: pl.BlockSpec((height, PAIR), lambda p, _: (0, p))
    operands = [query, key, value, *grad_blocks, hot, weight]
    in_specs = [column(base)] * 3 + [column(rows)] * 3 + [whole(hot.shape)]
    in_specs += [pl.BlockSpec((D, 3 * PAIR), lambda p, _: (0, p))]
    outs = [struct((2 * rows, 3 * HALF), BF), struct((rows, D), F32), struct((rows, D), BF)]
    outs += [struct((8, 3 * HALF), F32)]
    out_specs = [
        pl.BlockSpec((2 * rows, 3 * PAIR), lambda p, _: (0, p)),
        whole((rows, D)),
        whole((rows, D)),
        pl.BlockSpec((8, 3 * PAIR), lambda p, _: (0, p)),
    ]
    scratch = [
        pltpu.VMEM((base, base), F32),
        pltpu.VMEM((2 * rows, PAIR), F32),
        pltpu.VMEM((2 * rows, PAIR), F32),
        pltpu.VMEM((2 * rows, D), F32),
    ]
    return call(
        "attend_backward",
        body,
        scalars,
        operands,
        in_specs,
        outs,
        out_specs,
        (steps,),
        scratch,
        micros=18,
    )


def projection_grads(scalars, x, grads, rows):
    tall = 2 * rows

    def body(sc, x_ref, grad_ref, *refs):
        result_ref = refs[-1]
        result_ref[...] = dot_tn(x_ref[...], grad_ref[...])
        split_rows(result_ref, sc[1], refs[0], refs[1])

    outs = split_outs(3 * HALF)
    out_specs = [pl.BlockSpec((GROUPS // 2, BLOCK, 3 * PAIR), lambda p, _: (0, 0, p))] * 2
    return call(
        "projection_grads",
        body,
        scalars,
        [x, grads],
        [pl.BlockSpec((tall, D), lambda p, _: (0, 0)), pl.BlockSpec((tall, 3 * PAIR), lambda p, _: (0, p))],
        outs,
        out_specs,
        (HALF // PAIR,),
        [pltpu.VMEM((D, 3 * PAIR), F32)],
        micros=5,
    )


def combine(scalars, keep, received):
    count, rows, width = keep.shape
    chunk = width // 3

    def body(_, keep_ref, recv_ref, *refs):
        for k in range(count):
            total = keep_ref[k].astype(F32) + recv_ref[k].astype(F32)
            refs[k][...] = total.astype(refs[k].dtype)

    block = pl.BlockSpec((count, rows, chunk), lambda c, _: (0, 0, c))
    outs = [struct((rows, width), F32)] + [struct((rows, width), BF)] * (count - 1)
    spec = pl.BlockSpec((rows, chunk), lambda c, _: (0, c))
    return list(call(
        "combine",
        body, scalars, [keep, received], [block, block], outs, [spec] * count, (3,)))


def combine_both(scalars, keep, received, out_keep, out_received):
    count, rows, wide = keep.shape
    tall = rows + LABELS

    def body(_, keep_ref, recv_ref, out_keep_ref, out_recv_ref, *refs):
        for k in range(count):
            kind = refs[k].dtype
            refs[k][:rows, :wide] = (keep_ref[k].astype(F32) + recv_ref[k].astype(F32)).astype(kind)
            refs[k][rows:, :wide] = jnp.zeros((LABELS, wide), kind)
            total = out_keep_ref[k, :rows].astype(F32) + out_recv_ref[k, :rows].astype(F32)
            refs[k][:rows, wide:] = total.astype(kind)
            refs[k][rows:, wide:] = jnp.zeros((LABELS, D), kind)
            small = whole_of(out_keep_ref[k, rows:, :256]) + whole_of(out_recv_ref[k, rows:, :256])
            refs[k][rows:, wide : wide + 256] = halves(small).astype(kind)

    outs = [struct((tall, wide + D), F32)] + [struct((tall, wide + D), BF)] * (count - 1)
    return simple("combine_both", body, scalars, [keep, received, out_keep, out_received], outs, 2)


def total_feed(scalars, sums):
    rows = sums[0].shape[0]

    def body(_, *refs):
        keep_ref, send_ref = refs[-2:]
        total = refs[0][...]
        for ref in refs[1:-2]:
            total = total + ref[...].astype(F32)
        keep_ref[...] = total[:, : 2 * HID]
        send_ref[...] = total[:, 2 * HID :].astype(BF)

    outs = [struct((rows, 2 * HID), F32), struct((rows, 2 * HID), BF)]
    return simple("total_feed", body, scalars, sums, outs, 2)


def total_projection(scalars, sums, rows):
    tall = sums[0].shape[0]
    wide = 3 * HALF

    def body(sc, *refs):
        keep_ref, send_ref = refs[-2:]
        total = refs[0][:rows, :]
        for ref in refs[1:-2]:
            total = total + ref[:rows, :].astype(F32)
        near, far = [], []
        for kind in range(3):
            both = [total[:, (3 * p + kind) * PAIR : (3 * p + kind + 1) * PAIR] for p in range(3)]
            both = jnp.concatenate(both, axis=1)
            near.append(both[:, :QUARTER])
            far.append(both[:, QUARTER:])
        near.append(pltpu.roll(total[:, wide:], D - sc[2] * QUARTER, 1)[:, :QUARTER])
        far.append(pltpu.roll(total[:, wide:], D - (sc[2] ^ 2) * QUARTER, 1)[:, :QUARTER])
        keep_ref[:rows, :] = jnp.concatenate(near, axis=1)
        send_ref[:rows, :] = jnp.concatenate(far, axis=1).astype(BF)
        if tall > rows:
            small = jnp.zeros((LABELS, 128), F32)
            for ref in refs[:-2]:
                small = small + whole_of(ref[rows:, wide : wide + 256])
            keep_ref[rows:, :] = jnp.zeros((LABELS, D), F32)
            send_ref[rows:, :] = jnp.zeros((LABELS, D), BF)
            keep_ref[rows:, :128] = small
            send_ref[rows:, :256] = halves(small)

    outs = [struct((tall, D), F32), struct((tall, D), BF)]
    return simple("total_projection", body, scalars, sums, outs, 2)


def finish_feed(scalars, keep, received):
    rows = keep.shape[0]

    def body(_, keep_ref, recv_ref, up_ref, down_ref):
        up_ref[...] = keep_ref[:, :HID] + recv_ref[:, :HID].astype(F32)
        down_ref[...] = keep_ref[:, HID:] + recv_ref[:, HID:].astype(F32)

    outs = [struct((rows, HID), F32)] * 2
    return simple("finish_feed", body, scalars, [keep, received], outs)


def finish_projection(scalars, keep, received, rows):
    tall = keep.shape[0]

    def body(_, keep_ref, recv_ref, *refs):
        total = keep_ref[:rows, :] + recv_ref[:rows, :].astype(F32)
        for k in range(4):
            refs[k][...] = total[:, k * QUARTER : (k + 1) * QUARTER]
        if tall > rows:
            refs[4][...] = keep_ref[rows:, :128] + whole_of(recv_ref[rows:, :256])

    outs = [struct((rows, QUARTER), F32)] * 4 + ([struct((LABELS, 128), F32)] if tall > rows else [])
    return simple("finish_projection", body, scalars, [keep, received], outs)


def small_sums(scalars, sums_one, sums_two, sums_hidden, sums_projection):
    def body(sc, one_ref, two_ref, hidden_ref, projection_ref, out_ref, wide_ref, tall_ref):
        out_ref[...] = jnp.zeros_like(out_ref)
        lanes = lax.broadcasted_iota(jnp.int32, (1, D), 1)
        near, far = lanes < QUARTER, (lanes >= QUARTER) & (lanes < HALF)
        for row, kind in ((0, 0), (1, 2)):
            line = jnp.concatenate(
                [
                    projection_ref[0:1, (3 * p + kind) * PAIR : (3 * p + kind + 1) * PAIR]
                    for p in range(3)
                ]
                + [jnp.zeros((1, HALF), F32)],
                axis=1,
            )
            low = pltpu.roll(jnp.broadcast_to(jnp.where(near, line, 0.0), (8, D)), sc[2] * QUARTER, 1)
            high = jnp.broadcast_to(jnp.where(far, line, 0.0), (8, D))
            high = pltpu.roll(high, D - QUARTER + (sc[2] ^ 2) * QUARTER, 1)
            wide_ref[row : row + 1, :] = (low + high)[0:1]
        wide_ref[2:3, :] = one_ref[2:3, :]
        wide_ref[3:5, :] = one_ref[0:2, :]
        wide_ref[5:6, :] = two_ref[2:3, :]
        wide_ref[6:8, :] = two_ref[0:2, :]
        tall_ref[...] = jnp.zeros_like(tall_ref)
        for k in range(2):
            to = pl.multiple_of((sc[2] ^ (2 * k)) * HID, 128)
            tall_ref[0:1, pl.ds(to, HID)] = hidden_ref[0:1, k * HID : (k + 1) * HID]
        share = FF // GROUPS
        for d in range(GROUPS):
            out_ref[d, :VECS, :BLOCK] = wide_ref[:, d * BLOCK : (d + 1) * BLOCK]
            for c in range(share // 128):
                at = d * share + c * 128
                out_ref[d, VECS + c : VECS + c + 1, :] = tall_ref[0:1, at : at + 128]

    operands = [sums_one, sums_two, sums_hidden, sums_projection]
    shape = (GROUPS, LABELS, 128)
    return call(
        "small_sums",
        body,
        scalars,
        operands,
        [whole(o.shape) for o in operands],
        [struct(shape, F32)],
        [whole(shape)],
        (1,),
        [pltpu.VMEM((VECS, D), F32), pltpu.VMEM((8, FF), F32)],
    )[0]


def per_device(
    tokens,
    segments,
    query_weight,
    key_weight,
    value_weight,
    output_weight,
    query_bias,
    value_bias,
    output_bias,
    first_gain,
    first_shift,
    up_weight,
    up_bias,
    down_weight,
    down_bias,
    second_gain,
    second_shift,
    cotangent,
):
    seq_count = lax.axis_size("seq")
    count = lax.axis_size("dp")
    place_z = lax.axis_index("seq")
    assert seq_count == 4
    direct = count == GROUPS
    rows = tokens.shape[1]
    piece_rows = query_weight.shape[0]
    near = (place_z == 1) | (place_z == 2)
    base = lax.axis_index("dp") if direct else 0
    scalars = jnp.stack([near, base, place_z]).astype(jnp.int32)

    narrow = pack_narrow(scalars, [query_weight, key_weight, value_weight])
    narrow_far = swap(narrow, "seq", 2)
    output_side = swap(output_weight, "seq", 1)
    own = tokens[0]
    labelled, own_docs = label_rows(scalars, own, segments)
    wide = pack_wide(scalars, up_weight, down_weight.T, output_weight, output_side)
    wide_far = swap(wide, "seq", 2)
    partner = swap(labelled, "seq", 1)
    narrow_far, labelled = together(narrow_far, labelled)
    halo_near = lax.ppermute(labelled, "seq", [(1, 2), (2, 1)])
    halo_far = lax.ppermute(labelled, "seq", [(1, 3), (2, 0)])
    cot_own = cotangent[0]

    lines = [
        query_bias,
        value_bias,
        output_bias,
        first_gain,
        first_shift,
        down_bias,
        second_gain,
        second_shift,
    ]
    lines = [line[None] for line in lines] if direct else []
    columns = pack_columns(scalars, narrow, narrow_far, lines, up_bias[None])
    feed_piece = pack_feed(scalars, wide, wide_far)

    if direct:
        chip = chip_pieces(columns)
        projection_pieces, feed_piece = together(core_pieces(chip), feed_piece)
        feed_chip = chip_pieces(feed_piece)
    else:

        def label(table, line):
            table = jnp.pad(table, ((0, LABELS - table.shape[0]), (0, D - table.shape[1])))
            line = jnp.pad(line[None], ((0, LABELS - 1), (0, 0)))
            return jnp.concatenate([table, line], axis=1)

        vectors = jnp.stack(
            [
                query_bias,
                value_bias,
                output_bias,
                first_gain,
                first_shift,
                down_bias,
                second_gain,
                second_shift,
            ]
        )
        lines = lax.all_gather(vectors, "dp", axis=1, tiled=True).reshape(VECS, GROUPS, BLOCK)
        hidden_lines = lax.all_gather(up_bias, "dp", axis=0, tiled=True).reshape(GROUPS, -1)
        projection_pieces = [
            jnp.concatenate([block, label(lines[:, k], hidden_lines[k])], axis=0)
            for k, block in enumerate(gather_rows(columns))
        ]
        feed_chip = gather_rows(feed_piece)

    def rows_of(keep, send):
        return jnp.stack([keep, send], axis=1).reshape(GROUPS, -1, keep.shape[2]).astype(F32)

    def spread(sums):
        return [sums[0]] + [swap(sums[k], "dp", 2 * k) for k in range(1, len(sums))]

    def scattered(table):
        return [lax.psum_scatter(table, "dp", scatter_dimension=0, tiled=True)]

    query, key, value, *ctx_mine, x, weight, hot, vecs, hidden_bias = qkv_attend(
        scalars, own, partner, halo_near, halo_far, own_docs, projection_pieces, rows
    )
    ctx_mine, feed_chip[1:3], cot_own = together(ctx_mine, feed_chip[1:3], cot_own)
    ctx_partner = [None, None]
    ctx_partner[1] = swap(ctx_mine[1], "seq", 1)
    ctx_partner[0] = swap(ctx_mine[0], "seq", 1)
    ctx_partner, feed_chip = together(ctx_partner, feed_chip)
    weights = core_pieces(feed_chip) if direct else feed_chip
    cot_partner = swap(cot_own, "seq", 1)

    forward, slopes, part_far = [None, None], [None, None], [None, None]
    for block in (1, 0):
        forward[block], weights = feed_forward(
            scalars, block, ctx_mine[block], ctx_partner[block], x, vecs, hidden_bias, weights, rows
        )
        part_far[block] = swap(forward[block][5], "seq", 1)
    up, down, out_mine, _ = weights
    second, second_shared, first_part_far = [None, None], [], [None, None]
    for block in (1, 0):
        slopes[block] = gelu_slope(scalars, forward[block][3])
    for block in (1, 0):
        second[block], second_shared = second_norm(
            scalars,
            block,
            forward[block][5],
            part_far[block],
            forward[block][0],
            slopes[block],
            (cot_own, cot_partner),
            vecs,
            up,
            down,
            second_shared,
            rows,
        )
        if block == 1:
            first_part_far[block] = swap(second[block][3], "seq", 1)
    feed_parts = feed_forward_grads(
        scalars,
        [(forward[k][2], second[k][2], second[k][1], forward[k][4]) for k in range(2)],
        rows,
    )
    first_part_far[1], second, second_shared, feed_parts = together(
        first_part_far[1], second, second_shared, feed_parts
    )
    first_part_far[0] = swap(second[0][3], "seq", 1)
    layer_output, sums_two, sums_hidden = second_shared
    attention_grad, ctx_grad, first_shared = [None, None], [None, None], []

    def finish(block):
        attention_grad[block], ctx_grad[block], *shared = first_norm(
            scalars,
            block,
            second[block][3],
            first_part_far[block],
            second[block][0],
            forward[block][0],
            forward[block][1],
            vecs,
            out_mine,
            first_shared,
            rows,
        )
        return shared

    *first_shared, halo_send = finish(1)
    halo_grad = swap(halo_send, "seq", 2)
    if direct:
        feed_sums = combine(scalars, feed_parts[0], swap(feed_parts[1], "dp", 1))
        feed_sums[3], halo_grad = together(feed_sums[3], halo_grad)
        feed_sums, first_part_far[0] = together(feed_sums, first_part_far[0])
        feed_sums = spread(feed_sums)
    else:
        feed_sums = scattered(rows_of(*feed_parts).reshape(D, -1))
    own_grad, sums_one = finish(0)

    grads, input_keep, input_send, sums_projection = attend_backward(
        scalars, query, key, value, [*ctx_grad, halo_grad], hot, weight, rows
    )
    grads, sums_projection, input_send, feed_sums[1:3] = together(
        grads, sums_projection, input_send, feed_sums[1:3]
    )
    input_far = swap(input_send, "seq", 1)
    small = small_sums(scalars, sums_one, sums_two, sums_hidden, sums_projection)
    small_side = swap(small, "seq", 1)
    projection_parts = projection_grads(scalars, x, grads, rows)
    projection_parts, small_side, feed_sums = together(projection_parts, small_side, feed_sums)
    out_blocks = [(ctx_mine[k], ctx_partner[k], attention_grad[k]) for k in range(2)]
    if direct:
        projection_received = swap(projection_parts[1], "dp", 1)
        out_parts = output_grads(scalars, out_blocks, small, small_side)
        out_received = swap(out_parts[1], "dp", 1)
        feed_keep, feed_send = total_feed(scalars, feed_sums)
        feed_far = swap(feed_send, "seq", 2)
        sums = spread(
            combine_both(scalars, projection_parts[0], projection_received, out_parts[0], out_received)
        )
    else:
        out_parts = rows_of(*output_grads(scalars, out_blocks, small, small_side))
        sums = scattered(
            jnp.concatenate(
                [rows_of(*projection_parts).reshape(D, -1), out_parts[:, :BLOCK].reshape(D, -1)], axis=1
            )
        )
        feed_keep, feed_send = total_feed(scalars, feed_sums)
        feed_far = swap(feed_send, "seq", 2)
    up_grad, down_grad = finish_feed(scalars, feed_keep, feed_far)
    input_grad = own_grad + input_keep + input_far.astype(F32)
    if direct:
        sums, up_grad, input_grad = together(sums, up_grad, input_grad)
    keep, send = total_projection(scalars, sums, piece_rows)
    projections = list(finish_projection(scalars, keep, swap(send, "seq", 2), piece_rows))
    if direct:
        tile = projections.pop()
        wide_lines, tall_lines = tile[:VECS, :BLOCK], tile[VECS : VECS + 3].reshape(-1)
    else:
        tile = out_parts[:, BLOCK:, :128] + out_parts[:, BLOCK:, 128:256]
        tile = tile + swap(tile, "seq", 2)
        wide_lines = tile[:, :VECS, :BLOCK].transpose(1, 0, 2).reshape(VECS, D)
        wide_lines = lax.psum_scatter(wide_lines, "dp", scatter_dimension=1, tiled=True)
        tall_lines = lax.psum_scatter(tile[:, VECS : VECS + 3].reshape(-1), "dp", tiled=True)
    vec = [wide_lines[k] for k in range(VECS)]
    return (
        layer_output[None],
        input_grad[None],
        *projections,
        vec[0],
        vec[1],
        vec[2],
        vec[3],
        vec[4],
        up_grad,
        tall_lines,
        down_grad.T,
        vec[5],
        vec[6],
        vec[7],
    )


def solution(mesh):
    placed = (
        P("dp", "seq", None),
        P("dp", "seq"),
        P("dp", "seq"),
        P("dp", "seq"),
        P("dp", "seq"),
        P("dp", "seq"),
        P("dp"),
        P("dp"),
        P("dp"),
        P("dp"),
        P("dp"),
        P("dp", "seq"),
        P("dp"),
        P("seq", "dp"),
        P("dp"),
        P("dp"),
        P("dp"),
        P("dp", "seq", None),
    )
    return jax.shard_map(
        per_device,
        mesh=mesh,
        in_specs=placed,
        out_specs=(
            P("dp", "seq", None),
            P("dp", "seq", None),
            P("dp", "seq"),
            P("dp", "seq"),
            P("dp", "seq"),
            P("dp", "seq"),
            P("dp"),
            P("dp"),
            P("dp"),
            P("dp"),
            P("dp"),
            P("dp", "seq"),
            P("dp"),
            P("seq", "dp"),
            P("dp"),
            P("dp"),
            P("dp"),
        ),
        check_vma=False,
    )
```

```python
import jax
import jax.numpy as jnp
from jax import lax
from jax.experimental import pallas as pl
from jax.experimental.pallas import tpu as pltpu
from jax.sharding import PartitionSpec as P

D = 768
HEADS = 12
HEAD_DIM = 64
FF = 3072
EPS = 1e-05
MASKED = 1e30
PAIR = 2 * HEAD_DIM
QUARTER = D // 4
HALF = D // 2
HID = FF // 4
VECS = 8
GROUPS = 8
BLOCK = D // GROUPS
LABELS = 16
MARKS = 48
MICROS = 450
BF = jnp.bfloat16
F32 = jnp.float32
ROOT_HALF = 0.7071067811865476
ROOT_TWO_PI = 0.3989422804014327


def dot(a, b):
    return lax.dot_general(a, b, (((1,), (0,)), ((), ())), preferred_element_type=F32)


def dot_nt(a, b):
    return lax.dot_general(a, b, (((1,), (1,)), ((), ())), preferred_element_type=F32)


def dot_tn(a, b):
    return lax.dot_general(a, b, (((0,), (0,)), ((), ())), preferred_element_type=F32)


def swap(value, axis, mask):
    count = lax.axis_size(axis)
    return lax.ppermute(value, axis, [(k, k ^ mask) for k in range(count)])


def together(*values):
    return lax.optimization_barrier(values)


def whole(shape):
    return pl.BlockSpec(shape, lambda *_: (0,) * len(shape))


def params():
    return pltpu.CompilerParams(vmem_limit_bytes=22 * 1024 * 1024)


def call(name, body, scalars, operands, in_specs, outs, out_specs, grid, scratch=(), micros=1):
    spec = pltpu.PrefetchScalarGridSpec(
        num_scalar_prefetch=1,
        grid=grid,
        in_specs=in_specs,
        out_specs=out_specs,
        scratch_shapes=list(scratch),
    )
    return pl.pallas_call(
        body,
        out_shape=outs,
        grid_spec=spec,
        compiler_params=params(),
        cost_estimate=pl.CostEstimate(
            flops=int(micros * 1.0e7), transcendentals=0, bytes_accessed=1024
        ),
        name=name,
    )(scalars, *operands)


def struct(shape, dtype):
    return jax.ShapeDtypeStruct(shape, dtype)


def chip_pieces(piece):
    return [piece] + [swap(piece, "dp", j) for j in range(2, GROUPS, 2)]


def gather_rows(piece):
    full = lax.all_gather(piece, "dp", axis=0, tiled=True)
    full = full.reshape(GROUPS, D // GROUPS, piece.shape[1])
    return [full[0::2], full[1::2]]


def place(target, pair, base, source_cols, target_cols):
    for j in range(GROUPS):
        start = pl.multiple_of((base ^ j) * BLOCK, 16)
        target[pl.ds(start, BLOCK), target_cols] = pair[j % 2][j // 2, :BLOCK, source_cols]


def split_rows(result, base, keep, send):
    for j in range(GROUPS):
        block = result[pl.ds(pl.multiple_of((base ^ j) * BLOCK, 16), BLOCK), :].astype(BF)
        if j % 2:
            send[j // 2] = block
        else:
            keep[j // 2] = block


def simple(name, body, scalars, operands, outs, micros=1):
    return call(
        name,
        body,
        scalars,
        operands,
        [whole(o.shape) for o in operands],
        outs,
        [whole(o.shape) for o in outs],
        (1,),
        micros=micros,
    )


def pack_inputs(scalars, tables, tokens, segments, up, down, lines, tall):
    rows = tokens.shape[0]
    height = tables[0].shape[0]
    extra = LABELS if lines else 0
    operands = list(tables) + [tokens, segments, up, down] + lines + ([tall] if lines else [])
    count = len(operands)

    def body(_, *refs):
        sources, (send_ref, mine_ref, wide_ref, label_ref, docs_ref), refs = (
            refs[:count],
            refs[count : count + 5],
            refs[count + 5 :],
        )
        copies = [pltpu.make_async_copy(a, b, refs[-1].at[k]) for k, (a, b) in enumerate(zip(sources, refs))]
        for copy in copies:
            copy.start()
        for copy in copies:
            copy.wait()
        joined = jnp.concatenate([ref[...].astype(F32) for ref in refs[:4]], axis=1).astype(BF)
        send_ref[...] = joined
        mine_ref[:height, :HID] = refs[6][...]
        mine_ref[:height, HID : 2 * HID] = refs[7][...]
        mine_ref[:height, 2 * HID :] = joined[:, : 3 * QUARTER]
        wide_ref[:, :HID] = refs[6][...]
        wide_ref[:, HID:] = refs[7][...]
        docs = refs[5][...].astype(F32)
        docs_ref[...] = docs
        label_ref[:rows, :] = refs[4][...]
        label_ref[rows:, :] = jnp.zeros((MARKS, D), BF)
        label_ref[rows:, :rows] = jnp.broadcast_to(docs, (MARKS, rows)).astype(BF)
        if lines:
            share = FF // GROUPS
            table = [ref[...].astype(F32) for ref in refs[8 : 8 + VECS]]
            table = jnp.concatenate(table, axis=0)
            table = jnp.concatenate([table, jnp.zeros((VECS, share - BLOCK), F32)], axis=1)
            line = jnp.broadcast_to(refs[8 + VECS][...].astype(F32), (VECS, share))
            mine_ref[height:, :] = jnp.zeros((LABELS, 3 * QUARTER + 2 * HID), BF)
            mine_ref[height:, 2 * HID : 2 * HID + share] = jnp.concatenate([table, line], axis=0).astype(BF)

    outs = [
        struct((height, D), BF),
        struct((height + extra, 3 * QUARTER + 2 * HID), BF),
        struct((height, 2 * HID), BF),
        struct((rows + MARKS, D), BF),
        struct((1, rows), F32),
    ]
    operands = [pltpu.with_memory_space_constraint(o, pltpu.MemorySpace.HBM) for o in operands]
    return call(
        "pack_inputs",
        body,
        scalars,
        operands,
        [pl.BlockSpec(memory_space=pltpu.MemorySpace.HBM)] * count,
        outs,
        [whole(o.shape) for o in outs],
        (1,),
        [pltpu.VMEM(o.shape, o.dtype) for o in operands] + [pltpu.SemaphoreType.DMA((count,))],
    )


def split_arrived(scalars, arrived, wide, side, mine):
    rows, tall = arrived.shape[0], mine.shape[0]

    def body(_, far_ref, wide_ref, side_ref, mine_ref, narrow_ref, out_ref, both_ref):
        narrow_ref[...] = far_ref[:, : 3 * QUARTER]
        out_ref[:, : 2 * HID] = wide_ref[...]
        out_ref[:, 2 * HID :] = side_ref[...]
        both_ref[:tall, :] = mine_ref[:, 2 * HID :]
        both_ref[tall:, :] = far_ref[:, : 3 * QUARTER]

    outs = [
        struct((rows, 3 * QUARTER), BF),
        struct((rows, 2 * HID + QUARTER), BF),
        struct((rows + tall, 3 * QUARTER), BF),
    ]
    return simple("split_arrived", body, scalars, [arrived, wide, side, mine], outs)


def stack_narrow(scalars, mine_chip, far_chip, both_far):
    tall = mine_chip[0].shape[0]
    rows = far_chip[0].shape[0]

    def body(_, *refs):
        out_ref = refs[-1]
        for k in range(3):
            out_ref[k, :tall] = refs[k][:, 2 * HID :]
            out_ref[k, tall:] = refs[3 + k][...]
        out_ref[3] = refs[6][...]

    shape = (GROUPS // 2, tall + rows, 3 * QUARTER)
    operands = [*mine_chip, *far_chip, both_far]
    return simple("stack_narrow", body, scalars, operands, [struct(shape, BF)])[0]


def stack_wide(scalars, mine_chip, last, feed_chip):
    def body(_, *refs):
        out_ref = refs[-1]
        for k in range(3):
            out_ref[k, :, : 2 * HID] = refs[k][:BLOCK, : 2 * HID]
        out_ref[3, :, : 2 * HID] = refs[3][...]
        for k in range(4):
            out_ref[k, :, 2 * HID :] = refs[4 + k][...]

    shape = (GROUPS // 2, BLOCK, 4 * HID + D)
    return simple("stack_wide", body, scalars, [*mine_chip, last, *feed_chip], [struct(shape, BF)])[0]


def pack_feed(scalars, wide_far, first_send, arrived, side):
    rows = wide_far.shape[0]
    last = slice(3 * QUARTER, D)

    def body(sc, far_ref, own_ref, arrived_ref, side_ref, out_ref):
        out_ref[:, : 2 * HID] = far_ref[:, : 2 * HID]
        total = jnp.zeros((rows, D), F32)
        for k, part in enumerate(
            [own_ref[:, last], side_ref[...], arrived_ref[:, last], far_ref[:, 2 * HID :]]
        ):
            part = jnp.concatenate([part.astype(F32), jnp.zeros((rows, D - QUARTER), F32)], axis=1)
            total = total + pltpu.roll(part, (sc[2] ^ k) * QUARTER, 1)
        out_ref[:, 2 * HID :] = total.astype(BF)

    out = struct((rows, 2 * HID + D), BF)
    return simple("pack_feed", body, scalars, [wide_far, first_send, arrived, side], [out])[0]


def mark(docs, rows):
    number = lax.broadcasted_iota(jnp.int32, (LABELS, rows), 0).astype(F32)
    return jnp.where(jnp.broadcast_to(docs, (LABELS, rows)) == number, 1.0, 0.0).astype(BF)


def attend(query, key, value, mask):
    lane = lax.broadcasted_iota(jnp.int32, (1, PAIR), 1)
    total = jnp.zeros(query.shape, F32)
    for head in range(2):
        part = jnp.where((lane // HEAD_DIM) == head, 1.0, 0.0)
        mine = (query.astype(F32) * (part * HEAD_DIM**-0.5)).astype(BF)
        scores = dot_nt(mine, key) + mask
        expo = jnp.exp(scores - jnp.max(scores, axis=-1, keepdims=True))
        probs = expo * (1.0 / jnp.sum(expo, axis=-1, keepdims=True))
        total = total + dot(probs.astype(BF), value) * part
    return total.astype(BF)


def column(height):
    return pl.BlockSpec((height, PAIR), lambda p, _: (0, p))


def attend_pair(scalars, own, partner, own_docs, pieces, rows):
    base = 2 * rows
    tall = BLOCK + LABELS

    def body(sc, own_ref, partner_ref, docs_ref, *refs):
        weight_refs, refs = refs[:2], refs[2:]
        q_ref, k_ref, v_ref, ctx_ref, x_ref, w_ref, hot_ref, vec_ref, hidden_ref, bias_ref, mask_ref = refs
        step = pl.program_id(0)

        @pl.when(step == 0)
        def _():
            near = sc[0]
            own_at = pl.multiple_of(near * rows, rows)
            partner_at = pl.multiple_of((1 - near) * rows, rows)
            x_ref[pl.ds(own_at, rows), :] = own_ref[...]
            x_ref[pl.ds(partner_at, rows), :] = partner_ref[:rows, :]
            hot_ref[:, pl.ds(own_at, rows)] = mark(docs_ref[...], rows)
            docs = partner_ref[rows : rows + 1, :rows].astype(F32)
            hot_ref[:, pl.ds(partner_at, rows)] = mark(docs, rows)
            for j in range(GROUPS):
                at = pl.ds(pl.multiple_of((sc[1] ^ j) * BLOCK, 16), BLOCK)
                for kind in range(3):
                    part = slice(kind * QUARTER, (kind + 1) * QUARTER)
                    both = [weight_refs[j % 2][j // 2, top : top + BLOCK, part] for top in (0, tall)]
                    both = [half.astype(F32) for half in both]
                    both = jnp.concatenate(both, axis=1).astype(BF)
                    for p in range(3):
                        to = (3 * p + kind) * PAIR
                        w_ref[at, to : to + PAIR] = both[:, p * PAIR : (p + 1) * PAIR]
            hot = hot_ref[...]
            mask_ref[...] = (dot_tn(hot[:, :rows], hot) - 1.0) * MASKED
            vectors = jnp.zeros((LABELS, D), F32)
            for j in range(GROUPS):
                block = sc[1] ^ j
                line = weight_refs[j % 2][j // 2, BLOCK:tall, : FF // GROUPS].astype(F32)
                table = jnp.where(lax.broadcasted_iota(jnp.int32, line.shape, 1) < BLOCK, line, 0.0)
                table = jnp.concatenate([table, jnp.zeros((LABELS, D - FF // GROUPS), F32)], axis=1)
                vectors = vectors + pltpu.roll(table, block * BLOCK, 1)
                quarter = block // 2
                for k in range(2):

                    @pl.when(quarter == sc[2] ^ (2 * k))
                    def _():
                        to = pl.multiple_of((block % 2) * (HID // 2) + k * HID, 128)
                        hidden_ref[:, pl.ds(to, HID // 2)] = line[VECS:]

            vec_ref[...] = vectors[:VECS]
            lanes = lax.broadcasted_iota(jnp.int32, (VECS, HALF), 1)
            low = pltpu.roll(vectors[:VECS], D - sc[2] * QUARTER, 1)[:, :HALF]
            high = pltpu.roll(vectors[:VECS], D + QUARTER - (sc[2] ^ 2) * QUARTER, 1)[:, :HALF]
            bias_ref[...] = jnp.where(lanes < QUARTER, low, high)

        at = pl.multiple_of(step * 3 * PAIR, PAIR)
        both = dot(x_ref[...], w_ref[:, pl.ds(at, 3 * PAIR)])
        bias = bias_ref[:, pl.ds(pl.multiple_of(step * PAIR, PAIR), PAIR)]
        query = (both[:, :PAIR] + bias[0:1]).astype(BF)
        key = both[:, PAIR : 2 * PAIR].astype(BF)
        value = (both[:, 2 * PAIR :] + bias[1:2]).astype(BF)
        q_ref[...] = query
        k_ref[...] = key
        v_ref[...] = value
        ctx_ref[...] = attend(query[:rows], key, value, mask_ref[...])

    operands = [own, partner, own_docs, *pieces]
    in_specs = [whole(o.shape) for o in operands]
    outs = [
        struct((base, HALF), BF),
        struct((base, HALF), BF),
        struct((base, HALF), BF),
        struct((rows, HALF), BF),
        struct((base, D), BF),
        struct((D, 3 * HALF), BF),
        struct((LABELS, base), BF),
        struct((VECS, D), F32),
        struct((VECS, 2 * HID), F32),
        struct((VECS, HALF), F32),
    ]
    out_specs = [column(base)] * 3 + [column(rows)] + [whole(o.shape) for o in outs[4:]]
    return call(
        "attend_pair",
        body,
        scalars,
        operands,
        in_specs,
        outs,
        out_specs,
        (HALF // PAIR,),
        [pltpu.VMEM((rows, base), F32)],
        micros=8,
    )


def attend_halo(scalars, halo_near, halo_far, weight, bias, hot, query, key, value, rows):
    def body(sc, near_ref, far_ref, w_ref, bias_ref, hot_ref, q_ref, k_ref, v_ref, *refs):
        halo_refs, (ctx_ref, all_ref, x_ref, mask_ref) = refs[:3], refs[3:]

        @pl.when(pl.program_id(0) == 0)
        def _():
            all_ref[:, : 2 * rows] = hot_ref[...]

            def halo(ref):
                x_ref[...] = ref[:rows, :]
                all_ref[:, 2 * rows :] = mark(ref[rows : rows + 1, :rows].astype(F32), rows)

            pl.when(sc[0] == 1)(lambda: halo(near_ref))
            pl.when(sc[0] == 0)(lambda: halo(far_ref))
            mask_ref[...] = (dot_tn(all_ref[:, rows : 2 * rows], all_ref[...]) - 1.0) * MASKED

        both = dot(x_ref[...], w_ref[...])
        parts = [
            (both[:, :PAIR] + bias_ref[0:1, :]).astype(BF),
            both[:, PAIR : 2 * PAIR].astype(BF),
            (both[:, 2 * PAIR :] + bias_ref[1:2, :]).astype(BF),
        ]
        for ref, part in zip(halo_refs, parts):
            ref[...] = part
        keys = jnp.concatenate([k_ref[...], parts[1]], axis=0)
        values = jnp.concatenate([v_ref[...], parts[2]], axis=0)
        ctx_ref[...] = attend(q_ref[rows:, :], keys, values, mask_ref[...])

    operands = [halo_near, halo_far, weight, bias, hot, query, key, value]
    in_specs = [whole(o.shape) for o in operands]
    in_specs[2] = pl.BlockSpec((D, 3 * PAIR), lambda p, _: (0, p))
    in_specs[3] = column(VECS)
    in_specs[5:] = [column(2 * rows)] * 3
    outs = [struct((rows, HALF), BF)] * 4 + [struct((LABELS, 3 * rows), BF)]
    return call(
        "attend_halo",
        body,
        scalars,
        operands,
        in_specs,
        outs,
        [column(rows)] * 4 + [whole((LABELS, 3 * rows))],
        (HALF // PAIR,),
        [pltpu.VMEM((rows, D), BF), pltpu.VMEM((rows, 3 * rows), F32)],
        micros=6,
    )


def feed_forward(scalars, block, ctx_mine, ctx_partner, x, vecs, up_bias, weights, rows):
    count = len(weights)
    fresh = len(weights[0].shape) == 3

    def body(sc, mine_ref, partner_ref, x_ref, vec_ref, bias_ref, *refs):
        weight_refs, refs = refs[:count], refs[count:]
        (norm_ref, inv_ref, first_ref, gate_ref, active_ref, part_ref), refs = refs[:6], refs[6:]
        if fresh:
            up_ref, down_ref, out_ref, other_ref, full_ref = refs
            for k in range(2):
                at, to = 2 * k * HID, slice(k * HID, (k + 1) * HID)
                place(up_ref, weight_refs, sc[1], slice(at, at + HID), to)
                place(down_ref, weight_refs, sc[1], slice(at + HID, at + 2 * HID), to)
            place(full_ref, weight_refs, sc[1], slice(4 * HID, 4 * HID + D), slice(None))
            for ref, flip in ((out_ref, 0), (other_ref, 1)):
                for k in range(2):
                    at = pl.multiple_of((sc[2] ^ flip ^ (2 * k)) * QUARTER, 16)
                    ref[k * QUARTER : (k + 1) * QUARTER, :] = full_ref[pl.ds(at, QUARTER), :]
        else:
            up_ref, down_ref, out_ref, other_ref = weight_refs

        attention = dot(mine_ref[...], out_ref[...]) + dot(partner_ref[...], other_ref[...])
        total = x_ref[...].astype(F32) + (attention + vec_ref[2:3, :])
        center = total - jnp.mean(total, axis=-1, keepdims=True)
        inverse = lax.rsqrt(jnp.mean(center * center, axis=-1, keepdims=True) + EPS)
        normed = center * inverse
        norm_ref[...] = normed
        inv_ref[...] = jnp.broadcast_to(inverse, (rows, 128))
        first = (normed * vec_ref[3:4, :] + vec_ref[4:5, :]).astype(BF)
        first_ref[...] = first
        gate = dot(first, up_ref[...]) + bias_ref[0:1, :]
        gate_ref[...] = gate
        active = (gate * (1.0 + lax.erf(gate * ROOT_HALF)) * 0.5).astype(BF)
        active_ref[...] = active
        part_ref[...] = dot_nt(active, down_ref[...]).astype(BF)

    operands = [ctx_mine, ctx_partner, x, vecs, up_bias, *weights]
    in_specs = [whole(o.shape) for o in operands]
    in_specs[2] = pl.BlockSpec((rows, D), lambda *_: (block, 0))
    outs = [
        struct((rows, D), F32),
        struct((rows, 128), F32),
        struct((rows, D), BF),
        struct((rows, 2 * HID), F32),
        struct((rows, 2 * HID), BF),
        struct((rows, D), BF),
    ]
    scratch = []
    if fresh:
        outs += [struct((D, 2 * HID), BF)] * 2 + [struct((HALF, D), BF)] * 2
        scratch = [pltpu.VMEM((D, D), BF)]
    results = call(
        "feed_forward",
        body,
        scalars,
        operands,
        in_specs,
        outs,
        [whole(o.shape) for o in outs],
        (1,),
        scratch,
        micros=6,
    )
    return results[:6], (results[6:] if fresh else weights)


def gelu_slope(scalars, gate):
    rows = gate.shape[0] // 2

    def body(_, gate_ref, slope_ref):
        gate_here = gate_ref[...]
        bell = jnp.exp(gate_here * gate_here * -0.5) * ROOT_TWO_PI
        slope_ref[...] = 0.5 * (1.0 + lax.erf(gate_here * ROOT_HALF)) + gate_here * bell

    spec = pl.BlockSpec((rows, gate.shape[1]), lambda r, _: (r, 0))
    return call(
        "gelu_slope", body, scalars, [gate], [spec], [struct(gate.shape, F32)], [spec], (2,), micros=3
    )[0]


def second_norm(scalars, block, part, received, normed, slope, cotangent, vecs, up, down, earlier, rows):
    def body(sc, part_ref, recv_ref, norm_ref, slope_ref, cot_ref, other_ref, vec_ref, up_ref, down_ref, *refs):
        old, refs = refs[: len(earlier)], refs[len(earlier) :]
        (total_grad_ref, branch_grad_ref, gate_grad_ref, first_part_ref, out_ref, sums_ref, bias_ref) = refs
        mine = sc[0] == block
        first = norm_ref[...] * vec_ref[3:4, :] + vec_ref[4:5, :]
        branch = part_ref[...].astype(F32) + recv_ref[...].astype(F32) + vec_ref[5:6, :]
        total = first + branch
        center = total - jnp.mean(total, axis=-1, keepdims=True)
        inverse = lax.rsqrt(jnp.mean(center * center, axis=-1, keepdims=True) + EPS)
        here = center * inverse
        upstream = jnp.where(mine, cot_ref[...].astype(F32), other_ref[...].astype(F32))
        scaled = upstream * vec_ref[6:7, :]
        inner = (
            scaled
            - jnp.mean(scaled, axis=-1, keepdims=True)
            - here * jnp.mean(scaled * here, axis=-1, keepdims=True)
        )
        total_grad = inner * inverse
        total_grad_ref[...] = total_grad
        branch_grad = total_grad.astype(BF)
        branch_grad_ref[...] = branch_grad
        gate_grad = (dot(branch_grad, down_ref[...]) * slope_ref[...]).astype(BF)
        gate_grad_ref[...] = gate_grad
        hidden = jnp.broadcast_to(jnp.sum(gate_grad.astype(F32), axis=0, keepdims=True), (8, 2 * HID))
        bias_ref[...] = hidden + old[2][...] if old else hidden
        first_part_ref[...] = dot_nt(gate_grad, up_ref[...]).astype(BF)

        @pl.when(mine)
        def _():
            out_ref[...] = (here * vec_ref[6:7, :] + vec_ref[7:8, :]).astype(BF)
            sums_ref[...] = jnp.zeros_like(sums_ref)
            sums_ref[0:1, :] = jnp.sum(upstream * here, axis=0, keepdims=True)
            sums_ref[1:2, :] = jnp.sum(upstream, axis=0, keepdims=True)
            sums_ref[2:3, :] = jnp.sum(branch_grad.astype(F32), axis=0, keepdims=True)

        if old:

            @pl.when(jnp.logical_not(mine))
            def _():
                out_ref[...] = old[0][...]
                sums_ref[...] = old[1][...]

        else:

            @pl.when(jnp.logical_not(mine))
            def _():
                out_ref[...] = jnp.zeros_like(out_ref)
                sums_ref[...] = jnp.zeros_like(sums_ref)

    operands = [part, received, normed, slope, *cotangent, vecs, up, down, *earlier]
    outs = [
        struct((rows, D), F32),
        struct((rows, D), BF),
        struct((rows, 2 * HID), BF),
        struct((rows, D), BF),
        struct((rows, D), BF),
        struct((8, D), F32),
        struct((8, 2 * HID), F32),
    ]
    results = call(
        "second_norm",
        body,
        scalars,
        operands,
        [whole(o.shape) for o in operands],
        outs,
        [whole(o.shape) for o in outs],
        (1,),
        micros=5,
    )
    return results[:4], results[4:]


def split_outs(width):
    return [struct((GROUPS // 2, BLOCK, width), BF)] * 2


def feed_forward_grads(scalars, blocks, rows):
    def body(sc, *refs):
        keep_ref, send_ref, result_ref = refs[-3:]
        step = pl.program_id(0)

        @pl.when(step % 2 == 0)
        def _():
            result_ref[...] = dot_tn(refs[0][...], refs[1][...]) + dot_tn(refs[4][...], refs[5][...])

        @pl.when(step % 2 == 1)
        def _():
            result_ref[...] = dot_tn(refs[2][...], refs[3][...]) + dot_tn(refs[6][...], refs[7][...])

        split_rows(result_ref, sc[1], keep_ref, send_ref)

    half = pl.BlockSpec((rows, HID), lambda c, _: (0, c // 2))
    outs = split_outs(4 * HID)
    out_specs = [pl.BlockSpec((GROUPS // 2, BLOCK, HID), lambda c, _: (0, 0, c))] * 2
    return call(
        "feed_forward_grads",
        body,
        scalars,
        [value for block in blocks for value in block],
        [whole((rows, D)), half] * 4,
        outs,
        out_specs,
        (4,),
        [pltpu.VMEM((D, HID), F32)],
        micros=8,
    )


def first_norm(scalars, block, part, received, total_grad, normed, inverse, vecs, out_weight, earlier, rows):
    def body(sc, part_ref, recv_ref, grad_ref, norm_ref, inv_ref, vec_ref, weight_ref, *refs):
        old, refs = refs[: len(earlier)], refs[len(earlier) :]
        attention_ref, context_ref, own_ref, sums_ref = refs[:4]
        mine = sc[0] == block
        upstream = grad_ref[...] + part_ref[...].astype(F32) + recv_ref[...].astype(F32)
        here = norm_ref[...]
        scaled = upstream * vec_ref[3:4, :]
        inner = (
            scaled
            - jnp.mean(scaled, axis=-1, keepdims=True)
            - here * jnp.mean(scaled * here, axis=-1, keepdims=True)
        )
        total = inner * inv_ref[:, :1]
        attention = total.astype(BF)
        attention_ref[...] = attention
        context_ref[...] = dot_nt(attention, weight_ref[...]).astype(BF)
        if block == 1:
            turned = jnp.concatenate([weight_ref[QUARTER:, :], weight_ref[:QUARTER, :]], axis=0)
            refs[4][...] = dot_nt(attention, turned).astype(BF)

        @pl.when(mine)
        def _():
            own_ref[...] = total
            sums_ref[...] = jnp.zeros_like(sums_ref)
            sums_ref[0:1, :] = jnp.sum(upstream * here, axis=0, keepdims=True)
            sums_ref[1:2, :] = jnp.sum(upstream, axis=0, keepdims=True)
            sums_ref[2:3, :] = jnp.sum(attention.astype(F32), axis=0, keepdims=True)

        @pl.when(jnp.logical_not(mine))
        def _():
            own_ref[...] = old[0][...] if old else jnp.zeros_like(own_ref)
            sums_ref[...] = old[1][...] if old else jnp.zeros_like(sums_ref)

    operands = [part, received, total_grad, normed, inverse, vecs, out_weight, *earlier]
    outs = [
        struct((rows, D), BF),
        struct((rows, HALF), BF),
        struct((rows, D), F32),
        struct((8, D), F32),
        struct((rows, HALF), BF),
    ][: 5 if block == 1 else 4]
    return call(
        "first_norm",
        body,
        scalars,
        operands,
        [whole(o.shape) for o in operands],
        outs,
        [whole(o.shape) for o in outs],
        (1,),
        micros=3,
    )


def halves(value):
    high = value.astype(BF).astype(F32)
    return jnp.concatenate([high, value - high], axis=1).astype(BF)


def whole_of(table):
    return table[:, :128].astype(F32) + table[:, 128:].astype(F32)


def output_grads(scalars, blocks, small, small_side):
    def body(sc, *refs):
        small_ref, side_ref, keep_ref, send_ref, result_ref = refs[-5:]
        for side in range(2):
            part = dot_tn(refs[side][...], refs[2][...]) + dot_tn(refs[3 + side][...], refs[5][...])
            for k in range(2):
                at = pl.multiple_of((sc[2] ^ side ^ (2 * k)) * QUARTER, 16)
                result_ref[pl.ds(at, QUARTER), :] = part[k * QUARTER : (k + 1) * QUARTER, :]
        for j in range(GROUPS):
            target = (keep_ref, send_ref)[j % 2]
            block = sc[1] ^ j
            rows = pl.ds(pl.multiple_of(block * BLOCK, 16), BLOCK)
            target[j // 2, :BLOCK] = result_ref[rows, :].astype(BF)
            target[j // 2, BLOCK:] = jnp.zeros((LABELS, D), BF)
            target[j // 2, BLOCK:, :256] = halves(small_ref[block] + side_ref[block])

    outs = [struct((GROUPS // 2, BLOCK + LABELS, D), BF)] * 2
    operands = [value for block in blocks for value in block] + [small, small_side]
    return call(
        "output_grads",
        body,
        scalars,
        operands,
        [whole(o.shape) for o in operands],
        outs,
        [whole(o.shape) for o in outs],
        (1,),
        [pltpu.VMEM((D, D), F32)],
        micros=4,
    )


def attend_backward(scalars, pair, halo, grad_blocks, hot, weight, rows):
    base = 3 * rows
    steps = HALF // PAIR

    def body(sc, *refs):
        pair_refs, halo_refs, refs = refs[:3], refs[3:6], refs[6:]
        far_ref, near_ref, halo_ref, hot_ref, w_ref, *refs = refs
        out_ref, keep_ref, send_ref, sums_ref, mask_ref, key_ref, value_ref, acc_ref, q_ref, k_ref, v_ref = refs
        for target, first_part, last_part in zip((q_ref, k_ref, v_ref), pair_refs, halo_refs):
            target[: 2 * rows, :] = first_part[...]
            target[2 * rows :, :] = last_part[...]
        step = pl.program_id(0)

        @pl.when(step == 0)
        def _():
            mask_ref[...] = (dot_tn(hot_ref[...], hot_ref[...]) - 1.0) * MASKED

        key_ref[...] = jnp.zeros_like(key_ref)
        value_ref[...] = jnp.zeros_like(value_ref)
        lane = lax.broadcasted_iota(jnp.int32, (1, PAIR), 1)
        query_grads = [jnp.zeros((PAIR, rows), F32), jnp.zeros((PAIR, rows), F32)]
        for head in range(2):
            part = jnp.where((lane // HEAD_DIM) == head, 1.0, 0.0)
            key_turned = (k_ref[...].astype(F32) * part).T.astype(BF)
            for index, (low, high) in enumerate(((0, 2 * rows), (0, base), (rows, base))):
                start = index * rows
                mine = (q_ref[start : start + rows].astype(F32) * (part * HEAD_DIM**-0.5)).astype(BF)
                grads = (far_ref, near_ref, halo_ref)[index][...]
                grads = (grads.astype(F32) * part).astype(BF)
                scores = dot_nt(k_ref[low:high], mine) + mask_ref[low:high, start : start + rows]
                expo = jnp.exp(scores - jnp.max(scores, axis=0, keepdims=True))
                probs = expo * (1.0 / jnp.sum(expo, axis=0, keepdims=True))
                pulled = dot_nt(v_ref[low:high], grads)
                inner = jnp.sum(probs * pulled, axis=0, keepdims=True)
                score_grads = (probs * (pulled - inner)).astype(BF)
                top = min(high, 2 * rows)
                span = top - low
                value_ref[low:top, :] += dot(probs[:span].astype(BF), grads)
                key_ref[low:top, :] += dot(score_grads[:span], mine)
                if index < 2:
                    query_grads[index] = query_grads[index] + dot(key_turned[:, low:high], score_grads)
        for index in range(2):
            turned = (query_grads[index] * HEAD_DIM**-0.5).T.astype(BF)
            out_ref[index * rows : (index + 1) * rows, :PAIR] = turned
        out_ref[:, PAIR : 2 * PAIR] = key_ref[...].astype(BF)
        out_ref[:, 2 * PAIR :] = value_ref[...].astype(BF)
        sums = jnp.sum(out_ref[...].astype(F32), axis=0, keepdims=True)
        sums_ref[...] = jnp.broadcast_to(sums, (8, 3 * PAIR))
        product = dot_nt(out_ref[...], w_ref[...])

        @pl.when(step == 0)
        def _():
            acc_ref[...] = product

        @pl.when(step > 0)
        def _():
            acc_ref[...] += product

        @pl.when(step == steps - 1)
        def _():
            near = sc[0]
            keep_ref[...] = acc_ref[pl.ds(pl.multiple_of(near * rows, rows), rows), :]
            other = acc_ref[pl.ds(pl.multiple_of((1 - near) * rows, rows), rows), :]
            send_ref[...] = other.astype(BF)

    operands = [*pair, *halo, *grad_blocks, hot, weight]
    in_specs = [column(2 * rows)] * 3 + [column(rows)] * 6 + [whole(hot.shape)]
    in_specs += [pl.BlockSpec((D, 3 * PAIR), lambda p, _: (0, p))]
    outs = [struct((2 * rows, 3 * HALF), BF), struct((rows, D), F32), struct((rows, D), BF)]
    outs += [struct((8, 3 * HALF), F32)]
    out_specs = [
        pl.BlockSpec((2 * rows, 3 * PAIR), lambda p, _: (0, p)),
        whole((rows, D)),
        whole((rows, D)),
        pl.BlockSpec((8, 3 * PAIR), lambda p, _: (0, p)),
    ]
    scratch = [
        pltpu.VMEM((base, base), F32),
        pltpu.VMEM((2 * rows, PAIR), F32),
        pltpu.VMEM((2 * rows, PAIR), F32),
        pltpu.VMEM((2 * rows, D), F32),
    ] + [pltpu.VMEM((base, PAIR), BF)] * 3
    return call(
        "attend_backward",
        body,
        scalars,
        operands,
        in_specs,
        outs,
        out_specs,
        (steps,),
        scratch,
        micros=MICROS,
    )


def projection_grads(scalars, x, grads, rows):
    tall = 2 * rows

    def body(sc, x_ref, grad_ref, *refs):
        result_ref = refs[-1]
        result_ref[...] = dot_tn(x_ref[...], grad_ref[...])
        split_rows(result_ref, sc[1], refs[0], refs[1])

    outs = split_outs(3 * HALF)
    out_specs = [pl.BlockSpec((GROUPS // 2, BLOCK, 3 * PAIR), lambda p, _: (0, 0, p))] * 2
    return call(
        "projection_grads",
        body,
        scalars,
        [x, grads],
        [pl.BlockSpec((tall, D), lambda p, _: (0, 0)), pl.BlockSpec((tall, 3 * PAIR), lambda p, _: (0, p))],
        outs,
        out_specs,
        (HALF // PAIR,),
        [pltpu.VMEM((D, 3 * PAIR), F32)],
        micros=5,
    )


def combine(scalars, keep, received):
    count, rows, width = keep.shape
    chunk = width // 3

    def body(_, keep_ref, recv_ref, *refs):
        for k in range(count):
            total = keep_ref[k].astype(F32) + recv_ref[k].astype(F32)
            refs[k][...] = total.astype(refs[k].dtype)

    block = pl.BlockSpec((count, rows, chunk), lambda c, _: (0, 0, c))
    outs = [struct((rows, width), F32)] + [struct((rows, width), BF)] * (count - 1)
    spec = pl.BlockSpec((rows, chunk), lambda c, _: (0, c))
    return list(call(
        "combine",
        body, scalars, [keep, received], [block, block], outs, [spec] * count, (3,)))


def combine_both(scalars, keep, received, out_keep, out_received):
    count, rows, wide = keep.shape
    tall = rows + LABELS

    def body(_, keep_ref, recv_ref, out_keep_ref, out_recv_ref, *refs):
        for k in range(count):
            kind = refs[k].dtype
            refs[k][:rows, :wide] = (keep_ref[k].astype(F32) + recv_ref[k].astype(F32)).astype(kind)
            refs[k][rows:, :wide] = jnp.zeros((LABELS, wide), kind)
            total = out_keep_ref[k, :rows].astype(F32) + out_recv_ref[k, :rows].astype(F32)
            refs[k][:rows, wide:] = total.astype(kind)
            refs[k][rows:, wide:] = jnp.zeros((LABELS, D), kind)
            small = whole_of(out_keep_ref[k, rows:, :256]) + whole_of(out_recv_ref[k, rows:, :256])
            refs[k][rows:, wide : wide + 256] = halves(small).astype(kind)

    outs = [struct((tall, wide + D), F32)] + [struct((tall, wide + D), BF)] * (count - 1)
    return simple("combine_both", body, scalars, [keep, received, out_keep, out_received], outs, 2)


def total_feed(scalars, sums):
    rows = sums[0].shape[0]

    def body(_, *refs):
        keep_ref, send_ref = refs[-2:]
        total = refs[0][...]
        for ref in refs[1:-2]:
            total = total + ref[...].astype(F32)
        keep_ref[...] = total[:, : 2 * HID]
        send_ref[...] = total[:, 2 * HID :].astype(BF)

    outs = [struct((rows, 2 * HID), F32), struct((rows, 2 * HID), BF)]
    return simple("total_feed", body, scalars, sums, outs, 2)


def total_projection(scalars, sums, rows):
    tall = sums[0].shape[0]
    wide = 3 * HALF

    def body(sc, *refs):
        keep_ref, send_ref = refs[-2:]
        total = refs[0][:rows, :]
        for ref in refs[1:-2]:
            total = total + ref[:rows, :].astype(F32)
        near, far = [], []
        for kind in range(3):
            both = [total[:, (3 * p + kind) * PAIR : (3 * p + kind + 1) * PAIR] for p in range(3)]
            both = jnp.concatenate(both, axis=1)
            near.append(both[:, :QUARTER])
            far.append(both[:, QUARTER:])
        near.append(pltpu.roll(total[:, wide:], D - sc[2] * QUARTER, 1)[:, :QUARTER])
        far.append(pltpu.roll(total[:, wide:], D - (sc[2] ^ 2) * QUARTER, 1)[:, :QUARTER])
        keep_ref[:rows, :] = jnp.concatenate(near, axis=1)
        send_ref[:rows, :] = jnp.concatenate(far, axis=1).astype(BF)
        if tall > rows:
            small = jnp.zeros((LABELS, 128), F32)
            for ref in refs[:-2]:
                small = small + whole_of(ref[rows:, wide : wide + 256])
            keep_ref[rows:, :] = jnp.zeros((LABELS, D), F32)
            send_ref[rows:, :] = jnp.zeros((LABELS, D), BF)
            keep_ref[rows:, :128] = small
            send_ref[rows:, :256] = halves(small)

    outs = [struct((tall, D), F32), struct((tall, D), BF)]
    return simple("total_projection", body, scalars, sums, outs, 2)


def finish_feed(scalars, keep, received):
    rows = keep.shape[0]

    def body(_, keep_ref, recv_ref, up_ref, down_ref):
        up_ref[...] = keep_ref[:, :HID] + recv_ref[:, :HID].astype(F32)
        down_ref[...] = keep_ref[:, HID:] + recv_ref[:, HID:].astype(F32)

    outs = [struct((rows, HID), F32)] * 2
    return simple("finish_feed", body, scalars, [keep, received], outs)


def finish_projection(scalars, keep, received, rows):
    tall = keep.shape[0]

    def body(_, keep_ref, recv_ref, *refs):
        total = keep_ref[:rows, :] + recv_ref[:rows, :].astype(F32)
        for k in range(4):
            refs[k][...] = total[:, k * QUARTER : (k + 1) * QUARTER]
        if tall > rows:
            refs[4][...] = keep_ref[rows:, :128] + whole_of(recv_ref[rows:, :256])

    outs = [struct((rows, QUARTER), F32)] * 4 + ([struct((LABELS, 128), F32)] if tall > rows else [])
    return simple("finish_projection", body, scalars, [keep, received], outs)


def small_sums(scalars, sums_one, sums_two, sums_hidden, sums_projection):
    def body(sc, one_ref, two_ref, hidden_ref, projection_ref, out_ref, wide_ref, tall_ref):
        out_ref[...] = jnp.zeros_like(out_ref)
        lanes = lax.broadcasted_iota(jnp.int32, (1, D), 1)
        near, far = lanes < QUARTER, (lanes >= QUARTER) & (lanes < HALF)
        for row, kind in ((0, 0), (1, 2)):
            line = jnp.concatenate(
                [
                    projection_ref[0:1, (3 * p + kind) * PAIR : (3 * p + kind + 1) * PAIR]
                    for p in range(3)
                ]
                + [jnp.zeros((1, HALF), F32)],
                axis=1,
            )
            low = pltpu.roll(jnp.broadcast_to(jnp.where(near, line, 0.0), (8, D)), sc[2] * QUARTER, 1)
            high = jnp.broadcast_to(jnp.where(far, line, 0.0), (8, D))
            high = pltpu.roll(high, D - QUARTER + (sc[2] ^ 2) * QUARTER, 1)
            wide_ref[row : row + 1, :] = (low + high)[0:1]
        wide_ref[2:3, :] = one_ref[2:3, :]
        wide_ref[3:5, :] = one_ref[0:2, :]
        wide_ref[5:6, :] = two_ref[2:3, :]
        wide_ref[6:8, :] = two_ref[0:2, :]
        tall_ref[...] = jnp.zeros_like(tall_ref)
        for k in range(2):
            to = pl.multiple_of((sc[2] ^ (2 * k)) * HID, 128)
            tall_ref[0:1, pl.ds(to, HID)] = hidden_ref[0:1, k * HID : (k + 1) * HID]
        share = FF // GROUPS
        for d in range(GROUPS):
            out_ref[d, :VECS, :BLOCK] = wide_ref[:, d * BLOCK : (d + 1) * BLOCK]
            for c in range(share // 128):
                at = d * share + c * 128
                out_ref[d, VECS + c : VECS + c + 1, :] = tall_ref[0:1, at : at + 128]

    operands = [sums_one, sums_two, sums_hidden, sums_projection]
    shape = (GROUPS, LABELS, 128)
    return call(
        "small_sums",
        body,
        scalars,
        operands,
        [whole(o.shape) for o in operands],
        [struct(shape, F32)],
        [whole(shape)],
        (1,),
        [pltpu.VMEM((VECS, D), F32), pltpu.VMEM((8, FF), F32)],
    )[0]


def per_device(
    tokens,
    segments,
    query_weight,
    key_weight,
    value_weight,
    output_weight,
    query_bias,
    value_bias,
    output_bias,
    first_gain,
    first_shift,
    up_weight,
    up_bias,
    down_weight,
    down_bias,
    second_gain,
    second_shift,
    cotangent,
):
    seq_count = lax.axis_size("seq")
    count = lax.axis_size("dp")
    place_z = lax.axis_index("seq")
    assert seq_count == 4
    direct = count == GROUPS
    rows = tokens.shape[1]
    piece_rows = query_weight.shape[0]
    near = (place_z == 1) | (place_z == 2)
    base = lax.axis_index("dp") if direct else 0
    scalars = jnp.stack([near, base, place_z]).astype(jnp.int32)

    own = tokens[0]
    cot_own = cotangent[0]
    lines = [
        query_bias,
        value_bias,
        output_bias,
        first_gain,
        first_shift,
        down_bias,
        second_gain,
        second_shift,
    ]
    lines = [line[None] for line in lines] if direct else []
    first_send, mine, wide, labelled, own_docs = pack_inputs(
        scalars,
        [query_weight, key_weight, value_weight, output_weight],
        own,
        segments,
        up_weight,
        down_weight.T,
        lines,
        up_bias[None],
    )
    arrived = swap(first_send, "seq", 2)
    side = swap(output_weight, "seq", 1)
    if direct:
        mine_chip = [mine, swap(mine, "dp", 2), swap(mine, "dp", 4)]
        labelled, side, mine_chip, arrived = together(labelled, side, mine_chip, arrived)
    else:
        arrived, labelled, side = together(arrived, labelled, side)
    narrow_far, wide_send, both = split_arrived(scalars, arrived, wide, side, mine)
    wide_far = swap(wide_send, "seq", 2)
    if direct:
        far_chip = [narrow_far, swap(narrow_far, "dp", 2), swap(narrow_far, "dp", 4)]
        both_far = swap(both, "dp", 6)
        mine_chip, labelled, cot_own, wide, far_chip, both_far, wide_far = together(
            mine_chip, labelled, cot_own, wide, far_chip, both_far, wide_far
        )
        stacked = stack_narrow(scalars, mine_chip, far_chip, both_far)
        pieces = [stacked, swap(stacked, "dp", 1)]
    partner = swap(labelled, "seq", 1)
    halo_near = lax.ppermute(labelled, "seq", [(1, 2), (2, 1)])
    if direct:
        feed_piece = pack_feed(scalars, wide_far, first_send, arrived, side)
        feed_chip = [feed_piece, swap(feed_piece, "dp", 2), swap(feed_piece, "dp", 4)]
        wide, pieces, partner, feed_chip, halo_near = together(
            wide, pieces, partner, feed_chip, halo_near
        )
        feed_chip = feed_chip + [swap(feed_chip[0], "dp", 6)]
        wide_last = swap(wide, "dp", 6)
    halo_far = lax.ppermute(halo_near, "seq", [(1, 0), (2, 3)])
    if not direct:
        share = FF // GROUPS
        vectors = jnp.stack(
            [
                query_bias,
                value_bias,
                output_bias,
                first_gain,
                first_shift,
                down_bias,
                second_gain,
                second_shift,
            ]
        )
        lines = lax.all_gather(vectors, "dp", axis=1, tiled=True).reshape(VECS, GROUPS, BLOCK)
        lines = jnp.pad(lines, ((0, 0), (0, 0), (0, share - BLOCK)))
        tall = lax.all_gather(up_bias, "dp", axis=0, tiled=True).reshape(1, GROUPS, share)
        lines = jnp.concatenate([lines, jnp.broadcast_to(tall, (VECS, GROUPS, share))], axis=0)
        lines = jnp.pad(lines, ((0, 0), (0, 0), (0, 3 * QUARTER - share)))
        lines = lines.transpose(1, 0, 2)
        gathered = gather_rows(mine)
        pieces = [
            jnp.concatenate([half[:, :, 2 * HID :], lines[k::2], far], axis=1)
            for k, (half, far) in enumerate(zip(gathered, gather_rows(narrow_far)))
        ]
        feed = gather_rows(pack_feed(scalars, wide_far, first_send, arrived, side))
        weights = [
            jnp.concatenate([half[:, :, : 2 * HID], far], axis=2) for half, far in zip(gathered, feed)
        ]

    def rows_of(keep, send):
        return jnp.stack([keep, send], axis=1).reshape(GROUPS, -1, keep.shape[2]).astype(F32)

    def spread(sums):
        return [sums[0]] + [swap(sums[k], "dp", 2 * k) for k in range(1, len(sums))]

    def scattered(table):
        return [lax.psum_scatter(table, "dp", scatter_dimension=0, tiled=True)]

    *pair, ctx_far, x, weight, hot, vecs, hidden_bias, bias = attend_pair(
        scalars, own, partner, own_docs, pieces, rows
    )
    if direct:
        pair, ctx_far, cot_own, halo_far = together(pair, ctx_far, cot_own, halo_far)
    *halo, ctx_near, hot = attend_halo(scalars, halo_near, halo_far, weight, bias, hot, *pair, rows)
    ctx_mine = [ctx_far, ctx_near]
    ctx_partner = [swap(ctx_far, "seq", 1), None]
    if direct:
        ctx_mine[1], ctx_partner[0], wide_last, feed_chip = together(
            ctx_mine[1], ctx_partner[0], wide_last, feed_chip
        )
        stacked = stack_wide(scalars, mine_chip, wide_last, feed_chip)
        weights = [stacked, swap(stacked, "dp", 1)]
    ctx_partner[1] = swap(ctx_mine[1], "seq", 1)
    cot_partner = swap(cot_own, "seq", 1)

    forward, slopes, part_far = [None, None], [None, None], [None, None]
    for block in (1, 0):
        forward[block], weights = feed_forward(
            scalars, block, ctx_mine[block], ctx_partner[block], x, vecs, hidden_bias, weights, rows
        )
        part_far[block] = swap(forward[block][5], "seq", 1)
    up, down, out_mine, _ = weights
    second, second_shared, first_part_far = [None, None], [], [None, None]
    for block in (1, 0):
        slopes[block] = gelu_slope(scalars, forward[block][3])
    for block in (1, 0):
        second[block], second_shared = second_norm(
            scalars,
            block,
            forward[block][5],
            part_far[block],
            forward[block][0],
            slopes[block],
            (cot_own, cot_partner),
            vecs,
            up,
            down,
            second_shared,
            rows,
        )
        if block == 1:
            first_part_far[block] = swap(second[block][3], "seq", 1)
    feed_parts = feed_forward_grads(
        scalars,
        [(forward[k][2], second[k][2], second[k][1], forward[k][4]) for k in range(2)],
        rows,
    )
    first_part_far[1], second, second_shared, feed_parts = together(
        first_part_far[1], second, second_shared, feed_parts
    )
    first_part_far[0] = swap(second[0][3], "seq", 1)
    layer_output, sums_two, sums_hidden = second_shared
    attention_grad, ctx_grad, first_shared = [None, None], [None, None], []

    def finish(block):
        attention_grad[block], ctx_grad[block], *shared = first_norm(
            scalars,
            block,
            second[block][3],
            first_part_far[block],
            second[block][0],
            forward[block][0],
            forward[block][1],
            vecs,
            out_mine,
            first_shared,
            rows,
        )
        return shared

    *first_shared, halo_send = finish(1)
    halo_grad = swap(halo_send, "seq", 2)
    if direct:
        feed_sums = combine(scalars, feed_parts[0], swap(feed_parts[1], "dp", 1))
        feed_sums = spread(feed_sums)
    else:
        feed_sums = scattered(rows_of(*feed_parts).reshape(D, -1))
    own_grad, sums_one = finish(0)

    grads, input_keep, input_send, sums_projection = attend_backward(
        scalars, pair, halo, [*ctx_grad, halo_grad], hot, weight, rows
    )
    input_far = swap(input_send, "seq", 1)
    small = small_sums(scalars, sums_one, sums_two, sums_hidden, sums_projection)
    small_side = swap(small, "seq", 1)
    projection_parts = projection_grads(scalars, x, grads, rows)
    projection_parts, small_side, feed_sums = together(projection_parts, small_side, feed_sums)
    out_blocks = [(ctx_mine[k], ctx_partner[k], attention_grad[k]) for k in range(2)]
    if direct:
        projection_received = swap(projection_parts[1], "dp", 1)
        out_parts = output_grads(scalars, out_blocks, small, small_side)
        out_received = swap(out_parts[1], "dp", 1)
        feed_keep, feed_send = total_feed(scalars, feed_sums)
        feed_far = swap(feed_send, "seq", 2)
        sums = spread(
            combine_both(scalars, projection_parts[0], projection_received, out_parts[0], out_received)
        )
    else:
        out_parts = rows_of(*output_grads(scalars, out_blocks, small, small_side))
        sums = scattered(
            jnp.concatenate(
                [rows_of(*projection_parts).reshape(D, -1), out_parts[:, :BLOCK].reshape(D, -1)], axis=1
            )
        )
        feed_keep, feed_send = total_feed(scalars, feed_sums)
        feed_far = swap(feed_send, "seq", 2)
    up_grad, down_grad = finish_feed(scalars, feed_keep, feed_far)
    input_grad = own_grad + input_keep + input_far.astype(F32)
    if direct:
        sums, up_grad, input_grad = together(sums, up_grad, input_grad)
    keep, send = total_projection(scalars, sums, piece_rows)
    projections = list(finish_projection(scalars, keep, swap(send, "seq", 2), piece_rows))
    if direct:
        tile = projections.pop()
        wide_lines, tall_lines = tile[:VECS, :BLOCK], tile[VECS : VECS + 3].reshape(-1)
    else:
        tile = out_parts[:, BLOCK:, :128] + out_parts[:, BLOCK:, 128:256]
        tile = tile + swap(tile, "seq", 2)
        wide_lines = tile[:, :VECS, :BLOCK].transpose(1, 0, 2).reshape(VECS, D)
        wide_lines = lax.psum_scatter(wide_lines, "dp", scatter_dimension=1, tiled=True)
        tall_lines = lax.psum_scatter(tile[:, VECS : VECS + 3].reshape(-1), "dp", tiled=True)
    vec = [wide_lines[k] for k in range(VECS)]
    return (
        layer_output[None],
        input_grad[None],
        *projections,
        vec[0],
        vec[1],
        vec[2],
        vec[3],
        vec[4],
        up_grad,
        tall_lines,
        down_grad.T,
        vec[5],
        vec[6],
        vec[7],
    )


def solution(mesh):
    placed = (
        P("dp", "seq", None),
        P("dp", "seq"),
        P("dp", "seq"),
        P("dp", "seq"),
        P("dp", "seq"),
        P("dp", "seq"),
        P("dp"),
        P("dp"),
        P("dp"),
        P("dp"),
        P("dp"),
        P("dp", "seq"),
        P("dp"),
        P("seq", "dp"),
        P("dp"),
        P("dp"),
        P("dp"),
        P("dp", "seq", None),
    )
    return jax.shard_map(
        per_device,
        mesh=mesh,
        in_specs=placed,
        out_specs=(
            P("dp", "seq", None),
            P("dp", "seq", None),
            P("dp", "seq"),
            P("dp", "seq"),
            P("dp", "seq"),
            P("dp", "seq"),
            P("dp"),
            P("dp"),
            P("dp"),
            P("dp"),
            P("dp"),
            P("dp", "seq"),
            P("dp"),
            P("seq", "dp"),
            P("dp"),
            P("dp"),
            P("dp"),
        ),
        check_vma=False,
    )
```

```python
import jax
import jax.numpy as jnp
from jax import lax
from jax.experimental import pallas as pl
from jax.experimental.pallas import tpu as pltpu
from jax.sharding import PartitionSpec as P

D = 768
HEADS = 12
HEAD_DIM = 64
FF = 3072
EPS = 1e-05
MASKED = 1e30
PAIR = 2 * HEAD_DIM
QUARTER = D // 4
HALF = D // 2
HID = FF // 4
VECS = 8
GROUPS = 8
BLOCK = D // GROUPS
LABELS = 16
MARKS = 48
MICROS = 450
BF = jnp.bfloat16
F32 = jnp.float32
ROOT_HALF = 0.7071067811865476
ROOT_TWO_PI = 0.3989422804014327


def dot(a, b):
    return lax.dot_general(a, b, (((1,), (0,)), ((), ())), preferred_element_type=F32)


def dot_nt(a, b):
    return lax.dot_general(a, b, (((1,), (1,)), ((), ())), preferred_element_type=F32)


def dot_tn(a, b):
    return lax.dot_general(a, b, (((0,), (0,)), ((), ())), preferred_element_type=F32)


def swap(value, axis, mask):
    count = lax.axis_size(axis)
    return lax.ppermute(value, axis, [(k, k ^ mask) for k in range(count)])


def together(*values):
    return lax.optimization_barrier(values)


def whole(shape):
    return pl.BlockSpec(shape, lambda *_: (0,) * len(shape))


def params():
    return pltpu.CompilerParams(vmem_limit_bytes=22 * 1024 * 1024)


def call(name, body, scalars, operands, in_specs, outs, out_specs, grid, scratch=(), micros=1):
    spec = pltpu.PrefetchScalarGridSpec(
        num_scalar_prefetch=1,
        grid=grid,
        in_specs=in_specs,
        out_specs=out_specs,
        scratch_shapes=list(scratch),
    )
    return pl.pallas_call(
        body,
        out_shape=outs,
        grid_spec=spec,
        compiler_params=params(),
        cost_estimate=pl.CostEstimate(
            flops=int(micros * 1.0e7), transcendentals=0, bytes_accessed=1024
        ),
        name=name,
    )(scalars, *operands)


def struct(shape, dtype):
    return jax.ShapeDtypeStruct(shape, dtype)


def chip_pieces(piece):
    return [piece] + [swap(piece, "dp", j) for j in range(2, GROUPS, 2)]


def gather_rows(piece):
    full = lax.all_gather(piece, "dp", axis=0, tiled=True)
    full = full.reshape(GROUPS, D // GROUPS, piece.shape[1])
    return [full[0::2], full[1::2]]


def place(target, pair, base, source_cols, target_cols):
    for j in range(GROUPS):
        start = pl.multiple_of((base ^ j) * BLOCK, 16)
        target[pl.ds(start, BLOCK), target_cols] = pair[j % 2][j // 2, :BLOCK, source_cols]


def split_rows(result, base, keep, send):
    for j in range(GROUPS):
        block = result[pl.ds(pl.multiple_of((base ^ j) * BLOCK, 16), BLOCK), :].astype(BF)
        if j % 2:
            send[j // 2] = block
        else:
            keep[j // 2] = block


def simple(name, body, scalars, operands, outs, micros=1):
    return call(
        name,
        body,
        scalars,
        operands,
        [whole(o.shape) for o in operands],
        outs,
        [whole(o.shape) for o in outs],
        (1,),
        micros=micros,
    )


def pack_inputs(scalars, tables, tokens, segments, up, down, lines, tall):
    rows = tokens.shape[0]
    height = tables[0].shape[0]
    extra = LABELS if lines else 0
    operands = list(tables) + [tokens, segments, up, down] + lines + ([tall] if lines else [])
    count = len(operands)

    def body(_, *refs):
        sources, (send_ref, mine_ref, wide_ref, label_ref, docs_ref), refs = (
            refs[:count],
            refs[count : count + 5],
            refs[count + 5 :],
        )
        copies = [pltpu.make_async_copy(a, b, refs[-1].at[k]) for k, (a, b) in enumerate(zip(sources, refs))]
        for copy in copies:
            copy.start()
        for copy in copies:
            copy.wait()
        joined = jnp.concatenate([ref[...].astype(F32) for ref in refs[:4]], axis=1).astype(BF)
        send_ref[...] = joined
        mine_ref[:height, :HID] = refs[6][...]
        mine_ref[:height, HID : 2 * HID] = refs[7][...]
        mine_ref[:height, 2 * HID :] = joined[:, : 3 * QUARTER]
        wide_ref[:, :HID] = refs[6][...]
        wide_ref[:, HID:] = refs[7][...]
        docs = refs[5][...].astype(F32)
        docs_ref[...] = docs
        label_ref[:rows, :] = refs[4][...]
        label_ref[rows:, :] = jnp.zeros((MARKS, D), BF)
        label_ref[rows:, :rows] = jnp.broadcast_to(docs, (MARKS, rows)).astype(BF)
        if lines:
            share = FF // GROUPS
            table = [ref[...].astype(F32) for ref in refs[8 : 8 + VECS]]
            table = jnp.concatenate(table, axis=0)
            table = jnp.concatenate([table, jnp.zeros((VECS, share - BLOCK), F32)], axis=1)
            line = jnp.broadcast_to(refs[8 + VECS][...].astype(F32), (VECS, share))
            mine_ref[height:, :] = jnp.zeros((LABELS, 3 * QUARTER + 2 * HID), BF)
            mine_ref[height:, 2 * HID : 2 * HID + share] = jnp.concatenate([table, line], axis=0).astype(BF)

    outs = [
        struct((height, D), BF),
        struct((height + extra, 3 * QUARTER + 2 * HID), BF),
        struct((height, 2 * HID), BF),
        struct((rows + MARKS, D), BF),
        struct((1, rows), F32),
    ]
    operands = [pltpu.with_memory_space_constraint(o, pltpu.MemorySpace.HBM) for o in operands]
    return call(
        "pack_inputs",
        body,
        scalars,
        operands,
        [pl.BlockSpec(memory_space=pltpu.MemorySpace.HBM)] * count,
        outs,
        [whole(o.shape) for o in outs],
        (1,),
        [pltpu.VMEM(o.shape, o.dtype) for o in operands] + [pltpu.SemaphoreType.DMA((count,))],
    )


def split_arrived(scalars, arrived, wide, side, mine):
    rows, tall = arrived.shape[0], mine.shape[0]

    def body(_, far_ref, wide_ref, side_ref, mine_ref, narrow_ref, out_ref, both_ref):
        narrow_ref[...] = far_ref[:, : 3 * QUARTER]
        out_ref[:, : 2 * HID] = wide_ref[...]
        out_ref[:, 2 * HID :] = side_ref[...]
        both_ref[:tall, :] = mine_ref[:, 2 * HID :]
        both_ref[tall:, :] = far_ref[:, : 3 * QUARTER]

    outs = [
        struct((rows, 3 * QUARTER), BF),
        struct((rows, 2 * HID + QUARTER), BF),
        struct((rows + tall, 3 * QUARTER), BF),
    ]
    return simple("split_arrived", body, scalars, [arrived, wide, side, mine], outs)


def stack_narrow(scalars, mine_chip, far_chip, both_far):
    tall = mine_chip[0].shape[0]
    rows = far_chip[0].shape[0]

    def body(_, *refs):
        out_ref = refs[-1]
        for k in range(3):
            out_ref[k, :tall] = refs[k][:, 2 * HID :]
            out_ref[k, tall:] = refs[3 + k][...]
        out_ref[3] = refs[6][...]

    shape = (GROUPS // 2, tall + rows, 3 * QUARTER)
    operands = [*mine_chip, *far_chip, both_far]
    return simple("stack_narrow", body, scalars, operands, [struct(shape, BF)])[0]


def stack_wide(scalars, mine_chip, last, feed_chip):
    def body(_, *refs):
        out_ref = refs[-1]
        for k in range(3):
            out_ref[k, :, : 2 * HID] = refs[k][:BLOCK, : 2 * HID]
        out_ref[3, :, : 2 * HID] = refs[3][...]
        for k in range(4):
            out_ref[k, :, 2 * HID :] = refs[4 + k][...]

    shape = (GROUPS // 2, BLOCK, 4 * HID + D)
    return simple("stack_wide", body, scalars, [*mine_chip, last, *feed_chip], [struct(shape, BF)])[0]


def pack_feed(scalars, wide_far, first_send, arrived, side):
    rows = wide_far.shape[0]
    last = slice(3 * QUARTER, D)

    def body(sc, far_ref, own_ref, arrived_ref, side_ref, out_ref):
        out_ref[:, : 2 * HID] = far_ref[:, : 2 * HID]
        total = jnp.zeros((rows, D), F32)
        for k, part in enumerate(
            [own_ref[:, last], side_ref[...], arrived_ref[:, last], far_ref[:, 2 * HID :]]
        ):
            part = jnp.concatenate([part.astype(F32), jnp.zeros((rows, D - QUARTER), F32)], axis=1)
            total = total + pltpu.roll(part, (sc[2] ^ k) * QUARTER, 1)
        out_ref[:, 2 * HID :] = total.astype(BF)

    out = struct((rows, 2 * HID + D), BF)
    return simple("pack_feed", body, scalars, [wide_far, first_send, arrived, side], [out])[0]


def mark(docs, rows):
    number = lax.broadcasted_iota(jnp.int32, (LABELS, rows), 0).astype(F32)
    return jnp.where(jnp.broadcast_to(docs, (LABELS, rows)) == number, 1.0, 0.0).astype(BF)


def attend(query, key, value, mask, log_ref, step):
    lane = lax.broadcasted_iota(jnp.int32, (1, PAIR), 1)
    total = jnp.zeros(query.shape, F32)
    scaled = jnp.zeros(query.shape, F32)
    logs = jnp.zeros(query.shape, F32)
    value = jnp.concatenate([value, jnp.ones(value.shape, BF)], axis=1)
    for head in range(2):
        part = jnp.where((lane // HEAD_DIM) == head, 1.0, 0.0)
        mine = (query.astype(F32) * (part * HEAD_DIM**-0.5)).astype(BF)
        scores = dot_nt(mine, key) + mask
        top = jnp.max(scores, axis=-1, keepdims=True)
        expo = jnp.exp(scores - top)
        whole_sum = jnp.sum(expo, axis=-1, keepdims=True)
        probs = expo * (1.0 / whole_sum)
        rounded = probs.astype(BF)
        context = dot(rounded, value)
        total = total + context[:, :PAIR] * part
        scaled = scaled + context[:, :PAIR] * part / context[:, PAIR:]
        logs = jnp.where(lane == head, top + jnp.log(whole_sum), logs)
    turned = logs.T
    for head in range(2):
        log_ref[pl.ds(2 * step + head, 1), :] = turned[head : head + 1, :]
    return total.astype(BF), scaled


def column(height):
    return pl.BlockSpec((height, PAIR), lambda p, _: (0, p))


def attend_pair(scalars, own, partner, own_docs, pieces, rows):
    base = 2 * rows
    tall = BLOCK + LABELS

    def body(sc, own_ref, partner_ref, docs_ref, *refs):
        weight_refs, refs = refs[:2], refs[2:]
        q_ref, k_ref, v_ref, ctx_ref, x_ref, w_ref, hot_ref, vec_ref, hidden_ref, bias_ref, log_ref, *refs = refs
        scaled_ref, mask_ref = refs
        step = pl.program_id(0)

        @pl.when(step == 0)
        def _():
            near = sc[0]
            own_at = pl.multiple_of(near * rows, rows)
            partner_at = pl.multiple_of((1 - near) * rows, rows)
            x_ref[pl.ds(own_at, rows), :] = own_ref[...]
            x_ref[pl.ds(partner_at, rows), :] = partner_ref[:rows, :]
            hot_ref[:, pl.ds(own_at, rows)] = mark(docs_ref[...], rows)
            docs = partner_ref[rows : rows + 1, :rows].astype(F32)
            hot_ref[:, pl.ds(partner_at, rows)] = mark(docs, rows)
            for j in range(GROUPS):
                at = pl.ds(pl.multiple_of((sc[1] ^ j) * BLOCK, 16), BLOCK)
                for kind in range(3):
                    part = slice(kind * QUARTER, (kind + 1) * QUARTER)
                    both = [weight_refs[j % 2][j // 2, top : top + BLOCK, part] for top in (0, tall)]
                    both = [half.astype(F32) for half in both]
                    both = jnp.concatenate(both, axis=1).astype(BF)
                    for p in range(3):
                        to = (3 * p + kind) * PAIR
                        w_ref[at, to : to + PAIR] = both[:, p * PAIR : (p + 1) * PAIR]
            hot = hot_ref[...]
            mask_ref[...] = (dot_tn(hot[:, :rows], hot) - 1.0) * MASKED
            vectors = jnp.zeros((LABELS, D), F32)
            for j in range(GROUPS):
                block = sc[1] ^ j
                line = weight_refs[j % 2][j // 2, BLOCK:tall, : FF // GROUPS].astype(F32)
                table = jnp.where(lax.broadcasted_iota(jnp.int32, line.shape, 1) < BLOCK, line, 0.0)
                table = jnp.concatenate([table, jnp.zeros((LABELS, D - FF // GROUPS), F32)], axis=1)
                vectors = vectors + pltpu.roll(table, block * BLOCK, 1)
                quarter = block // 2
                for k in range(2):

                    @pl.when(quarter == sc[2] ^ (2 * k))
                    def _():
                        to = pl.multiple_of((block % 2) * (HID // 2) + k * HID, 128)
                        hidden_ref[:, pl.ds(to, HID // 2)] = line[VECS:]

            vec_ref[...] = vectors[:VECS]
            lanes = lax.broadcasted_iota(jnp.int32, (VECS, HALF), 1)
            low = pltpu.roll(vectors[:VECS], D - sc[2] * QUARTER, 1)[:, :HALF]
            high = pltpu.roll(vectors[:VECS], D + QUARTER - (sc[2] ^ 2) * QUARTER, 1)[:, :HALF]
            bias_ref[...] = jnp.where(lanes < QUARTER, low, high)
            log_ref[...] = jnp.zeros_like(log_ref)

        at = pl.multiple_of(step * 3 * PAIR, PAIR)
        both = dot(x_ref[...], w_ref[:, pl.ds(at, 3 * PAIR)])
        bias = bias_ref[:, pl.ds(pl.multiple_of(step * PAIR, PAIR), PAIR)]
        query = (both[:, :PAIR] + bias[0:1]).astype(BF)
        key = both[:, PAIR : 2 * PAIR].astype(BF)
        value = (both[:, 2 * PAIR :] + bias[1:2]).astype(BF)
        q_ref[...] = query
        k_ref[...] = key
        v_ref[...] = value
        ctx_ref[...], scaled_ref[...] = attend(query[:rows], key, value, mask_ref[...], log_ref, step)

    operands = [own, partner, own_docs, *pieces]
    in_specs = [whole(o.shape) for o in operands]
    outs = [
        struct((base, HALF), BF),
        struct((base, HALF), BF),
        struct((base, HALF), BF),
        struct((rows, HALF), BF),
        struct((base, D), BF),
        struct((D, 3 * HALF), BF),
        struct((LABELS, base), BF),
        struct((VECS, D), F32),
        struct((VECS, 2 * HID), F32),
        struct((VECS, HALF), F32),
        struct((VECS, rows), F32),
        struct((rows, HALF), F32),
    ]
    out_specs = [column(base)] * 3 + [column(rows)] + [whole(o.shape) for o in outs[4:-1]] + [column(rows)]
    return call(
        "attend_pair",
        body,
        scalars,
        operands,
        in_specs,
        outs,
        out_specs,
        (HALF // PAIR,),
        [pltpu.VMEM((rows, base), F32)],
        micros=8,
    )


def attend_halo(scalars, halo_near, halo_far, weight, bias, hot, query, key, value, rows):
    def body(sc, near_ref, far_ref, w_ref, bias_ref, hot_ref, q_ref, k_ref, v_ref, *refs):
        halo_refs, (ctx_ref, scaled_ref, all_ref, log_ref, x_ref, mask_ref) = refs[:3], refs[3:]

        @pl.when(pl.program_id(0) == 0)
        def _():
            all_ref[:, : 2 * rows] = hot_ref[...]

            def halo(ref):
                x_ref[...] = ref[:rows, :]
                all_ref[:, 2 * rows :] = mark(ref[rows : rows + 1, :rows].astype(F32), rows)

            pl.when(sc[0] == 1)(lambda: halo(near_ref))
            pl.when(sc[0] == 0)(lambda: halo(far_ref))
            mask_ref[...] = (dot_tn(all_ref[:, rows : 2 * rows], all_ref[...]) - 1.0) * MASKED
            log_ref[...] = jnp.zeros_like(log_ref)

        both = dot(x_ref[...], w_ref[...])
        parts = [
            (both[:, :PAIR] + bias_ref[0:1, :]).astype(BF),
            both[:, PAIR : 2 * PAIR].astype(BF),
            (both[:, 2 * PAIR :] + bias_ref[1:2, :]).astype(BF),
        ]
        for ref, part in zip(halo_refs, parts):
            ref[...] = part
        keys = jnp.concatenate([k_ref[...], parts[1]], axis=0)
        values = jnp.concatenate([v_ref[...], parts[2]], axis=0)
        ctx_ref[...], scaled_ref[...] = attend(
            q_ref[rows:, :], keys, values, mask_ref[...], log_ref, pl.program_id(0)
        )

    operands = [halo_near, halo_far, weight, bias, hot, query, key, value]
    in_specs = [whole(o.shape) for o in operands]
    in_specs[2] = pl.BlockSpec((D, 3 * PAIR), lambda p, _: (0, p))
    in_specs[3] = column(VECS)
    in_specs[5:] = [column(2 * rows)] * 3
    outs = [struct((rows, HALF), BF)] * 4 + [struct((rows, HALF), F32)]
    outs += [struct((LABELS, 3 * rows), BF), struct((VECS, rows), F32)]
    return call(
        "attend_halo",
        body,
        scalars,
        operands,
        in_specs,
        outs,
        [column(rows)] * 5 + [whole((LABELS, 3 * rows)), whole((VECS, rows))],
        (HALF // PAIR,),
        [pltpu.VMEM((rows, D), BF), pltpu.VMEM((rows, 3 * rows), F32)],
        micros=6,
    )


def feed_forward(scalars, block, ctx_mine, ctx_partner, x, vecs, up_bias, weights, rows):
    count = len(weights)
    fresh = len(weights[0].shape) == 3

    def body(sc, mine_ref, partner_ref, x_ref, vec_ref, bias_ref, *refs):
        weight_refs, refs = refs[:count], refs[count:]
        (norm_ref, inv_ref, first_ref, gate_ref, active_ref, part_ref), refs = refs[:6], refs[6:]
        if fresh:
            up_ref, down_ref, out_ref, other_ref, full_ref = refs
            for k in range(2):
                at, to = 2 * k * HID, slice(k * HID, (k + 1) * HID)
                place(up_ref, weight_refs, sc[1], slice(at, at + HID), to)
                place(down_ref, weight_refs, sc[1], slice(at + HID, at + 2 * HID), to)
            place(full_ref, weight_refs, sc[1], slice(4 * HID, 4 * HID + D), slice(None))
            for ref, flip in ((out_ref, 0), (other_ref, 1)):
                for k in range(2):
                    at = pl.multiple_of((sc[2] ^ flip ^ (2 * k)) * QUARTER, 16)
                    ref[k * QUARTER : (k + 1) * QUARTER, :] = full_ref[pl.ds(at, QUARTER), :]
        else:
            up_ref, down_ref, out_ref, other_ref = weight_refs

        attention = dot(mine_ref[...], out_ref[...]) + dot(partner_ref[...], other_ref[...])
        total = x_ref[...].astype(F32) + (attention + vec_ref[2:3, :])
        center = total - jnp.mean(total, axis=-1, keepdims=True)
        inverse = lax.rsqrt(jnp.mean(center * center, axis=-1, keepdims=True) + EPS)
        normed = center * inverse
        norm_ref[...] = normed
        inv_ref[...] = jnp.broadcast_to(inverse, (rows, 128))
        first = (normed * vec_ref[3:4, :] + vec_ref[4:5, :]).astype(BF)
        first_ref[...] = first
        gate = dot(first, up_ref[...]) + bias_ref[0:1, :]
        gate_ref[...] = gate
        active = (gate * (1.0 + lax.erf(gate * ROOT_HALF)) * 0.5).astype(BF)
        active_ref[...] = active
        part_ref[...] = dot_nt(active, down_ref[...]).astype(BF)

    operands = [ctx_mine, ctx_partner, x, vecs, up_bias, *weights]
    in_specs = [whole(o.shape) for o in operands]
    in_specs[2] = pl.BlockSpec((rows, D), lambda *_: (block, 0))
    outs = [
        struct((rows, D), F32),
        struct((rows, 128), F32),
        struct((rows, D), BF),
        struct((rows, 2 * HID), F32),
        struct((rows, 2 * HID), BF),
        struct((rows, D), BF),
    ]
    scratch = []
    if fresh:
        outs += [struct((D, 2 * HID), BF)] * 2 + [struct((HALF, D), BF)] * 2
        scratch = [pltpu.VMEM((D, D), BF)]
    results = call(
        "feed_forward",
        body,
        scalars,
        operands,
        in_specs,
        outs,
        [whole(o.shape) for o in outs],
        (1,),
        scratch,
        micros=6,
    )
    return results[:6], (results[6:] if fresh else weights)


def gelu_slope(scalars, gate):
    rows = gate.shape[0] // 2

    def body(_, gate_ref, slope_ref):
        gate_here = gate_ref[...]
        bell = jnp.exp(gate_here * gate_here * -0.5) * ROOT_TWO_PI
        slope_ref[...] = 0.5 * (1.0 + lax.erf(gate_here * ROOT_HALF)) + gate_here * bell

    spec = pl.BlockSpec((rows, gate.shape[1]), lambda r, _: (r, 0))
    return call(
        "gelu_slope", body, scalars, [gate], [spec], [struct(gate.shape, F32)], [spec], (2,), micros=3
    )[0]


def second_norm(scalars, block, part, received, normed, slope, cotangent, vecs, up, down, earlier, rows):
    def body(sc, part_ref, recv_ref, norm_ref, slope_ref, cot_ref, other_ref, vec_ref, up_ref, down_ref, *refs):
        old, refs = refs[: len(earlier)], refs[len(earlier) :]
        (total_grad_ref, branch_grad_ref, gate_grad_ref, first_part_ref, out_ref, sums_ref, bias_ref) = refs
        mine = sc[0] == block
        first = norm_ref[...] * vec_ref[3:4, :] + vec_ref[4:5, :]
        branch = part_ref[...].astype(F32) + recv_ref[...].astype(F32) + vec_ref[5:6, :]
        total = first + branch
        center = total - jnp.mean(total, axis=-1, keepdims=True)
        inverse = lax.rsqrt(jnp.mean(center * center, axis=-1, keepdims=True) + EPS)
        here = center * inverse
        upstream = jnp.where(mine, cot_ref[...].astype(F32), other_ref[...].astype(F32))
        scaled = upstream * vec_ref[6:7, :]
        inner = (
            scaled
            - jnp.mean(scaled, axis=-1, keepdims=True)
            - here * jnp.mean(scaled * here, axis=-1, keepdims=True)
        )
        total_grad = inner * inverse
        total_grad_ref[...] = total_grad
        branch_grad = total_grad.astype(BF)
        branch_grad_ref[...] = branch_grad
        gate_grad = (dot(branch_grad, down_ref[...]) * slope_ref[...]).astype(BF)
        gate_grad_ref[...] = gate_grad
        hidden = jnp.broadcast_to(jnp.sum(gate_grad.astype(F32), axis=0, keepdims=True), (8, 2 * HID))
        bias_ref[...] = hidden + old[2][...] if old else hidden
        first_part_ref[...] = dot_nt(gate_grad, up_ref[...]).astype(BF)

        @pl.when(mine)
        def _():
            out_ref[...] = (here * vec_ref[6:7, :] + vec_ref[7:8, :]).astype(BF)
            sums_ref[...] = jnp.zeros_like(sums_ref)
            sums_ref[0:1, :] = jnp.sum(upstream * here, axis=0, keepdims=True)
            sums_ref[1:2, :] = jnp.sum(upstream, axis=0, keepdims=True)
            sums_ref[2:3, :] = jnp.sum(branch_grad.astype(F32), axis=0, keepdims=True)

        if old:

            @pl.when(jnp.logical_not(mine))
            def _():
                out_ref[...] = old[0][...]
                sums_ref[...] = old[1][...]

        else:

            @pl.when(jnp.logical_not(mine))
            def _():
                out_ref[...] = jnp.zeros_like(out_ref)
                sums_ref[...] = jnp.zeros_like(sums_ref)

    operands = [part, received, normed, slope, *cotangent, vecs, up, down, *earlier]
    outs = [
        struct((rows, D), F32),
        struct((rows, D), BF),
        struct((rows, 2 * HID), BF),
        struct((rows, D), BF),
        struct((rows, D), BF),
        struct((8, D), F32),
        struct((8, 2 * HID), F32),
    ]
    results = call(
        "second_norm",
        body,
        scalars,
        operands,
        [whole(o.shape) for o in operands],
        outs,
        [whole(o.shape) for o in outs],
        (1,),
        micros=5,
    )
    return results[:4], results[4:]


def split_outs(width):
    return [struct((GROUPS // 2, BLOCK, width), BF)] * 2


def feed_forward_grads(scalars, blocks, rows):
    def body(sc, *refs):
        keep_ref, send_ref, result_ref = refs[-3:]
        step = pl.program_id(0)

        @pl.when(step % 2 == 0)
        def _():
            result_ref[...] = dot_tn(refs[0][...], refs[1][...]) + dot_tn(refs[4][...], refs[5][...])

        @pl.when(step % 2 == 1)
        def _():
            result_ref[...] = dot_tn(refs[2][...], refs[3][...]) + dot_tn(refs[6][...], refs[7][...])

        split_rows(result_ref, sc[1], keep_ref, send_ref)

    half = pl.BlockSpec((rows, HID), lambda c, _: (0, c // 2))
    outs = split_outs(4 * HID)
    out_specs = [pl.BlockSpec((GROUPS // 2, BLOCK, HID), lambda c, _: (0, 0, c))] * 2
    return call(
        "feed_forward_grads",
        body,
        scalars,
        [value for block in blocks for value in block],
        [whole((rows, D)), half] * 4,
        outs,
        out_specs,
        (4,),
        [pltpu.VMEM((D, HID), F32)],
        micros=8,
    )


def first_norm(
    scalars, block, part, received, total_grad, normed, inverse, vecs, out_weight, ctx, logs, earlier, rows
):
    def body(sc, part_ref, recv_ref, grad_ref, norm_ref, inv_ref, vec_ref, weight_ref, ctx_ref, log_ref, *refs):
        old, refs = refs[: len(earlier)], refs[len(earlier) :]
        attention_ref, context_ref, inner_ref, own_ref, sums_ref = refs[:5]
        mine = sc[0] == block
        upstream = grad_ref[...] + part_ref[...].astype(F32) + recv_ref[...].astype(F32)
        here = norm_ref[...]
        scaled = upstream * vec_ref[3:4, :]
        inner = (
            scaled
            - jnp.mean(scaled, axis=-1, keepdims=True)
            - here * jnp.mean(scaled * here, axis=-1, keepdims=True)
        )
        total = inner * inv_ref[:, :1]
        attention = total.astype(BF)
        attention_ref[...] = attention
        context = dot_nt(attention, weight_ref[...]).astype(BF)
        context_ref[...] = context
        lane = lax.broadcasted_iota(jnp.int32, (VECS, HALF), 1) // HEAD_DIM
        picks = jnp.where(lane == lax.broadcasted_iota(jnp.int32, (VECS, HALF), 0), 1.0, 0.0)
        inner = lax.dot_general(
            picks,
            context.astype(F32) * ctx_ref[...],
            (((1,), (1,)), ((), ())),
            precision=lax.Precision.HIGHEST,
            preferred_element_type=F32,
        )
        inner_ref[...] = inner
        if block == 1:
            send_ref = refs[5]
            turned = jnp.concatenate([weight_ref[QUARTER:, :], weight_ref[:QUARTER, :]], axis=0)
            send_ref[:rows, :] = dot_nt(attention, turned).astype(BF)
            rest = jnp.concatenate([log_ref[...], inner], axis=0)
            send_ref[rows:, :] = jnp.zeros((3 * LABELS, HALF), BF)
            for k in range(3):
                at = rows + k * LABELS
                piece = rest.astype(BF)
                send_ref[at : at + LABELS, :rows] = piece
                rest = rest - piece.astype(F32)

        @pl.when(mine)
        def _():
            own_ref[...] = total
            sums_ref[...] = jnp.zeros_like(sums_ref)
            sums_ref[0:1, :] = jnp.sum(upstream * here, axis=0, keepdims=True)
            sums_ref[1:2, :] = jnp.sum(upstream, axis=0, keepdims=True)
            sums_ref[2:3, :] = jnp.sum(attention.astype(F32), axis=0, keepdims=True)

        @pl.when(jnp.logical_not(mine))
        def _():
            own_ref[...] = old[0][...] if old else jnp.zeros_like(own_ref)
            sums_ref[...] = old[1][...] if old else jnp.zeros_like(sums_ref)

    operands = [part, received, total_grad, normed, inverse, vecs, out_weight, ctx, logs, *earlier]
    outs = [
        struct((rows, D), BF),
        struct((rows, HALF), BF),
        struct((VECS, rows), F32),
        struct((rows, D), F32),
        struct((8, D), F32),
        struct((rows + 3 * LABELS, HALF), BF),
    ][: 6 if block == 1 else 5]
    return call(
        "first_norm",
        body,
        scalars,
        operands,
        [whole(o.shape) for o in operands],
        outs,
        [whole(o.shape) for o in outs],
        (1,),
        micros=3,
    )


def halves(value):
    high = value.astype(BF).astype(F32)
    return jnp.concatenate([high, value - high], axis=1).astype(BF)


def whole_of(table):
    return table[:, :128].astype(F32) + table[:, 128:].astype(F32)


def output_grads(scalars, blocks, small, small_side):
    def body(sc, *refs):
        small_ref, side_ref, keep_ref, send_ref, result_ref = refs[-5:]
        for side in range(2):
            part = dot_tn(refs[side][...], refs[2][...]) + dot_tn(refs[3 + side][...], refs[5][...])
            for k in range(2):
                at = pl.multiple_of((sc[2] ^ side ^ (2 * k)) * QUARTER, 16)
                result_ref[pl.ds(at, QUARTER), :] = part[k * QUARTER : (k + 1) * QUARTER, :]
        for j in range(GROUPS):
            target = (keep_ref, send_ref)[j % 2]
            block = sc[1] ^ j
            rows = pl.ds(pl.multiple_of(block * BLOCK, 16), BLOCK)
            target[j // 2, :BLOCK] = result_ref[rows, :].astype(BF)
            target[j // 2, BLOCK:] = jnp.zeros((LABELS, D), BF)
            target[j // 2, BLOCK:, :256] = halves(small_ref[block] + side_ref[block])

    outs = [struct((GROUPS // 2, BLOCK + LABELS, D), BF)] * 2
    operands = [value for block in blocks for value in block] + [small, small_side]
    return call(
        "output_grads",
        body,
        scalars,
        operands,
        [whole(o.shape) for o in operands],
        outs,
        [whole(o.shape) for o in outs],
        (1,),
        [pltpu.VMEM((D, D), F32)],
        micros=4,
    )


def attend_backward(scalars, pair, halo, grad_blocks, logs, inners, hot, weight, rows):
    base = 3 * rows
    steps = HALF // PAIR

    def body(sc, *refs):
        pair_refs, halo_refs, refs = refs[:3], refs[3:6], refs[6:]
        far_ref, near_ref, halo_ref, stats_ref, *refs = refs
        log_refs, inner_refs, (hot_ref, w_ref, *refs) = refs[:2], refs[2:4], refs[4:]
        out_ref, keep_ref, send_ref, sums_ref, mask_ref, key_ref, value_ref, acc_ref, q_ref, k_ref, v_ref, line_ref = refs
        for target, first_part, last_part in zip((q_ref, k_ref, v_ref), pair_refs, halo_refs):
            target[: 2 * rows, :] = first_part[...]
            target[2 * rows :, :] = last_part[...]
        step = pl.program_id(0)

        @pl.when(step == 0)
        def _():
            mask_ref[...] = (dot_tn(hot_ref[...], hot_ref[...]) - 1.0) * MASKED
            lines = jnp.zeros((LABELS, rows), F32)
            for k in range(3):
                at = rows + k * LABELS
                lines = lines + stats_ref[at : at + LABELS, :rows].astype(F32)
            line_ref[...] = lines

        key_ref[...] = jnp.zeros_like(key_ref)
        value_ref[...] = jnp.zeros_like(value_ref)
        lane = lax.broadcasted_iota(jnp.int32, (1, PAIR), 1)
        query_grads = [jnp.zeros((PAIR, rows), F32), jnp.zeros((PAIR, rows), F32)]
        for head in range(2):
            part = jnp.where((lane // HEAD_DIM) == head, 1.0, 0.0)
            key_turned = (k_ref[...].astype(F32) * part).T.astype(BF)
            line = 2 * step + head
            other = lax.rem(line + 3, 6)
            lines = [(log_refs[k][pl.ds(line, 1), :], inner_refs[k][pl.ds(line, 1), :]) for k in range(2)]
            lines += [(line_ref[pl.ds(other, 1), :], line_ref[pl.ds(other + VECS, 1), :])]
            for index, (low, high) in enumerate(((0, 2 * rows), (0, base), (rows, 2 * rows))):
                start = index * rows
                mine = (q_ref[start : start + rows].astype(F32) * (part * HEAD_DIM**-0.5)).astype(BF)
                grads = (far_ref, near_ref, halo_ref)[index][:rows, :]
                grads = (grads.astype(F32) * part).astype(BF)
                scores = dot_nt(k_ref[low:high], mine) + mask_ref[low:high, start : start + rows]
                log_total, inner = lines[index]
                probs = jnp.exp(scores - log_total)
                pulled = dot_nt(v_ref[low:high], grads)
                score_grads = (probs * (pulled - inner)).astype(BF)
                top = min(high, 2 * rows)
                span = top - low
                value_ref[low:top, :] += dot(probs[:span].astype(BF), grads)
                key_ref[low:top, :] += dot(score_grads[:span], mine)
                if index < 2:
                    query_grads[index] = query_grads[index] + dot(key_turned[:, low:high], score_grads)
        for index in range(2):
            turned = (query_grads[index] * HEAD_DIM**-0.5).T.astype(BF)
            out_ref[index * rows : (index + 1) * rows, :PAIR] = turned
        out_ref[:, PAIR : 2 * PAIR] = key_ref[...].astype(BF)
        out_ref[:, 2 * PAIR :] = value_ref[...].astype(BF)
        sums = jnp.sum(out_ref[...].astype(F32), axis=0, keepdims=True)
        sums_ref[...] = jnp.broadcast_to(sums, (8, 3 * PAIR))
        product = dot_nt(out_ref[...], w_ref[...])

        @pl.when(step == 0)
        def _():
            acc_ref[...] = product

        @pl.when(step > 0)
        def _():
            acc_ref[...] += product

        @pl.when(step == steps - 1)
        def _():
            near = sc[0]
            keep_ref[...] = acc_ref[pl.ds(pl.multiple_of(near * rows, rows), rows), :]
            other = acc_ref[pl.ds(pl.multiple_of((1 - near) * rows, rows), rows), :]
            send_ref[...] = other.astype(BF)

    stats = grad_blocks[2]
    operands = [*pair, *halo, *grad_blocks, stats, *logs, *inners, hot, weight]
    in_specs = [column(2 * rows)] * 3 + [column(rows)] * 5 + [column(stats.shape[0])]
    in_specs += [whole(o.shape) for o in operands[9:15]]
    in_specs += [pl.BlockSpec((D, 3 * PAIR), lambda p, _: (0, p))]
    outs = [struct((2 * rows, 3 * HALF), BF), struct((rows, D), F32), struct((rows, D), BF)]
    outs += [struct((8, 3 * HALF), F32)]
    out_specs = [
        pl.BlockSpec((2 * rows, 3 * PAIR), lambda p, _: (0, p)),
        whole((rows, D)),
        whole((rows, D)),
        pl.BlockSpec((8, 3 * PAIR), lambda p, _: (0, p)),
    ]
    scratch = [
        pltpu.VMEM((base, base), F32),
        pltpu.VMEM((2 * rows, PAIR), F32),
        pltpu.VMEM((2 * rows, PAIR), F32),
        pltpu.VMEM((2 * rows, D), F32),
    ] + [pltpu.VMEM((base, PAIR), BF)] * 3
    scratch += [pltpu.VMEM((LABELS, rows), F32)]
    return call(
        "attend_backward",
        body,
        scalars,
        operands,
        in_specs,
        outs,
        out_specs,
        (steps,),
        scratch,
        micros=MICROS,
    )


def projection_grads(scalars, x, grads, rows):
    tall = 2 * rows

    def body(sc, x_ref, grad_ref, *refs):
        result_ref = refs[-1]
        result_ref[...] = dot_tn(x_ref[...], grad_ref[...])
        split_rows(result_ref, sc[1], refs[0], refs[1])

    outs = split_outs(3 * HALF)
    out_specs = [pl.BlockSpec((GROUPS // 2, BLOCK, 3 * PAIR), lambda p, _: (0, 0, p))] * 2
    return call(
        "projection_grads",
        body,
        scalars,
        [x, grads],
        [pl.BlockSpec((tall, D), lambda p, _: (0, 0)), pl.BlockSpec((tall, 3 * PAIR), lambda p, _: (0, p))],
        outs,
        out_specs,
        (HALF // PAIR,),
        [pltpu.VMEM((D, 3 * PAIR), F32)],
        micros=5,
    )


def combine(scalars, keep, received):
    count, rows, width = keep.shape
    chunk = width // 3

    def body(_, keep_ref, recv_ref, *refs):
        for k in range(count):
            total = keep_ref[k].astype(F32) + recv_ref[k].astype(F32)
            refs[k][...] = total.astype(refs[k].dtype)

    block = pl.BlockSpec((count, rows, chunk), lambda c, _: (0, 0, c))
    outs = [struct((rows, width), F32)] + [struct((rows, width), BF)] * (count - 1)
    spec = pl.BlockSpec((rows, chunk), lambda c, _: (0, c))
    return list(call(
        "combine",
        body, scalars, [keep, received], [block, block], outs, [spec] * count, (3,)))


def combine_both(scalars, keep, received, out_keep, out_received):
    count, rows, wide = keep.shape
    tall = rows + LABELS

    def body(_, keep_ref, recv_ref, out_keep_ref, out_recv_ref, *refs):
        for k in range(count):
            kind = refs[k].dtype
            refs[k][:rows, :wide] = (keep_ref[k].astype(F32) + recv_ref[k].astype(F32)).astype(kind)
            refs[k][rows:, :wide] = jnp.zeros((LABELS, wide), kind)
            total = out_keep_ref[k, :rows].astype(F32) + out_recv_ref[k, :rows].astype(F32)
            refs[k][:rows, wide:] = total.astype(kind)
            refs[k][rows:, wide:] = jnp.zeros((LABELS, D), kind)
            small = whole_of(out_keep_ref[k, rows:, :256]) + whole_of(out_recv_ref[k, rows:, :256])
            refs[k][rows:, wide : wide + 256] = halves(small).astype(kind)

    outs = [struct((tall, wide + D), F32)] + [struct((tall, wide + D), BF)] * (count - 1)
    return simple("combine_both", body, scalars, [keep, received, out_keep, out_received], outs, 2)


def total_feed(scalars, sums):
    rows = sums[0].shape[0]

    def body(_, *refs):
        keep_ref, send_ref = refs[-2:]
        total = refs[0][...]
        for ref in refs[1:-2]:
            total = total + ref[...].astype(F32)
        keep_ref[...] = total[:, : 2 * HID]
        send_ref[...] = total[:, 2 * HID :].astype(BF)

    outs = [struct((rows, 2 * HID), F32), struct((rows, 2 * HID), BF)]
    return simple("total_feed", body, scalars, sums, outs, 2)


def total_projection(scalars, sums, rows):
    tall = sums[0].shape[0]
    wide = 3 * HALF

    def body(sc, *refs):
        keep_ref, send_ref = refs[-2:]
        total = refs[0][:rows, :]
        for ref in refs[1:-2]:
            total = total + ref[:rows, :].astype(F32)
        near, far = [], []
        for kind in range(3):
            both = [total[:, (3 * p + kind) * PAIR : (3 * p + kind + 1) * PAIR] for p in range(3)]
            both = jnp.concatenate(both, axis=1)
            near.append(both[:, :QUARTER])
            far.append(both[:, QUARTER:])
        near.append(pltpu.roll(total[:, wide:], D - sc[2] * QUARTER, 1)[:, :QUARTER])
        far.append(pltpu.roll(total[:, wide:], D - (sc[2] ^ 2) * QUARTER, 1)[:, :QUARTER])
        keep_ref[:rows, :] = jnp.concatenate(near, axis=1)
        send_ref[:rows, :] = jnp.concatenate(far, axis=1).astype(BF)
        if tall > rows:
            small = jnp.zeros((LABELS, 128), F32)
            for ref in refs[:-2]:
                small = small + whole_of(ref[rows:, wide : wide + 256])
            keep_ref[rows:, :] = jnp.zeros((LABELS, D), F32)
            send_ref[rows:, :] = jnp.zeros((LABELS, D), BF)
            keep_ref[rows:, :128] = small
            send_ref[rows:, :256] = halves(small)

    outs = [struct((tall, D), F32), struct((tall, D), BF)]
    return simple("total_projection", body, scalars, sums, outs, 2)


def finish_feed(scalars, keep, received):
    rows = keep.shape[0]

    def body(_, keep_ref, recv_ref, up_ref, down_ref):
        up_ref[...] = keep_ref[:, :HID] + recv_ref[:, :HID].astype(F32)
        down_ref[...] = keep_ref[:, HID:] + recv_ref[:, HID:].astype(F32)

    outs = [struct((rows, HID), F32)] * 2
    return simple("finish_feed", body, scalars, [keep, received], outs)


def finish_projection(scalars, keep, received, rows):
    tall = keep.shape[0]

    def body(_, keep_ref, recv_ref, *refs):
        total = keep_ref[:rows, :] + recv_ref[:rows, :].astype(F32)
        for k in range(4):
            refs[k][...] = total[:, k * QUARTER : (k + 1) * QUARTER]
        if tall > rows:
            small = keep_ref[rows:, :128] + whole_of(recv_ref[rows:, :256])
            for k in range(VECS):
                refs[4 + k][...] = small[k, :BLOCK]
            for k in range(FF // GROUPS // 128):
                refs[4 + VECS][k * 128 : (k + 1) * 128] = small[VECS + k]

    outs = [struct((rows, QUARTER), F32)] * 4
    if tall > rows:
        outs += [struct((BLOCK,), F32)] * VECS + [struct((FF // GROUPS,), F32)]
    return simple("finish_projection", body, scalars, [keep, received], outs)


def small_sums(scalars, sums_one, sums_two, sums_hidden, sums_projection):
    def body(sc, one_ref, two_ref, hidden_ref, projection_ref, out_ref, wide_ref, tall_ref):
        out_ref[...] = jnp.zeros_like(out_ref)
        lanes = lax.broadcasted_iota(jnp.int32, (1, D), 1)
        near, far = lanes < QUARTER, (lanes >= QUARTER) & (lanes < HALF)
        for row, kind in ((0, 0), (1, 2)):
            line = jnp.concatenate(
                [
                    projection_ref[0:1, (3 * p + kind) * PAIR : (3 * p + kind + 1) * PAIR]
                    for p in range(3)
                ]
                + [jnp.zeros((1, HALF), F32)],
                axis=1,
            )
            low = pltpu.roll(jnp.broadcast_to(jnp.where(near, line, 0.0), (8, D)), sc[2] * QUARTER, 1)
            high = jnp.broadcast_to(jnp.where(far, line, 0.0), (8, D))
            high = pltpu.roll(high, D - QUARTER + (sc[2] ^ 2) * QUARTER, 1)
            wide_ref[row : row + 1, :] = (low + high)[0:1]
        wide_ref[2:3, :] = one_ref[2:3, :]
        wide_ref[3:5, :] = one_ref[0:2, :]
        wide_ref[5:6, :] = two_ref[2:3, :]
        wide_ref[6:8, :] = two_ref[0:2, :]
        tall_ref[...] = jnp.zeros_like(tall_ref)
        for k in range(2):
            to = pl.multiple_of((sc[2] ^ (2 * k)) * HID, 128)
            tall_ref[0:1, pl.ds(to, HID)] = hidden_ref[0:1, k * HID : (k + 1) * HID]
        share = FF // GROUPS
        for d in range(GROUPS):
            out_ref[d, :VECS, :BLOCK] = wide_ref[:, d * BLOCK : (d + 1) * BLOCK]
            for c in range(share // 128):
                at = d * share + c * 128
                out_ref[d, VECS + c : VECS + c + 1, :] = tall_ref[0:1, at : at + 128]

    operands = [sums_one, sums_two, sums_hidden, sums_projection]
    shape = (GROUPS, LABELS, 128)
    return call(
        "small_sums",
        body,
        scalars,
        operands,
        [whole(o.shape) for o in operands],
        [struct(shape, F32)],
        [whole(shape)],
        (1,),
        [pltpu.VMEM((VECS, D), F32), pltpu.VMEM((8, FF), F32)],
    )[0]


def per_device(
    tokens,
    segments,
    query_weight,
    key_weight,
    value_weight,
    output_weight,
    query_bias,
    value_bias,
    output_bias,
    first_gain,
    first_shift,
    up_weight,
    up_bias,
    down_weight,
    down_bias,
    second_gain,
    second_shift,
    cotangent,
):
    seq_count = lax.axis_size("seq")
    count = lax.axis_size("dp")
    place_z = lax.axis_index("seq")
    assert seq_count == 4
    direct = count == GROUPS
    rows = tokens.shape[1]
    piece_rows = query_weight.shape[0]
    near = (place_z == 1) | (place_z == 2)
    base = lax.axis_index("dp") if direct else 0
    scalars = jnp.stack([near, base, place_z]).astype(jnp.int32)

    own = tokens[0]
    cot_own = cotangent[0]
    lines = [
        query_bias,
        value_bias,
        output_bias,
        first_gain,
        first_shift,
        down_bias,
        second_gain,
        second_shift,
    ]
    lines = [line[None] for line in lines] if direct else []
    first_send, mine, wide, labelled, own_docs = pack_inputs(
        scalars,
        [query_weight, key_weight, value_weight, output_weight],
        own,
        segments,
        up_weight,
        down_weight.T,
        lines,
        up_bias[None],
    )
    arrived = swap(first_send, "seq", 2)
    side = swap(output_weight, "seq", 1)
    if direct:
        mine_chip = [mine, swap(mine, "dp", 2), swap(mine, "dp", 4)]
        labelled, side, mine_chip, arrived = together(labelled, side, mine_chip, arrived)
    else:
        arrived, labelled, side = together(arrived, labelled, side)
    narrow_far, wide_send, both = split_arrived(scalars, arrived, wide, side, mine)
    wide_far = swap(wide_send, "seq", 2)
    if direct:
        far_chip = [narrow_far, swap(narrow_far, "dp", 2), swap(narrow_far, "dp", 4)]
        both_far = swap(both, "dp", 6)
        mine_chip, labelled, cot_own, wide, far_chip, both_far, wide_far = together(
            mine_chip, labelled, cot_own, wide, far_chip, both_far, wide_far
        )
        stacked = stack_narrow(scalars, mine_chip, far_chip, both_far)
        pieces = [stacked, swap(stacked, "dp", 1)]
    partner = swap(labelled, "seq", 1)
    halo_near = lax.ppermute(labelled, "seq", [(1, 2), (2, 1)])
    if direct:
        feed_piece = pack_feed(scalars, wide_far, first_send, arrived, side)
        feed_chip = [feed_piece, swap(feed_piece, "dp", 2), swap(feed_piece, "dp", 4)]
        wide, pieces, partner, feed_chip, halo_near = together(
            wide, pieces, partner, feed_chip, halo_near
        )
        feed_chip = feed_chip + [swap(feed_chip[0], "dp", 6)]
        wide_last = swap(wide, "dp", 6)
    halo_far = lax.ppermute(halo_near, "seq", [(1, 0), (2, 3)])
    if not direct:
        share = FF // GROUPS
        vectors = jnp.stack(
            [
                query_bias,
                value_bias,
                output_bias,
                first_gain,
                first_shift,
                down_bias,
                second_gain,
                second_shift,
            ]
        )
        lines = lax.all_gather(vectors, "dp", axis=1, tiled=True).reshape(VECS, GROUPS, BLOCK)
        lines = jnp.pad(lines, ((0, 0), (0, 0), (0, share - BLOCK)))
        tall = lax.all_gather(up_bias, "dp", axis=0, tiled=True).reshape(1, GROUPS, share)
        lines = jnp.concatenate([lines, jnp.broadcast_to(tall, (VECS, GROUPS, share))], axis=0)
        lines = jnp.pad(lines, ((0, 0), (0, 0), (0, 3 * QUARTER - share)))
        lines = lines.transpose(1, 0, 2)
        gathered = gather_rows(mine)
        pieces = [
            jnp.concatenate([half[:, :, 2 * HID :], lines[k::2], far], axis=1)
            for k, (half, far) in enumerate(zip(gathered, gather_rows(narrow_far)))
        ]
        feed = gather_rows(pack_feed(scalars, wide_far, first_send, arrived, side))
        weights = [
            jnp.concatenate([half[:, :, : 2 * HID], far], axis=2) for half, far in zip(gathered, feed)
        ]

    def rows_of(keep, send):
        return jnp.stack([keep, send], axis=1).reshape(GROUPS, -1, keep.shape[2]).astype(F32)

    def spread(sums):
        return [sums[0]] + [swap(sums[k], "dp", 2 * k) for k in range(1, len(sums))]

    def scattered(table):
        return [lax.psum_scatter(table, "dp", scatter_dimension=0, tiled=True)]

    *pair, ctx_far, x, weight, hot, vecs, hidden_bias, bias, log_far, scaled_far = attend_pair(
        scalars, own, partner, own_docs, pieces, rows
    )
    if direct:
        pair, ctx_far, cot_own, halo_far = together(pair, ctx_far, cot_own, halo_far)
    *halo, ctx_near, scaled_near, hot, log_near = attend_halo(scalars, halo_near, halo_far, weight, bias, hot, *pair, rows)
    ctx_mine = [ctx_far, ctx_near]
    ctx_partner = [swap(ctx_far, "seq", 1), None]
    if direct:
        ctx_mine[1], ctx_partner[0], wide_last, feed_chip = together(
            ctx_mine[1], ctx_partner[0], wide_last, feed_chip
        )
        stacked = stack_wide(scalars, mine_chip, wide_last, feed_chip)
        weights = [stacked, swap(stacked, "dp", 1)]
    ctx_partner[1] = swap(ctx_mine[1], "seq", 1)
    cot_partner = swap(cot_own, "seq", 1)

    forward, slopes, part_far = [None, None], [None, None], [None, None]
    for block in (1, 0):
        forward[block], weights = feed_forward(
            scalars, block, ctx_mine[block], ctx_partner[block], x, vecs, hidden_bias, weights, rows
        )
        part_far[block] = swap(forward[block][5], "seq", 1)
    up, down, out_mine, _ = weights
    second, second_shared, first_part_far = [None, None], [], [None, None]
    for block in (1, 0):
        slopes[block] = gelu_slope(scalars, forward[block][3])
    for block in (1, 0):
        second[block], second_shared = second_norm(
            scalars,
            block,
            forward[block][5],
            part_far[block],
            forward[block][0],
            slopes[block],
            (cot_own, cot_partner),
            vecs,
            up,
            down,
            second_shared,
            rows,
        )
        if block == 1:
            first_part_far[block] = swap(second[block][3], "seq", 1)
    feed_parts = feed_forward_grads(
        scalars,
        [(forward[k][2], second[k][2], second[k][1], forward[k][4]) for k in range(2)],
        rows,
    )
    first_part_far[1], second, second_shared, feed_parts = together(
        first_part_far[1], second, second_shared, feed_parts
    )
    first_part_far[0] = swap(second[0][3], "seq", 1)
    layer_output, sums_two, sums_hidden = second_shared
    attention_grad, ctx_grad, inners, first_shared = [None, None], [None, None], [None, None], []
    logs, scaled = [log_far, log_near], [scaled_far, scaled_near]

    def finish(block):
        attention_grad[block], ctx_grad[block], inners[block], *shared = first_norm(
            scalars,
            block,
            second[block][3],
            first_part_far[block],
            second[block][0],
            forward[block][0],
            forward[block][1],
            vecs,
            out_mine,
            scaled[block],
            logs[block],
            first_shared,
            rows,
        )
        return shared

    *first_shared, halo_send = finish(1)
    halo_grad = swap(halo_send, "seq", 2)
    if direct:
        feed_sums = combine(scalars, feed_parts[0], swap(feed_parts[1], "dp", 1))
        feed_sums = spread(feed_sums)
    else:
        feed_sums = scattered(rows_of(*feed_parts).reshape(D, -1))
    own_grad, sums_one = finish(0)

    grads, input_keep, input_send, sums_projection = attend_backward(
        scalars, pair, halo, [*ctx_grad, halo_grad], logs, inners, hot, weight, rows
    )
    input_far = swap(input_send, "seq", 1)
    small = small_sums(scalars, sums_one, sums_two, sums_hidden, sums_projection)
    small_side = swap(small, "seq", 1)
    projection_parts = projection_grads(scalars, x, grads, rows)
    projection_parts, small_side, feed_sums = together(projection_parts, small_side, feed_sums)
    out_blocks = [(ctx_mine[k], ctx_partner[k], attention_grad[k]) for k in range(2)]
    if direct:
        projection_received = swap(projection_parts[1], "dp", 1)
        out_parts = output_grads(scalars, out_blocks, small, small_side)
        out_received = swap(out_parts[1], "dp", 1)
        feed_keep, feed_send = total_feed(scalars, feed_sums)
        feed_far = swap(feed_send, "seq", 2)
        sums = spread(
            combine_both(scalars, projection_parts[0], projection_received, out_parts[0], out_received)
        )
    else:
        out_parts = rows_of(*output_grads(scalars, out_blocks, small, small_side))
        sums = scattered(
            jnp.concatenate(
                [rows_of(*projection_parts).reshape(D, -1), out_parts[:, :BLOCK].reshape(D, -1)], axis=1
            )
        )
        feed_keep, feed_send = total_feed(scalars, feed_sums)
        feed_far = swap(feed_send, "seq", 2)
    up_grad, down_grad = finish_feed(scalars, feed_keep, feed_far)
    input_grad = own_grad + input_keep + input_far.astype(F32)
    if direct:
        sums, up_grad, input_grad = together(sums, up_grad, input_grad)
    keep, send = total_projection(scalars, sums, piece_rows)
    projections = list(finish_projection(scalars, keep, swap(send, "seq", 2), piece_rows))
    if direct:
        projections, vec, tall_lines = projections[:4], projections[4:-1], projections[-1]
    else:
        tile = out_parts[:, BLOCK:, :128] + out_parts[:, BLOCK:, 128:256]
        tile = tile + swap(tile, "seq", 2)
        wide_lines = tile[:, :VECS, :BLOCK].transpose(1, 0, 2).reshape(VECS, D)
        wide_lines = lax.psum_scatter(wide_lines, "dp", scatter_dimension=1, tiled=True)
        tall_lines = lax.psum_scatter(tile[:, VECS : VECS + 3].reshape(-1), "dp", tiled=True)
        vec = [wide_lines[k] for k in range(VECS)]
    return (
        layer_output[None],
        input_grad[None],
        *projections,
        vec[0],
        vec[1],
        vec[2],
        vec[3],
        vec[4],
        up_grad,
        tall_lines,
        down_grad.T,
        vec[5],
        vec[6],
        vec[7],
    )


def solution(mesh):
    placed = (
        P("dp", "seq", None),
        P("dp", "seq"),
        P("dp", "seq"),
        P("dp", "seq"),
        P("dp", "seq"),
        P("dp", "seq"),
        P("dp"),
        P("dp"),
        P("dp"),
        P("dp"),
        P("dp"),
        P("dp", "seq"),
        P("dp"),
        P("seq", "dp"),
        P("dp"),
        P("dp"),
        P("dp"),
        P("dp", "seq", None),
    )
    return jax.shard_map(
        per_device,
        mesh=mesh,
        in_specs=placed,
        out_specs=(
            P("dp", "seq", None),
            P("dp", "seq", None),
            P("dp", "seq"),
            P("dp", "seq"),
            P("dp", "seq"),
            P("dp", "seq"),
            P("dp"),
            P("dp"),
            P("dp"),
            P("dp"),
            P("dp"),
            P("dp", "seq"),
            P("dp"),
            P("seq", "dp"),
            P("dp"),
            P("dp"),
            P("dp"),
        ),
        check_vma=False,
    )
```

```python
import jax
import jax.numpy as jnp
from jax import lax
from jax.experimental import pallas as pl
from jax.experimental.pallas import tpu as pltpu
from jax.sharding import PartitionSpec as P

D = 768
HEADS = 12
HEAD_DIM = 64
FF = 3072
EPS = 1e-05
MASKED = 1e30
PAIR = 2 * HEAD_DIM
QUARTER = D // 4
HALF = D // 2
HID = FF // 4
VECS = 8
GROUPS = 8
SHARE = FF // GROUPS // 128
BLOCK = D // GROUPS
LABELS = 16
MARKS = 48
MICROS = 450
BF = jnp.bfloat16
F32 = jnp.float32
ROOT_HALF = 0.7071067811865476
ROOT_TWO_PI = 0.3989422804014327


def dot(a, b):
    return lax.dot_general(a, b, (((1,), (0,)), ((), ())), preferred_element_type=F32)


def dot_nt(a, b):
    return lax.dot_general(a, b, (((1,), (1,)), ((), ())), preferred_element_type=F32)


def dot_tn(a, b):
    return lax.dot_general(a, b, (((0,), (0,)), ((), ())), preferred_element_type=F32)


def swap(value, axis, mask):
    count = lax.axis_size(axis)
    return lax.ppermute(value, axis, [(k, k ^ mask) for k in range(count)])


def together(*values):
    return lax.optimization_barrier(values)


def whole(shape):
    return pl.BlockSpec(shape, lambda *_: (0,) * len(shape))


def params():
    return pltpu.CompilerParams(vmem_limit_bytes=22 * 1024 * 1024)


def call(name, body, scalars, operands, in_specs, outs, out_specs, grid, scratch=(), micros=1):
    spec = pltpu.PrefetchScalarGridSpec(
        num_scalar_prefetch=1,
        grid=grid,
        in_specs=in_specs,
        out_specs=out_specs,
        scratch_shapes=list(scratch),
    )
    return pl.pallas_call(
        body,
        out_shape=outs,
        grid_spec=spec,
        compiler_params=params(),
        cost_estimate=pl.CostEstimate(
            flops=int(micros * 1.0e7), transcendentals=0, bytes_accessed=1024
        ),
        name=name,
    )(scalars, *operands)


def struct(shape, dtype):
    return jax.ShapeDtypeStruct(shape, dtype)


def chip_pieces(piece):
    return [piece] + [swap(piece, "dp", j) for j in range(2, GROUPS, 2)]


def gather_rows(piece):
    full = lax.all_gather(piece, "dp", axis=0, tiled=True)
    full = full.reshape(GROUPS, D // GROUPS, piece.shape[1])
    return [full[0::2], full[1::2]]


def place(target, pair, base, source_cols, target_cols):
    for j in range(GROUPS):
        start = pl.multiple_of((base ^ j) * BLOCK, 16)
        target[pl.ds(start, BLOCK), target_cols] = pair[j % 2][j // 2, :BLOCK, source_cols]


def split_rows(result, base, keep, send):
    for j in range(GROUPS):
        block = result[pl.ds(pl.multiple_of((base ^ j) * BLOCK, 16), BLOCK), :].astype(BF)
        if j % 2:
            send[j // 2] = block
        else:
            keep[j // 2] = block


def simple(name, body, scalars, operands, outs, micros=1):
    return call(
        name,
        body,
        scalars,
        operands,
        [whole(o.shape) for o in operands],
        outs,
        [whole(o.shape) for o in outs],
        (1,),
        micros=micros,
    )


def pack_inputs(scalars, tables, tokens, segments, up, down, lines, tall):
    rows = tokens.shape[0]
    height = tables[0].shape[0]
    skip = 2 * HID + (128 if lines else 0)
    operands = list(tables) + [tokens, segments, up, down] + lines + ([tall] if lines else [])
    count = len(operands)

    def body(_, *refs):
        sources, (send_ref, mine_ref, wide_ref, label_ref, docs_ref), refs = (
            refs[:count],
            refs[count : count + 5],
            refs[count + 5 :],
        )
        copies = [pltpu.make_async_copy(a, b, refs[-1].at[k]) for k, (a, b) in enumerate(zip(sources, refs))]
        for copy in copies:
            copy.start()
        for copy in copies:
            copy.wait()
        joined = jnp.concatenate([ref[...].astype(F32) for ref in refs[:4]], axis=1).astype(BF)
        send_ref[:, :D] = joined
        send_ref[:, D : D + HID] = refs[6][...]
        send_ref[:, D + HID :] = refs[7][...]
        mine_ref[:, :HID] = refs[6][...]
        mine_ref[:, HID : 2 * HID] = refs[7][...]
        part = joined[:, : 3 * QUARTER].astype(F32)
        mine_ref[:, skip:] = part.astype(BF)
        wide_ref[:, :HID] = refs[6][...]
        wide_ref[:, HID:] = refs[7][...]
        docs = refs[5][...].astype(F32)
        docs_ref[...] = docs
        label_ref[:rows, :] = refs[4][...]
        label_ref[rows:, :] = jnp.zeros((MARKS, D), BF)
        label_ref[rows:, :rows] = jnp.broadcast_to(docs, (MARKS, rows)).astype(BF)
        if lines:
            table = [ref[...].astype(F32)[None, :] for ref in refs[8 : 8 + VECS]]
            table = jnp.concatenate(table, axis=0)
            table = [jnp.concatenate([table, jnp.zeros((VECS, 128 - BLOCK), F32)], axis=1)]
            line = refs[8 + VECS][...].astype(F32)[None, :]
            table += [line[:, c * 128 : (c + 1) * 128] for c in range(SHARE)]
            table += [jnp.zeros((height - VECS - SHARE, 128), F32)]
            mine_ref[:, 2 * HID : skip] = jnp.concatenate(table, axis=0).astype(BF)

    outs = [
        struct((height, D + 2 * HID), BF),
        struct((height, skip + 3 * QUARTER), BF),
        struct((height, 2 * HID), BF),
        struct((rows + MARKS, D), BF),
        struct((1, rows), F32),
    ]
    operands = [pltpu.with_memory_space_constraint(o, pltpu.MemorySpace.HBM) for o in operands]
    return call(
        "pack_inputs",
        body,
        scalars,
        operands,
        [pl.BlockSpec(memory_space=pltpu.MemorySpace.HBM)] * count,
        outs,
        [whole(o.shape) for o in outs],
        (1,),
        [pltpu.VMEM(o.shape, o.dtype) for o in operands] + [pltpu.SemaphoreType.DMA((count,))],
    )


def split_arrived(scalars, arrived, mine, labelled):
    rows = arrived.shape[0]
    tall = rows + LABELS
    skip = mine.shape[1] - 3 * QUARTER
    direct = skip > 2 * HID

    def body(_, far_ref, mine_ref, label_ref, narrow_ref, both_ref, send_ref):
        narrow_ref[...] = far_ref[:, : 3 * QUARTER]
        both_ref[:rows, :] = mine_ref[:, skip:]
        both_ref[tall:, :] = far_ref[:, : 3 * QUARTER]
        send_ref[...] = label_ref[...]
        if direct:
            both_ref[rows:tall, :] = jnp.zeros((LABELS, 3 * QUARTER), BF)
            both_ref[rows:tall, :128] = mine_ref[:LABELS, 2 * HID : skip]
            part = far_ref[:, 3 * QUARTER : D].astype(F32)
            step = rows // 4
            part = jnp.concatenate([part[k * step : (k + 1) * step] for k in range(4)], axis=1)
            part = jnp.concatenate([part, jnp.zeros((MARKS - LABELS - step, D), F32)], axis=0)
            send_ref[labelled.shape[0] - MARKS + LABELS :, :] = part.astype(BF)

    outs = [
        struct((rows, 3 * QUARTER), BF),
        struct((rows + tall, 3 * QUARTER), BF),
        struct(labelled.shape, BF),
    ]
    return simple("split_arrived", body, scalars, [arrived, mine, labelled], outs)


def stack_narrow(scalars, mine_chip, far_chip, both_far):
    rows = far_chip[0].shape[0]
    tall = rows + LABELS
    skip = mine_chip[0].shape[1] - 3 * QUARTER

    def body(_, *refs):
        out_ref = refs[-1]
        for k in range(3):
            out_ref[k, :rows] = refs[k][:, skip:]
            out_ref[k, rows:tall] = jnp.zeros((LABELS, 3 * QUARTER), BF)
            out_ref[k, rows:tall, :128] = refs[k][:LABELS, 2 * HID : skip]
            out_ref[k, tall:] = refs[3 + k][...]
        out_ref[3] = refs[6][...]

    shape = (GROUPS // 2, tall + rows, 3 * QUARTER)
    operands = [*mine_chip, *far_chip, both_far]
    return simple("stack_narrow", body, scalars, operands, [struct(shape, BF)])[0]


def stack_wide(scalars, mine_chip, last, feed_chip):
    def body(_, *refs):
        out_ref = refs[-1]
        for k in range(3):
            out_ref[k, :, : 2 * HID] = refs[k][:BLOCK, : 2 * HID]
        out_ref[3, :, : 2 * HID] = refs[3][...]
        for k in range(4):
            out_ref[k, :, 2 * HID :] = refs[4 + k][...]

    shape = (GROUPS // 2, BLOCK, 4 * HID + D)
    return simple("stack_wide", body, scalars, [*mine_chip, last, *feed_chip], [struct(shape, BF)])[0]


def pack_feed(scalars, first_send, arrived, side, last):
    rows = arrived.shape[0]
    columns = slice(3 * QUARTER, D)

    def body(sc, own_ref, arrived_ref, side_ref, last_ref, out_ref):
        out_ref[:, : 2 * HID] = arrived_ref[:, D:]
        final = last_ref[...].astype(F32)
        if last.shape[1] == D:
            step = rows // 4
            final = final[last.shape[0] - MARKS + LABELS :]
            final = [final[:step, k * QUARTER : (k + 1) * QUARTER] for k in range(4)]
            final = jnp.concatenate(final, axis=0)
        total = jnp.zeros((rows, D), F32)
        for k, part in enumerate([own_ref[:, columns], side_ref[...], arrived_ref[:, columns], final]):
            part = jnp.concatenate([part.astype(F32), jnp.zeros((rows, D - QUARTER), F32)], axis=1)
            total = total + pltpu.roll(part, (sc[2] ^ k) * QUARTER, 1)
        out_ref[:, 2 * HID :] = total.astype(BF)

    out = struct((rows, 2 * HID + D), BF)
    return simple("pack_feed", body, scalars, [first_send, arrived, side, last], [out])[0]


def mark(docs, rows):
    number = lax.broadcasted_iota(jnp.int32, (LABELS, rows), 0).astype(F32)
    return jnp.where(jnp.broadcast_to(docs, (LABELS, rows)) == number, 1.0, 0.0).astype(BF)


def attend(query, key, value, mask, log_ref, step):
    lane = lax.broadcasted_iota(jnp.int32, (1, PAIR), 1)
    total = jnp.zeros(query.shape, F32)
    scaled = jnp.zeros(query.shape, F32)
    logs = jnp.zeros(query.shape, F32)
    value = jnp.concatenate([value, jnp.ones(value.shape, BF)], axis=1)
    for head in range(2):
        part = jnp.where((lane // HEAD_DIM) == head, 1.0, 0.0)
        mine = (query.astype(F32) * (part * HEAD_DIM**-0.5)).astype(BF)
        scores = dot_nt(mine, key) + mask
        top = jnp.max(scores, axis=-1, keepdims=True)
        expo = jnp.exp(scores - top)
        whole_sum = jnp.sum(expo, axis=-1, keepdims=True)
        probs = expo * (1.0 / whole_sum)
        rounded = probs.astype(BF)
        context = dot(rounded, value)
        total = total + context[:, :PAIR] * part
        scaled = scaled + context[:, :PAIR] * part / context[:, PAIR:]
        logs = jnp.where(lane == head, top + jnp.log(whole_sum), logs)
    turned = logs.T
    for head in range(2):
        log_ref[pl.ds(2 * step + head, 1), :] = turned[head : head + 1, :]
    return total.astype(BF), scaled


def column(height):
    return pl.BlockSpec((height, PAIR), lambda p, _: (0, p))


def attend_pair(scalars, own, partner, own_docs, pieces, rows):
    base = 2 * rows
    tall = BLOCK + LABELS

    def body(sc, own_ref, partner_ref, docs_ref, *refs):
        weight_refs, refs = refs[:2], refs[2:]
        q_ref, k_ref, v_ref, ctx_ref, x_ref, w_ref, hot_ref, vec_ref, hidden_ref, bias_ref, log_ref, *refs = refs
        scaled_ref, mask_ref = refs
        step = pl.program_id(0)

        @pl.when(step == 0)
        def _():
            near = sc[0]
            own_at = pl.multiple_of(near * rows, rows)
            partner_at = pl.multiple_of((1 - near) * rows, rows)
            x_ref[pl.ds(own_at, rows), :] = own_ref[...]
            x_ref[pl.ds(partner_at, rows), :] = partner_ref[:rows, :]
            hot_ref[:, pl.ds(own_at, rows)] = mark(docs_ref[...], rows)
            docs = partner_ref[rows : rows + 1, :rows].astype(F32)
            hot_ref[:, pl.ds(partner_at, rows)] = mark(docs, rows)
            for j in range(GROUPS):
                at = pl.ds(pl.multiple_of((sc[1] ^ j) * BLOCK, 16), BLOCK)
                for kind in range(3):
                    part = slice(kind * QUARTER, (kind + 1) * QUARTER)
                    both = [weight_refs[j % 2][j // 2, top : top + BLOCK, part] for top in (0, tall)]
                    both = [half.astype(F32) for half in both]
                    both = jnp.concatenate(both, axis=1).astype(BF)
                    for p in range(3):
                        to = (3 * p + kind) * PAIR
                        w_ref[at, to : to + PAIR] = both[:, p * PAIR : (p + 1) * PAIR]
            hot = hot_ref[...]
            mask_ref[...] = (dot_tn(hot[:, :rows], hot) - 1.0) * MASKED
            vectors = jnp.zeros((LABELS, D), F32)
            for j in range(GROUPS):
                block = sc[1] ^ j
                line = weight_refs[j % 2][j // 2, BLOCK:tall, :128].astype(F32)
                table = jnp.where(lax.broadcasted_iota(jnp.int32, line.shape, 1) < BLOCK, line, 0.0)
                table = jnp.concatenate([table, jnp.zeros((LABELS, D - 128), F32)], axis=1)
                vectors = vectors + pltpu.roll(table, block * BLOCK, 1)
                quarter = block // 2
                for k in range(2):

                    @pl.when(quarter == sc[2] ^ (2 * k))
                    def _():
                        for c in range(SHARE):
                            to = pl.multiple_of((block % 2) * (HID // 2) + k * HID + c * 128, 128)
                            value = jnp.broadcast_to(line[VECS + c : VECS + c + 1], (VECS, 128))
                            hidden_ref[:, pl.ds(to, 128)] = value

            vec_ref[...] = vectors[:VECS]
            lanes = lax.broadcasted_iota(jnp.int32, (VECS, HALF), 1)
            low = pltpu.roll(vectors[:VECS], D - sc[2] * QUARTER, 1)[:, :HALF]
            high = pltpu.roll(vectors[:VECS], D + QUARTER - (sc[2] ^ 2) * QUARTER, 1)[:, :HALF]
            bias_ref[...] = jnp.where(lanes < QUARTER, low, high)
            log_ref[...] = jnp.zeros_like(log_ref)

        at = pl.multiple_of(step * 3 * PAIR, PAIR)
        both = dot(x_ref[...], w_ref[:, pl.ds(at, 3 * PAIR)])
        bias = bias_ref[:, pl.ds(pl.multiple_of(step * PAIR, PAIR), PAIR)]
        query = (both[:, :PAIR] + bias[0:1]).astype(BF)
        key = both[:, PAIR : 2 * PAIR].astype(BF)
        value = (both[:, 2 * PAIR :] + bias[1:2]).astype(BF)
        q_ref[...] = query
        k_ref[...] = key
        v_ref[...] = value
        ctx_ref[...], scaled_ref[...] = attend(query[:rows], key, value, mask_ref[...], log_ref, step)

    operands = [own, partner, own_docs, *pieces]
    in_specs = [whole(o.shape) for o in operands]
    outs = [
        struct((base, HALF), BF),
        struct((base, HALF), BF),
        struct((base, HALF), BF),
        struct((rows, HALF), BF),
        struct((base, D), BF),
        struct((D, 3 * HALF), BF),
        struct((LABELS, base), BF),
        struct((VECS, D), F32),
        struct((VECS, 2 * HID), F32),
        struct((VECS, HALF), F32),
        struct((VECS, rows), F32),
        struct((rows, HALF), F32),
    ]
    out_specs = [column(base)] * 3 + [column(rows)] + [whole(o.shape) for o in outs[4:-1]] + [column(rows)]
    return call(
        "attend_pair",
        body,
        scalars,
        operands,
        in_specs,
        outs,
        out_specs,
        (HALF // PAIR,),
        [pltpu.VMEM((rows, base), F32)],
        micros=8,
    )


def attend_halo(scalars, halo_near, halo_far, weight, bias, hot, query, key, value, rows):
    def body(sc, near_ref, far_ref, w_ref, bias_ref, hot_ref, q_ref, k_ref, v_ref, *refs):
        halo_refs, (ctx_ref, scaled_ref, all_ref, log_ref, x_ref, mask_ref) = refs[:3], refs[3:]

        @pl.when(pl.program_id(0) == 0)
        def _():
            all_ref[:, : 2 * rows] = hot_ref[...]

            def halo(ref):
                x_ref[...] = ref[:rows, :]
                all_ref[:, 2 * rows :] = mark(ref[rows : rows + 1, :rows].astype(F32), rows)

            pl.when(sc[0] == 1)(lambda: halo(near_ref))
            pl.when(sc[0] == 0)(lambda: halo(far_ref))
            mask_ref[...] = (dot_tn(all_ref[:, rows : 2 * rows], all_ref[...]) - 1.0) * MASKED
            log_ref[...] = jnp.zeros_like(log_ref)

        both = dot(x_ref[...], w_ref[...])
        parts = [
            (both[:, :PAIR] + bias_ref[0:1, :]).astype(BF),
            both[:, PAIR : 2 * PAIR].astype(BF),
            (both[:, 2 * PAIR :] + bias_ref[1:2, :]).astype(BF),
        ]
        for ref, part in zip(halo_refs, parts):
            ref[...] = part
        keys = jnp.concatenate([k_ref[...], parts[1]], axis=0)
        values = jnp.concatenate([v_ref[...], parts[2]], axis=0)
        ctx_ref[...], scaled_ref[...] = attend(
            q_ref[rows:, :], keys, values, mask_ref[...], log_ref, pl.program_id(0)
        )

    operands = [halo_near, halo_far, weight, bias, hot, query, key, value]
    in_specs = [whole(o.shape) for o in operands]
    in_specs[2] = pl.BlockSpec((D, 3 * PAIR), lambda p, _: (0, p))
    in_specs[3] = column(VECS)
    in_specs[5:] = [column(2 * rows)] * 3
    outs = [struct((rows, HALF), BF)] * 4 + [struct((rows, HALF), F32)]
    outs += [struct((LABELS, 3 * rows), BF), struct((VECS, rows), F32)]
    return call(
        "attend_halo",
        body,
        scalars,
        operands,
        in_specs,
        outs,
        [column(rows)] * 5 + [whole((LABELS, 3 * rows)), whole((VECS, rows))],
        (HALF // PAIR,),
        [pltpu.VMEM((rows, D), BF), pltpu.VMEM((rows, 3 * rows), F32)],
        micros=6,
    )


def feed_forward(scalars, block, ctx_mine, ctx_partner, x, vecs, up_bias, weights, rows):
    count = len(weights)
    fresh = len(weights[0].shape) == 3

    def body(sc, mine_ref, partner_ref, x_ref, vec_ref, bias_ref, *refs):
        weight_refs, refs = refs[:count], refs[count:]
        (norm_ref, inv_ref, first_ref, gate_ref, active_ref, part_ref), refs = refs[:6], refs[6:]
        if fresh:
            up_ref, down_ref, out_ref, other_ref, full_ref = refs
            for k in range(2):
                at, to = 2 * k * HID, slice(k * HID, (k + 1) * HID)
                place(up_ref, weight_refs, sc[1], slice(at, at + HID), to)
                place(down_ref, weight_refs, sc[1], slice(at + HID, at + 2 * HID), to)
            place(full_ref, weight_refs, sc[1], slice(4 * HID, 4 * HID + D), slice(None))
            for ref, flip in ((out_ref, 0), (other_ref, 1)):
                for k in range(2):
                    at = pl.multiple_of((sc[2] ^ flip ^ (2 * k)) * QUARTER, 16)
                    ref[k * QUARTER : (k + 1) * QUARTER, :] = full_ref[pl.ds(at, QUARTER), :]
        else:
            up_ref, down_ref, out_ref, other_ref = weight_refs

        attention = dot(mine_ref[...], out_ref[...]) + dot(partner_ref[...], other_ref[...])
        total = x_ref[...].astype(F32) + (attention + vec_ref[2:3, :])
        center = total - jnp.mean(total, axis=-1, keepdims=True)
        inverse = lax.rsqrt(jnp.mean(center * center, axis=-1, keepdims=True) + EPS)
        normed = center * inverse
        norm_ref[...] = normed
        inv_ref[...] = jnp.broadcast_to(inverse, (rows, 128))
        first = (normed * vec_ref[3:4, :] + vec_ref[4:5, :]).astype(BF)
        first_ref[...] = first
        gate = dot(first, up_ref[...]) + bias_ref[0:1, :]
        gate_ref[...] = gate
        active = (gate * (1.0 + lax.erf(gate * ROOT_HALF)) * 0.5).astype(BF)
        active_ref[...] = active
        part_ref[...] = dot_nt(active, down_ref[...]).astype(BF)

    operands = [ctx_mine, ctx_partner, x, vecs, up_bias, *weights]
    in_specs = [whole(o.shape) for o in operands]
    in_specs[2] = pl.BlockSpec((rows, D), lambda *_: (block, 0))
    outs = [
        struct((rows, D), F32),
        struct((rows, 128), F32),
        struct((rows, D), BF),
        struct((rows, 2 * HID), F32),
        struct((rows, 2 * HID), BF),
        struct((rows, D), BF),
    ]
    scratch = []
    if fresh:
        outs += [struct((D, 2 * HID), BF)] * 2 + [struct((HALF, D), BF)] * 2
        scratch = [pltpu.VMEM((D, D), BF)]
    results = call(
        "feed_forward",
        body,
        scalars,
        operands,
        in_specs,
        outs,
        [whole(o.shape) for o in outs],
        (1,),
        scratch,
        micros=6,
    )
    return results[:6], (results[6:] if fresh else weights)


def gelu_slope(scalars, gate):
    rows = gate.shape[0] // 2

    def body(_, gate_ref, slope_ref):
        gate_here = gate_ref[...]
        bell = jnp.exp(gate_here * gate_here * -0.5) * ROOT_TWO_PI
        slope_ref[...] = 0.5 * (1.0 + lax.erf(gate_here * ROOT_HALF)) + gate_here * bell

    spec = pl.BlockSpec((rows, gate.shape[1]), lambda r, _: (r, 0))
    return call(
        "gelu_slope", body, scalars, [gate], [spec], [struct(gate.shape, F32)], [spec], (2,), micros=3
    )[0]


def second_norm(scalars, block, part, received, normed, slope, cotangent, vecs, up, down, earlier, rows):
    def body(sc, part_ref, recv_ref, norm_ref, slope_ref, cot_ref, other_ref, vec_ref, up_ref, down_ref, *refs):
        old, refs = refs[: len(earlier)], refs[len(earlier) :]
        (total_grad_ref, branch_grad_ref, gate_grad_ref, first_part_ref, out_ref, sums_ref, bias_ref) = refs
        mine = sc[0] == block
        first = norm_ref[...] * vec_ref[3:4, :] + vec_ref[4:5, :]
        branch = part_ref[...].astype(F32) + recv_ref[...].astype(F32) + vec_ref[5:6, :]
        total = first + branch
        center = total - jnp.mean(total, axis=-1, keepdims=True)
        inverse = lax.rsqrt(jnp.mean(center * center, axis=-1, keepdims=True) + EPS)
        here = center * inverse
        upstream = jnp.where(mine, cot_ref[...].astype(F32), other_ref[...].astype(F32))
        scaled = upstream * vec_ref[6:7, :]
        inner = (
            scaled
            - jnp.mean(scaled, axis=-1, keepdims=True)
            - here * jnp.mean(scaled * here, axis=-1, keepdims=True)
        )
        total_grad = inner * inverse
        total_grad_ref[...] = total_grad
        branch_grad = total_grad.astype(BF)
        branch_grad_ref[...] = branch_grad
        gate_grad = (dot(branch_grad, down_ref[...]) * slope_ref[...]).astype(BF)
        gate_grad_ref[...] = gate_grad
        hidden = jnp.broadcast_to(jnp.sum(gate_grad.astype(F32), axis=0, keepdims=True), (8, 2 * HID))
        bias_ref[...] = hidden + old[2][...] if old else hidden
        first_part_ref[...] = dot_nt(gate_grad, up_ref[...]).astype(BF)

        @pl.when(mine)
        def _():
            out_ref[...] = (here * vec_ref[6:7, :] + vec_ref[7:8, :]).astype(BF)
            sums_ref[...] = jnp.zeros_like(sums_ref)
            sums_ref[0:1, :] = jnp.sum(upstream * here, axis=0, keepdims=True)
            sums_ref[1:2, :] = jnp.sum(upstream, axis=0, keepdims=True)
            sums_ref[2:3, :] = jnp.sum(branch_grad.astype(F32), axis=0, keepdims=True)

        if old:

            @pl.when(jnp.logical_not(mine))
            def _():
                out_ref[...] = old[0][...]
                sums_ref[...] = old[1][...]

        else:

            @pl.when(jnp.logical_not(mine))
            def _():
                out_ref[...] = jnp.zeros_like(out_ref)
                sums_ref[...] = jnp.zeros_like(sums_ref)

    operands = [part, received, normed, slope, *cotangent, vecs, up, down, *earlier]
    outs = [
        struct((rows, D), F32),
        struct((rows, D), BF),
        struct((rows, 2 * HID), BF),
        struct((rows, D), BF),
        struct((rows, D), BF),
        struct((8, D), F32),
        struct((8, 2 * HID), F32),
    ]
    results = call(
        "second_norm",
        body,
        scalars,
        operands,
        [whole(o.shape) for o in operands],
        outs,
        [whole(o.shape) for o in outs],
        (1,),
        micros=5,
    )
    return results[:4], results[4:]


def split_outs(width):
    return [struct((GROUPS // 2, BLOCK, width), BF)] * 2


def feed_forward_grads(scalars, blocks, rows):
    def body(sc, *refs):
        keep_ref, send_ref, result_ref = refs[-3:]
        step = pl.program_id(0)

        @pl.when(step % 2 == 0)
        def _():
            result_ref[...] = dot_tn(refs[0][...], refs[1][...]) + dot_tn(refs[4][...], refs[5][...])

        @pl.when(step % 2 == 1)
        def _():
            result_ref[...] = dot_tn(refs[2][...], refs[3][...]) + dot_tn(refs[6][...], refs[7][...])

        split_rows(result_ref, sc[1], keep_ref, send_ref)

    half = pl.BlockSpec((rows, HID), lambda c, _: (0, c // 2))
    outs = split_outs(4 * HID)
    out_specs = [pl.BlockSpec((GROUPS // 2, BLOCK, HID), lambda c, _: (0, 0, c))] * 2
    return call(
        "feed_forward_grads",
        body,
        scalars,
        [value for block in blocks for value in block],
        [whole((rows, D)), half] * 4,
        outs,
        out_specs,
        (4,),
        [pltpu.VMEM((D, HID), F32)],
        micros=8,
    )


def first_norm(
    scalars, block, part, received, total_grad, normed, inverse, vecs, out_weight, ctx, logs, earlier, rows
):
    def body(sc, part_ref, recv_ref, grad_ref, norm_ref, inv_ref, vec_ref, weight_ref, ctx_ref, log_ref, *refs):
        old, refs = refs[: len(earlier)], refs[len(earlier) :]
        attention_ref, context_ref, inner_ref, own_ref, sums_ref = refs[:5]
        mine = sc[0] == block
        upstream = grad_ref[...] + part_ref[...].astype(F32) + recv_ref[...].astype(F32)
        here = norm_ref[...]
        scaled = upstream * vec_ref[3:4, :]
        inner = (
            scaled
            - jnp.mean(scaled, axis=-1, keepdims=True)
            - here * jnp.mean(scaled * here, axis=-1, keepdims=True)
        )
        total = inner * inv_ref[:, :1]
        attention = total.astype(BF)
        attention_ref[...] = attention
        context = dot_nt(attention, weight_ref[...]).astype(BF)
        context_ref[...] = context
        lane = lax.broadcasted_iota(jnp.int32, (VECS, HALF), 1) // HEAD_DIM
        picks = jnp.where(lane == lax.broadcasted_iota(jnp.int32, (VECS, HALF), 0), 1.0, 0.0)
        inner = lax.dot_general(
            picks,
            context.astype(F32) * ctx_ref[...],
            (((1,), (1,)), ((), ())),
            precision=lax.Precision.HIGHEST,
            preferred_element_type=F32,
        )
        inner_ref[...] = inner
        if block == 1:
            send_ref = refs[5]
            turned = jnp.concatenate([weight_ref[QUARTER:, :], weight_ref[:QUARTER, :]], axis=0)
            send_ref[:rows, :] = dot_nt(attention, turned).astype(BF)
            rest = jnp.concatenate([log_ref[...], inner], axis=0)
            send_ref[rows:, :] = jnp.zeros((3 * LABELS, HALF), BF)
            for k in range(3):
                at = rows + k * LABELS
                piece = rest.astype(BF)
                send_ref[at : at + LABELS, :rows] = piece
                rest = rest - piece.astype(F32)

        @pl.when(mine)
        def _():
            own_ref[...] = total
            sums_ref[...] = jnp.zeros_like(sums_ref)
            sums_ref[0:1, :] = jnp.sum(upstream * here, axis=0, keepdims=True)
            sums_ref[1:2, :] = jnp.sum(upstream, axis=0, keepdims=True)
            sums_ref[2:3, :] = jnp.sum(attention.astype(F32), axis=0, keepdims=True)

        @pl.when(jnp.logical_not(mine))
        def _():
            own_ref[...] = old[0][...] if old else jnp.zeros_like(own_ref)
            sums_ref[...] = old[1][...] if old else jnp.zeros_like(sums_ref)

    operands = [part, received, total_grad, normed, inverse, vecs, out_weight, ctx, logs, *earlier]
    outs = [
        struct((rows, D), BF),
        struct((rows, HALF), BF),
        struct((VECS, rows), F32),
        struct((rows, D), F32),
        struct((8, D), F32),
        struct((rows + 3 * LABELS, HALF), BF),
    ][: 6 if block == 1 else 5]
    return call(
        "first_norm",
        body,
        scalars,
        operands,
        [whole(o.shape) for o in operands],
        outs,
        [whole(o.shape) for o in outs],
        (1,),
        micros=3,
    )


def halves(value):
    high = value.astype(BF).astype(F32)
    return jnp.concatenate([high, value - high], axis=0).astype(BF)


def whole_of(table):
    return table[:LABELS].astype(F32) + table[LABELS : 2 * LABELS].astype(F32)


def output_grads(scalars, blocks, small, small_side):
    def body(sc, *refs):
        small_ref, side_ref, keep_ref, send_ref, result_ref = refs[-5:]
        for side in range(2):
            part = dot_tn(refs[side][...], refs[2][...]) + dot_tn(refs[3 + side][...], refs[5][...])
            for k in range(2):
                at = pl.multiple_of((sc[2] ^ side ^ (2 * k)) * QUARTER, 16)
                result_ref[pl.ds(at, QUARTER), :] = part[k * QUARTER : (k + 1) * QUARTER, :]
        for j in range(GROUPS):
            target = (keep_ref, send_ref)[j % 2]
            block = sc[1] ^ j
            rows = pl.ds(pl.multiple_of(block * BLOCK, 16), BLOCK)
            target[j // 2, :, :D] = result_ref[rows, :].astype(BF)
            target[j // 2, :, D:] = jnp.zeros((BLOCK, 128), BF)
            target[j // 2, : 2 * LABELS, D:] = halves(small_ref[block] + side_ref[block])

    outs = [struct((GROUPS // 2, BLOCK, D + 128), BF)] * 2
    operands = [value for block in blocks for value in block] + [small, small_side]
    return call(
        "output_grads",
        body,
        scalars,
        operands,
        [whole(o.shape) for o in operands],
        outs,
        [whole(o.shape) for o in outs],
        (1,),
        [pltpu.VMEM((D, D), F32)],
        micros=4,
    )


def attend_backward(scalars, pair, halo, grad_blocks, logs, inners, hot, weight, rows):
    base = 3 * rows
    steps = HALF // PAIR

    def body(sc, *refs):
        pair_refs, halo_refs, refs = refs[:3], refs[3:6], refs[6:]
        far_ref, near_ref, halo_ref, stats_ref, *refs = refs
        log_refs, inner_refs, (hot_ref, w_ref, *refs) = refs[:2], refs[2:4], refs[4:]
        out_ref, keep_ref, send_ref, sums_ref, mask_ref, key_ref, value_ref, acc_ref, q_ref, k_ref, v_ref, line_ref = refs
        for target, first_part, last_part in zip((q_ref, k_ref, v_ref), pair_refs, halo_refs):
            target[: 2 * rows, :] = first_part[...]
            target[2 * rows :, :] = last_part[...]
        step = pl.program_id(0)

        @pl.when(step == 0)
        def _():
            mask_ref[...] = (dot_tn(hot_ref[...], hot_ref[...]) - 1.0) * MASKED
            lines = jnp.zeros((LABELS, rows), F32)
            for k in range(3):
                at = rows + k * LABELS
                lines = lines + stats_ref[at : at + LABELS, :rows].astype(F32)
            line_ref[...] = lines

        key_ref[...] = jnp.zeros_like(key_ref)
        value_ref[...] = jnp.zeros_like(value_ref)
        lane = lax.broadcasted_iota(jnp.int32, (1, PAIR), 1)
        query_grads = [jnp.zeros((PAIR, rows), F32), jnp.zeros((PAIR, rows), F32)]
        for head in range(2):
            part = jnp.where((lane // HEAD_DIM) == head, 1.0, 0.0)
            key_turned = (k_ref[...].astype(F32) * part).T.astype(BF)
            line = 2 * step + head
            other = lax.rem(line + 3, 6)
            lines = [(log_refs[k][pl.ds(line, 1), :], inner_refs[k][pl.ds(line, 1), :]) for k in range(2)]
            lines += [(line_ref[pl.ds(other, 1), :], line_ref[pl.ds(other + VECS, 1), :])]
            for index, (low, high) in enumerate(((0, 2 * rows), (0, base), (rows, 2 * rows))):
                start = index * rows
                mine = (q_ref[start : start + rows].astype(F32) * (part * HEAD_DIM**-0.5)).astype(BF)
                grads = (far_ref, near_ref, halo_ref)[index][:rows, :]
                grads = (grads.astype(F32) * part).astype(BF)
                scores = dot_nt(k_ref[low:high], mine) + mask_ref[low:high, start : start + rows]
                log_total, inner = lines[index]
                probs = jnp.exp(scores - log_total)
                pulled = dot_nt(v_ref[low:high], grads)
                score_grads = (probs * (pulled - inner)).astype(BF)
                top = min(high, 2 * rows)
                span = top - low
                value_ref[low:top, :] += dot(probs[:span].astype(BF), grads)
                key_ref[low:top, :] += dot(score_grads[:span], mine)
                if index < 2:
                    query_grads[index] = query_grads[index] + dot(key_turned[:, low:high], score_grads)
        for index in range(2):
            turned = (query_grads[index] * HEAD_DIM**-0.5).T.astype(BF)
            out_ref[index * rows : (index + 1) * rows, :PAIR] = turned
        out_ref[:, PAIR : 2 * PAIR] = key_ref[...].astype(BF)
        out_ref[:, 2 * PAIR :] = value_ref[...].astype(BF)
        sums = jnp.sum(out_ref[...].astype(F32), axis=0, keepdims=True)
        sums_ref[...] = jnp.broadcast_to(sums, (8, 3 * PAIR))
        product = dot_nt(out_ref[...], w_ref[...])

        @pl.when(step == 0)
        def _():
            acc_ref[...] = product

        @pl.when(step > 0)
        def _():
            acc_ref[...] += product

        @pl.when(step == steps - 1)
        def _():
            near = sc[0]
            keep_ref[...] = acc_ref[pl.ds(pl.multiple_of(near * rows, rows), rows), :]
            other = acc_ref[pl.ds(pl.multiple_of((1 - near) * rows, rows), rows), :]
            send_ref[...] = other.astype(BF)

    stats = grad_blocks[2]
    operands = [*pair, *halo, *grad_blocks, stats, *logs, *inners, hot, weight]
    in_specs = [column(2 * rows)] * 3 + [column(rows)] * 5 + [column(stats.shape[0])]
    in_specs += [whole(o.shape) for o in operands[9:15]]
    in_specs += [pl.BlockSpec((D, 3 * PAIR), lambda p, _: (0, p))]
    outs = [struct((2 * rows, 3 * HALF), BF), struct((rows, D), F32), struct((rows, D), BF)]
    outs += [struct((8, 3 * HALF), F32)]
    out_specs = [
        pl.BlockSpec((2 * rows, 3 * PAIR), lambda p, _: (0, p)),
        whole((rows, D)),
        whole((rows, D)),
        pl.BlockSpec((8, 3 * PAIR), lambda p, _: (0, p)),
    ]
    scratch = [
        pltpu.VMEM((base, base), F32),
        pltpu.VMEM((2 * rows, PAIR), F32),
        pltpu.VMEM((2 * rows, PAIR), F32),
        pltpu.VMEM((2 * rows, D), F32),
    ] + [pltpu.VMEM((base, PAIR), BF)] * 3
    scratch += [pltpu.VMEM((LABELS, rows), F32)]
    return call(
        "attend_backward",
        body,
        scalars,
        operands,
        in_specs,
        outs,
        out_specs,
        (steps,),
        scratch,
        micros=MICROS,
    )


def projection_grads(scalars, x, grads, rows):
    tall = 2 * rows

    def body(sc, x_ref, grad_ref, *refs):
        result_ref = refs[-1]
        result_ref[...] = dot_tn(x_ref[...], grad_ref[...])
        split_rows(result_ref, sc[1], refs[0], refs[1])

    outs = split_outs(3 * HALF)
    out_specs = [pl.BlockSpec((GROUPS // 2, BLOCK, 3 * PAIR), lambda p, _: (0, 0, p))] * 2
    return call(
        "projection_grads",
        body,
        scalars,
        [x, grads],
        [pl.BlockSpec((tall, D), lambda p, _: (0, 0)), pl.BlockSpec((tall, 3 * PAIR), lambda p, _: (0, p))],
        outs,
        out_specs,
        (HALF // PAIR,),
        [pltpu.VMEM((D, 3 * PAIR), F32)],
        micros=5,
    )


def combine(scalars, keep, received):
    count, rows, width = keep.shape
    chunk = width // 3

    def body(_, keep_ref, recv_ref, *refs):
        for k in range(count):
            total = keep_ref[k].astype(F32) + recv_ref[k].astype(F32)
            refs[k][...] = total.astype(refs[k].dtype)

    block = pl.BlockSpec((count, rows, chunk), lambda c, _: (0, 0, c))
    outs = [struct((rows, width), F32)] + [struct((rows, width), BF)] * (count - 1)
    spec = pl.BlockSpec((rows, chunk), lambda c, _: (0, c))
    return list(call(
        "combine",
        body, scalars, [keep, received], [block, block], outs, [spec] * count, (3,)))


def combine_both(scalars, keep, received, out_keep, out_received):
    count, rows, wide = keep.shape
    last = wide + D

    def body(_, keep_ref, recv_ref, out_keep_ref, out_recv_ref, *refs):
        for k in range(count):
            kind = refs[k].dtype
            refs[k][:, :wide] = (keep_ref[k].astype(F32) + recv_ref[k].astype(F32)).astype(kind)
            total = out_keep_ref[k, :, :D].astype(F32) + out_recv_ref[k, :, :D].astype(F32)
            refs[k][:, wide:last] = total.astype(kind)
            small = whole_of(out_keep_ref[k, :, D:]) + whole_of(out_recv_ref[k, :, D:])
            refs[k][:, last:] = jnp.zeros((rows, 128), kind)
            refs[k][: 2 * LABELS, last:] = halves(small).astype(kind)

    outs = [struct((rows, last + 128), F32)] + [struct((rows, last + 128), BF)] * (count - 1)
    return simple("combine_both", body, scalars, [keep, received, out_keep, out_received], outs, 2)


def total_feed(scalars, sums):
    rows = sums[0].shape[0]

    def body(_, *refs):
        keep_ref, send_ref = refs[-2:]
        total = refs[0][...]
        for ref in refs[1:-2]:
            total = total + ref[...].astype(F32)
        keep_ref[...] = total[:, : 2 * HID]
        send_ref[...] = total[:, 2 * HID :].astype(BF)

    outs = [struct((rows, 2 * HID), F32), struct((rows, 2 * HID), BF)]
    return simple("total_feed", body, scalars, sums, outs, 2)


def total_projection(scalars, sums):
    rows, width = sums[0].shape
    wide = 3 * HALF
    last = wide + D

    def body(sc, *refs):
        keep_ref, send_ref = refs[-2:]
        total = refs[0][:, :last]
        for ref in refs[1:-2]:
            total = total + ref[:, :last].astype(F32)
        near, far = [], []
        for kind in range(3):
            both = [total[:, (3 * p + kind) * PAIR : (3 * p + kind + 1) * PAIR] for p in range(3)]
            both = jnp.concatenate(both, axis=1)
            near.append(both[:, :QUARTER])
            far.append(both[:, QUARTER:])
        near.append(pltpu.roll(total[:, wide:], D - sc[2] * QUARTER, 1)[:, :QUARTER])
        far.append(pltpu.roll(total[:, wide:], D - (sc[2] ^ 2) * QUARTER, 1)[:, :QUARTER])
        keep_ref[:, :D] = jnp.concatenate(near, axis=1)
        send_ref[:, :D] = jnp.concatenate(far, axis=1).astype(BF)
        if width > last:
            small = jnp.zeros((LABELS, 128), F32)
            for ref in refs[:-2]:
                small = small + whole_of(ref[:, last:])
            keep_ref[:, D:] = jnp.zeros((rows, 128), F32)
            send_ref[:, D:] = jnp.zeros((rows, 128), BF)
            keep_ref[:LABELS, D:] = small
            send_ref[: 2 * LABELS, D:] = halves(small)

    width_out = D + width - last
    outs = [struct((rows, width_out), F32), struct((rows, width_out), BF)]
    return simple("total_projection", body, scalars, sums, outs, 2)


def finish_feed(scalars, keep, received):
    rows = keep.shape[0]

    def body(_, keep_ref, recv_ref, up_ref, down_ref):
        up_ref[...] = keep_ref[:, :HID] + recv_ref[:, :HID].astype(F32)
        down_ref[...] = keep_ref[:, HID:] + recv_ref[:, HID:].astype(F32)

    outs = [struct((rows, HID), F32)] * 2
    return simple("finish_feed", body, scalars, [keep, received], outs)


def finish_projection(scalars, keep, received):
    rows, width = keep.shape

    def body(_, keep_ref, recv_ref, *refs):
        total = keep_ref[:, :D] + recv_ref[:, :D].astype(F32)
        for k in range(4):
            refs[k][...] = total[:, k * QUARTER : (k + 1) * QUARTER]
        if width > D:
            small = keep_ref[:LABELS, D:] + whole_of(recv_ref[:, D:])
            for k in range(VECS):
                refs[4 + k][...] = small[k, :BLOCK]
            for k in range(SHARE):
                refs[4 + VECS][k * 128 : (k + 1) * 128] = small[VECS + k]

    outs = [struct((rows, QUARTER), F32)] * 4
    if width > D:
        outs += [struct((BLOCK,), F32)] * VECS + [struct((FF // GROUPS,), F32)]
    return simple("finish_projection", body, scalars, [keep, received], outs)


def small_sums(scalars, sums_one, sums_two, sums_hidden, sums_projection):
    def body(sc, one_ref, two_ref, hidden_ref, projection_ref, out_ref, wide_ref, tall_ref):
        out_ref[...] = jnp.zeros_like(out_ref)
        lanes = lax.broadcasted_iota(jnp.int32, (1, D), 1)
        near, far = lanes < QUARTER, (lanes >= QUARTER) & (lanes < HALF)
        for row, kind in ((0, 0), (1, 2)):
            line = jnp.concatenate(
                [
                    projection_ref[0:1, (3 * p + kind) * PAIR : (3 * p + kind + 1) * PAIR]
                    for p in range(3)
                ]
                + [jnp.zeros((1, HALF), F32)],
                axis=1,
            )
            low = pltpu.roll(jnp.broadcast_to(jnp.where(near, line, 0.0), (8, D)), sc[2] * QUARTER, 1)
            high = jnp.broadcast_to(jnp.where(far, line, 0.0), (8, D))
            high = pltpu.roll(high, D - QUARTER + (sc[2] ^ 2) * QUARTER, 1)
            wide_ref[row : row + 1, :] = (low + high)[0:1]
        wide_ref[2:3, :] = one_ref[2:3, :]
        wide_ref[3:5, :] = one_ref[0:2, :]
        wide_ref[5:6, :] = two_ref[2:3, :]
        wide_ref[6:8, :] = two_ref[0:2, :]
        tall_ref[...] = jnp.zeros_like(tall_ref)
        for k in range(2):
            to = pl.multiple_of((sc[2] ^ (2 * k)) * HID, 128)
            tall_ref[0:1, pl.ds(to, HID)] = hidden_ref[0:1, k * HID : (k + 1) * HID]
        share = FF // GROUPS
        for d in range(GROUPS):
            out_ref[d, :VECS, :BLOCK] = wide_ref[:, d * BLOCK : (d + 1) * BLOCK]
            for c in range(share // 128):
                at = d * share + c * 128
                out_ref[d, VECS + c : VECS + c + 1, :] = tall_ref[0:1, at : at + 128]

    operands = [sums_one, sums_two, sums_hidden, sums_projection]
    shape = (GROUPS, LABELS, 128)
    return call(
        "small_sums",
        body,
        scalars,
        operands,
        [whole(o.shape) for o in operands],
        [struct(shape, F32)],
        [whole(shape)],
        (1,),
        [pltpu.VMEM((VECS, D), F32), pltpu.VMEM((8, FF), F32)],
    )[0]


def per_device(
    tokens,
    segments,
    query_weight,
    key_weight,
    value_weight,
    output_weight,
    query_bias,
    value_bias,
    output_bias,
    first_gain,
    first_shift,
    up_weight,
    up_bias,
    down_weight,
    down_bias,
    second_gain,
    second_shift,
    cotangent,
):
    seq_count = lax.axis_size("seq")
    count = lax.axis_size("dp")
    place_z = lax.axis_index("seq")
    assert seq_count == 4
    direct = count == GROUPS
    rows = tokens.shape[1]
    piece_rows = query_weight.shape[0]
    near = (place_z == 1) | (place_z == 2)
    base = lax.axis_index("dp") if direct else 0
    scalars = jnp.stack([near, base, place_z]).astype(jnp.int32)

    own = tokens[0]
    cot_own = cotangent[0]
    lines = [
        query_bias,
        value_bias,
        output_bias,
        first_gain,
        first_shift,
        down_bias,
        second_gain,
        second_shift,
    ]
    lines = lines if direct else []
    first_send, mine, wide, labelled, own_docs = pack_inputs(
        scalars,
        [query_weight, key_weight, value_weight, output_weight],
        own,
        segments,
        up_weight,
        down_weight.T,
        lines,
        up_bias,
    )
    arrived = swap(first_send, "seq", 2)
    side = swap(output_weight, "seq", 1)
    if direct:
        mine_chip = [mine, swap(mine, "dp", 2), swap(mine, "dp", 4)]
        wide_last = swap(wide, "dp", 6)
        labelled, side, wide_last, mine_chip, arrived = together(
            labelled, side, wide_last, mine_chip, arrived
        )
    else:
        arrived, labelled, side = together(arrived, labelled, side)
    narrow_far, both, partner_send = split_arrived(scalars, arrived, mine, labelled)
    partner = swap(partner_send, "seq", 1)
    halo_near = lax.ppermute(labelled, "seq", [(1, 2), (2, 1)])
    if direct:
        far_chip = [narrow_far, swap(narrow_far, "dp", 2), swap(narrow_far, "dp", 4)]
        both_far = swap(both, "dp", 6)
        mine_chip, cot_own, far_chip, both_far, partner, halo_near = together(
            mine_chip, cot_own, far_chip, both_far, partner, halo_near
        )
        stacked = stack_narrow(scalars, mine_chip, far_chip, both_far)
        pieces = [stacked, swap(stacked, "dp", 1)]
        feed_chip = chip_pieces(pack_feed(scalars, first_send, arrived, side, partner))
    halo_far = lax.ppermute(halo_near, "seq", [(1, 0), (2, 3)])
    if not direct:
        vectors = jnp.stack(
            [
                query_bias,
                value_bias,
                output_bias,
                first_gain,
                first_shift,
                down_bias,
                second_gain,
                second_shift,
            ]
        )
        lines = lax.all_gather(vectors, "dp", axis=1, tiled=True).reshape(VECS, GROUPS, BLOCK)
        lines = jnp.pad(lines, ((0, 0), (0, 0), (0, 128 - BLOCK)))
        tall = lax.all_gather(up_bias, "dp", axis=0, tiled=True).reshape(GROUPS, SHARE, 128).transpose(1, 0, 2)
        lines = jnp.concatenate([lines, tall], axis=0)
        lines = jnp.pad(lines, ((0, LABELS - VECS - SHARE), (0, 0), (0, 3 * QUARTER - 128)))
        lines = lines.transpose(1, 0, 2)
        gathered = gather_rows(mine)
        pieces = [
            jnp.concatenate([half[:, :, 2 * HID :], lines[k::2], far], axis=1)
            for k, (half, far) in enumerate(zip(gathered, gather_rows(narrow_far)))
        ]
        last = swap(arrived[:, 3 * QUARTER : D], "seq", 1)
        feed = gather_rows(pack_feed(scalars, first_send, arrived, side, last))
        weights = [
            jnp.concatenate([half[:, :, : 2 * HID], far], axis=2) for half, far in zip(gathered, feed)
        ]

    def rows_of(keep, send):
        return jnp.stack([keep, send], axis=1).reshape(GROUPS, -1, keep.shape[2]).astype(F32)

    def spread(sums):
        return [sums[0]] + [swap(sums[k], "dp", 2 * k) for k in range(1, len(sums))]

    def scattered(table):
        return [lax.psum_scatter(table, "dp", scatter_dimension=0, tiled=True)]

    *pair, ctx_far, x, weight, hot, vecs, hidden_bias, bias, log_far, scaled_far = attend_pair(
        scalars, own, partner, own_docs, pieces, rows
    )
    if direct:
        pair, ctx_far, cot_own, halo_far = together(pair, ctx_far, cot_own, halo_far)
    *halo, ctx_near, scaled_near, hot, log_near = attend_halo(scalars, halo_near, halo_far, weight, bias, hot, *pair, rows)
    ctx_mine = [ctx_far, ctx_near]
    ctx_partner = [swap(ctx_far, "seq", 1), None]
    if direct:
        ctx_mine[1], ctx_partner[0], wide_last, feed_chip = together(
            ctx_mine[1], ctx_partner[0], wide_last, feed_chip
        )
        stacked = stack_wide(scalars, mine_chip, wide_last, feed_chip)
        weights = [stacked, swap(stacked, "dp", 1)]
    ctx_partner[1] = swap(ctx_mine[1], "seq", 1)
    cot_partner = swap(cot_own, "seq", 1)

    forward, slopes, part_far = [None, None], [None, None], [None, None]
    for block in (1, 0):
        forward[block], weights = feed_forward(
            scalars, block, ctx_mine[block], ctx_partner[block], x, vecs, hidden_bias, weights, rows
        )
        part_far[block] = swap(forward[block][5], "seq", 1)
    up, down, out_mine, _ = weights
    second, second_shared, first_part_far = [None, None], [], [None, None]
    for block in (1, 0):
        slopes[block] = gelu_slope(scalars, forward[block][3])
    for block in (1, 0):
        second[block], second_shared = second_norm(
            scalars,
            block,
            forward[block][5],
            part_far[block],
            forward[block][0],
            slopes[block],
            (cot_own, cot_partner),
            vecs,
            up,
            down,
            second_shared,
            rows,
        )
        if block == 1:
            first_part_far[block] = swap(second[block][3], "seq", 1)
    feed_parts = feed_forward_grads(
        scalars,
        [(forward[k][2], second[k][2], second[k][1], forward[k][4]) for k in range(2)],
        rows,
    )
    first_part_far[1], second, second_shared, feed_parts = together(
        first_part_far[1], second, second_shared, feed_parts
    )
    first_part_far[0] = swap(second[0][3], "seq", 1)
    layer_output, sums_two, sums_hidden = second_shared
    attention_grad, ctx_grad, inners, first_shared = [None, None], [None, None], [None, None], []
    logs, scaled = [log_far, log_near], [scaled_far, scaled_near]

    def finish(block):
        attention_grad[block], ctx_grad[block], inners[block], *shared = first_norm(
            scalars,
            block,
            second[block][3],
            first_part_far[block],
            second[block][0],
            forward[block][0],
            forward[block][1],
            vecs,
            out_mine,
            scaled[block],
            logs[block],
            first_shared,
            rows,
        )
        return shared

    *first_shared, halo_send = finish(1)
    halo_grad = swap(halo_send, "seq", 2)
    if direct:
        feed_sums = combine(scalars, feed_parts[0], swap(feed_parts[1], "dp", 1))
        feed_sums = spread(feed_sums)
    else:
        feed_sums = scattered(rows_of(*feed_parts).reshape(D, -1))
    own_grad, sums_one = finish(0)

    grads, input_keep, input_send, sums_projection = attend_backward(
        scalars, pair, halo, [*ctx_grad, halo_grad], logs, inners, hot, weight, rows
    )
    input_far = swap(input_send, "seq", 1)
    small = small_sums(scalars, sums_one, sums_two, sums_hidden, sums_projection)
    small_side = swap(small, "seq", 1)
    projection_parts = projection_grads(scalars, x, grads, rows)
    projection_parts, small_side, feed_sums = together(projection_parts, small_side, feed_sums)
    out_blocks = [(ctx_mine[k], ctx_partner[k], attention_grad[k]) for k in range(2)]
    if direct:
        projection_received = swap(projection_parts[1], "dp", 1)
        out_parts = output_grads(scalars, out_blocks, small, small_side)
        out_received = swap(out_parts[1], "dp", 1)
        feed_keep, feed_send = total_feed(scalars, feed_sums)
        feed_far = swap(feed_send, "seq", 2)
        sums = spread(
            combine_both(scalars, projection_parts[0], projection_received, out_parts[0], out_received)
        )
    else:
        out_parts = rows_of(*output_grads(scalars, out_blocks, small, small_side))
        sums = scattered(
            jnp.concatenate(
                [rows_of(*projection_parts).reshape(D, -1), out_parts[:, :, :D].reshape(D, -1)], axis=1
            )
        )
        feed_keep, feed_send = total_feed(scalars, feed_sums)
        feed_far = swap(feed_send, "seq", 2)
    up_grad, down_grad = finish_feed(scalars, feed_keep, feed_far)
    input_grad = own_grad + input_keep + input_far.astype(F32)
    if direct:
        sums, up_grad, input_grad = together(sums, up_grad, input_grad)
    keep, send = total_projection(scalars, sums)
    projections = list(finish_projection(scalars, keep, swap(send, "seq", 2)))
    if direct:
        projections, vec, tall_lines = projections[:4], projections[4:-1], projections[-1]
    else:
        tile = out_parts[:, :LABELS, D:] + out_parts[:, LABELS : 2 * LABELS, D:]
        tile = tile + swap(tile, "seq", 2)
        wide_lines = tile[:, :VECS, :BLOCK].transpose(1, 0, 2).reshape(VECS, D)
        wide_lines = lax.psum_scatter(wide_lines, "dp", scatter_dimension=1, tiled=True)
        tall_lines = lax.psum_scatter(tile[:, VECS : VECS + 3].reshape(-1), "dp", tiled=True)
        vec = [wide_lines[k] for k in range(VECS)]
    return (
        layer_output[None],
        input_grad[None],
        *projections,
        vec[0],
        vec[1],
        vec[2],
        vec[3],
        vec[4],
        up_grad,
        tall_lines,
        down_grad.T,
        vec[5],
        vec[6],
        vec[7],
    )


def solution(mesh):
    placed = (
        P("dp", "seq", None),
        P("dp", "seq"),
        P("dp", "seq"),
        P("dp", "seq"),
        P("dp", "seq"),
        P("dp", "seq"),
        P("dp"),
        P("dp"),
        P("dp"),
        P("dp"),
        P("dp"),
        P("dp", "seq"),
        P("dp"),
        P("seq", "dp"),
        P("dp"),
        P("dp"),
        P("dp"),
        P("dp", "seq", None),
    )
    return jax.shard_map(
        per_device,
        mesh=mesh,
        in_specs=placed,
        out_specs=(
            P("dp", "seq", None),
            P("dp", "seq", None),
            P("dp", "seq"),
            P("dp", "seq"),
            P("dp", "seq"),
            P("dp", "seq"),
            P("dp"),
            P("dp"),
            P("dp"),
            P("dp"),
            P("dp"),
            P("dp", "seq"),
            P("dp"),
            P("seq", "dp"),
            P("dp"),
            P("dp"),
            P("dp"),
        ),
        check_vma=False,
    )
```

```python
import jax
import jax.numpy as jnp
from jax import lax
from jax.experimental import pallas as pl
from jax.experimental.pallas import tpu as pltpu
from jax.sharding import PartitionSpec as P

D = 768
HEADS = 12
HEAD_DIM = 64
FF = 3072
EPS = 1e-05
MASKED = 1e30
PAIR = 2 * HEAD_DIM
QUARTER = D // 4
HALF = D // 2
HID = FF // 4
VECS = 8
GROUPS = 8
SHARE = FF // GROUPS // 128
BLOCK = D // GROUPS
LABELS = 16
MARKS = 48
MICROS = 450
FEED_MICROS = 300
BF = jnp.bfloat16
F32 = jnp.float32
ROOT_HALF = 0.7071067811865476
ROOT_TWO_PI = 0.3989422804014327


def dot(a, b):
    return lax.dot_general(a, b, (((1,), (0,)), ((), ())), preferred_element_type=F32)


def dot_nt(a, b):
    return lax.dot_general(a, b, (((1,), (1,)), ((), ())), preferred_element_type=F32)


def dot_tn(a, b):
    return lax.dot_general(a, b, (((0,), (0,)), ((), ())), preferred_element_type=F32)


def swap(value, axis, mask):
    count = lax.axis_size(axis)
    return lax.ppermute(value, axis, [(k, k ^ mask) for k in range(count)])


def together(*values):
    return lax.optimization_barrier(values)


def whole(shape):
    return pl.BlockSpec(shape, lambda *_: (0,) * len(shape))


def params():
    return pltpu.CompilerParams(vmem_limit_bytes=22 * 1024 * 1024)


def call(name, body, scalars, operands, in_specs, outs, out_specs, grid, scratch=(), micros=1):
    spec = pltpu.PrefetchScalarGridSpec(
        num_scalar_prefetch=1,
        grid=grid,
        in_specs=in_specs,
        out_specs=out_specs,
        scratch_shapes=list(scratch),
    )
    return pl.pallas_call(
        body,
        out_shape=outs,
        grid_spec=spec,
        compiler_params=params(),
        cost_estimate=pl.CostEstimate(
            flops=int(micros * 1.0e7), transcendentals=0, bytes_accessed=1024
        ),
        name=name,
    )(scalars, *operands)


def struct(shape, dtype):
    return jax.ShapeDtypeStruct(shape, dtype)


def chip_pieces(piece):
    return [piece] + [swap(piece, "dp", j) for j in range(2, GROUPS, 2)]


def gather_rows(piece):
    full = lax.all_gather(piece, "dp", axis=0, tiled=True)
    full = full.reshape(GROUPS, D // GROUPS, piece.shape[1])
    return [full[0::2], full[1::2]]


def place(target, pair, base, source_cols, target_cols):
    for j in range(GROUPS):
        start = pl.multiple_of((base ^ j) * BLOCK, 16)
        target[pl.ds(start, BLOCK), target_cols] = pair[j % 2][j // 2, :BLOCK, source_cols]


def split_rows(result, base, keep, send):
    for j in range(GROUPS):
        block = result[pl.ds(pl.multiple_of((base ^ j) * BLOCK, 16), BLOCK), :].astype(BF)
        if j % 2:
            send[j // 2] = block
        else:
            keep[j // 2] = block


def simple(name, body, scalars, operands, outs, micros=1):
    return call(
        name,
        body,
        scalars,
        operands,
        [whole(o.shape) for o in operands],
        outs,
        [whole(o.shape) for o in outs],
        (1,),
        micros=micros,
    )


def pack_inputs(scalars, tables, tokens, segments, up, down, lines, tall):
    rows = tokens.shape[0]
    height = tables[0].shape[0]
    skip = 2 * HID + (128 if lines else 0)
    operands = list(tables) + [tokens, segments, up, down] + lines + ([tall] if lines else [])
    count = len(operands)

    def body(_, *refs):
        sources, (send_ref, mine_ref, wide_ref, label_ref, docs_ref), refs = (
            refs[:count],
            refs[count : count + 5],
            refs[count + 5 :],
        )
        copies = [pltpu.make_async_copy(a, b, refs[-1].at[k]) for k, (a, b) in enumerate(zip(sources, refs))]
        for copy in copies:
            copy.start()
        for copy in copies:
            copy.wait()
        joined = jnp.concatenate([ref[...].astype(F32) for ref in refs[:4]], axis=1).astype(BF)
        send_ref[:, :D] = joined
        send_ref[:, D : D + HID] = refs[6][...]
        send_ref[:, D + HID :] = refs[7][...]
        mine_ref[:, :HID] = refs[6][...]
        mine_ref[:, HID : 2 * HID] = refs[7][...]
        part = joined[:, : 3 * QUARTER].astype(F32)
        mine_ref[:, skip:] = part.astype(BF)
        wide_ref[:, :HID] = refs[6][...]
        wide_ref[:, HID:] = refs[7][...]
        docs = refs[5][...].astype(F32)
        docs_ref[...] = docs
        label_ref[:rows, :] = refs[4][...]
        label_ref[rows:, :] = jnp.zeros((MARKS, D), BF)
        label_ref[rows:, :rows] = jnp.broadcast_to(docs, (MARKS, rows)).astype(BF)
        if lines:
            table = [ref[...].astype(F32)[None, :] for ref in refs[8 : 8 + VECS]]
            table = jnp.concatenate(table, axis=0)
            table = [jnp.concatenate([table, jnp.zeros((VECS, 128 - BLOCK), F32)], axis=1)]
            line = refs[8 + VECS][...].astype(F32)[None, :]
            table += [line[:, c * 128 : (c + 1) * 128] for c in range(SHARE)]
            table += [jnp.zeros((height - VECS - SHARE, 128), F32)]
            mine_ref[:, 2 * HID : skip] = jnp.concatenate(table, axis=0).astype(BF)

    outs = [
        struct((height, D + 2 * HID), BF),
        struct((height, skip + 3 * QUARTER), BF),
        struct((height, 2 * HID), BF),
        struct((rows + MARKS, D), BF),
        struct((1, rows), F32),
    ]
    operands = [pltpu.with_memory_space_constraint(o, pltpu.MemorySpace.HBM) for o in operands]
    return call(
        "pack_inputs",
        body,
        scalars,
        operands,
        [pl.BlockSpec(memory_space=pltpu.MemorySpace.HBM)] * count,
        outs,
        [whole(o.shape) for o in outs],
        (1,),
        [pltpu.VMEM(o.shape, o.dtype) for o in operands] + [pltpu.SemaphoreType.DMA((count,))],
    )


def split_arrived(scalars, arrived, mine, labelled):
    rows = arrived.shape[0]
    tall = rows + LABELS
    skip = mine.shape[1] - 3 * QUARTER
    direct = skip > 2 * HID

    def body(_, far_ref, mine_ref, label_ref, narrow_ref, both_ref, send_ref):
        narrow_ref[...] = far_ref[:, : 3 * QUARTER]
        both_ref[:rows, :] = mine_ref[:, skip:]
        both_ref[tall:, :] = far_ref[:, : 3 * QUARTER]
        send_ref[...] = label_ref[...]
        if direct:
            both_ref[rows:tall, :] = jnp.zeros((LABELS, 3 * QUARTER), BF)
            both_ref[rows:tall, :128] = mine_ref[:LABELS, 2 * HID : skip]
            part = far_ref[:, 3 * QUARTER : D].astype(F32)
            step = rows // 4
            part = jnp.concatenate([part[k * step : (k + 1) * step] for k in range(4)], axis=1)
            part = jnp.concatenate([part, jnp.zeros((MARKS - LABELS - step, D), F32)], axis=0)
            send_ref[labelled.shape[0] - MARKS + LABELS :, :] = part.astype(BF)

    outs = [
        struct((rows, 3 * QUARTER), BF),
        struct((rows + tall, 3 * QUARTER), BF),
        struct(labelled.shape, BF),
    ]
    return simple("split_arrived", body, scalars, [arrived, mine, labelled], outs)


def stack_narrow(scalars, mine_chip, far_chip, both_far):
    rows = far_chip[0].shape[0]
    tall = rows + LABELS
    skip = mine_chip[0].shape[1] - 3 * QUARTER

    def body(_, *refs):
        out_ref = refs[-1]
        for k in range(3):
            out_ref[k, :rows] = refs[k][:, skip:]
            out_ref[k, rows:tall] = jnp.zeros((LABELS, 3 * QUARTER), BF)
            out_ref[k, rows:tall, :128] = refs[k][:LABELS, 2 * HID : skip]
            out_ref[k, tall:] = refs[3 + k][...]
        out_ref[3] = refs[6][...]

    shape = (GROUPS // 2, tall + rows, 3 * QUARTER)
    operands = [*mine_chip, *far_chip, both_far]
    return simple("stack_narrow", body, scalars, operands, [struct(shape, BF)])[0]


def stack_wide(scalars, mine_chip, last, feed_chip):
    def body(_, *refs):
        out_ref = refs[-1]
        for k in range(3):
            out_ref[k, :, : 2 * HID] = refs[k][:BLOCK, : 2 * HID]
        out_ref[3, :, : 2 * HID] = refs[3][...]
        for k in range(4):
            out_ref[k, :, 2 * HID :] = refs[4 + k][...]

    shape = (GROUPS // 2, BLOCK, 4 * HID + D)
    return simple("stack_wide", body, scalars, [*mine_chip, last, *feed_chip], [struct(shape, BF)])[0]


def pack_feed(scalars, first_send, arrived, side, last):
    rows = arrived.shape[0]
    columns = slice(3 * QUARTER, D)

    def body(sc, own_ref, arrived_ref, side_ref, last_ref, out_ref):
        out_ref[:, : 2 * HID] = arrived_ref[:, D:]
        final = last_ref[...].astype(F32)
        if last.shape[1] == D:
            step = rows // 4
            final = final[last.shape[0] - MARKS + LABELS :]
            final = [final[:step, k * QUARTER : (k + 1) * QUARTER] for k in range(4)]
            final = jnp.concatenate(final, axis=0)
        total = jnp.zeros((rows, D), F32)
        for k, part in enumerate([own_ref[:, columns], side_ref[...], arrived_ref[:, columns], final]):
            part = jnp.concatenate([part.astype(F32), jnp.zeros((rows, D - QUARTER), F32)], axis=1)
            total = total + pltpu.roll(part, (sc[2] ^ k) * QUARTER, 1)
        out_ref[:, 2 * HID :] = total.astype(BF)

    out = struct((rows, 2 * HID + D), BF)
    return simple("pack_feed", body, scalars, [first_send, arrived, side, last], [out])[0]


def mark(docs, rows):
    number = lax.broadcasted_iota(jnp.int32, (LABELS, rows), 0).astype(F32)
    return jnp.where(jnp.broadcast_to(docs, (LABELS, rows)) == number, 1.0, 0.0).astype(BF)


def attend(query, key, value, mask, log_ref, step):
    lane = lax.broadcasted_iota(jnp.int32, (1, PAIR), 1)
    total = jnp.zeros(query.shape, F32)
    scaled = jnp.zeros(query.shape, F32)
    logs = jnp.zeros(query.shape, F32)
    value = jnp.concatenate([value, jnp.ones(value.shape, BF)], axis=1)
    for head in range(2):
        part = jnp.where((lane // HEAD_DIM) == head, 1.0, 0.0)
        mine = (query.astype(F32) * (part * HEAD_DIM**-0.5)).astype(BF)
        scores = dot_nt(mine, key) + mask
        top = jnp.max(scores, axis=-1, keepdims=True)
        expo = jnp.exp(scores - top)
        whole_sum = jnp.sum(expo, axis=-1, keepdims=True)
        probs = expo * (1.0 / whole_sum)
        rounded = probs.astype(BF)
        context = dot(rounded, value)
        total = total + context[:, :PAIR] * part
        scaled = scaled + context[:, :PAIR] * part / context[:, PAIR:]
        logs = jnp.where(lane == head, top + jnp.log(whole_sum), logs)
    turned = logs.T
    for head in range(2):
        log_ref[pl.ds(2 * step + head, 1), :] = turned[head : head + 1, :]
    return total.astype(BF), scaled


def column(height):
    return pl.BlockSpec((height, PAIR), lambda p, _: (0, p))


def attend_pair(scalars, own, partner, own_docs, pieces, rows):
    base = 2 * rows
    tall = BLOCK + LABELS

    def body(sc, own_ref, partner_ref, docs_ref, *refs):
        weight_refs, refs = refs[:2], refs[2:]
        q_ref, k_ref, v_ref, ctx_ref, x_ref, w_ref, hot_ref, vec_ref, hidden_ref, bias_ref, log_ref, *refs = refs
        scaled_ref, mask_ref = refs
        step = pl.program_id(0)

        @pl.when(step == 0)
        def _():
            near = sc[0]
            own_at = pl.multiple_of(near * rows, rows)
            partner_at = pl.multiple_of((1 - near) * rows, rows)
            x_ref[pl.ds(own_at, rows), :] = own_ref[...]
            x_ref[pl.ds(partner_at, rows), :] = partner_ref[:rows, :]
            hot_ref[:, pl.ds(own_at, rows)] = mark(docs_ref[...], rows)
            docs = partner_ref[rows : rows + 1, :rows].astype(F32)
            hot_ref[:, pl.ds(partner_at, rows)] = mark(docs, rows)
            for j in range(GROUPS):
                at = pl.ds(pl.multiple_of((sc[1] ^ j) * BLOCK, 16), BLOCK)
                for kind in range(3):
                    part = slice(kind * QUARTER, (kind + 1) * QUARTER)
                    both = [weight_refs[j % 2][j // 2, top : top + BLOCK, part] for top in (0, tall)]
                    both = [half.astype(F32) for half in both]
                    both = jnp.concatenate(both, axis=1).astype(BF)
                    for p in range(3):
                        to = (3 * p + kind) * PAIR
                        w_ref[at, to : to + PAIR] = both[:, p * PAIR : (p + 1) * PAIR]
            hot = hot_ref[...]
            mask_ref[...] = (dot_tn(hot[:, :rows], hot) - 1.0) * MASKED
            vectors = jnp.zeros((LABELS, D), F32)
            for j in range(GROUPS):
                block = sc[1] ^ j
                line = weight_refs[j % 2][j // 2, BLOCK:tall, :128].astype(F32)
                table = jnp.where(lax.broadcasted_iota(jnp.int32, line.shape, 1) < BLOCK, line, 0.0)
                table = jnp.concatenate([table, jnp.zeros((LABELS, D - 128), F32)], axis=1)
                vectors = vectors + pltpu.roll(table, block * BLOCK, 1)
                quarter = block // 2
                for k in range(2):

                    @pl.when(quarter == sc[2] ^ (2 * k))
                    def _():
                        for c in range(SHARE):
                            to = pl.multiple_of((block % 2) * (HID // 2) + k * HID + c * 128, 128)
                            value = jnp.broadcast_to(line[VECS + c : VECS + c + 1], (VECS, 128))
                            hidden_ref[:, pl.ds(to, 128)] = value

            vec_ref[...] = vectors[:VECS]
            lanes = lax.broadcasted_iota(jnp.int32, (VECS, HALF), 1)
            low = pltpu.roll(vectors[:VECS], D - sc[2] * QUARTER, 1)[:, :HALF]
            high = pltpu.roll(vectors[:VECS], D + QUARTER - (sc[2] ^ 2) * QUARTER, 1)[:, :HALF]
            bias_ref[...] = jnp.where(lanes < QUARTER, low, high)
            log_ref[...] = jnp.zeros_like(log_ref)

        at = pl.multiple_of(step * 3 * PAIR, PAIR)
        both = dot(x_ref[...], w_ref[:, pl.ds(at, 3 * PAIR)])
        bias = bias_ref[:, pl.ds(pl.multiple_of(step * PAIR, PAIR), PAIR)]
        query = (both[:, :PAIR] + bias[0:1]).astype(BF)
        key = both[:, PAIR : 2 * PAIR].astype(BF)
        value = (both[:, 2 * PAIR :] + bias[1:2]).astype(BF)
        q_ref[...] = query
        k_ref[...] = key
        v_ref[...] = value
        ctx_ref[...], scaled_ref[...] = attend(query[:rows], key, value, mask_ref[...], log_ref, step)

    operands = [own, partner, own_docs, *pieces]
    in_specs = [whole(o.shape) for o in operands]
    outs = [
        struct((base, HALF), BF),
        struct((base, HALF), BF),
        struct((base, HALF), BF),
        struct((rows, HALF), BF),
        struct((base, D), BF),
        struct((D, 3 * HALF), BF),
        struct((LABELS, base), BF),
        struct((VECS, D), F32),
        struct((VECS, 2 * HID), F32),
        struct((VECS, HALF), F32),
        struct((VECS, rows), F32),
        struct((rows, HALF), F32),
    ]
    out_specs = [column(base)] * 3 + [column(rows)] + [whole(o.shape) for o in outs[4:-1]] + [column(rows)]
    return call(
        "attend_pair",
        body,
        scalars,
        operands,
        in_specs,
        outs,
        out_specs,
        (HALF // PAIR,),
        [pltpu.VMEM((rows, base), F32)],
        micros=8,
    )


def attend_halo(scalars, halo_near, halo_far, weight, bias, hot, query, key, value, rows):
    def body(sc, near_ref, far_ref, w_ref, bias_ref, hot_ref, q_ref, k_ref, v_ref, *refs):
        halo_refs, (ctx_ref, scaled_ref, all_ref, log_ref, x_ref, mask_ref) = refs[:3], refs[3:]

        @pl.when(pl.program_id(0) == 0)
        def _():
            all_ref[:, : 2 * rows] = hot_ref[...]

            def halo(ref):
                x_ref[...] = ref[:rows, :]
                all_ref[:, 2 * rows :] = mark(ref[rows : rows + 1, :rows].astype(F32), rows)

            pl.when(sc[0] == 1)(lambda: halo(near_ref))
            pl.when(sc[0] == 0)(lambda: halo(far_ref))
            mask_ref[...] = (dot_tn(all_ref[:, rows : 2 * rows], all_ref[...]) - 1.0) * MASKED
            log_ref[...] = jnp.zeros_like(log_ref)

        both = dot(x_ref[...], w_ref[...])
        parts = [
            (both[:, :PAIR] + bias_ref[0:1, :]).astype(BF),
            both[:, PAIR : 2 * PAIR].astype(BF),
            (both[:, 2 * PAIR :] + bias_ref[1:2, :]).astype(BF),
        ]
        for ref, part in zip(halo_refs, parts):
            ref[...] = part
        keys = jnp.concatenate([k_ref[...], parts[1]], axis=0)
        values = jnp.concatenate([v_ref[...], parts[2]], axis=0)
        ctx_ref[...], scaled_ref[...] = attend(
            q_ref[rows:, :], keys, values, mask_ref[...], log_ref, pl.program_id(0)
        )

    operands = [halo_near, halo_far, weight, bias, hot, query, key, value]
    in_specs = [whole(o.shape) for o in operands]
    in_specs[2] = pl.BlockSpec((D, 3 * PAIR), lambda p, _: (0, p))
    in_specs[3] = column(VECS)
    in_specs[5:] = [column(2 * rows)] * 3
    outs = [struct((rows, HALF), BF)] * 4 + [struct((rows, HALF), F32)]
    outs += [struct((LABELS, 3 * rows), BF), struct((VECS, rows), F32)]
    return call(
        "attend_halo",
        body,
        scalars,
        operands,
        in_specs,
        outs,
        [column(rows)] * 5 + [whole((LABELS, 3 * rows)), whole((VECS, rows))],
        (HALF // PAIR,),
        [pltpu.VMEM((rows, D), BF), pltpu.VMEM((rows, 3 * rows), F32)],
        micros=6,
    )


def feed_forward(scalars, block, ctx_mine, ctx_partner, x, vecs, up_bias, weights, rows):
    count = len(weights)
    fresh = len(weights[0].shape) == 3

    def body(sc, mine_ref, partner_ref, x_ref, vec_ref, bias_ref, *refs):
        weight_refs, refs = refs[:count], refs[count:]
        (norm_ref, inv_ref, first_ref, gate_ref, active_ref, part_ref), refs = refs[:6], refs[6:]
        if fresh:
            up_ref, down_ref, out_ref, other_ref, full_ref = refs
            for k in range(2):
                at, to = 2 * k * HID, slice(k * HID, (k + 1) * HID)
                place(up_ref, weight_refs, sc[1], slice(at, at + HID), to)
                place(down_ref, weight_refs, sc[1], slice(at + HID, at + 2 * HID), to)
            place(full_ref, weight_refs, sc[1], slice(4 * HID, 4 * HID + D), slice(None))
            for ref, flip in ((out_ref, 0), (other_ref, 1)):
                for k in range(2):
                    at = pl.multiple_of((sc[2] ^ flip ^ (2 * k)) * QUARTER, 16)
                    ref[k * QUARTER : (k + 1) * QUARTER, :] = full_ref[pl.ds(at, QUARTER), :]
        else:
            up_ref, down_ref, out_ref, other_ref = weight_refs

        attention = dot(mine_ref[...], out_ref[...]) + dot(partner_ref[...], other_ref[...])
        total = x_ref[...].astype(F32) + (attention + vec_ref[2:3, :])
        center = total - jnp.mean(total, axis=-1, keepdims=True)
        inverse = lax.rsqrt(jnp.mean(center * center, axis=-1, keepdims=True) + EPS)
        normed = center * inverse
        norm_ref[...] = normed
        inv_ref[...] = jnp.broadcast_to(inverse, (rows, 128))
        first = (normed * vec_ref[3:4, :] + vec_ref[4:5, :]).astype(BF)
        first_ref[...] = first
        gate = dot(first, up_ref[...]) + bias_ref[0:1, :]
        gate_ref[...] = gate
        active = (gate * (1.0 + lax.erf(gate * ROOT_HALF)) * 0.5).astype(BF)
        active_ref[...] = active
        part_ref[...] = dot_nt(active, down_ref[...]).astype(BF)

    operands = [ctx_mine, ctx_partner, x, vecs, up_bias, *weights]
    in_specs = [whole(o.shape) for o in operands]
    in_specs[2] = pl.BlockSpec((rows, D), lambda *_: (block, 0))
    outs = [
        struct((rows, D), F32),
        struct((rows, 128), F32),
        struct((rows, D), BF),
        struct((rows, 2 * HID), F32),
        struct((rows, 2 * HID), BF),
        struct((rows, D), BF),
    ]
    scratch = []
    if fresh:
        outs += [struct((D, 2 * HID), BF)] * 2 + [struct((HALF, D), BF)] * 2
        scratch = [pltpu.VMEM((D, D), BF)]
    results = call(
        "feed_forward",
        body,
        scalars,
        operands,
        in_specs,
        outs,
        [whole(o.shape) for o in outs],
        (1,),
        scratch,
        micros=6,
    )
    return results[:6], (results[6:] if fresh else weights)


def gelu_slope(scalars, gate):
    rows = gate.shape[0] // 2

    def body(_, gate_ref, slope_ref):
        gate_here = gate_ref[...]
        bell = jnp.exp(gate_here * gate_here * -0.5) * ROOT_TWO_PI
        slope_ref[...] = 0.5 * (1.0 + lax.erf(gate_here * ROOT_HALF)) + gate_here * bell

    spec = pl.BlockSpec((rows, gate.shape[1]), lambda r, _: (r, 0))
    return call(
        "gelu_slope", body, scalars, [gate], [spec], [struct(gate.shape, F32)], [spec], (2,), micros=3
    )[0]


def second_norm(scalars, block, part, received, normed, slope, cotangent, vecs, up, down, earlier, rows):
    def body(sc, part_ref, recv_ref, norm_ref, slope_ref, cot_ref, other_ref, vec_ref, up_ref, down_ref, *refs):
        old, refs = refs[: len(earlier)], refs[len(earlier) :]
        (total_grad_ref, branch_grad_ref, gate_grad_ref, first_part_ref, out_ref, sums_ref, bias_ref) = refs
        mine = sc[0] == block
        first = norm_ref[...] * vec_ref[3:4, :] + vec_ref[4:5, :]
        branch = part_ref[...].astype(F32) + recv_ref[...].astype(F32) + vec_ref[5:6, :]
        total = first + branch
        center = total - jnp.mean(total, axis=-1, keepdims=True)
        inverse = lax.rsqrt(jnp.mean(center * center, axis=-1, keepdims=True) + EPS)
        here = center * inverse
        upstream = jnp.where(mine, cot_ref[...].astype(F32), other_ref[...].astype(F32))
        scaled = upstream * vec_ref[6:7, :]
        inner = (
            scaled
            - jnp.mean(scaled, axis=-1, keepdims=True)
            - here * jnp.mean(scaled * here, axis=-1, keepdims=True)
        )
        total_grad = inner * inverse
        total_grad_ref[...] = total_grad
        branch_grad = total_grad.astype(BF)
        branch_grad_ref[...] = branch_grad
        gate_grad = (dot(branch_grad, down_ref[...]) * slope_ref[...]).astype(BF)
        gate_grad_ref[...] = gate_grad
        hidden = jnp.broadcast_to(jnp.sum(gate_grad.astype(F32), axis=0, keepdims=True), (8, 2 * HID))
        bias_ref[...] = hidden + old[2][...] if old else hidden
        first_part_ref[...] = dot_nt(gate_grad, up_ref[...]).astype(BF)

        @pl.when(mine)
        def _():
            out_ref[...] = (here * vec_ref[6:7, :] + vec_ref[7:8, :]).astype(BF)
            sums_ref[...] = jnp.zeros_like(sums_ref)
            sums_ref[0:1, :] = jnp.sum(upstream * here, axis=0, keepdims=True)
            sums_ref[1:2, :] = jnp.sum(upstream, axis=0, keepdims=True)
            sums_ref[2:3, :] = jnp.sum(branch_grad.astype(F32), axis=0, keepdims=True)

        if old:

            @pl.when(jnp.logical_not(mine))
            def _():
                out_ref[...] = old[0][...]
                sums_ref[...] = old[1][...]

        else:

            @pl.when(jnp.logical_not(mine))
            def _():
                out_ref[...] = jnp.zeros_like(out_ref)
                sums_ref[...] = jnp.zeros_like(sums_ref)

    operands = [part, received, normed, slope, *cotangent, vecs, up, down, *earlier]
    outs = [
        struct((rows, D), F32),
        struct((rows, D), BF),
        struct((rows, 2 * HID), BF),
        struct((rows, D), BF),
        struct((rows, D), BF),
        struct((8, D), F32),
        struct((8, 2 * HID), F32),
    ]
    results = call(
        "second_norm",
        body,
        scalars,
        operands,
        [whole(o.shape) for o in operands],
        outs,
        [whole(o.shape) for o in outs],
        (1,),
        micros=5,
    )
    return results[:4], results[4:]


def split_outs(width):
    return [struct((GROUPS // 2, BLOCK, width), BF)] * 2


def feed_forward_grads(scalars, blocks, rows):
    def body(sc, *refs):
        keep_ref, send_ref, result_ref = refs[-3:]
        step = pl.program_id(0)

        @pl.when(step % 2 == 0)
        def _():
            result_ref[...] = dot_tn(refs[0][...], refs[1][...]) + dot_tn(refs[4][...], refs[5][...])

        @pl.when(step % 2 == 1)
        def _():
            result_ref[...] = dot_tn(refs[2][...], refs[3][...]) + dot_tn(refs[6][...], refs[7][...])

        split_rows(result_ref, sc[1], keep_ref, send_ref)

    half = pl.BlockSpec((rows, HID), lambda c, _: (0, c // 2))
    outs = split_outs(4 * HID)
    out_specs = [pl.BlockSpec((GROUPS // 2, BLOCK, HID), lambda c, _: (0, 0, c))] * 2
    return call(
        "feed_forward_grads",
        body,
        scalars,
        [value for block in blocks for value in block],
        [whole((rows, D)), half] * 4,
        outs,
        out_specs,
        (4,),
        [pltpu.VMEM((D, HID), F32)],
        micros=8,
    )


def first_norm(
    scalars, block, part, received, total_grad, normed, inverse, vecs, out_weight, ctx, logs, earlier, rows
):
    def body(sc, part_ref, recv_ref, grad_ref, norm_ref, inv_ref, vec_ref, weight_ref, ctx_ref, log_ref, *refs):
        old, refs = refs[: len(earlier)], refs[len(earlier) :]
        attention_ref, context_ref, inner_ref, own_ref, sums_ref = refs[:5]
        mine = sc[0] == block
        upstream = grad_ref[...] + part_ref[...].astype(F32) + recv_ref[...].astype(F32)
        here = norm_ref[...]
        scaled = upstream * vec_ref[3:4, :]
        inner = (
            scaled
            - jnp.mean(scaled, axis=-1, keepdims=True)
            - here * jnp.mean(scaled * here, axis=-1, keepdims=True)
        )
        total = inner * inv_ref[:, :1]
        attention = total.astype(BF)
        attention_ref[...] = attention
        context = dot_nt(attention, weight_ref[...]).astype(BF)
        context_ref[...] = context
        lane = lax.broadcasted_iota(jnp.int32, (VECS, HALF), 1) // HEAD_DIM
        picks = jnp.where(lane == lax.broadcasted_iota(jnp.int32, (VECS, HALF), 0), 1.0, 0.0)
        inner = lax.dot_general(
            picks,
            context.astype(F32) * ctx_ref[...],
            (((1,), (1,)), ((), ())),
            precision=lax.Precision.HIGHEST,
            preferred_element_type=F32,
        )
        inner_ref[...] = inner
        if block == 1:
            send_ref = refs[5]
            turned = jnp.concatenate([weight_ref[QUARTER:, :], weight_ref[:QUARTER, :]], axis=0)
            send_ref[:rows, :] = dot_nt(attention, turned).astype(BF)
            rest = jnp.concatenate([log_ref[...], inner], axis=0)
            send_ref[rows:, :] = jnp.zeros((3 * LABELS, HALF), BF)
            for k in range(3):
                at = rows + k * LABELS
                piece = rest.astype(BF)
                send_ref[at : at + LABELS, :rows] = piece
                rest = rest - piece.astype(F32)

        @pl.when(mine)
        def _():
            own_ref[...] = total
            sums_ref[...] = jnp.zeros_like(sums_ref)
            sums_ref[0:1, :] = jnp.sum(upstream * here, axis=0, keepdims=True)
            sums_ref[1:2, :] = jnp.sum(upstream, axis=0, keepdims=True)
            sums_ref[2:3, :] = jnp.sum(attention.astype(F32), axis=0, keepdims=True)

        @pl.when(jnp.logical_not(mine))
        def _():
            own_ref[...] = old[0][...] if old else jnp.zeros_like(own_ref)
            sums_ref[...] = old[1][...] if old else jnp.zeros_like(sums_ref)

    operands = [part, received, total_grad, normed, inverse, vecs, out_weight, ctx, logs, *earlier]
    outs = [
        struct((rows, D), BF),
        struct((rows, HALF), BF),
        struct((VECS, rows), F32),
        struct((rows, D), F32),
        struct((8, D), F32),
        struct((rows + 3 * LABELS, HALF), BF),
    ][: 6 if block == 1 else 5]
    return call(
        "first_norm",
        body,
        scalars,
        operands,
        [whole(o.shape) for o in operands],
        outs,
        [whole(o.shape) for o in outs],
        (1,),
        micros=3,
    )


def halves(value):
    high = value.astype(BF).astype(F32)
    return jnp.concatenate([high, value - high], axis=0).astype(BF)


def whole_of(table):
    return table[:LABELS].astype(F32) + table[LABELS : 2 * LABELS].astype(F32)


def output_grads(scalars, blocks, small, small_side):
    def body(sc, *refs):
        small_ref, side_ref, keep_ref, send_ref, result_ref = refs[-5:]
        grads = []
        for ref in (refs[2], refs[5]):
            turned = pltpu.roll(ref[...].astype(F32), D - sc[2] * QUARTER, 1)
            turned = [turned[:, :QUARTER], turned[:, HALF : HALF + QUARTER]]
            grads.append(jnp.concatenate(turned, axis=1).astype(BF))
        for side in range(2):
            part = dot_tn(refs[side][...], grads[0]) + dot_tn(refs[3 + side][...], grads[1])
            for k in range(2):
                at = pl.multiple_of((sc[2] ^ side ^ (2 * k)) * QUARTER, 16)
                result_ref[pl.ds(at, QUARTER), :] = part[k * QUARTER : (k + 1) * QUARTER, :]
        for j in range(GROUPS):
            target = (keep_ref, send_ref)[j % 2]
            block = sc[1] ^ j
            rows = pl.ds(pl.multiple_of(block * BLOCK, 16), BLOCK)
            target[j // 2, :, :HALF] = result_ref[rows, :].astype(BF)
            target[j // 2, :, HALF:] = jnp.zeros((BLOCK, 128), BF)
            target[j // 2, : 2 * LABELS, HALF:] = halves(small_ref[block] + side_ref[block])

    outs = [struct((GROUPS // 2, BLOCK, HALF + 128), BF)] * 2
    operands = [value for block in blocks for value in block] + [small, small_side]
    return call(
        "output_grads",
        body,
        scalars,
        operands,
        [whole(o.shape) for o in operands],
        outs,
        [whole(o.shape) for o in outs],
        (1,),
        [pltpu.VMEM((D, HALF), F32)],
        micros=4,
    )


def attend_backward(scalars, pair, halo, grad_blocks, logs, inners, hot, weight, rows):
    base = 3 * rows
    steps = HALF // PAIR

    def body(sc, *refs):
        pair_refs, halo_refs, refs = refs[:3], refs[3:6], refs[6:]
        far_ref, near_ref, halo_ref, stats_ref, *refs = refs
        log_refs, inner_refs, (hot_ref, w_ref, *refs) = refs[:2], refs[2:4], refs[4:]
        out_ref, keep_ref, send_ref, sums_ref, mask_ref, key_ref, value_ref, acc_ref, q_ref, k_ref, v_ref, line_ref = refs
        for target, first_part, last_part in zip((q_ref, k_ref, v_ref), pair_refs, halo_refs):
            target[: 2 * rows, :] = first_part[...]
            target[2 * rows :, :] = last_part[...]
        step = pl.program_id(0)

        @pl.when(step == 0)
        def _():
            mask_ref[...] = (dot_tn(hot_ref[...], hot_ref[...]) - 1.0) * MASKED
            lines = jnp.zeros((LABELS, rows), F32)
            for k in range(3):
                at = rows + k * LABELS
                lines = lines + stats_ref[at : at + LABELS, :rows].astype(F32)
            line_ref[...] = lines

        key_ref[...] = jnp.zeros_like(key_ref)
        value_ref[...] = jnp.zeros_like(value_ref)
        lane = lax.broadcasted_iota(jnp.int32, (1, PAIR), 1)
        query_grads = [jnp.zeros((PAIR, rows), F32), jnp.zeros((PAIR, rows), F32)]
        for head in range(2):
            part = jnp.where((lane // HEAD_DIM) == head, 1.0, 0.0)
            key_turned = (k_ref[...].astype(F32) * part).T.astype(BF)
            line = 2 * step + head
            other = lax.rem(line + 3, 6)
            lines = [(log_refs[k][pl.ds(line, 1), :], inner_refs[k][pl.ds(line, 1), :]) for k in range(2)]
            lines += [(line_ref[pl.ds(other, 1), :], line_ref[pl.ds(other + VECS, 1), :])]
            for index, (low, high) in enumerate(((0, 2 * rows), (0, base), (rows, 2 * rows))):
                start = index * rows
                mine = (q_ref[start : start + rows].astype(F32) * (part * HEAD_DIM**-0.5)).astype(BF)
                grads = (far_ref, near_ref, halo_ref)[index][:rows, :]
                grads = (grads.astype(F32) * part).astype(BF)
                scores = dot_nt(k_ref[low:high], mine) + mask_ref[low:high, start : start + rows]
                log_total, inner = lines[index]
                probs = jnp.exp(scores - log_total)
                pulled = dot_nt(v_ref[low:high], grads)
                score_grads = (probs * (pulled - inner)).astype(BF)
                top = min(high, 2 * rows)
                span = top - low
                value_ref[low:top, :] += dot(probs[:span].astype(BF), grads)
                key_ref[low:top, :] += dot(score_grads[:span], mine)
                if index < 2:
                    query_grads[index] = query_grads[index] + dot(key_turned[:, low:high], score_grads)
        for index in range(2):
            turned = (query_grads[index] * HEAD_DIM**-0.5).T.astype(BF)
            out_ref[index * rows : (index + 1) * rows, :PAIR] = turned
        out_ref[:, PAIR : 2 * PAIR] = key_ref[...].astype(BF)
        out_ref[:, 2 * PAIR :] = value_ref[...].astype(BF)
        sums = jnp.sum(out_ref[...].astype(F32), axis=0, keepdims=True)
        sums_ref[...] = jnp.broadcast_to(sums, (8, 3 * PAIR))
        product = dot_nt(out_ref[...], w_ref[...])

        @pl.when(step == 0)
        def _():
            acc_ref[...] = product

        @pl.when(step > 0)
        def _():
            acc_ref[...] += product

        @pl.when(step == steps - 1)
        def _():
            near = sc[0]
            keep_ref[...] = acc_ref[pl.ds(pl.multiple_of(near * rows, rows), rows), :]
            other = acc_ref[pl.ds(pl.multiple_of((1 - near) * rows, rows), rows), :]
            send_ref[...] = other.astype(BF)

    stats = grad_blocks[2]
    operands = [*pair, *halo, *grad_blocks, stats, *logs, *inners, hot, weight]
    in_specs = [column(2 * rows)] * 3 + [column(rows)] * 5 + [column(stats.shape[0])]
    in_specs += [whole(o.shape) for o in operands[9:15]]
    in_specs += [pl.BlockSpec((D, 3 * PAIR), lambda p, _: (0, p))]
    outs = [struct((2 * rows, 3 * HALF), BF), struct((rows, D), F32), struct((rows, D), BF)]
    outs += [struct((8, 3 * HALF), F32)]
    out_specs = [
        pl.BlockSpec((2 * rows, 3 * PAIR), lambda p, _: (0, p)),
        whole((rows, D)),
        whole((rows, D)),
        pl.BlockSpec((8, 3 * PAIR), lambda p, _: (0, p)),
    ]
    scratch = [
        pltpu.VMEM((base, base), F32),
        pltpu.VMEM((2 * rows, PAIR), F32),
        pltpu.VMEM((2 * rows, PAIR), F32),
        pltpu.VMEM((2 * rows, D), F32),
    ] + [pltpu.VMEM((base, PAIR), BF)] * 3
    scratch += [pltpu.VMEM((LABELS, rows), F32)]
    return call(
        "attend_backward",
        body,
        scalars,
        operands,
        in_specs,
        outs,
        out_specs,
        (steps,),
        scratch,
        micros=MICROS,
    )


def projection_grads(scalars, x, grads, rows):
    tall = 2 * rows

    def body(sc, x_ref, grad_ref, *refs):
        result_ref = refs[-1]
        result_ref[...] = dot_tn(x_ref[...], grad_ref[...])
        split_rows(result_ref, sc[1], refs[0], refs[1])

    outs = split_outs(3 * HALF)
    out_specs = [pl.BlockSpec((GROUPS // 2, BLOCK, 3 * PAIR), lambda p, _: (0, 0, p))] * 2
    return call(
        "projection_grads",
        body,
        scalars,
        [x, grads],
        [pl.BlockSpec((tall, D), lambda p, _: (0, 0)), pl.BlockSpec((tall, 3 * PAIR), lambda p, _: (0, p))],
        outs,
        out_specs,
        (HALF // PAIR,),
        [pltpu.VMEM((D, 3 * PAIR), F32)],
        micros=5,
    )


def combine(scalars, keep, received):
    count, rows, width = keep.shape
    chunk = width // 3

    def body(_, keep_ref, recv_ref, *refs):
        for k in range(count):
            total = keep_ref[k].astype(F32) + recv_ref[k].astype(F32)
            refs[k][...] = total.astype(refs[k].dtype)

    block = pl.BlockSpec((count, rows, chunk), lambda c, _: (0, 0, c))
    outs = [struct((rows, width), F32)] + [struct((rows, width), BF)] * (count - 1)
    spec = pl.BlockSpec((rows, chunk), lambda c, _: (0, c))
    return list(call(
        "combine",
        body, scalars, [keep, received], [block, block], outs, [spec] * count, (3,)))


def combine_both(scalars, keep, received, out_keep, out_received):
    count, rows, wide = keep.shape
    last = wide + HALF

    def body(_, keep_ref, recv_ref, out_keep_ref, out_recv_ref, *refs):
        for k in range(count):
            kind = refs[k].dtype
            refs[k][:, :wide] = (keep_ref[k].astype(F32) + recv_ref[k].astype(F32)).astype(kind)
            total = out_keep_ref[k, :, :HALF].astype(F32) + out_recv_ref[k, :, :HALF].astype(F32)
            refs[k][:, wide:last] = total.astype(kind)
            small = whole_of(out_keep_ref[k, :, HALF:]) + whole_of(out_recv_ref[k, :, HALF:])
            refs[k][:, last:] = jnp.zeros((rows, 128), kind)
            refs[k][: 2 * LABELS, last:] = halves(small).astype(kind)

    outs = [struct((rows, last + 128), F32)] + [struct((rows, last + 128), BF)] * (count - 1)
    return simple("combine_both", body, scalars, [keep, received, out_keep, out_received], outs, 2)


def total_feed(scalars, sums):
    rows = sums[0].shape[0]

    def body(_, *refs):
        keep_ref, send_ref = refs[-2:]
        total = refs[0][...]
        for ref in refs[1:-2]:
            total = total + ref[...].astype(F32)
        keep_ref[...] = total[:, : 2 * HID]
        send_ref[:, : 2 * HID] = total[:, 2 * HID :].astype(BF)
        send_ref[:, 2 * HID :] = jnp.zeros((rows, 256), BF)

    outs = [struct((rows, 2 * HID), F32), struct((rows, 2 * HID + 256), BF)]
    return simple("total_feed", body, scalars, sums, outs, 2)


def total_projection(scalars, sums):
    rows, width = sums[0].shape
    wide = 3 * HALF
    last = wide + HALF

    def body(_, *refs):
        keep_ref, send_ref = refs[-2:]
        total = refs[0][:, :last]
        for ref in refs[1:-2]:
            total = total + ref[:, :last].astype(F32)
        near, far = [], []
        for kind in range(3):
            both = [total[:, (3 * p + kind) * PAIR : (3 * p + kind + 1) * PAIR] for p in range(3)]
            both = jnp.concatenate(both, axis=1)
            near.append(both[:, :QUARTER])
            far.append(both[:, QUARTER:])
        near.append(total[:, wide : wide + QUARTER])
        far.append(total[:, wide + QUARTER : last])
        keep_ref[:, :D] = jnp.concatenate(near, axis=1)
        send_ref[:, :D] = jnp.concatenate(far, axis=1).astype(BF)
        if width > last:
            small = jnp.zeros((LABELS, 128), F32)
            for ref in refs[:-2]:
                small = small + whole_of(ref[:, last:])
            keep_ref[:, D:] = jnp.zeros((rows, 128), F32)
            send_ref[:, D:] = jnp.zeros((rows, 128), BF)
            keep_ref[:LABELS, D:] = small
            send_ref[: 2 * LABELS, D:] = halves(small)

    width_out = D + width - last
    outs = [struct((rows, width_out), F32), struct((rows, width_out), BF)]
    return simple("total_projection", body, scalars, sums, outs, 2)


def finish_feed(scalars, keep, received):
    rows = keep.shape[0]

    def body(_, keep_ref, recv_ref, up_ref, down_ref):
        up_ref[...] = keep_ref[:, :HID] + recv_ref[:, :HID].astype(F32)
        down_ref[...] = keep_ref[:, HID:] + recv_ref[:, HID : 2 * HID].astype(F32)

    outs = [struct((rows, HID), F32)] * 2
    return simple("finish_feed", body, scalars, [keep, received], outs, FEED_MICROS)


def finish_projection(scalars, keep, received):
    rows, width = keep.shape

    def body(_, keep_ref, recv_ref, *refs):
        total = keep_ref[:, :D] + recv_ref[:, :D].astype(F32)
        for k in range(4):
            refs[k][...] = total[:, k * QUARTER : (k + 1) * QUARTER]
        if width > D:
            small = keep_ref[:LABELS, D:] + whole_of(recv_ref[:, D:])
            for k in range(VECS):
                refs[4 + k][...] = small[k, :BLOCK]
            for k in range(SHARE):
                refs[4 + VECS][k * 128 : (k + 1) * 128] = small[VECS + k]

    outs = [struct((rows, QUARTER), F32)] * 4
    if width > D:
        outs += [struct((BLOCK,), F32)] * VECS + [struct((FF // GROUPS,), F32)]
    return simple("finish_projection", body, scalars, [keep, received], outs)


def small_sums(scalars, sums_one, sums_two, sums_hidden, sums_projection):
    def body(sc, one_ref, two_ref, hidden_ref, projection_ref, out_ref, wide_ref, tall_ref):
        out_ref[...] = jnp.zeros_like(out_ref)
        lanes = lax.broadcasted_iota(jnp.int32, (1, D), 1)
        near, far = lanes < QUARTER, (lanes >= QUARTER) & (lanes < HALF)
        for row, kind in ((0, 0), (1, 2)):
            line = jnp.concatenate(
                [
                    projection_ref[0:1, (3 * p + kind) * PAIR : (3 * p + kind + 1) * PAIR]
                    for p in range(3)
                ]
                + [jnp.zeros((1, HALF), F32)],
                axis=1,
            )
            low = pltpu.roll(jnp.broadcast_to(jnp.where(near, line, 0.0), (8, D)), sc[2] * QUARTER, 1)
            high = jnp.broadcast_to(jnp.where(far, line, 0.0), (8, D))
            high = pltpu.roll(high, D - QUARTER + (sc[2] ^ 2) * QUARTER, 1)
            wide_ref[row : row + 1, :] = (low + high)[0:1]
        wide_ref[2:3, :] = one_ref[2:3, :]
        wide_ref[3:5, :] = one_ref[0:2, :]
        wide_ref[5:6, :] = two_ref[2:3, :]
        wide_ref[6:8, :] = two_ref[0:2, :]
        tall_ref[...] = jnp.zeros_like(tall_ref)
        for k in range(2):
            to = pl.multiple_of((sc[2] ^ (2 * k)) * HID, 128)
            tall_ref[0:1, pl.ds(to, HID)] = hidden_ref[0:1, k * HID : (k + 1) * HID]
        share = FF // GROUPS
        for d in range(GROUPS):
            out_ref[d, :VECS, :BLOCK] = wide_ref[:, d * BLOCK : (d + 1) * BLOCK]
            for c in range(share // 128):
                at = d * share + c * 128
                out_ref[d, VECS + c : VECS + c + 1, :] = tall_ref[0:1, at : at + 128]

    operands = [sums_one, sums_two, sums_hidden, sums_projection]
    shape = (GROUPS, LABELS, 128)
    return call(
        "small_sums",
        body,
        scalars,
        operands,
        [whole(o.shape) for o in operands],
        [struct(shape, F32)],
        [whole(shape)],
        (1,),
        [pltpu.VMEM((VECS, D), F32), pltpu.VMEM((8, FF), F32)],
    )[0]


def per_device(
    tokens,
    segments,
    query_weight,
    key_weight,
    value_weight,
    output_weight,
    query_bias,
    value_bias,
    output_bias,
    first_gain,
    first_shift,
    up_weight,
    up_bias,
    down_weight,
    down_bias,
    second_gain,
    second_shift,
    cotangent,
):
    seq_count = lax.axis_size("seq")
    count = lax.axis_size("dp")
    place_z = lax.axis_index("seq")
    assert seq_count == 4
    direct = count == GROUPS
    rows = tokens.shape[1]
    piece_rows = query_weight.shape[0]
    near = (place_z == 1) | (place_z == 2)
    base = lax.axis_index("dp") if direct else 0
    scalars = jnp.stack([near, base, place_z]).astype(jnp.int32)

    own = tokens[0]
    cot_own = cotangent[0]
    lines = [
        query_bias,
        value_bias,
        output_bias,
        first_gain,
        first_shift,
        down_bias,
        second_gain,
        second_shift,
    ]
    lines = lines if direct else []
    first_send, mine, wide, labelled, own_docs = pack_inputs(
        scalars,
        [query_weight, key_weight, value_weight, output_weight],
        own,
        segments,
        up_weight,
        down_weight.T,
        lines,
        up_bias,
    )
    arrived = swap(first_send, "seq", 2)
    side = swap(output_weight, "seq", 1)
    if direct:
        mine_chip = [mine, swap(mine, "dp", 2), swap(mine, "dp", 4)]
        wide_last = swap(wide, "dp", 6)
        labelled, side, wide_last, mine_chip, arrived = together(
            labelled, side, wide_last, mine_chip, arrived
        )
    else:
        arrived, labelled, side = together(arrived, labelled, side)
    narrow_far, both, partner_send = split_arrived(scalars, arrived, mine, labelled)
    partner = swap(partner_send, "seq", 1)
    halo_near = lax.ppermute(labelled, "seq", [(1, 2), (2, 1)])
    if direct:
        far_chip = [narrow_far, swap(narrow_far, "dp", 2), swap(narrow_far, "dp", 4)]
        both_far = swap(both, "dp", 6)
        mine_chip, cot_own, far_chip, both_far, partner, halo_near = together(
            mine_chip, cot_own, far_chip, both_far, partner, halo_near
        )
        stacked = stack_narrow(scalars, mine_chip, far_chip, both_far)
        pieces = [stacked, swap(stacked, "dp", 1)]
        feed_chip = chip_pieces(pack_feed(scalars, first_send, arrived, side, partner))
    halo_far = lax.ppermute(halo_near, "seq", [(1, 0), (2, 3)])
    if not direct:
        vectors = jnp.stack(
            [
                query_bias,
                value_bias,
                output_bias,
                first_gain,
                first_shift,
                down_bias,
                second_gain,
                second_shift,
            ]
        )
        lines = lax.all_gather(vectors, "dp", axis=1, tiled=True).reshape(VECS, GROUPS, BLOCK)
        lines = jnp.pad(lines, ((0, 0), (0, 0), (0, 128 - BLOCK)))
        tall = lax.all_gather(up_bias, "dp", axis=0, tiled=True).reshape(GROUPS, SHARE, 128).transpose(1, 0, 2)
        lines = jnp.concatenate([lines, tall], axis=0)
        lines = jnp.pad(lines, ((0, LABELS - VECS - SHARE), (0, 0), (0, 3 * QUARTER - 128)))
        lines = lines.transpose(1, 0, 2)
        gathered = gather_rows(mine)
        pieces = [
            jnp.concatenate([half[:, :, 2 * HID :], lines[k::2], far], axis=1)
            for k, (half, far) in enumerate(zip(gathered, gather_rows(narrow_far)))
        ]
        last = swap(arrived[:, 3 * QUARTER : D], "seq", 1)
        feed = gather_rows(pack_feed(scalars, first_send, arrived, side, last))
        weights = [
            jnp.concatenate([half[:, :, : 2 * HID], far], axis=2) for half, far in zip(gathered, feed)
        ]

    def rows_of(keep, send):
        return jnp.stack([keep, send], axis=1).reshape(GROUPS, -1, keep.shape[2]).astype(F32)

    def spread(sums):
        return [sums[0]] + [swap(sums[k], "dp", 2 * k) for k in range(1, len(sums))]

    def scattered(table):
        return [lax.psum_scatter(table, "dp", scatter_dimension=0, tiled=True)]

    *pair, ctx_far, x, weight, hot, vecs, hidden_bias, bias, log_far, scaled_far = attend_pair(
        scalars, own, partner, own_docs, pieces, rows
    )
    if direct:
        pair, ctx_far, cot_own, halo_far = together(pair, ctx_far, cot_own, halo_far)
    *halo, ctx_near, scaled_near, hot, log_near = attend_halo(scalars, halo_near, halo_far, weight, bias, hot, *pair, rows)
    ctx_mine = [ctx_far, ctx_near]
    ctx_partner = [swap(ctx_far, "seq", 1), None]
    if direct:
        ctx_mine[1], ctx_partner[0], wide_last, feed_chip = together(
            ctx_mine[1], ctx_partner[0], wide_last, feed_chip
        )
        stacked = stack_wide(scalars, mine_chip, wide_last, feed_chip)
        weights = [stacked, swap(stacked, "dp", 1)]
    ctx_partner[1] = swap(ctx_mine[1], "seq", 1)
    cot_partner = swap(cot_own, "seq", 1)

    forward, slopes, part_far = [None, None], [None, None], [None, None]
    for block in (1, 0):
        forward[block], weights = feed_forward(
            scalars, block, ctx_mine[block], ctx_partner[block], x, vecs, hidden_bias, weights, rows
        )
        part_far[block] = swap(forward[block][5], "seq", 1)
    up, down, out_mine, _ = weights
    second, second_shared, first_part_far = [None, None], [], [None, None]
    for block in (1, 0):
        slopes[block] = gelu_slope(scalars, forward[block][3])
    for block in (1, 0):
        second[block], second_shared = second_norm(
            scalars,
            block,
            forward[block][5],
            part_far[block],
            forward[block][0],
            slopes[block],
            (cot_own, cot_partner),
            vecs,
            up,
            down,
            second_shared,
            rows,
        )
        if block == 1:
            first_part_far[block] = swap(second[block][3], "seq", 1)
    feed_parts = feed_forward_grads(
        scalars,
        [(forward[k][2], second[k][2], second[k][1], forward[k][4]) for k in range(2)],
        rows,
    )
    first_part_far[1], second, second_shared, feed_parts = together(
        first_part_far[1], second, second_shared, feed_parts
    )
    first_part_far[0] = swap(second[0][3], "seq", 1)
    layer_output, sums_two, sums_hidden = second_shared
    attention_grad, ctx_grad, inners, first_shared = [None, None], [None, None], [None, None], []
    logs, scaled = [log_far, log_near], [scaled_far, scaled_near]

    def finish(block):
        attention_grad[block], ctx_grad[block], inners[block], *shared = first_norm(
            scalars,
            block,
            second[block][3],
            first_part_far[block],
            second[block][0],
            forward[block][0],
            forward[block][1],
            vecs,
            out_mine,
            scaled[block],
            logs[block],
            first_shared,
            rows,
        )
        return shared

    *first_shared, halo_send = finish(1)
    halo_grad = swap(halo_send, "seq", 2)
    if direct:
        feed_sums = combine(scalars, feed_parts[0], swap(feed_parts[1], "dp", 1))
        feed_sums = spread(feed_sums)
    else:
        feed_sums = scattered(rows_of(*feed_parts).reshape(D, -1))
    own_grad, sums_one = finish(0)

    grads, input_keep, input_send, sums_projection = attend_backward(
        scalars, pair, halo, [*ctx_grad, halo_grad], logs, inners, hot, weight, rows
    )
    input_far = swap(input_send, "seq", 1)
    small = small_sums(scalars, sums_one, sums_two, sums_hidden, sums_projection)
    small_side = swap(small, "seq", 1)
    projection_parts = projection_grads(scalars, x, grads, rows)
    projection_parts, small_side, feed_sums = together(projection_parts, small_side, feed_sums)
    if direct:
        feed_keep, feed_send = total_feed(scalars, feed_sums)
        attention_grad, feed_send = together(attention_grad, feed_send)
    out_blocks = [(ctx_mine[k], ctx_partner[k], attention_grad[k]) for k in range(2)]
    if direct:
        projection_received = swap(projection_parts[1], "dp", 1)
        out_parts = output_grads(scalars, out_blocks, small, small_side)
        out_received = swap(out_parts[1], "dp", 1)
        feed_far = swap(feed_send, "seq", 2)
        sums = spread(
            combine_both(scalars, projection_parts[0], projection_received, out_parts[0], out_received)
        )
    else:
        out_parts = rows_of(*output_grads(scalars, out_blocks, small, small_side))
        sums = scattered(
            jnp.concatenate(
                [rows_of(*projection_parts).reshape(D, -1), out_parts[:, :, :HALF].reshape(D, -1)], axis=1
            )
        )
        feed_keep, feed_send = total_feed(scalars, feed_sums)
        feed_far = swap(feed_send, "seq", 2)
    if direct:
        sums, feed_far, input_far = together(sums, feed_far, input_far)
    keep, send = total_projection(scalars, sums)
    received = swap(send, "seq", 2)
    up_grad, down_grad = finish_feed(scalars, feed_keep, feed_far)
    input_grad = own_grad + input_keep + input_far.astype(F32)
    if direct:
        received, up_grad, input_grad = together(received, up_grad, input_grad)
    projections = list(finish_projection(scalars, keep, received))
    if direct:
        projections, vec, tall_lines = projections[:4], projections[4:-1], projections[-1]
    else:
        tile = out_parts[:, :LABELS, HALF:] + out_parts[:, LABELS : 2 * LABELS, HALF:]
        tile = tile + swap(tile, "seq", 2)
        wide_lines = tile[:, :VECS, :BLOCK].transpose(1, 0, 2).reshape(VECS, D)
        wide_lines = lax.psum_scatter(wide_lines, "dp", scatter_dimension=1, tiled=True)
        tall_lines = lax.psum_scatter(tile[:, VECS : VECS + 3].reshape(-1), "dp", tiled=True)
        vec = [wide_lines[k] for k in range(VECS)]
    return (
        layer_output[None],
        input_grad[None],
        *projections,
        vec[0],
        vec[1],
        vec[2],
        vec[3],
        vec[4],
        up_grad,
        tall_lines,
        down_grad.T,
        vec[5],
        vec[6],
        vec[7],
    )


def solution(mesh):
    placed = (
        P("dp", "seq", None),
        P("dp", "seq"),
        P("dp", "seq"),
        P("dp", "seq"),
        P("dp", "seq"),
        P("dp", "seq"),
        P("dp"),
        P("dp"),
        P("dp"),
        P("dp"),
        P("dp"),
        P("dp", "seq"),
        P("dp"),
        P("seq", "dp"),
        P("dp"),
        P("dp"),
        P("dp"),
        P("dp", "seq", None),
    )
    return jax.shard_map(
        per_device,
        mesh=mesh,
        in_specs=placed,
        out_specs=(
            P("dp", "seq", None),
            P("dp", "seq", None),
            P("dp", "seq"),
            P("dp", "seq"),
            P("dp", "seq"),
            P("dp", "seq"),
            P("dp"),
            P("dp"),
            P("dp"),
            P("dp"),
            P("dp"),
            P("dp", "seq"),
            P("dp"),
            P("seq", "dp"),
            P("dp"),
            P("dp"),
            P("dp"),
        ),
        check_vma=False,
    )
```

```python
import jax
import jax.numpy as jnp
from jax import lax
from jax.experimental import pallas as pl
from jax.experimental.pallas import tpu as pltpu
from jax.sharding import PartitionSpec as P

D = 768
HEADS = 12
HEAD_DIM = 64
FF = 3072
EPS = 1e-05
MASKED = 1e30
PAIR = 2 * HEAD_DIM
QUARTER = D // 4
HALF = D // 2
HID = FF // 4
VECS = 8
GROUPS = 8
SHARE = FF // GROUPS // 128
BLOCK = D // GROUPS
LABELS = 16
MARKS = 48
MICROS = 450
FEED_MICROS = 300
BF = jnp.bfloat16
F32 = jnp.float32
ROOT_HALF = 0.7071067811865476
ROOT_TWO_PI = 0.3989422804014327


def dot(a, b):
    return lax.dot_general(a, b, (((1,), (0,)), ((), ())), preferred_element_type=F32)


def dot_nt(a, b):
    return lax.dot_general(a, b, (((1,), (1,)), ((), ())), preferred_element_type=F32)


def dot_tn(a, b):
    return lax.dot_general(a, b, (((0,), (0,)), ((), ())), preferred_element_type=F32)


def swap(value, axis, mask):
    count = lax.axis_size(axis)
    return lax.ppermute(value, axis, [(k, k ^ mask) for k in range(count)])


def together(*values):
    return lax.optimization_barrier(values)


def whole(shape):
    return pl.BlockSpec(shape, lambda *_: (0,) * len(shape))


def params():
    return pltpu.CompilerParams(vmem_limit_bytes=22 * 1024 * 1024)


def call(name, body, scalars, operands, in_specs, outs, out_specs, grid, scratch=(), micros=1):
    spec = pltpu.PrefetchScalarGridSpec(
        num_scalar_prefetch=1,
        grid=grid,
        in_specs=in_specs,
        out_specs=out_specs,
        scratch_shapes=list(scratch),
    )
    return pl.pallas_call(
        body,
        out_shape=outs,
        grid_spec=spec,
        compiler_params=params(),
        cost_estimate=pl.CostEstimate(
            flops=int(micros * 1.0e7), transcendentals=0, bytes_accessed=1024
        ),
        name=name,
    )(scalars, *operands)


def turn(quarters):
    return lax.rem(quarters + 4, 4) * QUARTER


def struct(shape, dtype):
    return jax.ShapeDtypeStruct(shape, dtype)


def chip_pieces(piece):
    return [piece] + [swap(piece, "dp", j) for j in range(2, GROUPS, 2)]


def gather_rows(piece):
    full = lax.all_gather(piece, "dp", axis=0, tiled=True)
    full = full.reshape(GROUPS, D // GROUPS, piece.shape[1])
    return [full[0::2], full[1::2]]


def place(target, pair, base, source_cols, target_cols):
    for j in range(GROUPS):
        start = pl.multiple_of((base ^ j) * BLOCK, 16)
        target[pl.ds(start, BLOCK), target_cols] = pair[j % 2][j // 2, :BLOCK, source_cols]


def split_rows(result, base, keep, send):
    for j in range(GROUPS):
        block = result[pl.ds(pl.multiple_of((base ^ j) * BLOCK, 16), BLOCK), :].astype(BF)
        if j % 2:
            send[j // 2] = block
        else:
            keep[j // 2] = block


def simple(name, body, scalars, operands, outs, micros=1):
    return call(
        name,
        body,
        scalars,
        operands,
        [whole(o.shape) for o in operands],
        outs,
        [whole(o.shape) for o in outs],
        (1,),
        micros=micros,
    )


def pack_inputs(scalars, tables, tokens, segments, up, down, lines, tall):
    rows = tokens.shape[0]
    height = tables[0].shape[0]
    skip = 2 * HID + (128 if lines else 0)
    operands = list(tables) + [tokens, segments, up, down] + lines + ([tall] if lines else [])
    count = len(operands)

    def body(_, *refs):
        sources, (send_ref, mine_ref, wide_ref, label_ref, docs_ref), refs = (
            refs[:count],
            refs[count : count + 5],
            refs[count + 5 :],
        )
        copies = [pltpu.make_async_copy(a, b, refs[-1].at[k]) for k, (a, b) in enumerate(zip(sources, refs))]
        for copy in copies:
            copy.start()
        for copy in copies:
            copy.wait()
        joined = jnp.concatenate([ref[...].astype(F32) for ref in refs[:4]], axis=1).astype(BF)
        send_ref[:, :D] = joined
        send_ref[:, D : D + HID] = refs[6][...]
        send_ref[:, D + HID :] = refs[7][...]
        mine_ref[:, :HID] = refs[6][...]
        mine_ref[:, HID : 2 * HID] = refs[7][...]
        part = joined[:, : 3 * QUARTER].astype(F32)
        mine_ref[:, skip:] = part.astype(BF)
        wide_ref[:, :HID] = refs[6][...]
        wide_ref[:, HID:] = refs[7][...]
        docs = refs[5][...].astype(F32)
        docs_ref[...] = docs
        label_ref[:rows, :] = refs[4][...]
        label_ref[rows:, :] = jnp.zeros((MARKS, D), BF)
        label_ref[rows:, :rows] = jnp.broadcast_to(docs, (MARKS, rows)).astype(BF)
        if lines:
            table = [ref[...].astype(F32)[None, :] for ref in refs[8 : 8 + VECS]]
            table = jnp.concatenate(table, axis=0)
            table = [jnp.concatenate([table, jnp.zeros((VECS, 128 - BLOCK), F32)], axis=1)]
            line = refs[8 + VECS][...].astype(F32)[None, :]
            table += [line[:, c * 128 : (c + 1) * 128] for c in range(SHARE)]
            table += [jnp.zeros((height - VECS - SHARE, 128), F32)]
            mine_ref[:, 2 * HID : skip] = jnp.concatenate(table, axis=0).astype(BF)

    outs = [
        struct((height, D + 2 * HID), BF),
        struct((height, skip + 3 * QUARTER), BF),
        struct((height, 2 * HID), BF),
        struct((rows + MARKS, D), BF),
        struct((1, rows), F32),
    ]
    operands = [pltpu.with_memory_space_constraint(o, pltpu.MemorySpace.HBM) for o in operands]
    return call(
        "pack_inputs",
        body,
        scalars,
        operands,
        [pl.BlockSpec(memory_space=pltpu.MemorySpace.HBM)] * count,
        outs,
        [whole(o.shape) for o in outs],
        (1,),
        [pltpu.VMEM(o.shape, o.dtype) for o in operands] + [pltpu.SemaphoreType.DMA((count,))],
    )


def split_arrived(scalars, arrived, mine, labelled):
    rows = arrived.shape[0]
    tall = rows + LABELS
    skip = mine.shape[1] - 3 * QUARTER
    direct = skip > 2 * HID

    def body(_, far_ref, mine_ref, label_ref, narrow_ref, both_ref, send_ref):
        narrow_ref[...] = far_ref[:, : 3 * QUARTER]
        both_ref[:rows, :] = mine_ref[:, skip:]
        both_ref[tall:, :] = far_ref[:, : 3 * QUARTER]
        send_ref[...] = label_ref[...]
        if direct:
            both_ref[rows:tall, :] = jnp.zeros((LABELS, 3 * QUARTER), BF)
            both_ref[rows:tall, :128] = mine_ref[:LABELS, 2 * HID : skip]
            part = far_ref[:, 3 * QUARTER : D].astype(F32)
            step = rows // 4
            part = jnp.concatenate([part[k * step : (k + 1) * step] for k in range(4)], axis=1)
            part = jnp.concatenate([part, jnp.zeros((MARKS - LABELS - step, D), F32)], axis=0)
            send_ref[labelled.shape[0] - MARKS + LABELS :, :] = part.astype(BF)

    outs = [
        struct((rows, 3 * QUARTER), BF),
        struct((rows + tall, 3 * QUARTER), BF),
        struct(labelled.shape, BF),
    ]
    return simple("split_arrived", body, scalars, [arrived, mine, labelled], outs)


def stack_narrow(scalars, mine_chip, far_chip, both_far):
    rows = far_chip[0].shape[0]
    tall = rows + LABELS
    skip = mine_chip[0].shape[1] - 3 * QUARTER

    def body(_, *refs):
        out_ref = refs[-1]
        for k in range(3):
            out_ref[k, :rows] = refs[k][:, skip:]
            out_ref[k, rows:tall] = jnp.zeros((LABELS, 3 * QUARTER), BF)
            out_ref[k, rows:tall, :128] = refs[k][:LABELS, 2 * HID : skip]
            out_ref[k, tall:] = refs[3 + k][...]
        out_ref[3] = refs[6][...]

    shape = (GROUPS // 2, tall + rows, 3 * QUARTER)
    operands = [*mine_chip, *far_chip, both_far]
    return simple("stack_narrow", body, scalars, operands, [struct(shape, BF)])[0]


def stack_wide(scalars, mine_chip, last, feed_chip):
    def body(_, *refs):
        out_ref = refs[-1]
        for k in range(3):
            out_ref[k, :, : 2 * HID] = refs[k][:BLOCK, : 2 * HID]
        out_ref[3, :, : 2 * HID] = refs[3][...]
        for k in range(4):
            out_ref[k, :, 2 * HID :] = refs[4 + k][...]

    shape = (GROUPS // 2, BLOCK, 4 * HID + D)
    return simple("stack_wide", body, scalars, [*mine_chip, last, *feed_chip], [struct(shape, BF)])[0]


def pack_feed(scalars, first_send, arrived, side, last):
    rows = arrived.shape[0]
    columns = slice(3 * QUARTER, D)

    def body(sc, own_ref, arrived_ref, side_ref, last_ref, out_ref):
        out_ref[:, : 2 * HID] = arrived_ref[:, D:]
        final = last_ref[...].astype(F32)
        if last.shape[1] == D:
            step = rows // 4
            final = final[last.shape[0] - MARKS + LABELS :]
            final = [final[:step, k * QUARTER : (k + 1) * QUARTER] for k in range(4)]
            final = jnp.concatenate(final, axis=0)
        total = jnp.zeros((rows, D), F32)
        for k, part in enumerate([own_ref[:, columns], side_ref[...], arrived_ref[:, columns], final]):
            part = jnp.concatenate([part.astype(F32), jnp.zeros((rows, D - QUARTER), F32)], axis=1)
            total = total + pltpu.roll(part, (sc[2] ^ k) * QUARTER, 1)
        out_ref[:, 2 * HID :] = total.astype(BF)

    out = struct((rows, 2 * HID + D), BF)
    return simple("pack_feed", body, scalars, [first_send, arrived, side, last], [out])[0]


def mark(docs, rows):
    number = lax.broadcasted_iota(jnp.int32, (LABELS, rows), 0).astype(F32)
    return jnp.where(jnp.broadcast_to(docs, (LABELS, rows)) == number, 1.0, 0.0).astype(BF)


def attend(query, key, value, mask, log_ref, step):
    lane = lax.broadcasted_iota(jnp.int32, (1, PAIR), 1)
    total = jnp.zeros(query.shape, F32)
    scaled = jnp.zeros(query.shape, F32)
    logs = jnp.zeros(query.shape, F32)
    value = jnp.concatenate([value, jnp.ones(value.shape, BF)], axis=1)
    for head in range(2):
        part = jnp.where((lane // HEAD_DIM) == head, 1.0, 0.0)
        mine = (query.astype(F32) * (part * HEAD_DIM**-0.5)).astype(BF)
        scores = dot_nt(mine, key) + mask
        top = jnp.max(scores, axis=-1, keepdims=True)
        expo = jnp.exp(scores - top)
        whole_sum = jnp.sum(expo, axis=-1, keepdims=True)
        probs = expo * (1.0 / whole_sum)
        rounded = probs.astype(BF)
        context = dot(rounded, value)
        total = total + context[:, :PAIR] * part
        scaled = scaled + context[:, :PAIR] * part / context[:, PAIR:]
        logs = jnp.where(lane == head, top + jnp.log(whole_sum), logs)
    turned = logs.T
    for head in range(2):
        log_ref[pl.ds(2 * step + head, 1), :] = turned[head : head + 1, :]
    return total.astype(BF), scaled


def column(height):
    return pl.BlockSpec((height, PAIR), lambda p, _: (0, p))


def attend_pair(scalars, own, partner, own_docs, pieces, rows):
    base = 2 * rows
    tall = BLOCK + LABELS

    def body(sc, own_ref, partner_ref, docs_ref, *refs):
        weight_refs, refs = refs[:2], refs[2:]
        q_ref, k_ref, v_ref, ctx_ref, x_ref, w_ref, hot_ref, vec_ref, hidden_ref, bias_ref, log_ref, *refs = refs
        scaled_ref, mask_ref = refs
        step = pl.program_id(0)

        @pl.when(step == 0)
        def _():
            near = sc[0]
            own_at = pl.multiple_of(near * rows, rows)
            partner_at = pl.multiple_of((1 - near) * rows, rows)
            x_ref[pl.ds(own_at, rows), :] = own_ref[...]
            x_ref[pl.ds(partner_at, rows), :] = partner_ref[:rows, :]
            hot_ref[:, pl.ds(own_at, rows)] = mark(docs_ref[...], rows)
            docs = partner_ref[rows : rows + 1, :rows].astype(F32)
            hot_ref[:, pl.ds(partner_at, rows)] = mark(docs, rows)
            for j in range(GROUPS):
                at = pl.ds(pl.multiple_of((sc[1] ^ j) * BLOCK, 16), BLOCK)
                for kind in range(3):
                    part = slice(kind * QUARTER, (kind + 1) * QUARTER)
                    both = [weight_refs[j % 2][j // 2, top : top + BLOCK, part] for top in (0, tall)]
                    both = [half.astype(F32) for half in both]
                    both = jnp.concatenate(both, axis=1).astype(BF)
                    for p in range(3):
                        to = (3 * p + kind) * PAIR
                        w_ref[at, to : to + PAIR] = both[:, p * PAIR : (p + 1) * PAIR]
            hot = hot_ref[...]
            mask_ref[...] = (dot_tn(hot[:, :rows], hot) - 1.0) * MASKED
            vectors = jnp.zeros((LABELS, D), F32)
            for j in range(GROUPS):
                block = sc[1] ^ j
                line = weight_refs[j % 2][j // 2, BLOCK:tall, :128].astype(F32)
                table = jnp.where(lax.broadcasted_iota(jnp.int32, line.shape, 1) < BLOCK, line, 0.0)
                table = jnp.concatenate([table, jnp.zeros((LABELS, D - 128), F32)], axis=1)
                vectors = vectors + pltpu.roll(table, block * BLOCK, 1)
                quarter = block // 2
                for k in range(2):

                    @pl.when(quarter == sc[2] ^ (2 * k))
                    def _():
                        for c in range(SHARE):
                            to = pl.multiple_of((block % 2) * (HID // 2) + k * HID + c * 128, 128)
                            value = jnp.broadcast_to(line[VECS + c : VECS + c + 1], (VECS, 128))
                            hidden_ref[:, pl.ds(to, 128)] = value

            vec_ref[...] = vectors[:VECS]
            lanes = lax.broadcasted_iota(jnp.int32, (VECS, HALF), 1)
            low = pltpu.roll(vectors[:VECS], turn(-sc[2]), 1)[:, :HALF]
            high = pltpu.roll(vectors[:VECS], turn(1 - (sc[2] ^ 2)), 1)[:, :HALF]
            bias_ref[...] = jnp.where(lanes < QUARTER, low, high)
            log_ref[...] = jnp.zeros_like(log_ref)

        at = pl.multiple_of(step * 3 * PAIR, PAIR)
        both = dot(x_ref[...], w_ref[:, pl.ds(at, 3 * PAIR)])
        bias = bias_ref[:, pl.ds(pl.multiple_of(step * PAIR, PAIR), PAIR)]
        query = (both[:, :PAIR] + bias[0:1]).astype(BF)
        key = both[:, PAIR : 2 * PAIR].astype(BF)
        value = (both[:, 2 * PAIR :] + bias[1:2]).astype(BF)
        q_ref[...] = query
        k_ref[...] = key
        v_ref[...] = value
        ctx_ref[...], scaled_ref[...] = attend(query[:rows], key, value, mask_ref[...], log_ref, step)

    operands = [own, partner, own_docs, *pieces]
    in_specs = [whole(o.shape) for o in operands]
    outs = [
        struct((base, HALF), BF),
        struct((base, HALF), BF),
        struct((base, HALF), BF),
        struct((rows, HALF), BF),
        struct((base, D), BF),
        struct((D, 3 * HALF), BF),
        struct((LABELS, base), BF),
        struct((VECS, D), F32),
        struct((VECS, 2 * HID), F32),
        struct((VECS, HALF), F32),
        struct((VECS, rows), F32),
        struct((rows, HALF), F32),
    ]
    out_specs = [column(base)] * 3 + [column(rows)] + [whole(o.shape) for o in outs[4:-1]] + [column(rows)]
    return call(
        "attend_pair",
        body,
        scalars,
        operands,
        in_specs,
        outs,
        out_specs,
        (HALF // PAIR,),
        [pltpu.VMEM((rows, base), F32)],
        micros=8,
    )


def attend_halo(scalars, halo_near, halo_far, weight, bias, hot, query, key, value, rows):
    def body(sc, near_ref, far_ref, w_ref, bias_ref, hot_ref, q_ref, k_ref, v_ref, *refs):
        halo_refs, (ctx_ref, scaled_ref, all_ref, log_ref, x_ref, mask_ref) = refs[:3], refs[3:]

        @pl.when(pl.program_id(0) == 0)
        def _():
            all_ref[:, : 2 * rows] = hot_ref[...]

            def halo(ref):
                x_ref[...] = ref[:rows, :]
                all_ref[:, 2 * rows :] = mark(ref[rows : rows + 1, :rows].astype(F32), rows)

            pl.when(sc[0] == 1)(lambda: halo(near_ref))
            pl.when(sc[0] == 0)(lambda: halo(far_ref))
            mask_ref[...] = (dot_tn(all_ref[:, rows : 2 * rows], all_ref[...]) - 1.0) * MASKED
            log_ref[...] = jnp.zeros_like(log_ref)

        both = dot(x_ref[...], w_ref[...])
        parts = [
            (both[:, :PAIR] + bias_ref[0:1, :]).astype(BF),
            both[:, PAIR : 2 * PAIR].astype(BF),
            (both[:, 2 * PAIR :] + bias_ref[1:2, :]).astype(BF),
        ]
        for ref, part in zip(halo_refs, parts):
            ref[...] = part
        keys = jnp.concatenate([k_ref[...], parts[1]], axis=0)
        values = jnp.concatenate([v_ref[...], parts[2]], axis=0)
        ctx_ref[...], scaled_ref[...] = attend(
            q_ref[rows:, :], keys, values, mask_ref[...], log_ref, pl.program_id(0)
        )

    operands = [halo_near, halo_far, weight, bias, hot, query, key, value]
    in_specs = [whole(o.shape) for o in operands]
    in_specs[2] = pl.BlockSpec((D, 3 * PAIR), lambda p, _: (0, p))
    in_specs[3] = column(VECS)
    in_specs[5:] = [column(2 * rows)] * 3
    outs = [struct((rows, HALF), BF)] * 4 + [struct((rows, HALF), F32)]
    outs += [struct((LABELS, 3 * rows), BF), struct((VECS, rows), F32)]
    return call(
        "attend_halo",
        body,
        scalars,
        operands,
        in_specs,
        outs,
        [column(rows)] * 5 + [whole((LABELS, 3 * rows)), whole((VECS, rows))],
        (HALF // PAIR,),
        [pltpu.VMEM((rows, D), BF), pltpu.VMEM((rows, 3 * rows), F32)],
        micros=6,
    )


def feed_forward(scalars, block, ctx_mine, ctx_partner, x, vecs, up_bias, weights, rows):
    count = len(weights)
    fresh = len(weights[0].shape) == 3

    def body(sc, mine_ref, partner_ref, x_ref, vec_ref, bias_ref, *refs):
        weight_refs, refs = refs[:count], refs[count:]
        (norm_ref, inv_ref, first_ref, gate_ref, active_ref, part_ref), refs = refs[:6], refs[6:]
        if fresh:
            up_ref, down_ref, out_ref, other_ref, full_ref = refs
            for k in range(2):
                at, to = 2 * k * HID, slice(k * HID, (k + 1) * HID)
                place(up_ref, weight_refs, sc[1], slice(at, at + HID), to)
                place(down_ref, weight_refs, sc[1], slice(at + HID, at + 2 * HID), to)
            place(full_ref, weight_refs, sc[1], slice(4 * HID, 4 * HID + D), slice(None))
            for ref, flip in ((out_ref, 0), (other_ref, 1)):
                for k in range(2):
                    at = pl.multiple_of((sc[2] ^ flip ^ (2 * k)) * QUARTER, 16)
                    ref[k * QUARTER : (k + 1) * QUARTER, :] = full_ref[pl.ds(at, QUARTER), :]
        else:
            up_ref, down_ref, out_ref, other_ref = weight_refs

        attention = dot(mine_ref[...], out_ref[...]) + dot(partner_ref[...], other_ref[...])
        total = x_ref[...].astype(F32) + (attention + vec_ref[2:3, :])
        center = total - jnp.mean(total, axis=-1, keepdims=True)
        inverse = lax.rsqrt(jnp.mean(center * center, axis=-1, keepdims=True) + EPS)
        normed = center * inverse
        norm_ref[...] = normed
        inv_ref[...] = jnp.broadcast_to(inverse, (rows, 128))
        first = (normed * vec_ref[3:4, :] + vec_ref[4:5, :]).astype(BF)
        first_ref[...] = first
        gate = dot(first, up_ref[...]) + bias_ref[0:1, :]
        gate_ref[...] = gate
        active = (gate * (1.0 + lax.erf(gate * ROOT_HALF)) * 0.5).astype(BF)
        active_ref[...] = active
        part_ref[...] = dot_nt(active, down_ref[...]).astype(BF)

    operands = [ctx_mine, ctx_partner, x, vecs, up_bias, *weights]
    in_specs = [whole(o.shape) for o in operands]
    in_specs[2] = pl.BlockSpec((rows, D), lambda *_: (block, 0))
    outs = [
        struct((rows, D), F32),
        struct((rows, 128), F32),
        struct((rows, D), BF),
        struct((rows, 2 * HID), F32),
        struct((rows, 2 * HID), BF),
        struct((rows, D), BF),
    ]
    scratch = []
    if fresh:
        outs += [struct((D, 2 * HID), BF)] * 2 + [struct((HALF, D), BF)] * 2
        scratch = [pltpu.VMEM((D, D), BF)]
    results = call(
        "feed_forward",
        body,
        scalars,
        operands,
        in_specs,
        outs,
        [whole(o.shape) for o in outs],
        (1,),
        scratch,
        micros=6,
    )
    return results[:6], (results[6:] if fresh else weights)


def gelu_slope(scalars, gate):
    rows = gate.shape[0] // 2

    def body(_, gate_ref, slope_ref):
        gate_here = gate_ref[...]
        bell = jnp.exp(gate_here * gate_here * -0.5) * ROOT_TWO_PI
        slope_ref[...] = 0.5 * (1.0 + lax.erf(gate_here * ROOT_HALF)) + gate_here * bell

    spec = pl.BlockSpec((rows, gate.shape[1]), lambda r, _: (r, 0))
    return call(
        "gelu_slope", body, scalars, [gate], [spec], [struct(gate.shape, F32)], [spec], (2,), micros=3
    )[0]


def second_norm(scalars, block, part, received, normed, slope, cotangent, vecs, up, down, earlier, rows):
    def body(sc, part_ref, recv_ref, norm_ref, slope_ref, cot_ref, other_ref, vec_ref, up_ref, down_ref, *refs):
        old, refs = refs[: len(earlier)], refs[len(earlier) :]
        (total_grad_ref, branch_grad_ref, gate_grad_ref, first_part_ref, out_ref, sums_ref, bias_ref) = refs
        mine = sc[0] == block
        first = norm_ref[...] * vec_ref[3:4, :] + vec_ref[4:5, :]
        branch = part_ref[...].astype(F32) + recv_ref[...].astype(F32) + vec_ref[5:6, :]
        total = first + branch
        center = total - jnp.mean(total, axis=-1, keepdims=True)
        inverse = lax.rsqrt(jnp.mean(center * center, axis=-1, keepdims=True) + EPS)
        here = center * inverse
        upstream = jnp.where(mine, cot_ref[...].astype(F32), other_ref[...].astype(F32))
        scaled = upstream * vec_ref[6:7, :]
        inner = (
            scaled
            - jnp.mean(scaled, axis=-1, keepdims=True)
            - here * jnp.mean(scaled * here, axis=-1, keepdims=True)
        )
        total_grad = inner * inverse
        total_grad_ref[...] = total_grad
        branch_grad = total_grad.astype(BF)
        branch_grad_ref[...] = branch_grad
        gate_grad = (dot(branch_grad, down_ref[...]) * slope_ref[...]).astype(BF)
        gate_grad_ref[...] = gate_grad
        hidden = jnp.broadcast_to(jnp.sum(gate_grad.astype(F32), axis=0, keepdims=True), (8, 2 * HID))
        bias_ref[...] = hidden + old[2][...] if old else hidden
        first_part_ref[...] = dot_nt(gate_grad, up_ref[...]).astype(BF)

        @pl.when(mine)
        def _():
            out_ref[...] = (here * vec_ref[6:7, :] + vec_ref[7:8, :]).astype(BF)
            sums_ref[...] = jnp.zeros_like(sums_ref)
            sums_ref[0:1, :] = jnp.sum(upstream * here, axis=0, keepdims=True)
            sums_ref[1:2, :] = jnp.sum(upstream, axis=0, keepdims=True)
            sums_ref[2:3, :] = jnp.sum(branch_grad.astype(F32), axis=0, keepdims=True)

        if old:

            @pl.when(jnp.logical_not(mine))
            def _():
                out_ref[...] = old[0][...]
                sums_ref[...] = old[1][...]

        else:

            @pl.when(jnp.logical_not(mine))
            def _():
                out_ref[...] = jnp.zeros_like(out_ref)
                sums_ref[...] = jnp.zeros_like(sums_ref)

    operands = [part, received, normed, slope, *cotangent, vecs, up, down, *earlier]
    outs = [
        struct((rows, D), F32),
        struct((rows, D), BF),
        struct((rows, 2 * HID), BF),
        struct((rows, D), BF),
        struct((rows, D), BF),
        struct((8, D), F32),
        struct((8, 2 * HID), F32),
    ]
    results = call(
        "second_norm",
        body,
        scalars,
        operands,
        [whole(o.shape) for o in operands],
        outs,
        [whole(o.shape) for o in outs],
        (1,),
        micros=5,
    )
    return results[:4], results[4:]


def split_outs(width):
    return [struct((GROUPS // 2, BLOCK, width), BF)] * 2


def feed_forward_grads(scalars, blocks, rows):
    def body(sc, *refs):
        keep_ref, send_ref, result_ref = refs[-3:]
        step = pl.program_id(0)

        @pl.when(step % 2 == 0)
        def _():
            result_ref[...] = dot_tn(refs[0][...], refs[1][...]) + dot_tn(refs[4][...], refs[5][...])

        @pl.when(step % 2 == 1)
        def _():
            result_ref[...] = dot_tn(refs[2][...], refs[3][...]) + dot_tn(refs[6][...], refs[7][...])

        split_rows(result_ref, sc[1], keep_ref, send_ref)

    half = pl.BlockSpec((rows, HID), lambda c, _: (0, c // 2))
    outs = split_outs(4 * HID)
    out_specs = [pl.BlockSpec((GROUPS // 2, BLOCK, HID), lambda c, _: (0, 0, c))] * 2
    return call(
        "feed_forward_grads",
        body,
        scalars,
        [value for block in blocks for value in block],
        [whole((rows, D)), half] * 4,
        outs,
        out_specs,
        (4,),
        [pltpu.VMEM((D, HID), F32)],
        micros=8,
    )


def first_norm(
    scalars, block, part, received, total_grad, normed, inverse, vecs, out_weight, ctx, logs, earlier, rows
):
    def body(sc, part_ref, recv_ref, grad_ref, norm_ref, inv_ref, vec_ref, weight_ref, ctx_ref, log_ref, *refs):
        old, refs = refs[: len(earlier)], refs[len(earlier) :]
        attention_ref, context_ref, inner_ref, own_ref, sums_ref = refs[:5]
        mine = sc[0] == block
        upstream = grad_ref[...] + part_ref[...].astype(F32) + recv_ref[...].astype(F32)
        here = norm_ref[...]
        scaled = upstream * vec_ref[3:4, :]
        inner = (
            scaled
            - jnp.mean(scaled, axis=-1, keepdims=True)
            - here * jnp.mean(scaled * here, axis=-1, keepdims=True)
        )
        total = inner * inv_ref[:, :1]
        attention = total.astype(BF)
        attention_ref[...] = attention
        context = dot_nt(attention, weight_ref[...]).astype(BF)
        context_ref[...] = context
        lane = lax.broadcasted_iota(jnp.int32, (VECS, HALF), 1) // HEAD_DIM
        picks = jnp.where(lane == lax.broadcasted_iota(jnp.int32, (VECS, HALF), 0), 1.0, 0.0)
        inner = lax.dot_general(
            picks,
            context.astype(F32) * ctx_ref[...],
            (((1,), (1,)), ((), ())),
            precision=lax.Precision.HIGHEST,
            preferred_element_type=F32,
        )
        inner_ref[...] = inner
        if block == 1:
            send_ref = refs[5]
            turned = jnp.concatenate([weight_ref[QUARTER:, :], weight_ref[:QUARTER, :]], axis=0)
            send_ref[:rows, :] = dot_nt(attention, turned).astype(BF)
            rest = jnp.concatenate([log_ref[...], inner], axis=0)
            send_ref[rows:, :] = jnp.zeros((3 * LABELS, HALF), BF)
            for k in range(3):
                at = rows + k * LABELS
                piece = rest.astype(BF)
                send_ref[at : at + LABELS, :rows] = piece
                rest = rest - piece.astype(F32)

        @pl.when(mine)
        def _():
            own_ref[...] = total
            sums_ref[...] = jnp.zeros_like(sums_ref)
            sums_ref[0:1, :] = jnp.sum(upstream * here, axis=0, keepdims=True)
            sums_ref[1:2, :] = jnp.sum(upstream, axis=0, keepdims=True)
            sums_ref[2:3, :] = jnp.sum(attention.astype(F32), axis=0, keepdims=True)

        @pl.when(jnp.logical_not(mine))
        def _():
            own_ref[...] = old[0][...] if old else jnp.zeros_like(own_ref)
            sums_ref[...] = old[1][...] if old else jnp.zeros_like(sums_ref)

    operands = [part, received, total_grad, normed, inverse, vecs, out_weight, ctx, logs, *earlier]
    outs = [
        struct((rows, D), BF),
        struct((rows, HALF), BF),
        struct((VECS, rows), F32),
        struct((rows, D), F32),
        struct((8, D), F32),
        struct((rows + 3 * LABELS, HALF), BF),
    ][: 6 if block == 1 else 5]
    return call(
        "first_norm",
        body,
        scalars,
        operands,
        [whole(o.shape) for o in operands],
        outs,
        [whole(o.shape) for o in outs],
        (1,),
        micros=3,
    )


def halves(value):
    high = value.astype(BF).astype(F32)
    return jnp.concatenate([high, value - high], axis=0).astype(BF)


def whole_of(table):
    return table[:LABELS].astype(F32) + table[LABELS : 2 * LABELS].astype(F32)


def output_grads(scalars, blocks, small, small_side):
    def body(sc, *refs):
        small_ref, side_ref, keep_ref, send_ref, result_ref = refs[-5:]
        grads = []
        for ref in (refs[2], refs[5]):
            turned = pltpu.roll(ref[...].astype(F32), turn(-sc[2]), 1)
            turned = [turned[:, :QUARTER], turned[:, HALF : HALF + QUARTER]]
            grads.append(jnp.concatenate(turned, axis=1).astype(BF))
        for side in range(2):
            part = dot_tn(refs[side][...], grads[0]) + dot_tn(refs[3 + side][...], grads[1])
            for k in range(2):
                at = pl.multiple_of((sc[2] ^ side ^ (2 * k)) * QUARTER, 16)
                result_ref[pl.ds(at, QUARTER), :] = part[k * QUARTER : (k + 1) * QUARTER, :]
        for j in range(GROUPS):
            target = (keep_ref, send_ref)[j % 2]
            block = sc[1] ^ j
            rows = pl.ds(pl.multiple_of(block * BLOCK, 16), BLOCK)
            target[j // 2, :, :HALF] = result_ref[rows, :].astype(BF)
            target[j // 2, :, HALF:] = jnp.zeros((BLOCK, 128), BF)
            target[j // 2, : 2 * LABELS, HALF:] = halves(small_ref[block] + side_ref[block])

    outs = [struct((GROUPS // 2, BLOCK, HALF + 128), BF)] * 2
    operands = [value for block in blocks for value in block] + [small, small_side]
    return call(
        "output_grads",
        body,
        scalars,
        operands,
        [whole(o.shape) for o in operands],
        outs,
        [whole(o.shape) for o in outs],
        (1,),
        [pltpu.VMEM((D, HALF), F32)],
        micros=4,
    )


def attend_backward(scalars, pair, halo, grad_blocks, logs, inners, hot, weight, rows):
    base = 3 * rows
    steps = HALF // PAIR

    def body(sc, *refs):
        pair_refs, halo_refs, refs = refs[:3], refs[3:6], refs[6:]
        far_ref, near_ref, halo_ref, stats_ref, *refs = refs
        log_refs, inner_refs, (hot_ref, w_ref, *refs) = refs[:2], refs[2:4], refs[4:]
        out_ref, keep_ref, send_ref, sums_ref, mask_ref, key_ref, value_ref, acc_ref, q_ref, k_ref, v_ref, line_ref = refs
        for target, first_part, last_part in zip((q_ref, k_ref, v_ref), pair_refs, halo_refs):
            target[: 2 * rows, :] = first_part[...]
            target[2 * rows :, :] = last_part[...]
        step = pl.program_id(0)

        @pl.when(step == 0)
        def _():
            mask_ref[...] = (dot_tn(hot_ref[...], hot_ref[...]) - 1.0) * MASKED
            lines = jnp.zeros((LABELS, rows), F32)
            for k in range(3):
                at = rows + k * LABELS
                lines = lines + stats_ref[at : at + LABELS, :rows].astype(F32)
            line_ref[...] = lines

        key_ref[...] = jnp.zeros_like(key_ref)
        value_ref[...] = jnp.zeros_like(value_ref)
        lane = lax.broadcasted_iota(jnp.int32, (1, PAIR), 1)
        query_grads = [jnp.zeros((PAIR, rows), F32), jnp.zeros((PAIR, rows), F32)]
        for head in range(2):
            part = jnp.where((lane // HEAD_DIM) == head, 1.0, 0.0)
            key_turned = (k_ref[...].astype(F32) * part).T.astype(BF)
            line = 2 * step + head
            other = lax.rem(line + 3, 6)
            lines = [(log_refs[k][pl.ds(line, 1), :], inner_refs[k][pl.ds(line, 1), :]) for k in range(2)]
            lines += [(line_ref[pl.ds(other, 1), :], line_ref[pl.ds(other + VECS, 1), :])]
            for index, (low, high) in enumerate(((0, 2 * rows), (0, base), (rows, 2 * rows))):
                start = index * rows
                mine = (q_ref[start : start + rows].astype(F32) * (part * HEAD_DIM**-0.5)).astype(BF)
                grads = (far_ref, near_ref, halo_ref)[index][:rows, :]
                grads = (grads.astype(F32) * part).astype(BF)
                scores = dot_nt(k_ref[low:high], mine) + mask_ref[low:high, start : start + rows]
                log_total, inner = lines[index]
                probs = jnp.exp(scores - log_total)
                pulled = dot_nt(v_ref[low:high], grads)
                score_grads = (probs * (pulled - inner)).astype(BF)
                top = min(high, 2 * rows)
                span = top - low
                value_ref[low:top, :] += dot(probs[:span].astype(BF), grads)
                key_ref[low:top, :] += dot(score_grads[:span], mine)
                if index < 2:
                    query_grads[index] = query_grads[index] + dot(key_turned[:, low:high], score_grads)
        for index in range(2):
            turned = (query_grads[index] * HEAD_DIM**-0.5).T.astype(BF)
            out_ref[index * rows : (index + 1) * rows, :PAIR] = turned
        out_ref[:, PAIR : 2 * PAIR] = key_ref[...].astype(BF)
        out_ref[:, 2 * PAIR :] = value_ref[...].astype(BF)
        sums = jnp.sum(out_ref[...].astype(F32), axis=0, keepdims=True)
        sums_ref[...] = jnp.broadcast_to(sums, (8, 3 * PAIR))
        product = dot_nt(out_ref[...], w_ref[...])

        @pl.when(step == 0)
        def _():
            acc_ref[...] = product

        @pl.when(step > 0)
        def _():
            acc_ref[...] += product

        @pl.when(step == steps - 1)
        def _():
            near = sc[0]
            keep_ref[...] = acc_ref[pl.ds(pl.multiple_of(near * rows, rows), rows), :]
            other = acc_ref[pl.ds(pl.multiple_of((1 - near) * rows, rows), rows), :]
            send_ref[...] = other.astype(BF)

    stats = grad_blocks[2]
    operands = [*pair, *halo, *grad_blocks, stats, *logs, *inners, hot, weight]
    in_specs = [column(2 * rows)] * 3 + [column(rows)] * 5 + [column(stats.shape[0])]
    in_specs += [whole(o.shape) for o in operands[9:15]]
    in_specs += [pl.BlockSpec((D, 3 * PAIR), lambda p, _: (0, p))]
    outs = [struct((2 * rows, 3 * HALF), BF), struct((rows, D), F32), struct((rows, D), BF)]
    outs += [struct((8, 3 * HALF), F32)]
    out_specs = [
        pl.BlockSpec((2 * rows, 3 * PAIR), lambda p, _: (0, p)),
        whole((rows, D)),
        whole((rows, D)),
        pl.BlockSpec((8, 3 * PAIR), lambda p, _: (0, p)),
    ]
    scratch = [
        pltpu.VMEM((base, base), F32),
        pltpu.VMEM((2 * rows, PAIR), F32),
        pltpu.VMEM((2 * rows, PAIR), F32),
        pltpu.VMEM((2 * rows, D), F32),
    ] + [pltpu.VMEM((base, PAIR), BF)] * 3
    scratch += [pltpu.VMEM((LABELS, rows), F32)]
    return call(
        "attend_backward",
        body,
        scalars,
        operands,
        in_specs,
        outs,
        out_specs,
        (steps,),
        scratch,
        micros=MICROS,
    )


def projection_grads(scalars, x, grads, rows):
    tall = 2 * rows

    def body(sc, x_ref, grad_ref, *refs):
        result_ref = refs[-1]
        result_ref[...] = dot_tn(x_ref[...], grad_ref[...])
        split_rows(result_ref, sc[1], refs[0], refs[1])

    outs = split_outs(3 * HALF)
    out_specs = [pl.BlockSpec((GROUPS // 2, BLOCK, 3 * PAIR), lambda p, _: (0, 0, p))] * 2
    return call(
        "projection_grads",
        body,
        scalars,
        [x, grads],
        [pl.BlockSpec((tall, D), lambda p, _: (0, 0)), pl.BlockSpec((tall, 3 * PAIR), lambda p, _: (0, p))],
        outs,
        out_specs,
        (HALF // PAIR,),
        [pltpu.VMEM((D, 3 * PAIR), F32)],
        micros=5,
    )


def combine(scalars, keep, received):
    count, rows, width = keep.shape
    chunk = width // 3

    def body(_, keep_ref, recv_ref, *refs):
        for k in range(count):
            total = keep_ref[k].astype(F32) + recv_ref[k].astype(F32)
            refs[k][...] = total.astype(refs[k].dtype)

    block = pl.BlockSpec((count, rows, chunk), lambda c, _: (0, 0, c))
    outs = [struct((rows, width), F32)] + [struct((rows, width), BF)] * (count - 1)
    spec = pl.BlockSpec((rows, chunk), lambda c, _: (0, c))
    return list(call(
        "combine",
        body, scalars, [keep, received], [block, block], outs, [spec] * count, (3,)))


def combine_both(scalars, keep, received, out_keep, out_received):
    count, rows, wide = keep.shape
    last = wide + HALF

    def body(_, keep_ref, recv_ref, out_keep_ref, out_recv_ref, *refs):
        for k in range(count):
            kind = refs[k].dtype
            refs[k][:, :wide] = (keep_ref[k].astype(F32) + recv_ref[k].astype(F32)).astype(kind)
            total = out_keep_ref[k, :, :HALF].astype(F32) + out_recv_ref[k, :, :HALF].astype(F32)
            refs[k][:, wide:last] = total.astype(kind)
            small = whole_of(out_keep_ref[k, :, HALF:]) + whole_of(out_recv_ref[k, :, HALF:])
            refs[k][:, last:] = jnp.zeros((rows, 128), kind)
            refs[k][: 2 * LABELS, last:] = halves(small).astype(kind)

    outs = [struct((rows, last + 128), F32)] + [struct((rows, last + 128), BF)] * (count - 1)
    return simple("combine_both", body, scalars, [keep, received, out_keep, out_received], outs, 2)


def total_feed(scalars, sums):
    rows = sums[0].shape[0]

    def body(_, *refs):
        keep_ref, send_ref = refs[-2:]
        total = refs[0][...]
        for ref in refs[1:-2]:
            total = total + ref[...].astype(F32)
        keep_ref[...] = total[:, : 2 * HID]
        send_ref[:, : 2 * HID] = total[:, 2 * HID :].astype(BF)
        send_ref[:, 2 * HID :] = jnp.zeros((rows, 256), BF)

    outs = [struct((rows, 2 * HID), F32), struct((rows, 2 * HID + 256), BF)]
    return simple("total_feed", body, scalars, sums, outs, 2)


def total_projection(scalars, sums):
    rows, width = sums[0].shape
    wide = 3 * HALF
    last = wide + HALF

    def body(_, *refs):
        keep_ref, send_ref = refs[-2:]
        total = refs[0][:, :last]
        for ref in refs[1:-2]:
            total = total + ref[:, :last].astype(F32)
        near, far = [], []
        for kind in range(3):
            both = [total[:, (3 * p + kind) * PAIR : (3 * p + kind + 1) * PAIR] for p in range(3)]
            both = jnp.concatenate(both, axis=1)
            near.append(both[:, :QUARTER])
            far.append(both[:, QUARTER:])
        near.append(total[:, wide : wide + QUARTER])
        far.append(total[:, wide + QUARTER : last])
        keep_ref[:, :D] = jnp.concatenate(near, axis=1)
        send_ref[:, :D] = jnp.concatenate(far, axis=1).astype(BF)
        if width > last:
            small = jnp.zeros((LABELS, 128), F32)
            for ref in refs[:-2]:
                small = small + whole_of(ref[:, last:])
            keep_ref[:, D:] = jnp.zeros((rows, 128), F32)
            send_ref[:, D:] = jnp.zeros((rows, 128), BF)
            keep_ref[:LABELS, D:] = small
            send_ref[: 2 * LABELS, D:] = halves(small)

    width_out = D + width - last
    outs = [struct((rows, width_out), F32), struct((rows, width_out), BF)]
    return simple("total_projection", body, scalars, sums, outs, 2)


def finish_feed(scalars, keep, received):
    rows = keep.shape[0]

    def body(_, keep_ref, recv_ref, up_ref, down_ref):
        up_ref[...] = keep_ref[:, :HID] + recv_ref[:, :HID].astype(F32)
        down_ref[...] = keep_ref[:, HID:] + recv_ref[:, HID : 2 * HID].astype(F32)

    outs = [struct((rows, HID), F32)] * 2
    return simple("finish_feed", body, scalars, [keep, received], outs, FEED_MICROS)


def finish_projection(scalars, keep, received):
    rows, width = keep.shape

    def body(_, keep_ref, recv_ref, *refs):
        total = keep_ref[:, :D] + recv_ref[:, :D].astype(F32)
        for k in range(4):
            refs[k][...] = total[:, k * QUARTER : (k + 1) * QUARTER]
        if width > D:
            small = keep_ref[:LABELS, D:] + whole_of(recv_ref[:, D:])
            for k in range(VECS):
                refs[4 + k][...] = small[k, :BLOCK]
            for k in range(SHARE):
                refs[4 + VECS][k * 128 : (k + 1) * 128] = small[VECS + k]

    outs = [struct((rows, QUARTER), F32)] * 4
    if width > D:
        outs += [struct((BLOCK,), F32)] * VECS + [struct((FF // GROUPS,), F32)]
    return simple("finish_projection", body, scalars, [keep, received], outs)


def small_sums(scalars, sums_one, sums_two, sums_hidden, sums_projection):
    def body(sc, one_ref, two_ref, hidden_ref, projection_ref, out_ref, wide_ref, tall_ref):
        out_ref[...] = jnp.zeros_like(out_ref)
        lanes = lax.broadcasted_iota(jnp.int32, (1, D), 1)
        near, far = lanes < QUARTER, (lanes >= QUARTER) & (lanes < HALF)
        for row, kind in ((0, 0), (1, 2)):
            line = jnp.concatenate(
                [
                    projection_ref[0:1, (3 * p + kind) * PAIR : (3 * p + kind + 1) * PAIR]
                    for p in range(3)
                ]
                + [jnp.zeros((1, HALF), F32)],
                axis=1,
            )
            low = pltpu.roll(jnp.broadcast_to(jnp.where(near, line, 0.0), (8, D)), sc[2] * QUARTER, 1)
            high = jnp.broadcast_to(jnp.where(far, line, 0.0), (8, D))
            high = pltpu.roll(high, turn((sc[2] ^ 2) - 1), 1)
            wide_ref[row : row + 1, :] = (low + high)[0:1]
        wide_ref[2:3, :] = one_ref[2:3, :]
        wide_ref[3:5, :] = one_ref[0:2, :]
        wide_ref[5:6, :] = two_ref[2:3, :]
        wide_ref[6:8, :] = two_ref[0:2, :]
        tall_ref[...] = jnp.zeros_like(tall_ref)
        for k in range(2):
            to = pl.multiple_of((sc[2] ^ (2 * k)) * HID, 128)
            tall_ref[0:1, pl.ds(to, HID)] = hidden_ref[0:1, k * HID : (k + 1) * HID]
        share = FF // GROUPS
        for d in range(GROUPS):
            out_ref[d, :VECS, :BLOCK] = wide_ref[:, d * BLOCK : (d + 1) * BLOCK]
            for c in range(share // 128):
                at = d * share + c * 128
                out_ref[d, VECS + c : VECS + c + 1, :] = tall_ref[0:1, at : at + 128]

    operands = [sums_one, sums_two, sums_hidden, sums_projection]
    shape = (GROUPS, LABELS, 128)
    return call(
        "small_sums",
        body,
        scalars,
        operands,
        [whole(o.shape) for o in operands],
        [struct(shape, F32)],
        [whole(shape)],
        (1,),
        [pltpu.VMEM((VECS, D), F32), pltpu.VMEM((8, FF), F32)],
    )[0]


def per_device(
    tokens,
    segments,
    query_weight,
    key_weight,
    value_weight,
    output_weight,
    query_bias,
    value_bias,
    output_bias,
    first_gain,
    first_shift,
    up_weight,
    up_bias,
    down_weight,
    down_bias,
    second_gain,
    second_shift,
    cotangent,
):
    seq_count = lax.axis_size("seq")
    count = lax.axis_size("dp")
    place_z = lax.axis_index("seq")
    assert seq_count == 4
    direct = count == GROUPS
    rows = tokens.shape[1]
    piece_rows = query_weight.shape[0]
    near = (place_z == 1) | (place_z == 2)
    base = lax.axis_index("dp") if direct else 0
    scalars = jnp.stack([near, base, place_z]).astype(jnp.int32)

    own = tokens[0]
    cot_own = cotangent[0]
    lines = [
        query_bias,
        value_bias,
        output_bias,
        first_gain,
        first_shift,
        down_bias,
        second_gain,
        second_shift,
    ]
    lines = lines if direct else []
    first_send, mine, wide, labelled, own_docs = pack_inputs(
        scalars,
        [query_weight, key_weight, value_weight, output_weight],
        own,
        segments,
        up_weight,
        down_weight.T,
        lines,
        up_bias,
    )
    arrived = swap(first_send, "seq", 2)
    side = swap(output_weight, "seq", 1)
    if direct:
        mine_chip = [mine, swap(mine, "dp", 2), swap(mine, "dp", 4)]
        wide_last = swap(wide, "dp", 6)
        labelled, side, wide_last, mine_chip, arrived = together(
            labelled, side, wide_last, mine_chip, arrived
        )
    else:
        arrived, labelled, side = together(arrived, labelled, side)
    narrow_far, both, partner_send = split_arrived(scalars, arrived, mine, labelled)
    partner = swap(partner_send, "seq", 1)
    halo_near = lax.ppermute(labelled, "seq", [(1, 2), (2, 1)])
    if direct:
        far_chip = [narrow_far, swap(narrow_far, "dp", 2), swap(narrow_far, "dp", 4)]
        both_far = swap(both, "dp", 6)
        mine_chip, cot_own, far_chip, both_far, partner, halo_near = together(
            mine_chip, cot_own, far_chip, both_far, partner, halo_near
        )
        stacked = stack_narrow(scalars, mine_chip, far_chip, both_far)
        pieces = [stacked, swap(stacked, "dp", 1)]
        feed_chip = chip_pieces(pack_feed(scalars, first_send, arrived, side, partner))
    halo_far = lax.ppermute(halo_near, "seq", [(1, 0), (2, 3)])
    if not direct:
        vectors = jnp.stack(
            [
                query_bias,
                value_bias,
                output_bias,
                first_gain,
                first_shift,
                down_bias,
                second_gain,
                second_shift,
            ]
        )
        lines = lax.all_gather(vectors, "dp", axis=1, tiled=True).reshape(VECS, GROUPS, BLOCK)
        lines = jnp.pad(lines, ((0, 0), (0, 0), (0, 128 - BLOCK)))
        tall = lax.all_gather(up_bias, "dp", axis=0, tiled=True).reshape(GROUPS, SHARE, 128).transpose(1, 0, 2)
        lines = jnp.concatenate([lines, tall], axis=0)
        lines = jnp.pad(lines, ((0, LABELS - VECS - SHARE), (0, 0), (0, 3 * QUARTER - 128)))
        lines = lines.transpose(1, 0, 2)
        gathered = gather_rows(mine)
        pieces = [
            jnp.concatenate([half[:, :, 2 * HID :], lines[k::2], far], axis=1)
            for k, (half, far) in enumerate(zip(gathered, gather_rows(narrow_far)))
        ]
        last = swap(arrived[:, 3 * QUARTER : D], "seq", 1)
        feed = gather_rows(pack_feed(scalars, first_send, arrived, side, last))
        weights = [
            jnp.concatenate([half[:, :, : 2 * HID], far], axis=2) for half, far in zip(gathered, feed)
        ]

    def rows_of(keep, send):
        return jnp.stack([keep, send], axis=1).reshape(GROUPS, -1, keep.shape[2]).astype(F32)

    def spread(sums):
        return [sums[0]] + [swap(sums[k], "dp", 2 * k) for k in range(1, len(sums))]

    def scattered(table):
        return [lax.psum_scatter(table, "dp", scatter_dimension=0, tiled=True)]

    *pair, ctx_far, x, weight, hot, vecs, hidden_bias, bias, log_far, scaled_far = attend_pair(
        scalars, own, partner, own_docs, pieces, rows
    )
    if direct:
        pair, ctx_far, cot_own, halo_far = together(pair, ctx_far, cot_own, halo_far)
    *halo, ctx_near, scaled_near, hot, log_near = attend_halo(scalars, halo_near, halo_far, weight, bias, hot, *pair, rows)
    ctx_mine = [ctx_far, ctx_near]
    ctx_partner = [swap(ctx_far, "seq", 1), None]
    if direct:
        ctx_mine[1], ctx_partner[0], wide_last, feed_chip = together(
            ctx_mine[1], ctx_partner[0], wide_last, feed_chip
        )
        stacked = stack_wide(scalars, mine_chip, wide_last, feed_chip)
        weights = [stacked, swap(stacked, "dp", 1)]
    ctx_partner[1] = swap(ctx_mine[1], "seq", 1)
    cot_partner = swap(cot_own, "seq", 1)

    forward, slopes, part_far = [None, None], [None, None], [None, None]
    for block in (1, 0):
        forward[block], weights = feed_forward(
            scalars, block, ctx_mine[block], ctx_partner[block], x, vecs, hidden_bias, weights, rows
        )
        part_far[block] = swap(forward[block][5], "seq", 1)
    up, down, out_mine, _ = weights
    second, second_shared, first_part_far = [None, None], [], [None, None]
    for block in (1, 0):
        slopes[block] = gelu_slope(scalars, forward[block][3])
    for block in (1, 0):
        second[block], second_shared = second_norm(
            scalars,
            block,
            forward[block][5],
            part_far[block],
            forward[block][0],
            slopes[block],
            (cot_own, cot_partner),
            vecs,
            up,
            down,
            second_shared,
            rows,
        )
        if block == 1:
            first_part_far[block] = swap(second[block][3], "seq", 1)
    feed_parts = feed_forward_grads(
        scalars,
        [(forward[k][2], second[k][2], second[k][1], forward[k][4]) for k in range(2)],
        rows,
    )
    first_part_far[1], second, second_shared, feed_parts = together(
        first_part_far[1], second, second_shared, feed_parts
    )
    first_part_far[0] = swap(second[0][3], "seq", 1)
    layer_output, sums_two, sums_hidden = second_shared
    attention_grad, ctx_grad, inners, first_shared = [None, None], [None, None], [None, None], []
    logs, scaled = [log_far, log_near], [scaled_far, scaled_near]

    def finish(block):
        attention_grad[block], ctx_grad[block], inners[block], *shared = first_norm(
            scalars,
            block,
            second[block][3],
            first_part_far[block],
            second[block][0],
            forward[block][0],
            forward[block][1],
            vecs,
            out_mine,
            scaled[block],
            logs[block],
            first_shared,
            rows,
        )
        return shared

    *first_shared, halo_send = finish(1)
    halo_grad = swap(halo_send, "seq", 2)
    if direct:
        feed_sums = combine(scalars, feed_parts[0], swap(feed_parts[1], "dp", 1))
        feed_sums = spread(feed_sums)
    else:
        feed_sums = scattered(rows_of(*feed_parts).reshape(D, -1))
    own_grad, sums_one = finish(0)

    grads, input_keep, input_send, sums_projection = attend_backward(
        scalars, pair, halo, [*ctx_grad, halo_grad], logs, inners, hot, weight, rows
    )
    input_far = swap(input_send, "seq", 1)
    small = small_sums(scalars, sums_one, sums_two, sums_hidden, sums_projection)
    small_side = swap(small, "seq", 1)
    projection_parts = projection_grads(scalars, x, grads, rows)
    projection_parts, small_side, feed_sums = together(projection_parts, small_side, feed_sums)
    if direct:
        feed_keep, feed_send = total_feed(scalars, feed_sums)
        attention_grad, feed_send = together(attention_grad, feed_send)
    out_blocks = [(ctx_mine[k], ctx_partner[k], attention_grad[k]) for k in range(2)]
    if direct:
        projection_received = swap(projection_parts[1], "dp", 1)
        out_parts = output_grads(scalars, out_blocks, small, small_side)
        out_received = swap(out_parts[1], "dp", 1)
        feed_far = swap(feed_send, "seq", 2)
        sums = spread(
            combine_both(scalars, projection_parts[0], projection_received, out_parts[0], out_received)
        )
    else:
        out_parts = rows_of(*output_grads(scalars, out_blocks, small, small_side))
        sums = scattered(
            jnp.concatenate(
                [rows_of(*projection_parts).reshape(D, -1), out_parts[:, :, :HALF].reshape(D, -1)], axis=1
            )
        )
        feed_keep, feed_send = total_feed(scalars, feed_sums)
        feed_far = swap(feed_send, "seq", 2)
    if direct:
        sums, feed_far, input_far = together(sums, feed_far, input_far)
    keep, send = total_projection(scalars, sums)
    received = swap(send, "seq", 2)
    up_grad, down_grad = finish_feed(scalars, feed_keep, feed_far)
    input_grad = own_grad + input_keep + input_far.astype(F32)
    if direct:
        received, up_grad, input_grad = together(received, up_grad, input_grad)
    projections = list(finish_projection(scalars, keep, received))
    if direct:
        projections, vec, tall_lines = projections[:4], projections[4:-1], projections[-1]
    else:
        tile = out_parts[:, :LABELS, HALF:] + out_parts[:, LABELS : 2 * LABELS, HALF:]
        tile = tile + swap(tile, "seq", 2)
        wide_lines = tile[:, :VECS, :BLOCK].transpose(1, 0, 2).reshape(VECS, D)
        wide_lines = lax.psum_scatter(wide_lines, "dp", scatter_dimension=1, tiled=True)
        tall_lines = lax.psum_scatter(tile[:, VECS : VECS + 3].reshape(-1), "dp", tiled=True)
        vec = [wide_lines[k] for k in range(VECS)]
    return (
        layer_output[None],
        input_grad[None],
        *projections,
        vec[0],
        vec[1],
        vec[2],
        vec[3],
        vec[4],
        up_grad,
        tall_lines,
        down_grad.T,
        vec[5],
        vec[6],
        vec[7],
    )


def solution(mesh):
    placed = (
        P("dp", "seq", None),
        P("dp", "seq"),
        P("dp", "seq"),
        P("dp", "seq"),
        P("dp", "seq"),
        P("dp", "seq"),
        P("dp"),
        P("dp"),
        P("dp"),
        P("dp"),
        P("dp"),
        P("dp", "seq"),
        P("dp"),
        P("seq", "dp"),
        P("dp"),
        P("dp"),
        P("dp"),
        P("dp", "seq", None),
    )
    return jax.shard_map(
        per_device,
        mesh=mesh,
        in_specs=placed,
        out_specs=(
            P("dp", "seq", None),
            P("dp", "seq", None),
            P("dp", "seq"),
            P("dp", "seq"),
            P("dp", "seq"),
            P("dp", "seq"),
            P("dp"),
            P("dp"),
            P("dp"),
            P("dp"),
            P("dp"),
            P("dp", "seq"),
            P("dp"),
            P("seq", "dp"),
            P("dp"),
            P("dp"),
            P("dp"),
        ),
        check_vma=False,
    )
```

```python
import jax
import jax.numpy as jnp
from jax import lax
from jax.experimental import pallas as pl
from jax.experimental.pallas import tpu as pltpu
from jax.sharding import PartitionSpec as P

D = 768
HEADS = 12
HEAD_DIM = 64
FF = 3072
EPS = 1e-05
MASKED = 1e30
PAIR = 2 * HEAD_DIM
QUARTER = D // 4
HALF = D // 2
HID = FF // 4
VECS = 8
GROUPS = 8
SHARE = FF // GROUPS // 128
BLOCK = D // GROUPS
LABELS = 16
MARKS = 48
MICROS = 450
FEED_MICROS = 300
BF = jnp.bfloat16
F32 = jnp.float32
ROOT_HALF = 0.7071067811865476
ROOT_TWO_PI = 0.3989422804014327


def dot(a, b):
    return lax.dot_general(a, b, (((1,), (0,)), ((), ())), preferred_element_type=F32)


def dot_nt(a, b):
    return lax.dot_general(a, b, (((1,), (1,)), ((), ())), preferred_element_type=F32)


def dot_tn(a, b):
    return lax.dot_general(a, b, (((0,), (0,)), ((), ())), preferred_element_type=F32)


def swap(value, axis, mask):
    count = lax.axis_size(axis)
    return lax.ppermute(value, axis, [(k, k ^ mask) for k in range(count)])


def together(*values):
    return lax.optimization_barrier(values)


def whole(shape):
    return pl.BlockSpec(shape, lambda *_: (0,) * len(shape))


def params():
    return pltpu.CompilerParams(vmem_limit_bytes=22 * 1024 * 1024)


def call(name, body, scalars, operands, in_specs, outs, out_specs, grid, scratch=(), micros=1):
    spec = pltpu.PrefetchScalarGridSpec(
        num_scalar_prefetch=1,
        grid=grid,
        in_specs=in_specs,
        out_specs=out_specs,
        scratch_shapes=list(scratch),
    )
    return pl.pallas_call(
        body,
        out_shape=outs,
        grid_spec=spec,
        compiler_params=params(),
        cost_estimate=pl.CostEstimate(
            flops=int(micros * 1.0e7), transcendentals=0, bytes_accessed=1024
        ),
        name=name,
    )(scalars, *operands)


def turn(quarters):
    return lax.rem(quarters + 4, 4) * QUARTER


def struct(shape, dtype):
    return jax.ShapeDtypeStruct(shape, dtype)


def chip_pieces(piece):
    return [piece] + [swap(piece, "dp", j) for j in range(2, GROUPS, 2)]


def gather_rows(piece):
    full = lax.all_gather(piece, "dp", axis=0, tiled=True)
    full = full.reshape(GROUPS, D // GROUPS, piece.shape[1])
    return [full[0::2], full[1::2]]


def place(target, pair, base, source_cols, target_cols):
    for j in range(GROUPS):
        start = pl.multiple_of((base ^ j) * BLOCK, 16)
        target[pl.ds(start, BLOCK), target_cols] = pair[j % 2][j // 2, :BLOCK, source_cols]


def split_rows(result, base, keep, send):
    for j in range(GROUPS):
        block = result[pl.ds(pl.multiple_of((base ^ j) * BLOCK, 16), BLOCK), :].astype(BF)
        if j % 2:
            send[j // 2] = block
        else:
            keep[j // 2] = block


def simple(name, body, scalars, operands, outs, micros=1):
    return call(
        name,
        body,
        scalars,
        operands,
        [whole(o.shape) for o in operands],
        outs,
        [whole(o.shape) for o in outs],
        (1,),
        micros=micros,
    )


def pack_inputs(scalars, tables, tokens, segments, up, down, lines, tall):
    rows = tokens.shape[0]
    height = tables[0].shape[0]
    skip = 2 * HID + (128 if lines else 0)
    operands = list(tables) + [tokens, segments, up, down] + lines + ([tall] if lines else [])
    count = len(operands)

    def body(_, *refs):
        sources, (send_ref, mine_ref, wide_ref, label_ref, docs_ref), refs = (
            refs[:count],
            refs[count : count + 5],
            refs[count + 5 :],
        )
        copies = [pltpu.make_async_copy(a, b, refs[-1].at[k]) for k, (a, b) in enumerate(zip(sources, refs))]
        for copy in copies:
            copy.start()
        for copy in copies:
            copy.wait()
        joined = jnp.concatenate([ref[...].astype(F32) for ref in refs[:4]], axis=1).astype(BF)
        send_ref[:, :D] = joined
        send_ref[:, D : D + HID] = refs[6][...]
        send_ref[:, D + HID :] = refs[7][...]
        mine_ref[:, :HID] = refs[6][...]
        mine_ref[:, HID : 2 * HID] = refs[7][...]
        part = joined[:, : 3 * QUARTER].astype(F32)
        mine_ref[:, skip:] = part.astype(BF)
        wide_ref[:, :HID] = refs[6][...]
        wide_ref[:, HID:] = refs[7][...]
        docs = refs[5][...].astype(F32)
        docs_ref[...] = docs
        label_ref[:rows, :] = refs[4][...]
        label_ref[rows:, :] = jnp.zeros((MARKS, D), BF)
        label_ref[rows:, :rows] = jnp.broadcast_to(docs, (MARKS, rows)).astype(BF)
        if lines:
            table = [ref[...].astype(F32)[None, :] for ref in refs[8 : 8 + VECS]]
            table = jnp.concatenate(table, axis=0)
            table = [jnp.concatenate([table, jnp.zeros((VECS, 128 - BLOCK), F32)], axis=1)]
            line = refs[8 + VECS][...].astype(F32)[None, :]
            table += [line[:, c * 128 : (c + 1) * 128] for c in range(SHARE)]
            table += [jnp.zeros((height - VECS - SHARE, 128), F32)]
            mine_ref[:, 2 * HID : skip] = jnp.concatenate(table, axis=0).astype(BF)

    outs = [
        struct((height, D + 2 * HID), BF),
        struct((height, skip + 3 * QUARTER), BF),
        struct((height, 2 * HID), BF),
        struct((rows + MARKS, D), BF),
        struct((1, rows), F32),
    ]
    operands = [pltpu.with_memory_space_constraint(o, pltpu.MemorySpace.HBM) for o in operands]
    return call(
        "pack_inputs",
        body,
        scalars,
        operands,
        [pl.BlockSpec(memory_space=pltpu.MemorySpace.HBM)] * count,
        outs,
        [whole(o.shape) for o in outs],
        (1,),
        [pltpu.VMEM(o.shape, o.dtype) for o in operands] + [pltpu.SemaphoreType.DMA((count,))],
    )


def split_arrived(scalars, arrived, mine, labelled):
    rows = arrived.shape[0]
    tall = rows + LABELS
    skip = mine.shape[1] - 3 * QUARTER
    direct = skip > 2 * HID

    def body(_, far_ref, mine_ref, label_ref, narrow_ref, both_ref, send_ref):
        narrow_ref[...] = far_ref[:, : 3 * QUARTER]
        both_ref[:rows, :] = mine_ref[:, skip:]
        both_ref[tall:, :] = far_ref[:, : 3 * QUARTER]
        send_ref[...] = label_ref[...]
        if direct:
            both_ref[rows:tall, :] = jnp.zeros((LABELS, 3 * QUARTER), BF)
            both_ref[rows:tall, :128] = mine_ref[:LABELS, 2 * HID : skip]
            part = far_ref[:, 3 * QUARTER : D].astype(F32)
            step = rows // 4
            part = jnp.concatenate([part[k * step : (k + 1) * step] for k in range(4)], axis=1)
            part = jnp.concatenate([part, jnp.zeros((MARKS - LABELS - step, D), F32)], axis=0)
            send_ref[labelled.shape[0] - MARKS + LABELS :, :] = part.astype(BF)

    outs = [
        struct((rows, 3 * QUARTER), BF),
        struct((rows + tall, 3 * QUARTER), BF),
        struct(labelled.shape, BF),
    ]
    return simple("split_arrived", body, scalars, [arrived, mine, labelled], outs)


def stack_narrow(scalars, mine_chip, far_chip, both_far):
    rows = far_chip[0].shape[0]
    tall = rows + LABELS
    skip = mine_chip[0].shape[1] - 3 * QUARTER

    def body(_, *refs):
        out_ref = refs[-1]
        for k in range(3):
            out_ref[k, :rows] = refs[k][:, skip:]
            out_ref[k, rows:tall] = jnp.zeros((LABELS, 3 * QUARTER), BF)
            out_ref[k, rows:tall, :128] = refs[k][:LABELS, 2 * HID : skip]
            out_ref[k, tall:] = refs[3 + k][...]
        out_ref[3] = refs[6][...]

    shape = (GROUPS // 2, tall + rows, 3 * QUARTER)
    operands = [*mine_chip, *far_chip, both_far]
    return simple("stack_narrow", body, scalars, operands, [struct(shape, BF)])[0]


def stack_wide(scalars, mine_chip, last, feed_chip):
    def body(_, *refs):
        out_ref = refs[-1]
        for k in range(3):
            out_ref[k, :, : 2 * HID] = refs[k][:BLOCK, : 2 * HID]
        out_ref[3, :, : 2 * HID] = refs[3][...]
        for k in range(4):
            out_ref[k, :, 2 * HID :] = refs[4 + k][...]

    shape = (GROUPS // 2, BLOCK, 4 * HID + D)
    return simple("stack_wide", body, scalars, [*mine_chip, last, *feed_chip], [struct(shape, BF)])[0]


def pack_feed(scalars, first_send, arrived, side, last):
    rows = arrived.shape[0]
    columns = slice(3 * QUARTER, D)

    def body(sc, own_ref, arrived_ref, side_ref, last_ref, out_ref):
        out_ref[:, : 2 * HID] = arrived_ref[:, D:]
        final = last_ref[...].astype(F32)
        if last.shape[1] == D:
            step = rows // 4
            final = final[last.shape[0] - MARKS + LABELS :]
            final = [final[:step, k * QUARTER : (k + 1) * QUARTER] for k in range(4)]
            final = jnp.concatenate(final, axis=0)
        total = jnp.zeros((rows, D), F32)
        for k, part in enumerate([own_ref[:, columns], side_ref[...], arrived_ref[:, columns], final]):
            part = jnp.concatenate([part.astype(F32), jnp.zeros((rows, D - QUARTER), F32)], axis=1)
            total = total + pltpu.roll(part, (sc[2] ^ k) * QUARTER, 1)
        out_ref[:, 2 * HID :] = total.astype(BF)

    out = struct((rows, 2 * HID + D), BF)
    return simple("pack_feed", body, scalars, [first_send, arrived, side, last], [out])[0]


def mark(docs, rows):
    number = lax.broadcasted_iota(jnp.int32, (LABELS, rows), 0).astype(F32)
    return jnp.where(jnp.broadcast_to(docs, (LABELS, rows)) == number, 1.0, 0.0).astype(BF)


def attend(query, key, value, mask, log_ref, step):
    lane = lax.broadcasted_iota(jnp.int32, (1, PAIR), 1)
    total = jnp.zeros(query.shape, F32)
    scaled = jnp.zeros(query.shape, F32)
    logs = jnp.zeros(query.shape, F32)
    value = jnp.concatenate([value, jnp.ones(value.shape, BF)], axis=1)
    for head in range(2):
        part = jnp.where((lane // HEAD_DIM) == head, 1.0, 0.0)
        mine = (query.astype(F32) * (part * HEAD_DIM**-0.5)).astype(BF)
        scores = dot_nt(mine, key) + mask
        top = jnp.max(scores, axis=-1, keepdims=True)
        expo = jnp.exp(scores - top)
        whole_sum = jnp.sum(expo, axis=-1, keepdims=True)
        probs = expo * (1.0 / whole_sum)
        rounded = probs.astype(BF)
        context = dot(rounded, value)
        total = total + context[:, :PAIR] * part
        scaled = scaled + context[:, :PAIR] * part / context[:, PAIR:]
        logs = jnp.where(lane == head, top + jnp.log(whole_sum), logs)
    turned = logs.T
    for head in range(2):
        log_ref[pl.ds(2 * step + head, 1), :] = turned[head : head + 1, :]
    return total.astype(BF), scaled


def column(height):
    return pl.BlockSpec((height, PAIR), lambda p, _: (0, p))


def attend_pair(scalars, own, partner, own_docs, pieces, rows):
    base = 2 * rows
    tall = BLOCK + LABELS

    def body(sc, own_ref, partner_ref, docs_ref, *refs):
        weight_refs, refs = refs[:2], refs[2:]
        q_ref, k_ref, v_ref, ctx_ref, x_ref, w_ref, hot_ref, vec_ref, hidden_ref, bias_ref, log_ref, *refs = refs
        scaled_ref, mask_ref = refs
        step = pl.program_id(0)

        @pl.when(step == 0)
        def _():
            near = sc[0]
            own_at = pl.multiple_of(near * rows, rows)
            partner_at = pl.multiple_of((1 - near) * rows, rows)
            x_ref[pl.ds(own_at, rows), :] = own_ref[...]
            x_ref[pl.ds(partner_at, rows), :] = partner_ref[:rows, :]
            hot_ref[:, pl.ds(own_at, rows)] = mark(docs_ref[...], rows)
            docs = partner_ref[rows : rows + 1, :rows].astype(F32)
            hot_ref[:, pl.ds(partner_at, rows)] = mark(docs, rows)
            for j in range(GROUPS):
                at = pl.ds(pl.multiple_of((sc[1] ^ j) * BLOCK, 16), BLOCK)
                for kind in range(3):
                    part = slice(kind * QUARTER, (kind + 1) * QUARTER)
                    both = [weight_refs[j % 2][j // 2, top : top + BLOCK, part] for top in (0, tall)]
                    both = [half.astype(F32) for half in both]
                    both = jnp.concatenate(both, axis=1).astype(BF)
                    for p in range(3):
                        to = (3 * p + kind) * PAIR
                        w_ref[at, to : to + PAIR] = both[:, p * PAIR : (p + 1) * PAIR]
            hot = hot_ref[...]
            mask_ref[...] = (dot_tn(hot[:, :rows], hot) - 1.0) * MASKED
            vectors = jnp.zeros((LABELS, D), F32)
            for j in range(GROUPS):
                block = sc[1] ^ j
                line = weight_refs[j % 2][j // 2, BLOCK:tall, :128].astype(F32)
                table = jnp.where(lax.broadcasted_iota(jnp.int32, line.shape, 1) < BLOCK, line, 0.0)
                table = jnp.concatenate([table, jnp.zeros((LABELS, D - 128), F32)], axis=1)
                vectors = vectors + pltpu.roll(table, block * BLOCK, 1)
                quarter = block // 2
                for k in range(2):

                    @pl.when(quarter == sc[2] ^ (2 * k))
                    def _():
                        for c in range(SHARE):
                            to = pl.multiple_of((block % 2) * (HID // 2) + k * HID + c * 128, 128)
                            value = jnp.broadcast_to(line[VECS + c : VECS + c + 1], (VECS, 128))
                            hidden_ref[:, pl.ds(to, 128)] = value

            vec_ref[...] = vectors[:VECS]
            lanes = lax.broadcasted_iota(jnp.int32, (VECS, HALF), 1)
            low = pltpu.roll(vectors[:VECS], turn(-sc[2]), 1)[:, :HALF]
            high = pltpu.roll(vectors[:VECS], turn(1 - (sc[2] ^ 2)), 1)[:, :HALF]
            bias_ref[...] = jnp.where(lanes < QUARTER, low, high)
            log_ref[...] = jnp.zeros_like(log_ref)

        at = pl.multiple_of(step * 3 * PAIR, PAIR)
        both = dot(x_ref[...], w_ref[:, pl.ds(at, 3 * PAIR)])
        bias = bias_ref[:, pl.ds(pl.multiple_of(step * PAIR, PAIR), PAIR)]
        query = (both[:, :PAIR] + bias[0:1]).astype(BF)
        key = both[:, PAIR : 2 * PAIR].astype(BF)
        value = (both[:, 2 * PAIR :] + bias[1:2]).astype(BF)
        q_ref[...] = query
        k_ref[...] = key
        v_ref[...] = value
        ctx_ref[...], scaled_ref[...] = attend(query[:rows], key, value, mask_ref[...], log_ref, step)

    operands = [own, partner, own_docs, *pieces]
    in_specs = [whole(o.shape) for o in operands]
    outs = [
        struct((base, HALF), BF),
        struct((base, HALF), BF),
        struct((base, HALF), BF),
        struct((rows, HALF), BF),
        struct((base, D), BF),
        struct((D, 3 * HALF), BF),
        struct((LABELS, base), BF),
        struct((VECS, D), F32),
        struct((VECS, 2 * HID), F32),
        struct((VECS, HALF), F32),
        struct((VECS, rows), F32),
        struct((rows, HALF), F32),
    ]
    out_specs = [column(base)] * 3 + [column(rows)] + [whole(o.shape) for o in outs[4:-1]] + [column(rows)]
    return call(
        "attend_pair",
        body,
        scalars,
        operands,
        in_specs,
        outs,
        out_specs,
        (HALF // PAIR,),
        [pltpu.VMEM((rows, base), F32)],
        micros=8,
    )


def attend_halo(scalars, halo_near, halo_far, weight, bias, hot, query, key, value, rows):
    def body(sc, near_ref, far_ref, w_ref, bias_ref, hot_ref, q_ref, k_ref, v_ref, *refs):
        halo_refs, (ctx_ref, scaled_ref, all_ref, log_ref, x_ref, mask_ref) = refs[:3], refs[3:]

        @pl.when(pl.program_id(0) == 0)
        def _():
            all_ref[:, : 2 * rows] = hot_ref[...]

            def halo(ref):
                x_ref[...] = ref[:rows, :]
                all_ref[:, 2 * rows :] = mark(ref[rows : rows + 1, :rows].astype(F32), rows)

            pl.when(sc[0] == 1)(lambda: halo(near_ref))
            pl.when(sc[0] == 0)(lambda: halo(far_ref))
            mask_ref[...] = (dot_tn(all_ref[:, rows : 2 * rows], all_ref[...]) - 1.0) * MASKED
            log_ref[...] = jnp.zeros_like(log_ref)

        both = dot(x_ref[...], w_ref[...])
        parts = [
            (both[:, :PAIR] + bias_ref[0:1, :]).astype(BF),
            both[:, PAIR : 2 * PAIR].astype(BF),
            (both[:, 2 * PAIR :] + bias_ref[1:2, :]).astype(BF),
        ]
        for ref, part in zip(halo_refs, parts):
            ref[...] = part
        keys = jnp.concatenate([k_ref[...], parts[1]], axis=0)
        values = jnp.concatenate([v_ref[...], parts[2]], axis=0)
        ctx_ref[...], scaled_ref[...] = attend(
            q_ref[rows:, :], keys, values, mask_ref[...], log_ref, pl.program_id(0)
        )

    operands = [halo_near, halo_far, weight, bias, hot, query, key, value]
    in_specs = [whole(o.shape) for o in operands]
    in_specs[2] = pl.BlockSpec((D, 3 * PAIR), lambda p, _: (0, p))
    in_specs[3] = column(VECS)
    in_specs[5:] = [column(2 * rows)] * 3
    outs = [struct((rows, HALF), BF)] * 4 + [struct((rows, HALF), F32)]
    outs += [struct((LABELS, 3 * rows), BF), struct((VECS, rows), F32)]
    return call(
        "attend_halo",
        body,
        scalars,
        operands,
        in_specs,
        outs,
        [column(rows)] * 5 + [whole((LABELS, 3 * rows)), whole((VECS, rows))],
        (HALF // PAIR,),
        [pltpu.VMEM((rows, D), BF), pltpu.VMEM((rows, 3 * rows), F32)],
        micros=6,
    )


def feed_forward(scalars, block, ctx_mine, ctx_partner, x, vecs, up_bias, weights, rows):
    count = len(weights)
    fresh = len(weights[0].shape) == 3

    def body(sc, mine_ref, partner_ref, x_ref, vec_ref, bias_ref, *refs):
        weight_refs, refs = refs[:count], refs[count:]
        (norm_ref, inv_ref, first_ref, gate_ref, active_ref, part_ref), refs = refs[:6], refs[6:]
        if fresh:
            up_ref, down_ref, out_ref, other_ref, full_ref = refs
            for k in range(2):
                at, to = 2 * k * HID, slice(k * HID, (k + 1) * HID)
                place(up_ref, weight_refs, sc[1], slice(at, at + HID), to)
                place(down_ref, weight_refs, sc[1], slice(at + HID, at + 2 * HID), to)
            place(full_ref, weight_refs, sc[1], slice(4 * HID, 4 * HID + D), slice(None))
            for ref, flip in ((out_ref, 0), (other_ref, 1)):
                for k in range(2):
                    at = pl.multiple_of((sc[2] ^ flip ^ (2 * k)) * QUARTER, 16)
                    ref[k * QUARTER : (k + 1) * QUARTER, :] = full_ref[pl.ds(at, QUARTER), :]
        else:
            up_ref, down_ref, out_ref, other_ref = weight_refs

        attention = dot(mine_ref[...], out_ref[...]) + dot(partner_ref[...], other_ref[...])
        total = x_ref[...].astype(F32) + (attention + vec_ref[2:3, :])
        center = total - jnp.mean(total, axis=-1, keepdims=True)
        inverse = lax.rsqrt(jnp.mean(center * center, axis=-1, keepdims=True) + EPS)
        normed = center * inverse
        norm_ref[...] = normed
        inv_ref[...] = jnp.broadcast_to(inverse, (rows, 128))
        first = (normed * vec_ref[3:4, :] + vec_ref[4:5, :]).astype(BF)
        first_ref[...] = first
        gate = dot(first, up_ref[...]) + bias_ref[0:1, :]
        gate_ref[...] = gate
        active = (gate * (1.0 + lax.erf(gate * ROOT_HALF)) * 0.5).astype(BF)
        active_ref[...] = active
        part_ref[...] = dot_nt(active, down_ref[...]).astype(BF)

    operands = [ctx_mine, ctx_partner, x, vecs, up_bias, *weights]
    in_specs = [whole(o.shape) for o in operands]
    in_specs[2] = pl.BlockSpec((rows, D), lambda *_: (block, 0))
    outs = [
        struct((rows, D), F32),
        struct((rows, 128), F32),
        struct((rows, D), BF),
        struct((rows, 2 * HID), F32),
        struct((rows, 2 * HID), BF),
        struct((rows, D), BF),
    ]
    scratch = []
    if fresh:
        outs += [struct((D, 2 * HID), BF)] * 2 + [struct((HALF, D), BF)] * 2
        scratch = [pltpu.VMEM((D, D), BF)]
    results = call(
        "feed_forward",
        body,
        scalars,
        operands,
        in_specs,
        outs,
        [whole(o.shape) for o in outs],
        (1,),
        scratch,
        micros=6,
    )
    return results[:6], (results[6:] if fresh else weights)


def gelu_slope(scalars, gate):
    rows = gate.shape[0] // 2

    def body(_, gate_ref, slope_ref):
        gate_here = gate_ref[...]
        bell = jnp.exp(gate_here * gate_here * -0.5) * ROOT_TWO_PI
        slope_ref[...] = 0.5 * (1.0 + lax.erf(gate_here * ROOT_HALF)) + gate_here * bell

    spec = pl.BlockSpec((rows, gate.shape[1]), lambda r, _: (r, 0))
    return call(
        "gelu_slope", body, scalars, [gate], [spec], [struct(gate.shape, F32)], [spec], (2,), micros=3
    )[0]


def second_norm(scalars, block, part, received, normed, slope, cotangent, vecs, up, down, earlier, rows):
    def body(sc, part_ref, recv_ref, norm_ref, slope_ref, cot_ref, other_ref, vec_ref, up_ref, down_ref, *refs):
        old, refs = refs[: len(earlier)], refs[len(earlier) :]
        (total_grad_ref, branch_grad_ref, gate_grad_ref, first_part_ref, out_ref, sums_ref, bias_ref) = refs
        mine = sc[0] == block
        first = norm_ref[...] * vec_ref[3:4, :] + vec_ref[4:5, :]
        branch = part_ref[...].astype(F32) + recv_ref[...].astype(F32) + vec_ref[5:6, :]
        total = first + branch
        center = total - jnp.mean(total, axis=-1, keepdims=True)
        inverse = lax.rsqrt(jnp.mean(center * center, axis=-1, keepdims=True) + EPS)
        here = center * inverse
        upstream = jnp.where(mine, cot_ref[...].astype(F32), other_ref[...].astype(F32))
        scaled = upstream * vec_ref[6:7, :]
        inner = (
            scaled
            - jnp.mean(scaled, axis=-1, keepdims=True)
            - here * jnp.mean(scaled * here, axis=-1, keepdims=True)
        )
        total_grad = inner * inverse
        total_grad_ref[...] = total_grad
        branch_grad = total_grad.astype(BF)
        branch_grad_ref[...] = branch_grad
        gate_grad = (dot(branch_grad, down_ref[...]) * slope_ref[...]).astype(BF)
        gate_grad_ref[...] = gate_grad
        hidden = jnp.broadcast_to(jnp.sum(gate_grad.astype(F32), axis=0, keepdims=True), (8, 2 * HID))
        bias_ref[...] = hidden + old[2][...] if old else hidden
        first_part_ref[...] = dot_nt(gate_grad, up_ref[...]).astype(BF)

        @pl.when(mine)
        def _():
            out_ref[...] = (here * vec_ref[6:7, :] + vec_ref[7:8, :]).astype(BF)
            sums_ref[...] = jnp.zeros_like(sums_ref)
            sums_ref[0:1, :] = jnp.sum(upstream * here, axis=0, keepdims=True)
            sums_ref[1:2, :] = jnp.sum(upstream, axis=0, keepdims=True)
            sums_ref[2:3, :] = jnp.sum(branch_grad.astype(F32), axis=0, keepdims=True)

        if old:

            @pl.when(jnp.logical_not(mine))
            def _():
                out_ref[...] = old[0][...]
                sums_ref[...] = old[1][...]

        else:

            @pl.when(jnp.logical_not(mine))
            def _():
                out_ref[...] = jnp.zeros_like(out_ref)
                sums_ref[...] = jnp.zeros_like(sums_ref)

    operands = [part, received, normed, slope, *cotangent, vecs, up, down, *earlier]
    outs = [
        struct((rows, D), F32),
        struct((rows, D), BF),
        struct((rows, 2 * HID), BF),
        struct((rows, D), BF),
        struct((rows, D), BF),
        struct((8, D), F32),
        struct((8, 2 * HID), F32),
    ]
    results = call(
        "second_norm",
        body,
        scalars,
        operands,
        [whole(o.shape) for o in operands],
        outs,
        [whole(o.shape) for o in outs],
        (1,),
        micros=5,
    )
    return results[:4], results[4:]


def split_outs(width):
    return [struct((GROUPS // 2, BLOCK, width), BF)] * 2


def feed_forward_grads(scalars, blocks, rows):
    def body(sc, *refs):
        keep_ref, send_ref, result_ref = refs[-3:]
        step = pl.program_id(0)

        @pl.when(step % 2 == 0)
        def _():
            result_ref[...] = dot_tn(refs[0][...], refs[1][...]) + dot_tn(refs[4][...], refs[5][...])

        @pl.when(step % 2 == 1)
        def _():
            result_ref[...] = dot_tn(refs[2][...], refs[3][...]) + dot_tn(refs[6][...], refs[7][...])

        split_rows(result_ref, sc[1], keep_ref, send_ref)

    half = pl.BlockSpec((rows, HID), lambda c, _: (0, c // 2))
    outs = split_outs(4 * HID)
    out_specs = [pl.BlockSpec((GROUPS // 2, BLOCK, HID), lambda c, _: (0, 0, c))] * 2
    return call(
        "feed_forward_grads",
        body,
        scalars,
        [value for block in blocks for value in block],
        [whole((rows, D)), half] * 4,
        outs,
        out_specs,
        (4,),
        [pltpu.VMEM((D, HID), F32)],
        micros=8,
    )


def first_norm(
    scalars, block, part, received, total_grad, normed, inverse, vecs, out_weight, ctx, logs, earlier, rows
):
    def body(sc, part_ref, recv_ref, grad_ref, norm_ref, inv_ref, vec_ref, weight_ref, ctx_ref, log_ref, *refs):
        old, refs = refs[: len(earlier)], refs[len(earlier) :]
        attention_ref, context_ref, inner_ref, own_ref, sums_ref = refs[:5]
        mine = sc[0] == block
        upstream = grad_ref[...] + part_ref[...].astype(F32) + recv_ref[...].astype(F32)
        here = norm_ref[...]
        scaled = upstream * vec_ref[3:4, :]
        inner = (
            scaled
            - jnp.mean(scaled, axis=-1, keepdims=True)
            - here * jnp.mean(scaled * here, axis=-1, keepdims=True)
        )
        total = inner * inv_ref[:, :1]
        attention = total.astype(BF)
        attention_ref[...] = attention
        context = dot_nt(attention, weight_ref[...]).astype(BF)
        context_ref[...] = context
        lane = lax.broadcasted_iota(jnp.int32, (VECS, HALF), 1) // HEAD_DIM
        picks = jnp.where(lane == lax.broadcasted_iota(jnp.int32, (VECS, HALF), 0), 1.0, 0.0)
        products = context.astype(F32) * ctx_ref[...]
        inner = jnp.zeros((VECS, rows), F32)
        for _ in range(3):
            piece = products.astype(BF)
            inner = inner + dot_nt(picks.astype(BF), piece)
            products = products - piece.astype(F32)
        inner_ref[...] = inner
        if block == 1:
            send_ref = refs[5]
            turned = jnp.concatenate([weight_ref[QUARTER:, :], weight_ref[:QUARTER, :]], axis=0)
            send_ref[:rows, :] = dot_nt(attention, turned).astype(BF)
            rest = jnp.concatenate([log_ref[...], inner], axis=0)
            send_ref[rows:, :] = jnp.zeros((3 * LABELS, HALF), BF)
            for k in range(3):
                at = rows + k * LABELS
                piece = rest.astype(BF)
                send_ref[at : at + LABELS, :rows] = piece
                rest = rest - piece.astype(F32)

        @pl.when(mine)
        def _():
            own_ref[...] = total
            sums_ref[...] = jnp.zeros_like(sums_ref)
            sums_ref[0:1, :] = jnp.sum(upstream * here, axis=0, keepdims=True)
            sums_ref[1:2, :] = jnp.sum(upstream, axis=0, keepdims=True)
            sums_ref[2:3, :] = jnp.sum(attention.astype(F32), axis=0, keepdims=True)

        @pl.when(jnp.logical_not(mine))
        def _():
            own_ref[...] = old[0][...] if old else jnp.zeros_like(own_ref)
            sums_ref[...] = old[1][...] if old else jnp.zeros_like(sums_ref)

    operands = [part, received, total_grad, normed, inverse, vecs, out_weight, ctx, logs, *earlier]
    outs = [
        struct((rows, D), BF),
        struct((rows, HALF), BF),
        struct((VECS, rows), F32),
        struct((rows, D), F32),
        struct((8, D), F32),
        struct((rows + 3 * LABELS, HALF), BF),
    ][: 6 if block == 1 else 5]
    return call(
        "first_norm",
        body,
        scalars,
        operands,
        [whole(o.shape) for o in operands],
        outs,
        [whole(o.shape) for o in outs],
        (1,),
        micros=3,
    )


def halves(value):
    high = value.astype(BF).astype(F32)
    return jnp.concatenate([high, value - high], axis=0).astype(BF)


def whole_of(table):
    return table[:LABELS].astype(F32) + table[LABELS : 2 * LABELS].astype(F32)


def output_grads(scalars, blocks, small, small_side):
    def body(sc, *refs):
        small_ref, side_ref, keep_ref, send_ref, result_ref = refs[-5:]
        grads = []
        for ref in (refs[2], refs[5]):
            turned = pltpu.roll(ref[...].astype(F32), turn(-sc[2]), 1)
            turned = [turned[:, :QUARTER], turned[:, HALF : HALF + QUARTER]]
            grads.append(jnp.concatenate(turned, axis=1).astype(BF))
        for side in range(2):
            part = dot_tn(refs[side][...], grads[0]) + dot_tn(refs[3 + side][...], grads[1])
            for k in range(2):
                at = pl.multiple_of((sc[2] ^ side ^ (2 * k)) * QUARTER, 16)
                result_ref[pl.ds(at, QUARTER), :] = part[k * QUARTER : (k + 1) * QUARTER, :]
        for j in range(GROUPS):
            target = (keep_ref, send_ref)[j % 2]
            block = sc[1] ^ j
            rows = pl.ds(pl.multiple_of(block * BLOCK, 16), BLOCK)
            target[j // 2, :, :HALF] = result_ref[rows, :].astype(BF)
            target[j // 2, :, HALF:] = jnp.zeros((BLOCK, 128), BF)
            target[j // 2, : 2 * LABELS, HALF:] = halves(small_ref[block] + side_ref[block])

    outs = [struct((GROUPS // 2, BLOCK, HALF + 128), BF)] * 2
    operands = [value for block in blocks for value in block] + [small, small_side]
    return call(
        "output_grads",
        body,
        scalars,
        operands,
        [whole(o.shape) for o in operands],
        outs,
        [whole(o.shape) for o in outs],
        (1,),
        [pltpu.VMEM((D, HALF), F32)],
        micros=4,
    )


def attend_backward(scalars, pair, halo, grad_blocks, logs, inners, hot, weight, rows):
    base = 3 * rows
    steps = HALF // PAIR

    def body(sc, *refs):
        pair_refs, halo_refs, refs = refs[:3], refs[3:6], refs[6:]
        far_ref, near_ref, halo_ref, stats_ref, *refs = refs
        log_refs, inner_refs, (hot_ref, w_ref, *refs) = refs[:2], refs[2:4], refs[4:]
        out_ref, keep_ref, send_ref, sums_ref, mask_ref, key_ref, value_ref, acc_ref, q_ref, k_ref, v_ref, line_ref = refs
        for target, first_part, last_part in zip((q_ref, k_ref, v_ref), pair_refs, halo_refs):
            target[: 2 * rows, :] = first_part[...]
            target[2 * rows :, :] = last_part[...]
        step = pl.program_id(0)

        @pl.when(step == 0)
        def _():
            mask_ref[...] = (dot_tn(hot_ref[...], hot_ref[...]) - 1.0) * MASKED
            lines = jnp.zeros((LABELS, rows), F32)
            for k in range(3):
                at = rows + k * LABELS
                lines = lines + stats_ref[at : at + LABELS, :rows].astype(F32)
            line_ref[...] = lines

        key_ref[...] = jnp.zeros_like(key_ref)
        value_ref[...] = jnp.zeros_like(value_ref)
        lane = lax.broadcasted_iota(jnp.int32, (1, PAIR), 1)
        query_grads = [jnp.zeros((PAIR, rows), F32), jnp.zeros((PAIR, rows), F32)]
        for head in range(2):
            part = jnp.where((lane // HEAD_DIM) == head, 1.0, 0.0)
            key_turned = (k_ref[...].astype(F32) * part).T.astype(BF)
            line = 2 * step + head
            other = lax.rem(line + 3, 6)
            lines = [(log_refs[k][pl.ds(line, 1), :], inner_refs[k][pl.ds(line, 1), :]) for k in range(2)]
            lines += [(line_ref[pl.ds(other, 1), :], line_ref[pl.ds(other + VECS, 1), :])]
            for index, (low, high) in enumerate(((0, 2 * rows), (0, base), (rows, 2 * rows))):
                start = index * rows
                mine = (q_ref[start : start + rows].astype(F32) * (part * HEAD_DIM**-0.5)).astype(BF)
                grads = (far_ref, near_ref, halo_ref)[index][:rows, :]
                grads = (grads.astype(F32) * part).astype(BF)
                scores = dot_nt(k_ref[low:high], mine) + mask_ref[low:high, start : start + rows]
                log_total, inner = lines[index]
                probs = jnp.exp(scores - log_total)
                pulled = dot_nt(v_ref[low:high], grads)
                score_grads = (probs * (pulled - inner)).astype(BF)
                top = min(high, 2 * rows)
                span = top - low
                value_ref[low:top, :] += dot(probs[:span].astype(BF), grads)
                key_ref[low:top, :] += dot(score_grads[:span], mine)
                if index < 2:
                    query_grads[index] = query_grads[index] + dot(key_turned[:, low:high], score_grads)
        for index in range(2):
            turned = (query_grads[index] * HEAD_DIM**-0.5).T.astype(BF)
            out_ref[index * rows : (index + 1) * rows, :PAIR] = turned
        out_ref[:, PAIR : 2 * PAIR] = key_ref[...].astype(BF)
        out_ref[:, 2 * PAIR :] = value_ref[...].astype(BF)
        sums = jnp.sum(out_ref[...].astype(F32), axis=0, keepdims=True)
        sums_ref[...] = jnp.broadcast_to(sums, (8, 3 * PAIR))
        product = dot_nt(out_ref[...], w_ref[...])

        @pl.when(step == 0)
        def _():
            acc_ref[...] = product

        @pl.when(step > 0)
        def _():
            acc_ref[...] += product

        @pl.when(step == steps - 1)
        def _():
            near = sc[0]
            keep_ref[...] = acc_ref[pl.ds(pl.multiple_of(near * rows, rows), rows), :]
            other = acc_ref[pl.ds(pl.multiple_of((1 - near) * rows, rows), rows), :]
            send_ref[...] = other.astype(BF)

    stats = grad_blocks[2]
    operands = [*pair, *halo, *grad_blocks, stats, *logs, *inners, hot, weight]
    in_specs = [column(2 * rows)] * 3 + [column(rows)] * 5 + [column(stats.shape[0])]
    in_specs += [whole(o.shape) for o in operands[9:15]]
    in_specs += [pl.BlockSpec((D, 3 * PAIR), lambda p, _: (0, p))]
    outs = [struct((2 * rows, 3 * HALF), BF), struct((rows, D), F32), struct((rows, D), BF)]
    outs += [struct((8, 3 * HALF), F32)]
    out_specs = [
        pl.BlockSpec((2 * rows, 3 * PAIR), lambda p, _: (0, p)),
        whole((rows, D)),
        whole((rows, D)),
        pl.BlockSpec((8, 3 * PAIR), lambda p, _: (0, p)),
    ]
    scratch = [
        pltpu.VMEM((base, base), F32),
        pltpu.VMEM((2 * rows, PAIR), F32),
        pltpu.VMEM((2 * rows, PAIR), F32),
        pltpu.VMEM((2 * rows, D), F32),
    ] + [pltpu.VMEM((base, PAIR), BF)] * 3
    scratch += [pltpu.VMEM((LABELS, rows), F32)]
    return call(
        "attend_backward",
        body,
        scalars,
        operands,
        in_specs,
        outs,
        out_specs,
        (steps,),
        scratch,
        micros=MICROS,
    )


def projection_grads(scalars, x, grads, rows):
    tall = 2 * rows

    def body(sc, x_ref, grad_ref, *refs):
        result_ref = refs[-1]
        result_ref[...] = dot_tn(x_ref[...], grad_ref[...])
        split_rows(result_ref, sc[1], refs[0], refs[1])

    outs = split_outs(3 * HALF)
    out_specs = [pl.BlockSpec((GROUPS // 2, BLOCK, 3 * PAIR), lambda p, _: (0, 0, p))] * 2
    return call(
        "projection_grads",
        body,
        scalars,
        [x, grads],
        [pl.BlockSpec((tall, D), lambda p, _: (0, 0)), pl.BlockSpec((tall, 3 * PAIR), lambda p, _: (0, p))],
        outs,
        out_specs,
        (HALF // PAIR,),
        [pltpu.VMEM((D, 3 * PAIR), F32)],
        micros=5,
    )


def combine(scalars, keep, received):
    count, rows, width = keep.shape
    chunk = width // 3

    def body(_, keep_ref, recv_ref, *refs):
        for k in range(count):
            total = keep_ref[k].astype(F32) + recv_ref[k].astype(F32)
            refs[k][...] = total.astype(refs[k].dtype)

    block = pl.BlockSpec((count, rows, chunk), lambda c, _: (0, 0, c))
    outs = [struct((rows, width), F32)] + [struct((rows, width), BF)] * (count - 1)
    spec = pl.BlockSpec((rows, chunk), lambda c, _: (0, c))
    return list(call(
        "combine",
        body, scalars, [keep, received], [block, block], outs, [spec] * count, (3,)))


def combine_both(scalars, keep, received, out_keep, out_received):
    count, rows, wide = keep.shape
    last = wide + HALF

    def body(_, keep_ref, recv_ref, out_keep_ref, out_recv_ref, *refs):
        for k in range(count):
            kind = refs[k].dtype
            refs[k][:, :wide] = (keep_ref[k].astype(F32) + recv_ref[k].astype(F32)).astype(kind)
            total = out_keep_ref[k, :, :HALF].astype(F32) + out_recv_ref[k, :, :HALF].astype(F32)
            refs[k][:, wide:last] = total.astype(kind)
            small = whole_of(out_keep_ref[k, :, HALF:]) + whole_of(out_recv_ref[k, :, HALF:])
            refs[k][:, last:] = jnp.zeros((rows, 128), kind)
            refs[k][: 2 * LABELS, last:] = halves(small).astype(kind)

    outs = [struct((rows, last + 128), F32)] + [struct((rows, last + 128), BF)] * (count - 1)
    return simple("combine_both", body, scalars, [keep, received, out_keep, out_received], outs, 2)


def total_feed(scalars, sums):
    rows = sums[0].shape[0]

    def body(_, *refs):
        keep_ref, send_ref = refs[-2:]
        total = refs[0][...]
        for ref in refs[1:-2]:
            total = total + ref[...].astype(F32)
        keep_ref[...] = total[:, : 2 * HID]
        send_ref[:, : 2 * HID] = total[:, 2 * HID :].astype(BF)
        send_ref[:, 2 * HID :] = jnp.zeros((rows, 256), BF)

    outs = [struct((rows, 2 * HID), F32), struct((rows, 2 * HID + 256), BF)]
    return simple("total_feed", body, scalars, sums, outs, 2)


def total_projection(scalars, sums):
    rows, width = sums[0].shape
    wide = 3 * HALF
    last = wide + HALF

    def body(_, *refs):
        keep_ref, send_ref = refs[-2:]
        total = refs[0][:, :last]
        for ref in refs[1:-2]:
            total = total + ref[:, :last].astype(F32)
        near, far = [], []
        for kind in range(3):
            both = [total[:, (3 * p + kind) * PAIR : (3 * p + kind + 1) * PAIR] for p in range(3)]
            both = jnp.concatenate(both, axis=1)
            near.append(both[:, :QUARTER])
            far.append(both[:, QUARTER:])
        near.append(total[:, wide : wide + QUARTER])
        far.append(total[:, wide + QUARTER : last])
        keep_ref[:, :D] = jnp.concatenate(near, axis=1)
        send_ref[:, :D] = jnp.concatenate(far, axis=1).astype(BF)
        if width > last:
            small = jnp.zeros((LABELS, 128), F32)
            for ref in refs[:-2]:
                small = small + whole_of(ref[:, last:])
            keep_ref[:, D:] = jnp.zeros((rows, 128), F32)
            send_ref[:, D:] = jnp.zeros((rows, 128), BF)
            keep_ref[:LABELS, D:] = small
            send_ref[: 2 * LABELS, D:] = halves(small)

    width_out = D + width - last
    outs = [struct((rows, width_out), F32), struct((rows, width_out), BF)]
    return simple("total_projection", body, scalars, sums, outs, 2)


def finish_feed(scalars, keep, received):
    rows = keep.shape[0]

    def body(_, keep_ref, recv_ref, up_ref, down_ref):
        up_ref[...] = keep_ref[:, :HID] + recv_ref[:, :HID].astype(F32)
        down_ref[...] = keep_ref[:, HID:] + recv_ref[:, HID : 2 * HID].astype(F32)

    outs = [struct((rows, HID), F32)] * 2
    return simple("finish_feed", body, scalars, [keep, received], outs, FEED_MICROS)


def finish_projection(scalars, keep, received):
    rows, width = keep.shape

    def body(_, keep_ref, recv_ref, *refs):
        total = keep_ref[:, :D] + recv_ref[:, :D].astype(F32)
        for k in range(4):
            refs[k][...] = total[:, k * QUARTER : (k + 1) * QUARTER]
        if width > D:
            small = keep_ref[:LABELS, D:] + whole_of(recv_ref[:, D:])
            for k in range(VECS):
                refs[4 + k][...] = small[k, :BLOCK]
            for k in range(SHARE):
                refs[4 + VECS][k * 128 : (k + 1) * 128] = small[VECS + k]

    outs = [struct((rows, QUARTER), F32)] * 4
    if width > D:
        outs += [struct((BLOCK,), F32)] * VECS + [struct((FF // GROUPS,), F32)]
    return simple("finish_projection", body, scalars, [keep, received], outs)


def small_sums(scalars, sums_one, sums_two, sums_hidden, sums_projection):
    def body(sc, one_ref, two_ref, hidden_ref, projection_ref, out_ref, wide_ref, tall_ref):
        out_ref[...] = jnp.zeros_like(out_ref)
        lanes = lax.broadcasted_iota(jnp.int32, (1, D), 1)
        near, far = lanes < QUARTER, (lanes >= QUARTER) & (lanes < HALF)
        for row, kind in ((0, 0), (1, 2)):
            line = jnp.concatenate(
                [
                    projection_ref[0:1, (3 * p + kind) * PAIR : (3 * p + kind + 1) * PAIR]
                    for p in range(3)
                ]
                + [jnp.zeros((1, HALF), F32)],
                axis=1,
            )
            low = pltpu.roll(jnp.broadcast_to(jnp.where(near, line, 0.0), (8, D)), sc[2] * QUARTER, 1)
            high = jnp.broadcast_to(jnp.where(far, line, 0.0), (8, D))
            high = pltpu.roll(high, turn((sc[2] ^ 2) - 1), 1)
            wide_ref[row : row + 1, :] = (low + high)[0:1]
        wide_ref[2:3, :] = one_ref[2:3, :]
        wide_ref[3:5, :] = one_ref[0:2, :]
        wide_ref[5:6, :] = two_ref[2:3, :]
        wide_ref[6:8, :] = two_ref[0:2, :]
        tall_ref[...] = jnp.zeros_like(tall_ref)
        for k in range(2):
            to = pl.multiple_of((sc[2] ^ (2 * k)) * HID, 128)
            tall_ref[0:1, pl.ds(to, HID)] = hidden_ref[0:1, k * HID : (k + 1) * HID]
        share = FF // GROUPS
        for d in range(GROUPS):
            out_ref[d, :VECS, :BLOCK] = wide_ref[:, d * BLOCK : (d + 1) * BLOCK]
            for c in range(share // 128):
                at = d * share + c * 128
                out_ref[d, VECS + c : VECS + c + 1, :] = tall_ref[0:1, at : at + 128]

    operands = [sums_one, sums_two, sums_hidden, sums_projection]
    shape = (GROUPS, LABELS, 128)
    return call(
        "small_sums",
        body,
        scalars,
        operands,
        [whole(o.shape) for o in operands],
        [struct(shape, F32)],
        [whole(shape)],
        (1,),
        [pltpu.VMEM((VECS, D), F32), pltpu.VMEM((8, FF), F32)],
    )[0]


def per_device(
    tokens,
    segments,
    query_weight,
    key_weight,
    value_weight,
    output_weight,
    query_bias,
    value_bias,
    output_bias,
    first_gain,
    first_shift,
    up_weight,
    up_bias,
    down_weight,
    down_bias,
    second_gain,
    second_shift,
    cotangent,
):
    seq_count = lax.axis_size("seq")
    count = lax.axis_size("dp")
    place_z = lax.axis_index("seq")
    assert seq_count == 4
    direct = count == GROUPS
    rows = tokens.shape[1]
    piece_rows = query_weight.shape[0]
    near = (place_z == 1) | (place_z == 2)
    base = lax.axis_index("dp") if direct else 0
    scalars = jnp.stack([near, base, place_z]).astype(jnp.int32)

    own = tokens[0]
    cot_own = cotangent[0]
    lines = [
        query_bias,
        value_bias,
        output_bias,
        first_gain,
        first_shift,
        down_bias,
        second_gain,
        second_shift,
    ]
    lines = lines if direct else []
    first_send, mine, wide, labelled, own_docs = pack_inputs(
        scalars,
        [query_weight, key_weight, value_weight, output_weight],
        own,
        segments,
        up_weight,
        down_weight.T,
        lines,
        up_bias,
    )
    arrived = swap(first_send, "seq", 2)
    side = swap(output_weight, "seq", 1)
    if direct:
        mine_chip = [mine, swap(mine, "dp", 2), swap(mine, "dp", 4)]
        wide_last = swap(wide, "dp", 6)
        labelled, side, wide_last, mine_chip, arrived = together(
            labelled, side, wide_last, mine_chip, arrived
        )
    else:
        arrived, labelled, side = together(arrived, labelled, side)
    narrow_far, both, partner_send = split_arrived(scalars, arrived, mine, labelled)
    partner = swap(partner_send, "seq", 1)
    halo_near = lax.ppermute(labelled, "seq", [(1, 2), (2, 1)])
    if direct:
        far_chip = [narrow_far, swap(narrow_far, "dp", 2), swap(narrow_far, "dp", 4)]
        both_far = swap(both, "dp", 6)
        mine_chip, cot_own, far_chip, both_far, partner, halo_near = together(
            mine_chip, cot_own, far_chip, both_far, partner, halo_near
        )
        stacked = stack_narrow(scalars, mine_chip, far_chip, both_far)
        pieces = [stacked, swap(stacked, "dp", 1)]
        feed_chip = chip_pieces(pack_feed(scalars, first_send, arrived, side, partner))
    halo_far = lax.ppermute(halo_near, "seq", [(1, 0), (2, 3)])
    if not direct:
        vectors = jnp.stack(
            [
                query_bias,
                value_bias,
                output_bias,
                first_gain,
                first_shift,
                down_bias,
                second_gain,
                second_shift,
            ]
        )
        lines = lax.all_gather(vectors, "dp", axis=1, tiled=True).reshape(VECS, GROUPS, BLOCK)
        lines = jnp.pad(lines, ((0, 0), (0, 0), (0, 128 - BLOCK)))
        tall = lax.all_gather(up_bias, "dp", axis=0, tiled=True).reshape(GROUPS, SHARE, 128).transpose(1, 0, 2)
        lines = jnp.concatenate([lines, tall], axis=0)
        lines = jnp.pad(lines, ((0, LABELS - VECS - SHARE), (0, 0), (0, 3 * QUARTER - 128)))
        lines = lines.transpose(1, 0, 2)
        gathered = gather_rows(mine)
        pieces = [
            jnp.concatenate([half[:, :, 2 * HID :], lines[k::2], far], axis=1)
            for k, (half, far) in enumerate(zip(gathered, gather_rows(narrow_far)))
        ]
        last = swap(arrived[:, 3 * QUARTER : D], "seq", 1)
        feed = gather_rows(pack_feed(scalars, first_send, arrived, side, last))
        weights = [
            jnp.concatenate([half[:, :, : 2 * HID], far], axis=2) for half, far in zip(gathered, feed)
        ]

    def rows_of(keep, send):
        return jnp.stack([keep, send], axis=1).reshape(GROUPS, -1, keep.shape[2]).astype(F32)

    def spread(sums):
        return [sums[0]] + [swap(sums[k], "dp", 2 * k) for k in range(1, len(sums))]

    def scattered(table):
        return [lax.psum_scatter(table, "dp", scatter_dimension=0, tiled=True)]

    *pair, ctx_far, x, weight, hot, vecs, hidden_bias, bias, log_far, scaled_far = attend_pair(
        scalars, own, partner, own_docs, pieces, rows
    )
    if direct:
        pair, ctx_far, cot_own, halo_far = together(pair, ctx_far, cot_own, halo_far)
    *halo, ctx_near, scaled_near, hot, log_near = attend_halo(scalars, halo_near, halo_far, weight, bias, hot, *pair, rows)
    ctx_mine = [ctx_far, ctx_near]
    ctx_partner = [swap(ctx_far, "seq", 1), None]
    if direct:
        ctx_mine[1], ctx_partner[0], wide_last, feed_chip = together(
            ctx_mine[1], ctx_partner[0], wide_last, feed_chip
        )
        stacked = stack_wide(scalars, mine_chip, wide_last, feed_chip)
        weights = [stacked, swap(stacked, "dp", 1)]
    ctx_partner[1] = swap(ctx_mine[1], "seq", 1)
    cot_partner = swap(cot_own, "seq", 1)

    forward, slopes, part_far = [None, None], [None, None], [None, None]
    for block in (1, 0):
        forward[block], weights = feed_forward(
            scalars, block, ctx_mine[block], ctx_partner[block], x, vecs, hidden_bias, weights, rows
        )
        part_far[block] = swap(forward[block][5], "seq", 1)
    up, down, out_mine, _ = weights
    second, second_shared, first_part_far = [None, None], [], [None, None]
    for block in (1, 0):
        slopes[block] = gelu_slope(scalars, forward[block][3])
    for block in (1, 0):
        second[block], second_shared = second_norm(
            scalars,
            block,
            forward[block][5],
            part_far[block],
            forward[block][0],
            slopes[block],
            (cot_own, cot_partner),
            vecs,
            up,
            down,
            second_shared,
            rows,
        )
        if block == 1:
            first_part_far[block] = swap(second[block][3], "seq", 1)
    feed_parts = feed_forward_grads(
        scalars,
        [(forward[k][2], second[k][2], second[k][1], forward[k][4]) for k in range(2)],
        rows,
    )
    first_part_far[1], second, second_shared, feed_parts = together(
        first_part_far[1], second, second_shared, feed_parts
    )
    first_part_far[0] = swap(second[0][3], "seq", 1)
    layer_output, sums_two, sums_hidden = second_shared
    attention_grad, ctx_grad, inners, first_shared = [None, None], [None, None], [None, None], []
    logs, scaled = [log_far, log_near], [scaled_far, scaled_near]

    def finish(block):
        attention_grad[block], ctx_grad[block], inners[block], *shared = first_norm(
            scalars,
            block,
            second[block][3],
            first_part_far[block],
            second[block][0],
            forward[block][0],
            forward[block][1],
            vecs,
            out_mine,
            scaled[block],
            logs[block],
            first_shared,
            rows,
        )
        return shared

    *first_shared, halo_send = finish(1)
    halo_grad = swap(halo_send, "seq", 2)
    if direct:
        feed_sums = combine(scalars, feed_parts[0], swap(feed_parts[1], "dp", 1))
        feed_sums = spread(feed_sums)
    else:
        feed_sums = scattered(rows_of(*feed_parts).reshape(D, -1))
    own_grad, sums_one = finish(0)

    grads, input_keep, input_send, sums_projection = attend_backward(
        scalars, pair, halo, [*ctx_grad, halo_grad], logs, inners, hot, weight, rows
    )
    input_far = swap(input_send, "seq", 1)
    small = small_sums(scalars, sums_one, sums_two, sums_hidden, sums_projection)
    small_side = swap(small, "seq", 1)
    projection_parts = projection_grads(scalars, x, grads, rows)
    projection_parts, small_side, feed_sums = together(projection_parts, small_side, feed_sums)
    if direct:
        feed_keep, feed_send = total_feed(scalars, feed_sums)
        attention_grad, feed_send = together(attention_grad, feed_send)
    out_blocks = [(ctx_mine[k], ctx_partner[k], attention_grad[k]) for k in range(2)]
    if direct:
        projection_received = swap(projection_parts[1], "dp", 1)
        out_parts = output_grads(scalars, out_blocks, small, small_side)
        out_received = swap(out_parts[1], "dp", 1)
        feed_far = swap(feed_send, "seq", 2)
        sums = spread(
            combine_both(scalars, projection_parts[0], projection_received, out_parts[0], out_received)
        )
    else:
        out_parts = rows_of(*output_grads(scalars, out_blocks, small, small_side))
        sums = scattered(
            jnp.concatenate(
                [rows_of(*projection_parts).reshape(D, -1), out_parts[:, :, :HALF].reshape(D, -1)], axis=1
            )
        )
        feed_keep, feed_send = total_feed(scalars, feed_sums)
        feed_far = swap(feed_send, "seq", 2)
    if direct:
        sums, feed_far, input_far = together(sums, feed_far, input_far)
    keep, send = total_projection(scalars, sums)
    received = swap(send, "seq", 2)
    up_grad, down_grad = finish_feed(scalars, feed_keep, feed_far)
    input_grad = own_grad + input_keep + input_far.astype(F32)
    if direct:
        received, up_grad, input_grad = together(received, up_grad, input_grad)
    projections = list(finish_projection(scalars, keep, received))
    if direct:
        projections, vec, tall_lines = projections[:4], projections[4:-1], projections[-1]
    else:
        tile = out_parts[:, :LABELS, HALF:] + out_parts[:, LABELS : 2 * LABELS, HALF:]
        tile = tile + swap(tile, "seq", 2)
        wide_lines = tile[:, :VECS, :BLOCK].transpose(1, 0, 2).reshape(VECS, D)
        wide_lines = lax.psum_scatter(wide_lines, "dp", scatter_dimension=1, tiled=True)
        tall_lines = lax.psum_scatter(tile[:, VECS : VECS + 3].reshape(-1), "dp", tiled=True)
        vec = [wide_lines[k] for k in range(VECS)]
    return (
        layer_output[None],
        input_grad[None],
        *projections,
        vec[0],
        vec[1],
        vec[2],
        vec[3],
        vec[4],
        up_grad,
        tall_lines,
        down_grad.T,
        vec[5],
        vec[6],
        vec[7],
    )


def solution(mesh):
    placed = (
        P("dp", "seq", None),
        P("dp", "seq"),
        P("dp", "seq"),
        P("dp", "seq"),
        P("dp", "seq"),
        P("dp", "seq"),
        P("dp"),
        P("dp"),
        P("dp"),
        P("dp"),
        P("dp"),
        P("dp", "seq"),
        P("dp"),
        P("seq", "dp"),
        P("dp"),
        P("dp"),
        P("dp"),
        P("dp", "seq", None),
    )
    return jax.shard_map(
        per_device,
        mesh=mesh,
        in_specs=placed,
        out_specs=(
            P("dp", "seq", None),
            P("dp", "seq", None),
            P("dp", "seq"),
            P("dp", "seq"),
            P("dp", "seq"),
            P("dp", "seq"),
            P("dp"),
            P("dp"),
            P("dp"),
            P("dp"),
            P("dp"),
            P("dp", "seq"),
            P("dp"),
            P("seq", "dp"),
            P("dp"),
            P("dp"),
            P("dp"),
        ),
        check_vma=False,
    )
```

```python
import jax
import jax.numpy as jnp
from jax import lax
from jax.experimental import pallas as pl
from jax.experimental.pallas import tpu as pltpu
from jax.sharding import PartitionSpec as P

D = 768
HEADS = 12
HEAD_DIM = 64
FF = 3072
EPS = 1e-05
MASKED = 1e30
PAIR = 2 * HEAD_DIM
QUARTER = D // 4
HALF = D // 2
HID = FF // 4
VECS = 8
GROUPS = 8
SHARE = FF // GROUPS // 128
BLOCK = D // GROUPS
LABELS = 16
MARKS = 48
MICROS = 450
FEED_MICROS = 300
BF = jnp.bfloat16
F32 = jnp.float32
ROOT_HALF = 0.7071067811865476
ROOT_TWO_PI = 0.3989422804014327


def dot(a, b):
    return lax.dot_general(a, b, (((1,), (0,)), ((), ())), preferred_element_type=F32)


def dot_nt(a, b):
    return lax.dot_general(a, b, (((1,), (1,)), ((), ())), preferred_element_type=F32)


def dot_tn(a, b):
    return lax.dot_general(a, b, (((0,), (0,)), ((), ())), preferred_element_type=F32)


def swap(value, axis, mask):
    count = lax.axis_size(axis)
    return lax.ppermute(value, axis, [(k, k ^ mask) for k in range(count)])


def together(*values):
    return lax.optimization_barrier(values)


def whole(shape):
    return pl.BlockSpec(shape, lambda *_: (0,) * len(shape))


def params():
    return pltpu.CompilerParams(vmem_limit_bytes=22 * 1024 * 1024)


def call(name, body, scalars, operands, in_specs, outs, out_specs, grid, scratch=(), micros=1):
    spec = pltpu.PrefetchScalarGridSpec(
        num_scalar_prefetch=1,
        grid=grid,
        in_specs=in_specs,
        out_specs=out_specs,
        scratch_shapes=list(scratch),
    )
    return pl.pallas_call(
        body,
        out_shape=outs,
        grid_spec=spec,
        compiler_params=params(),
        cost_estimate=pl.CostEstimate(
            flops=int(micros * 1.0e7), transcendentals=0, bytes_accessed=1024
        ),
        name=name,
    )(scalars, *operands)


def turn(quarters):
    return lax.rem(quarters + 4, 4) * QUARTER


def struct(shape, dtype):
    return jax.ShapeDtypeStruct(shape, dtype)


def chip_pieces(piece):
    return [piece] + [swap(piece, "dp", j) for j in range(2, GROUPS, 2)]


def gather_rows(piece):
    full = lax.all_gather(piece, "dp", axis=0, tiled=True)
    full = full.reshape(GROUPS, D // GROUPS, piece.shape[1])
    return [full[0::2], full[1::2]]


def place(target, pair, base, source_cols, target_cols):
    for j in range(GROUPS):
        start = pl.multiple_of((base ^ j) * BLOCK, 16)
        target[pl.ds(start, BLOCK), target_cols] = pair[j % 2][j // 2, :BLOCK, source_cols]


def split_rows(result, base, keep, send):
    for j in range(GROUPS):
        block = result[pl.ds(pl.multiple_of((base ^ j) * BLOCK, 16), BLOCK), :].astype(BF)
        if j % 2:
            send[j // 2] = block
        else:
            keep[j // 2] = block


def simple(name, body, scalars, operands, outs, micros=1):
    return call(
        name,
        body,
        scalars,
        operands,
        [whole(o.shape) for o in operands],
        outs,
        [whole(o.shape) for o in outs],
        (1,),
        micros=micros,
    )


def pack_inputs(scalars, tables, tokens, segments, up, down, lines, tall):
    rows = tokens.shape[0]
    height = tables[0].shape[0]
    skip = 2 * HID + (128 if lines else 0)
    operands = list(tables) + [tokens, segments, up, down] + lines + ([tall] if lines else [])
    count = len(operands)

    def body(_, *refs):
        sources, (send_ref, mine_ref, wide_ref, label_ref, docs_ref), refs = (
            refs[:count],
            refs[count : count + 5],
            refs[count + 5 :],
        )
        copies = [pltpu.make_async_copy(a, b, refs[-1].at[k]) for k, (a, b) in enumerate(zip(sources, refs))]
        for copy in copies:
            copy.start()
        for copy in copies:
            copy.wait()
        joined = jnp.concatenate([ref[...].astype(F32) for ref in refs[:4]], axis=1).astype(BF)
        send_ref[:, :D] = joined
        send_ref[:, D : D + HID] = refs[6][...]
        send_ref[:, D + HID :] = refs[7][...]
        mine_ref[:, :HID] = refs[6][...]
        mine_ref[:, HID : 2 * HID] = refs[7][...]
        part = joined[:, : 3 * QUARTER].astype(F32)
        mine_ref[:, skip:] = part.astype(BF)
        wide_ref[:, :HID] = refs[6][...]
        wide_ref[:, HID:] = refs[7][...]
        docs = refs[5][...].astype(F32)
        docs_ref[...] = docs
        label_ref[:rows, :] = refs[4][...]
        label_ref[rows:, :] = jnp.zeros((LABELS, D), BF)
        label_ref[rows:, :rows] = jnp.broadcast_to(docs, (LABELS, rows)).astype(BF)
        if lines:
            table = [ref[...].astype(F32)[None, :] for ref in refs[8 : 8 + VECS]]
            table = jnp.concatenate(table, axis=0)
            table = [jnp.concatenate([table, jnp.zeros((VECS, 128 - BLOCK), F32)], axis=1)]
            line = refs[8 + VECS][...].astype(F32)[None, :]
            table += [line[:, c * 128 : (c + 1) * 128] for c in range(SHARE)]
            table += [jnp.zeros((height - VECS - SHARE, 128), F32)]
            mine_ref[:, 2 * HID : skip] = jnp.concatenate(table, axis=0).astype(BF)

    outs = [
        struct((height, D + 2 * HID), BF),
        struct((height, skip + 3 * QUARTER), BF),
        struct((height, 2 * HID), BF),
        struct((rows + LABELS, D), BF),
        struct((1, rows), F32),
    ]
    operands = [pltpu.with_memory_space_constraint(o, pltpu.MemorySpace.HBM) for o in operands]
    return call(
        "pack_inputs",
        body,
        scalars,
        operands,
        [pl.BlockSpec(memory_space=pltpu.MemorySpace.HBM)] * count,
        outs,
        [whole(o.shape) for o in outs],
        (1,),
        [pltpu.VMEM(o.shape, o.dtype) for o in operands] + [pltpu.SemaphoreType.DMA((count,))],
    )


def split_arrived(scalars, arrived, mine, labelled):
    rows = arrived.shape[0]
    tall = rows + LABELS
    skip = mine.shape[1] - 3 * QUARTER
    direct = skip > 2 * HID
    known = labelled.shape[0]

    def body(_, far_ref, mine_ref, label_ref, narrow_ref, both_ref, send_ref):
        narrow_ref[...] = far_ref[:, : 3 * QUARTER]
        both_ref[:rows, :] = mine_ref[:, skip:]
        both_ref[tall:, :] = far_ref[:, : 3 * QUARTER]
        send_ref[:known, :] = label_ref[...]
        if direct:
            both_ref[rows:tall, :] = jnp.zeros((LABELS, 3 * QUARTER), BF)
            both_ref[rows:tall, :128] = mine_ref[:LABELS, 2 * HID : skip]
            part = far_ref[:, 3 * QUARTER : D].astype(F32)
            step = rows // 4
            part = jnp.concatenate([part[k * step : (k + 1) * step] for k in range(4)], axis=1)
            part = jnp.concatenate([part, jnp.zeros((MARKS - LABELS - step, D), F32)], axis=0)
            send_ref[known:, :] = part.astype(BF)

    outs = [
        struct((rows, 3 * QUARTER), BF),
        struct((rows + tall, 3 * QUARTER), BF),
        struct((known + (MARKS - LABELS if direct else 0), D), BF),
    ]
    return simple("split_arrived", body, scalars, [arrived, mine, labelled], outs)


def stack_narrow(scalars, mine_chip, far_chip, both_far):
    rows = far_chip[0].shape[0]
    tall = rows + LABELS
    skip = mine_chip[0].shape[1] - 3 * QUARTER

    def body(_, *refs):
        out_ref = refs[-1]
        for k in range(3):
            out_ref[k, :rows] = refs[k][:, skip:]
            out_ref[k, rows:tall] = jnp.zeros((LABELS, 3 * QUARTER), BF)
            out_ref[k, rows:tall, :128] = refs[k][:LABELS, 2 * HID : skip]
            out_ref[k, tall:] = refs[3 + k][...]
        out_ref[3] = refs[6][...]

    shape = (GROUPS // 2, tall + rows, 3 * QUARTER)
    operands = [*mine_chip, *far_chip, both_far]
    return simple("stack_narrow", body, scalars, operands, [struct(shape, BF)])[0]


def stack_wide(scalars, mine_chip, last, feed_chip):
    def body(_, *refs):
        out_ref = refs[-1]
        for k in range(3):
            out_ref[k, :, : 2 * HID] = refs[k][:BLOCK, : 2 * HID]
        out_ref[3, :, : 2 * HID] = refs[3][...]
        for k in range(4):
            out_ref[k, :, 2 * HID :] = refs[4 + k][...]

    shape = (GROUPS // 2, BLOCK, 4 * HID + D)
    return simple("stack_wide", body, scalars, [*mine_chip, last, *feed_chip], [struct(shape, BF)])[0]


def pack_feed(scalars, first_send, arrived, side, last):
    rows = arrived.shape[0]
    columns = slice(3 * QUARTER, D)

    def body(sc, own_ref, arrived_ref, side_ref, last_ref, out_ref):
        out_ref[:, : 2 * HID] = arrived_ref[:, D:]
        final = last_ref[...].astype(F32)
        if last.shape[1] == D:
            step = rows // 4
            final = final[last.shape[0] - MARKS + LABELS :]
            final = [final[:step, k * QUARTER : (k + 1) * QUARTER] for k in range(4)]
            final = jnp.concatenate(final, axis=0)
        total = jnp.zeros((rows, D), F32)
        for k, part in enumerate([own_ref[:, columns], side_ref[...], arrived_ref[:, columns], final]):
            part = jnp.concatenate([part.astype(F32), jnp.zeros((rows, D - QUARTER), F32)], axis=1)
            total = total + pltpu.roll(part, (sc[2] ^ k) * QUARTER, 1)
        out_ref[:, 2 * HID :] = total.astype(BF)

    out = struct((rows, 2 * HID + D), BF)
    return simple("pack_feed", body, scalars, [first_send, arrived, side, last], [out])[0]


def mark(docs, rows):
    number = lax.broadcasted_iota(jnp.int32, (LABELS, rows), 0).astype(F32)
    return jnp.where(jnp.broadcast_to(docs, (LABELS, rows)) == number, 1.0, 0.0).astype(BF)


def attend(query, key, value, mask, log_ref, step):
    lane = lax.broadcasted_iota(jnp.int32, (1, PAIR), 1)
    total = jnp.zeros(query.shape, F32)
    scaled = jnp.zeros(query.shape, F32)
    logs = jnp.zeros(query.shape, F32)
    value = jnp.concatenate([value, jnp.ones(value.shape, BF)], axis=1)
    for head in range(2):
        part = jnp.where((lane // HEAD_DIM) == head, 1.0, 0.0)
        mine = (query.astype(F32) * (part * HEAD_DIM**-0.5)).astype(BF)
        scores = dot_nt(mine, key) + mask
        top = jnp.max(scores, axis=-1, keepdims=True)
        expo = jnp.exp(scores - top)
        whole_sum = jnp.sum(expo, axis=-1, keepdims=True)
        probs = expo * (1.0 / whole_sum)
        rounded = probs.astype(BF)
        context = dot(rounded, value)
        total = total + context[:, :PAIR] * part
        scaled = scaled + context[:, :PAIR] * part / context[:, PAIR:]
        logs = jnp.where(lane == head, top + jnp.log(whole_sum), logs)
    turned = logs.T
    for head in range(2):
        log_ref[pl.ds(2 * step + head, 1), :] = turned[head : head + 1, :]
    return total.astype(BF), scaled


def column(height):
    return pl.BlockSpec((height, PAIR), lambda p, _: (0, p))


def attend_pair(scalars, own, partner, own_docs, pieces, rows):
    base = 2 * rows
    tall = BLOCK + LABELS

    def body(sc, own_ref, partner_ref, docs_ref, *refs):
        weight_refs, refs = refs[:2], refs[2:]
        q_ref, k_ref, v_ref, ctx_ref, x_ref, w_ref, hot_ref, vec_ref, hidden_ref, bias_ref, log_ref, *refs = refs
        scaled_ref, mask_ref = refs
        step = pl.program_id(0)

        @pl.when(step == 0)
        def _():
            near = sc[0]
            own_at = pl.multiple_of(near * rows, rows)
            partner_at = pl.multiple_of((1 - near) * rows, rows)
            x_ref[pl.ds(own_at, rows), :] = own_ref[...]
            x_ref[pl.ds(partner_at, rows), :] = partner_ref[:rows, :]
            hot_ref[:, pl.ds(own_at, rows)] = mark(docs_ref[...], rows)
            docs = partner_ref[rows : rows + 1, :rows].astype(F32)
            hot_ref[:, pl.ds(partner_at, rows)] = mark(docs, rows)
            for j in range(GROUPS):
                at = pl.ds(pl.multiple_of((sc[1] ^ j) * BLOCK, 16), BLOCK)
                for kind in range(3):
                    part = slice(kind * QUARTER, (kind + 1) * QUARTER)
                    both = [weight_refs[j % 2][j // 2, top : top + BLOCK, part] for top in (0, tall)]
                    both = [half.astype(F32) for half in both]
                    both = jnp.concatenate(both, axis=1).astype(BF)
                    for p in range(3):
                        to = (3 * p + kind) * PAIR
                        w_ref[at, to : to + PAIR] = both[:, p * PAIR : (p + 1) * PAIR]
            hot = hot_ref[...]
            mask_ref[...] = (dot_tn(hot[:, :rows], hot) - 1.0) * MASKED
            vectors = jnp.zeros((LABELS, D), F32)
            for j in range(GROUPS):
                block = sc[1] ^ j
                line = weight_refs[j % 2][j // 2, BLOCK:tall, :128].astype(F32)
                table = jnp.where(lax.broadcasted_iota(jnp.int32, line.shape, 1) < BLOCK, line, 0.0)
                table = jnp.concatenate([table, jnp.zeros((LABELS, D - 128), F32)], axis=1)
                vectors = vectors + pltpu.roll(table, block * BLOCK, 1)
                quarter = block // 2
                for k in range(2):

                    @pl.when(quarter == sc[2] ^ (2 * k))
                    def _():
                        for c in range(SHARE):
                            to = pl.multiple_of((block % 2) * (HID // 2) + k * HID + c * 128, 128)
                            value = jnp.broadcast_to(line[VECS + c : VECS + c + 1], (VECS, 128))
                            hidden_ref[:, pl.ds(to, 128)] = value

            vec_ref[...] = vectors[:VECS]
            lanes = lax.broadcasted_iota(jnp.int32, (VECS, HALF), 1)
            low = pltpu.roll(vectors[:VECS], turn(-sc[2]), 1)[:, :HALF]
            high = pltpu.roll(vectors[:VECS], turn(1 - (sc[2] ^ 2)), 1)[:, :HALF]
            bias_ref[...] = jnp.where(lanes < QUARTER, low, high)
            log_ref[...] = jnp.zeros_like(log_ref)

        at = pl.multiple_of(step * 3 * PAIR, PAIR)
        both = dot(x_ref[...], w_ref[:, pl.ds(at, 3 * PAIR)])
        bias = bias_ref[:, pl.ds(pl.multiple_of(step * PAIR, PAIR), PAIR)]
        query = (both[:, :PAIR] + bias[0:1]).astype(BF)
        key = both[:, PAIR : 2 * PAIR].astype(BF)
        value = (both[:, 2 * PAIR :] + bias[1:2]).astype(BF)
        q_ref[...] = query
        k_ref[...] = key
        v_ref[...] = value
        ctx_ref[...], scaled_ref[...] = attend(query[:rows], key, value, mask_ref[...], log_ref, step)

    operands = [own, partner, own_docs, *pieces]
    in_specs = [whole(o.shape) for o in operands]
    outs = [
        struct((base, HALF), BF),
        struct((base, HALF), BF),
        struct((base, HALF), BF),
        struct((rows, HALF), BF),
        struct((base, D), BF),
        struct((D, 3 * HALF), BF),
        struct((LABELS, base), BF),
        struct((VECS, D), F32),
        struct((VECS, 2 * HID), F32),
        struct((VECS, HALF), F32),
        struct((VECS, rows), F32),
        struct((rows, HALF), F32),
    ]
    out_specs = [column(base)] * 3 + [column(rows)] + [whole(o.shape) for o in outs[4:-1]] + [column(rows)]
    return call(
        "attend_pair",
        body,
        scalars,
        operands,
        in_specs,
        outs,
        out_specs,
        (HALF // PAIR,),
        [pltpu.VMEM((rows, base), F32)],
        micros=8,
    )


def attend_halo(scalars, halo_near, halo_far, weight, bias, hot, query, key, value, rows):
    def body(sc, near_ref, far_ref, w_ref, bias_ref, hot_ref, q_ref, k_ref, v_ref, *refs):
        halo_refs, (ctx_ref, scaled_ref, all_ref, log_ref, x_ref, mask_ref) = refs[:3], refs[3:]

        @pl.when(pl.program_id(0) == 0)
        def _():
            all_ref[:, : 2 * rows] = hot_ref[...]

            def halo(ref):
                x_ref[...] = ref[:rows, :]
                all_ref[:, 2 * rows :] = mark(ref[rows : rows + 1, :rows].astype(F32), rows)

            pl.when(sc[0] == 1)(lambda: halo(near_ref))
            pl.when(sc[0] == 0)(lambda: halo(far_ref))
            mask_ref[...] = (dot_tn(all_ref[:, rows : 2 * rows], all_ref[...]) - 1.0) * MASKED
            log_ref[...] = jnp.zeros_like(log_ref)

        both = dot(x_ref[...], w_ref[...])
        parts = [
            (both[:, :PAIR] + bias_ref[0:1, :]).astype(BF),
            both[:, PAIR : 2 * PAIR].astype(BF),
            (both[:, 2 * PAIR :] + bias_ref[1:2, :]).astype(BF),
        ]
        for ref, part in zip(halo_refs, parts):
            ref[...] = part
        keys = jnp.concatenate([k_ref[...], parts[1]], axis=0)
        values = jnp.concatenate([v_ref[...], parts[2]], axis=0)
        ctx_ref[...], scaled_ref[...] = attend(
            q_ref[rows:, :], keys, values, mask_ref[...], log_ref, pl.program_id(0)
        )

    operands = [halo_near, halo_far, weight, bias, hot, query, key, value]
    in_specs = [whole(o.shape) for o in operands]
    in_specs[2] = pl.BlockSpec((D, 3 * PAIR), lambda p, _: (0, p))
    in_specs[3] = column(VECS)
    in_specs[5:] = [column(2 * rows)] * 3
    outs = [struct((rows, HALF), BF)] * 4 + [struct((rows, HALF), F32)]
    outs += [struct((LABELS, 3 * rows), BF), struct((VECS, rows), F32)]
    return call(
        "attend_halo",
        body,
        scalars,
        operands,
        in_specs,
        outs,
        [column(rows)] * 5 + [whole((LABELS, 3 * rows)), whole((VECS, rows))],
        (HALF // PAIR,),
        [pltpu.VMEM((rows, D), BF), pltpu.VMEM((rows, 3 * rows), F32)],
        micros=6,
    )


def feed_forward(scalars, block, ctx_mine, ctx_partner, x, vecs, up_bias, weights, rows):
    count = len(weights)
    fresh = len(weights[0].shape) == 3

    def body(sc, mine_ref, partner_ref, x_ref, vec_ref, bias_ref, *refs):
        weight_refs, refs = refs[:count], refs[count:]
        (norm_ref, inv_ref, first_ref, gate_ref, active_ref, part_ref), refs = refs[:6], refs[6:]
        if fresh:
            up_ref, down_ref, out_ref, other_ref, full_ref = refs
            for k in range(2):
                at, to = 2 * k * HID, slice(k * HID, (k + 1) * HID)
                place(up_ref, weight_refs, sc[1], slice(at, at + HID), to)
                place(down_ref, weight_refs, sc[1], slice(at + HID, at + 2 * HID), to)
            place(full_ref, weight_refs, sc[1], slice(4 * HID, 4 * HID + D), slice(None))
            for ref, flip in ((out_ref, 0), (other_ref, 1)):
                for k in range(2):
                    at = pl.multiple_of((sc[2] ^ flip ^ (2 * k)) * QUARTER, 16)
                    ref[k * QUARTER : (k + 1) * QUARTER, :] = full_ref[pl.ds(at, QUARTER), :]
        else:
            up_ref, down_ref, out_ref, other_ref = weight_refs

        attention = dot(mine_ref[...], out_ref[...]) + dot(partner_ref[...], other_ref[...])
        total = x_ref[...].astype(F32) + (attention + vec_ref[2:3, :])
        center = total - jnp.mean(total, axis=-1, keepdims=True)
        inverse = lax.rsqrt(jnp.mean(center * center, axis=-1, keepdims=True) + EPS)
        normed = center * inverse
        norm_ref[...] = normed
        inv_ref[...] = jnp.broadcast_to(inverse, (rows, 128))
        first = (normed * vec_ref[3:4, :] + vec_ref[4:5, :]).astype(BF)
        first_ref[...] = first
        gate = dot(first, up_ref[...]) + bias_ref[0:1, :]
        gate_ref[...] = gate
        active = (gate * (1.0 + lax.erf(gate * ROOT_HALF)) * 0.5).astype(BF)
        active_ref[...] = active
        part_ref[...] = dot_nt(active, down_ref[...]).astype(BF)

    operands = [ctx_mine, ctx_partner, x, vecs, up_bias, *weights]
    in_specs = [whole(o.shape) for o in operands]
    in_specs[2] = pl.BlockSpec((rows, D), lambda *_: (block, 0))
    outs = [
        struct((rows, D), F32),
        struct((rows, 128), F32),
        struct((rows, D), BF),
        struct((rows, 2 * HID), F32),
        struct((rows, 2 * HID), BF),
        struct((rows, D), BF),
    ]
    scratch = []
    if fresh:
        outs += [struct((D, 2 * HID), BF)] * 2 + [struct((HALF, D), BF)] * 2
        scratch = [pltpu.VMEM((D, D), BF)]
    results = call(
        "feed_forward",
        body,
        scalars,
        operands,
        in_specs,
        outs,
        [whole(o.shape) for o in outs],
        (1,),
        scratch,
        micros=6,
    )
    return results[:6], (results[6:] if fresh else weights)


def gelu_slope(scalars, gate):
    rows = gate.shape[0] // 2

    def body(_, gate_ref, slope_ref):
        gate_here = gate_ref[...]
        bell = jnp.exp(gate_here * gate_here * -0.5) * ROOT_TWO_PI
        slope_ref[...] = 0.5 * (1.0 + lax.erf(gate_here * ROOT_HALF)) + gate_here * bell

    spec = pl.BlockSpec((rows, gate.shape[1]), lambda r, _: (r, 0))
    return call(
        "gelu_slope", body, scalars, [gate], [spec], [struct(gate.shape, F32)], [spec], (2,), micros=3
    )[0]


def second_norm(scalars, block, part, received, normed, slope, cotangent, vecs, up, down, earlier, rows):
    def body(sc, part_ref, recv_ref, norm_ref, slope_ref, cot_ref, other_ref, vec_ref, up_ref, down_ref, *refs):
        old, refs = refs[: len(earlier)], refs[len(earlier) :]
        (total_grad_ref, branch_grad_ref, gate_grad_ref, first_part_ref, out_ref, sums_ref, bias_ref) = refs
        mine = sc[0] == block
        first = norm_ref[...] * vec_ref[3:4, :] + vec_ref[4:5, :]
        branch = part_ref[...].astype(F32) + recv_ref[...].astype(F32) + vec_ref[5:6, :]
        total = first + branch
        center = total - jnp.mean(total, axis=-1, keepdims=True)
        inverse = lax.rsqrt(jnp.mean(center * center, axis=-1, keepdims=True) + EPS)
        here = center * inverse
        upstream = jnp.where(mine, cot_ref[...].astype(F32), other_ref[...].astype(F32))
        scaled = upstream * vec_ref[6:7, :]
        inner = (
            scaled
            - jnp.mean(scaled, axis=-1, keepdims=True)
            - here * jnp.mean(scaled * here, axis=-1, keepdims=True)
        )
        total_grad = inner * inverse
        total_grad_ref[...] = total_grad
        branch_grad = total_grad.astype(BF)
        branch_grad_ref[...] = branch_grad
        gate_grad = (dot(branch_grad, down_ref[...]) * slope_ref[...]).astype(BF)
        gate_grad_ref[...] = gate_grad
        hidden = jnp.broadcast_to(jnp.sum(gate_grad.astype(F32), axis=0, keepdims=True), (8, 2 * HID))
        bias_ref[...] = hidden + old[2][...] if old else hidden
        first_part_ref[...] = dot_nt(gate_grad, up_ref[...]).astype(BF)

        @pl.when(mine)
        def _():
            out_ref[...] = (here * vec_ref[6:7, :] + vec_ref[7:8, :]).astype(BF)
            sums_ref[...] = jnp.zeros_like(sums_ref)
            sums_ref[0:1, :] = jnp.sum(upstream * here, axis=0, keepdims=True)
            sums_ref[1:2, :] = jnp.sum(upstream, axis=0, keepdims=True)
            sums_ref[2:3, :] = jnp.sum(branch_grad.astype(F32), axis=0, keepdims=True)

        if old:

            @pl.when(jnp.logical_not(mine))
            def _():
                out_ref[...] = old[0][...]
                sums_ref[...] = old[1][...]

        else:

            @pl.when(jnp.logical_not(mine))
            def _():
                out_ref[...] = jnp.zeros_like(out_ref)
                sums_ref[...] = jnp.zeros_like(sums_ref)

    operands = [part, received, normed, slope, *cotangent, vecs, up, down, *earlier]
    outs = [
        struct((rows, D), F32),
        struct((rows, D), BF),
        struct((rows, 2 * HID), BF),
        struct((rows, D), BF),
        struct((rows, D), BF),
        struct((8, D), F32),
        struct((8, 2 * HID), F32),
    ]
    results = call(
        "second_norm",
        body,
        scalars,
        operands,
        [whole(o.shape) for o in operands],
        outs,
        [whole(o.shape) for o in outs],
        (1,),
        micros=5,
    )
    return results[:4], results[4:]


def split_outs(width):
    return [struct((GROUPS // 2, BLOCK, width), BF)] * 2


def feed_forward_grads(scalars, blocks, rows):
    def body(sc, *refs):
        keep_ref, send_ref, result_ref = refs[-3:]
        step = pl.program_id(0)

        @pl.when(step % 2 == 0)
        def _():
            result_ref[...] = dot_tn(refs[0][...], refs[1][...]) + dot_tn(refs[4][...], refs[5][...])

        @pl.when(step % 2 == 1)
        def _():
            result_ref[...] = dot_tn(refs[2][...], refs[3][...]) + dot_tn(refs[6][...], refs[7][...])

        split_rows(result_ref, sc[1], keep_ref, send_ref)

    half = pl.BlockSpec((rows, HID), lambda c, _: (0, c // 2))
    outs = split_outs(4 * HID)
    out_specs = [pl.BlockSpec((GROUPS // 2, BLOCK, HID), lambda c, _: (0, 0, c))] * 2
    return call(
        "feed_forward_grads",
        body,
        scalars,
        [value for block in blocks for value in block],
        [whole((rows, D)), half] * 4,
        outs,
        out_specs,
        (4,),
        [pltpu.VMEM((D, HID), F32)],
        micros=8,
    )


def first_norm(
    scalars, block, part, received, total_grad, normed, inverse, vecs, out_weight, ctx, logs, earlier, rows
):
    def body(sc, part_ref, recv_ref, grad_ref, norm_ref, inv_ref, vec_ref, weight_ref, ctx_ref, log_ref, *refs):
        old, refs = refs[: len(earlier)], refs[len(earlier) :]
        attention_ref, context_ref, inner_ref, own_ref, sums_ref = refs[:5]
        mine = sc[0] == block
        upstream = grad_ref[...] + part_ref[...].astype(F32) + recv_ref[...].astype(F32)
        here = norm_ref[...]
        scaled = upstream * vec_ref[3:4, :]
        inner = (
            scaled
            - jnp.mean(scaled, axis=-1, keepdims=True)
            - here * jnp.mean(scaled * here, axis=-1, keepdims=True)
        )
        total = inner * inv_ref[:, :1]
        attention = total.astype(BF)
        attention_ref[...] = attention
        context = dot_nt(attention, weight_ref[...]).astype(BF)
        context_ref[...] = context
        lane = lax.broadcasted_iota(jnp.int32, (VECS, HALF), 1) // HEAD_DIM
        picks = jnp.where(lane == lax.broadcasted_iota(jnp.int32, (VECS, HALF), 0), 1.0, 0.0)
        products = context.astype(F32) * ctx_ref[...]
        inner = jnp.zeros((VECS, rows), F32)
        for _ in range(3):
            piece = products.astype(BF)
            inner = inner + dot_nt(picks.astype(BF), piece)
            products = products - piece.astype(F32)
        inner_ref[...] = inner
        if block == 1:
            send_ref = refs[5]
            turned = jnp.concatenate([weight_ref[QUARTER:, :], weight_ref[:QUARTER, :]], axis=0)
            send_ref[:rows, :] = dot_nt(attention, turned).astype(BF)
            rest = jnp.concatenate([log_ref[...], inner], axis=0)
            send_ref[rows:, :] = jnp.zeros((3 * LABELS, HALF), BF)
            for k in range(3):
                at = rows + k * LABELS
                piece = rest.astype(BF)
                send_ref[at : at + LABELS, :rows] = piece
                rest = rest - piece.astype(F32)

        @pl.when(mine)
        def _():
            own_ref[...] = total
            sums_ref[...] = jnp.zeros_like(sums_ref)
            sums_ref[0:1, :] = jnp.sum(upstream * here, axis=0, keepdims=True)
            sums_ref[1:2, :] = jnp.sum(upstream, axis=0, keepdims=True)
            sums_ref[2:3, :] = jnp.sum(attention.astype(F32), axis=0, keepdims=True)

        @pl.when(jnp.logical_not(mine))
        def _():
            own_ref[...] = old[0][...] if old else jnp.zeros_like(own_ref)
            sums_ref[...] = old[1][...] if old else jnp.zeros_like(sums_ref)

    operands = [part, received, total_grad, normed, inverse, vecs, out_weight, ctx, logs, *earlier]
    outs = [
        struct((rows, D), BF),
        struct((rows, HALF), BF),
        struct((VECS, rows), F32),
        struct((rows, D), F32),
        struct((8, D), F32),
        struct((rows + 3 * LABELS, HALF), BF),
    ][: 6 if block == 1 else 5]
    return call(
        "first_norm",
        body,
        scalars,
        operands,
        [whole(o.shape) for o in operands],
        outs,
        [whole(o.shape) for o in outs],
        (1,),
        micros=3,
    )


def halves(value):
    high = value.astype(BF).astype(F32)
    return jnp.concatenate([high, value - high], axis=0).astype(BF)


def whole_of(table):
    return table[:LABELS].astype(F32) + table[LABELS : 2 * LABELS].astype(F32)


def output_grads(scalars, blocks, small, small_side):
    def body(sc, *refs):
        small_ref, side_ref, keep_ref, send_ref, result_ref = refs[-5:]
        grads = []
        for ref in (refs[2], refs[5]):
            turned = pltpu.roll(ref[...].astype(F32), turn(-sc[2]), 1)
            turned = [turned[:, :QUARTER], turned[:, HALF : HALF + QUARTER]]
            grads.append(jnp.concatenate(turned, axis=1).astype(BF))
        for side in range(2):
            part = dot_tn(refs[side][...], grads[0]) + dot_tn(refs[3 + side][...], grads[1])
            for k in range(2):
                at = pl.multiple_of((sc[2] ^ side ^ (2 * k)) * QUARTER, 16)
                result_ref[pl.ds(at, QUARTER), :] = part[k * QUARTER : (k + 1) * QUARTER, :]
        for j in range(GROUPS):
            target = (keep_ref, send_ref)[j % 2]
            block = sc[1] ^ j
            rows = pl.ds(pl.multiple_of(block * BLOCK, 16), BLOCK)
            target[j // 2, :, :HALF] = result_ref[rows, :].astype(BF)
            target[j // 2, :, HALF:] = jnp.zeros((BLOCK, 128), BF)
            target[j // 2, : 2 * LABELS, HALF:] = halves(small_ref[block] + side_ref[block])

    outs = [struct((GROUPS // 2, BLOCK, HALF + 128), BF)] * 2
    operands = [value for block in blocks for value in block] + [small, small_side]
    return call(
        "output_grads",
        body,
        scalars,
        operands,
        [whole(o.shape) for o in operands],
        outs,
        [whole(o.shape) for o in outs],
        (1,),
        [pltpu.VMEM((D, HALF), F32)],
        micros=4,
    )


def attend_backward(scalars, pair, halo, grad_blocks, logs, inners, hot, weight, rows):
    base = 3 * rows
    steps = HALF // PAIR

    def body(sc, *refs):
        pair_refs, halo_refs, refs = refs[:3], refs[3:6], refs[6:]
        far_ref, near_ref, halo_ref, stats_ref, *refs = refs
        log_refs, inner_refs, (hot_ref, w_ref, *refs) = refs[:2], refs[2:4], refs[4:]
        out_ref, keep_ref, send_ref, sums_ref, mask_ref, key_ref, value_ref, acc_ref, q_ref, k_ref, v_ref, line_ref = refs
        for target, first_part, last_part in zip((q_ref, k_ref, v_ref), pair_refs, halo_refs):
            target[: 2 * rows, :] = first_part[...]
            target[2 * rows :, :] = last_part[...]
        step = pl.program_id(0)

        @pl.when(step == 0)
        def _():
            mask_ref[...] = (dot_tn(hot_ref[...], hot_ref[...]) - 1.0) * MASKED
            lines = jnp.zeros((LABELS, rows), F32)
            for k in range(3):
                at = rows + k * LABELS
                lines = lines + stats_ref[at : at + LABELS, :rows].astype(F32)
            line_ref[...] = lines

        key_ref[...] = jnp.zeros_like(key_ref)
        value_ref[...] = jnp.zeros_like(value_ref)
        lane = lax.broadcasted_iota(jnp.int32, (1, PAIR), 1)
        query_grads = [jnp.zeros((PAIR, rows), F32), jnp.zeros((PAIR, rows), F32)]
        for head in range(2):
            part = jnp.where((lane // HEAD_DIM) == head, 1.0, 0.0)
            key_turned = (k_ref[...].astype(F32) * part).T.astype(BF)
            line = 2 * step + head
            other = lax.rem(line + 3, 6)
            lines = [(log_refs[k][pl.ds(line, 1), :], inner_refs[k][pl.ds(line, 1), :]) for k in range(2)]
            lines += [(line_ref[pl.ds(other, 1), :], line_ref[pl.ds(other + VECS, 1), :])]
            for index, (low, high) in enumerate(((0, 2 * rows), (0, base), (rows, 2 * rows))):
                start = index * rows
                mine = (q_ref[start : start + rows].astype(F32) * (part * HEAD_DIM**-0.5)).astype(BF)
                grads = (far_ref, near_ref, halo_ref)[index][:rows, :]
                grads = (grads.astype(F32) * part).astype(BF)
                scores = dot_nt(k_ref[low:high], mine) + mask_ref[low:high, start : start + rows]
                log_total, inner = lines[index]
                probs = jnp.exp(scores - log_total)
                pulled = dot_nt(v_ref[low:high], grads)
                score_grads = (probs * (pulled - inner)).astype(BF)
                top = min(high, 2 * rows)
                span = top - low
                value_ref[low:top, :] += dot(probs[:span].astype(BF), grads)
                key_ref[low:top, :] += dot(score_grads[:span], mine)
                if index < 2:
                    query_grads[index] = query_grads[index] + dot(key_turned[:, low:high], score_grads)
        for index in range(2):
            turned = (query_grads[index] * HEAD_DIM**-0.5).T.astype(BF)
            out_ref[index * rows : (index + 1) * rows, :PAIR] = turned
        out_ref[:, PAIR : 2 * PAIR] = key_ref[...].astype(BF)
        out_ref[:, 2 * PAIR :] = value_ref[...].astype(BF)
        sums = jnp.sum(out_ref[...].astype(F32), axis=0, keepdims=True)
        sums_ref[...] = jnp.broadcast_to(sums, (8, 3 * PAIR))
        product = dot_nt(out_ref[...], w_ref[...])

        @pl.when(step == 0)
        def _():
            acc_ref[...] = product

        @pl.when(step > 0)
        def _():
            acc_ref[...] += product

        @pl.when(step == steps - 1)
        def _():
            near = sc[0]
            keep_ref[...] = acc_ref[pl.ds(pl.multiple_of(near * rows, rows), rows), :]
            other = acc_ref[pl.ds(pl.multiple_of((1 - near) * rows, rows), rows), :]
            send_ref[...] = other.astype(BF)

    stats = grad_blocks[2]
    operands = [*pair, *halo, *grad_blocks, stats, *logs, *inners, hot, weight]
    in_specs = [column(2 * rows)] * 3 + [column(rows)] * 5 + [column(stats.shape[0])]
    in_specs += [whole(o.shape) for o in operands[9:15]]
    in_specs += [pl.BlockSpec((D, 3 * PAIR), lambda p, _: (0, p))]
    outs = [struct((2 * rows, 3 * HALF), BF), struct((rows, D), F32), struct((rows, D), BF)]
    outs += [struct((8, 3 * HALF), F32)]
    out_specs = [
        pl.BlockSpec((2 * rows, 3 * PAIR), lambda p, _: (0, p)),
        whole((rows, D)),
        whole((rows, D)),
        pl.BlockSpec((8, 3 * PAIR), lambda p, _: (0, p)),
    ]
    scratch = [
        pltpu.VMEM((base, base), F32),
        pltpu.VMEM((2 * rows, PAIR), F32),
        pltpu.VMEM((2 * rows, PAIR), F32),
        pltpu.VMEM((2 * rows, D), F32),
    ] + [pltpu.VMEM((base, PAIR), BF)] * 3
    scratch += [pltpu.VMEM((LABELS, rows), F32)]
    return call(
        "attend_backward",
        body,
        scalars,
        operands,
        in_specs,
        outs,
        out_specs,
        (steps,),
        scratch,
        micros=MICROS,
    )


def projection_grads(scalars, x, grads, rows):
    tall = 2 * rows

    def body(sc, x_ref, grad_ref, *refs):
        result_ref = refs[-1]
        result_ref[...] = dot_tn(x_ref[...], grad_ref[...])
        split_rows(result_ref, sc[1], refs[0], refs[1])

    outs = split_outs(3 * HALF)
    out_specs = [pl.BlockSpec((GROUPS // 2, BLOCK, 3 * PAIR), lambda p, _: (0, 0, p))] * 2
    return call(
        "projection_grads",
        body,
        scalars,
        [x, grads],
        [pl.BlockSpec((tall, D), lambda p, _: (0, 0)), pl.BlockSpec((tall, 3 * PAIR), lambda p, _: (0, p))],
        outs,
        out_specs,
        (HALF // PAIR,),
        [pltpu.VMEM((D, 3 * PAIR), F32)],
        micros=5,
    )


def combine(scalars, keep, received):
    count, rows, width = keep.shape
    chunk = width // 3

    def body(_, keep_ref, recv_ref, *refs):
        for k in range(count):
            total = keep_ref[k].astype(F32) + recv_ref[k].astype(F32)
            refs[k][...] = total.astype(refs[k].dtype)

    block = pl.BlockSpec((count, rows, chunk), lambda c, _: (0, 0, c))
    outs = [struct((rows, width), F32)] + [struct((rows, width), BF)] * (count - 1)
    spec = pl.BlockSpec((rows, chunk), lambda c, _: (0, c))
    return list(call(
        "combine",
        body, scalars, [keep, received], [block, block], outs, [spec] * count, (3,)))


def combine_both(scalars, keep, received, out_keep, out_received):
    count, rows, wide = keep.shape
    last = wide + HALF

    def body(_, keep_ref, recv_ref, out_keep_ref, out_recv_ref, *refs):
        for k in range(count):
            kind = refs[k].dtype
            refs[k][:, :wide] = (keep_ref[k].astype(F32) + recv_ref[k].astype(F32)).astype(kind)
            total = out_keep_ref[k, :, :HALF].astype(F32) + out_recv_ref[k, :, :HALF].astype(F32)
            refs[k][:, wide:last] = total.astype(kind)
            small = whole_of(out_keep_ref[k, :, HALF:]) + whole_of(out_recv_ref[k, :, HALF:])
            refs[k][:, last:] = jnp.zeros((rows, 128), kind)
            refs[k][: 2 * LABELS, last:] = halves(small).astype(kind)

    outs = [struct((rows, last + 128), F32)] + [struct((rows, last + 128), BF)] * (count - 1)
    return simple("combine_both", body, scalars, [keep, received, out_keep, out_received], outs, 2)


def total_feed(scalars, sums):
    rows = sums[0].shape[0]

    def body(_, *refs):
        keep_ref, send_ref = refs[-2:]
        total = refs[0][...]
        for ref in refs[1:-2]:
            total = total + ref[...].astype(F32)
        keep_ref[...] = total[:, : 2 * HID]
        send_ref[:, : 2 * HID] = total[:, 2 * HID :].astype(BF)
        send_ref[:, 2 * HID :] = jnp.zeros((rows, 256), BF)

    outs = [struct((rows, 2 * HID), F32), struct((rows, 2 * HID + 256), BF)]
    return simple("total_feed", body, scalars, sums, outs, 2)


def total_projection(scalars, sums):
    rows, width = sums[0].shape
    wide = 3 * HALF
    last = wide + HALF

    def body(_, *refs):
        keep_ref, send_ref = refs[-2:]
        total = refs[0][:, :last]
        for ref in refs[1:-2]:
            total = total + ref[:, :last].astype(F32)
        near, far = [], []
        for kind in range(3):
            both = [total[:, (3 * p + kind) * PAIR : (3 * p + kind + 1) * PAIR] for p in range(3)]
            both = jnp.concatenate(both, axis=1)
            near.append(both[:, :QUARTER])
            far.append(both[:, QUARTER:])
        near.append(total[:, wide : wide + QUARTER])
        far.append(total[:, wide + QUARTER : last])
        keep_ref[:, :D] = jnp.concatenate(near, axis=1)
        send_ref[:, :D] = jnp.concatenate(far, axis=1).astype(BF)
        if width > last:
            small = jnp.zeros((LABELS, 128), F32)
            for ref in refs[:-2]:
                small = small + whole_of(ref[:, last:])
            keep_ref[:, D:] = jnp.zeros((rows, 128), F32)
            send_ref[:, D:] = jnp.zeros((rows, 128), BF)
            keep_ref[:LABELS, D:] = small
            send_ref[: 2 * LABELS, D:] = halves(small)

    width_out = D + width - last
    outs = [struct((rows, width_out), F32), struct((rows, width_out), BF)]
    return simple("total_projection", body, scalars, sums, outs, 2)


def finish_feed(scalars, keep, received):
    rows = keep.shape[0]

    def body(_, keep_ref, recv_ref, up_ref, down_ref):
        up_ref[...] = keep_ref[:, :HID] + recv_ref[:, :HID].astype(F32)
        down_ref[...] = keep_ref[:, HID:] + recv_ref[:, HID : 2 * HID].astype(F32)

    outs = [struct((rows, HID), F32)] * 2
    return simple("finish_feed", body, scalars, [keep, received], outs, FEED_MICROS)


def finish_projection(scalars, keep, received):
    rows, width = keep.shape

    def body(_, keep_ref, recv_ref, *refs):
        total = keep_ref[:, :D] + recv_ref[:, :D].astype(F32)
        for k in range(4):
            refs[k][...] = total[:, k * QUARTER : (k + 1) * QUARTER]
        if width > D:
            small = keep_ref[:LABELS, D:] + whole_of(recv_ref[:, D:])
            for k in range(VECS):
                refs[4 + k][...] = small[k, :BLOCK]
            for k in range(SHARE):
                refs[4 + VECS][k * 128 : (k + 1) * 128] = small[VECS + k]

    outs = [struct((rows, QUARTER), F32)] * 4
    if width > D:
        outs += [struct((BLOCK,), F32)] * VECS + [struct((FF // GROUPS,), F32)]
    return simple("finish_projection", body, scalars, [keep, received], outs)


def small_sums(scalars, sums_one, sums_two, sums_hidden, sums_projection):
    def body(sc, one_ref, two_ref, hidden_ref, projection_ref, out_ref, wide_ref, tall_ref):
        out_ref[...] = jnp.zeros_like(out_ref)
        lanes = lax.broadcasted_iota(jnp.int32, (1, D), 1)
        near, far = lanes < QUARTER, (lanes >= QUARTER) & (lanes < HALF)
        for row, kind in ((0, 0), (1, 2)):
            line = jnp.concatenate(
                [
                    projection_ref[0:1, (3 * p + kind) * PAIR : (3 * p + kind + 1) * PAIR]
                    for p in range(3)
                ]
                + [jnp.zeros((1, HALF), F32)],
                axis=1,
            )
            low = pltpu.roll(jnp.broadcast_to(jnp.where(near, line, 0.0), (8, D)), sc[2] * QUARTER, 1)
            high = jnp.broadcast_to(jnp.where(far, line, 0.0), (8, D))
            high = pltpu.roll(high, turn((sc[2] ^ 2) - 1), 1)
            wide_ref[row : row + 1, :] = (low + high)[0:1]
        wide_ref[2:3, :] = one_ref[2:3, :]
        wide_ref[3:5, :] = one_ref[0:2, :]
        wide_ref[5:6, :] = two_ref[2:3, :]
        wide_ref[6:8, :] = two_ref[0:2, :]
        tall_ref[...] = jnp.zeros_like(tall_ref)
        for k in range(2):
            to = pl.multiple_of((sc[2] ^ (2 * k)) * HID, 128)
            tall_ref[0:1, pl.ds(to, HID)] = hidden_ref[0:1, k * HID : (k + 1) * HID]
        share = FF // GROUPS
        for d in range(GROUPS):
            out_ref[d, :VECS, :BLOCK] = wide_ref[:, d * BLOCK : (d + 1) * BLOCK]
            for c in range(share // 128):
                at = d * share + c * 128
                out_ref[d, VECS + c : VECS + c + 1, :] = tall_ref[0:1, at : at + 128]

    operands = [sums_one, sums_two, sums_hidden, sums_projection]
    shape = (GROUPS, LABELS, 128)
    return call(
        "small_sums",
        body,
        scalars,
        operands,
        [whole(o.shape) for o in operands],
        [struct(shape, F32)],
        [whole(shape)],
        (1,),
        [pltpu.VMEM((VECS, D), F32), pltpu.VMEM((8, FF), F32)],
    )[0]


def per_device(
    tokens,
    segments,
    query_weight,
    key_weight,
    value_weight,
    output_weight,
    query_bias,
    value_bias,
    output_bias,
    first_gain,
    first_shift,
    up_weight,
    up_bias,
    down_weight,
    down_bias,
    second_gain,
    second_shift,
    cotangent,
):
    seq_count = lax.axis_size("seq")
    count = lax.axis_size("dp")
    place_z = lax.axis_index("seq")
    assert seq_count == 4
    direct = count == GROUPS
    rows = tokens.shape[1]
    piece_rows = query_weight.shape[0]
    near = (place_z == 1) | (place_z == 2)
    base = lax.axis_index("dp") if direct else 0
    scalars = jnp.stack([near, base, place_z]).astype(jnp.int32)

    own = tokens[0]
    cot_own = cotangent[0]
    lines = [
        query_bias,
        value_bias,
        output_bias,
        first_gain,
        first_shift,
        down_bias,
        second_gain,
        second_shift,
    ]
    lines = lines if direct else []
    first_send, mine, wide, labelled, own_docs = pack_inputs(
        scalars,
        [query_weight, key_weight, value_weight, output_weight],
        own,
        segments,
        up_weight,
        down_weight.T,
        lines,
        up_bias,
    )
    arrived = swap(first_send, "seq", 2)
    side = swap(output_weight, "seq", 1)
    if direct:
        mine_chip = [mine, swap(mine, "dp", 2), swap(mine, "dp", 4)]
        wide_last = swap(wide, "dp", 6)
        labelled, side, wide_last, mine_chip, arrived = together(
            labelled, side, wide_last, mine_chip, arrived
        )
    else:
        arrived, labelled, side = together(arrived, labelled, side)
    narrow_far, both, partner_send = split_arrived(scalars, arrived, mine, labelled)
    partner = swap(partner_send, "seq", 1)
    halo_near = lax.ppermute(labelled, "seq", [(1, 2), (2, 1)])
    if direct:
        far_chip = [narrow_far, swap(narrow_far, "dp", 2), swap(narrow_far, "dp", 4)]
        both_far = swap(both, "dp", 6)
        mine_chip, cot_own, far_chip, both_far, partner, halo_near = together(
            mine_chip, cot_own, far_chip, both_far, partner, halo_near
        )
        stacked = stack_narrow(scalars, mine_chip, far_chip, both_far)
        pieces = [stacked, swap(stacked, "dp", 1)]
        feed_chip = chip_pieces(pack_feed(scalars, first_send, arrived, side, partner))
    halo_far = lax.ppermute(halo_near, "seq", [(1, 0), (2, 3)])
    if not direct:
        vectors = jnp.stack(
            [
                query_bias,
                value_bias,
                output_bias,
                first_gain,
                first_shift,
                down_bias,
                second_gain,
                second_shift,
            ]
        )
        lines = lax.all_gather(vectors, "dp", axis=1, tiled=True).reshape(VECS, GROUPS, BLOCK)
        lines = jnp.pad(lines, ((0, 0), (0, 0), (0, 128 - BLOCK)))
        tall = lax.all_gather(up_bias, "dp", axis=0, tiled=True).reshape(GROUPS, SHARE, 128).transpose(1, 0, 2)
        lines = jnp.concatenate([lines, tall], axis=0)
        lines = jnp.pad(lines, ((0, LABELS - VECS - SHARE), (0, 0), (0, 3 * QUARTER - 128)))
        lines = lines.transpose(1, 0, 2)
        gathered = gather_rows(mine)
        pieces = [
            jnp.concatenate([half[:, :, 2 * HID :], lines[k::2], far], axis=1)
            for k, (half, far) in enumerate(zip(gathered, gather_rows(narrow_far)))
        ]
        last = swap(arrived[:, 3 * QUARTER : D], "seq", 1)
        feed = gather_rows(pack_feed(scalars, first_send, arrived, side, last))
        weights = [
            jnp.concatenate([half[:, :, : 2 * HID], far], axis=2) for half, far in zip(gathered, feed)
        ]

    def rows_of(keep, send):
        return jnp.stack([keep, send], axis=1).reshape(GROUPS, -1, keep.shape[2]).astype(F32)

    def spread(sums):
        return [sums[0]] + [swap(sums[k], "dp", 2 * k) for k in range(1, len(sums))]

    def scattered(table):
        return [lax.psum_scatter(table, "dp", scatter_dimension=0, tiled=True)]

    *pair, ctx_far, x, weight, hot, vecs, hidden_bias, bias, log_far, scaled_far = attend_pair(
        scalars, own, partner, own_docs, pieces, rows
    )
    if direct:
        pair, ctx_far, cot_own, halo_far = together(pair, ctx_far, cot_own, halo_far)
    *halo, ctx_near, scaled_near, hot, log_near = attend_halo(scalars, halo_near, halo_far, weight, bias, hot, *pair, rows)
    ctx_mine = [ctx_far, ctx_near]
    ctx_partner = [swap(ctx_far, "seq", 1), None]
    if direct:
        ctx_mine[1], ctx_partner[0], wide_last, feed_chip = together(
            ctx_mine[1], ctx_partner[0], wide_last, feed_chip
        )
        stacked = stack_wide(scalars, mine_chip, wide_last, feed_chip)
        weights = [stacked, swap(stacked, "dp", 1)]
    ctx_partner[1] = swap(ctx_mine[1], "seq", 1)
    cot_partner = swap(cot_own, "seq", 1)

    forward, slopes, part_far = [None, None], [None, None], [None, None]
    for block in (1, 0):
        forward[block], weights = feed_forward(
            scalars, block, ctx_mine[block], ctx_partner[block], x, vecs, hidden_bias, weights, rows
        )
        part_far[block] = swap(forward[block][5], "seq", 1)
    up, down, out_mine, _ = weights
    second, second_shared, first_part_far = [None, None], [], [None, None]
    for block in (1, 0):
        slopes[block] = gelu_slope(scalars, forward[block][3])
    for block in (1, 0):
        second[block], second_shared = second_norm(
            scalars,
            block,
            forward[block][5],
            part_far[block],
            forward[block][0],
            slopes[block],
            (cot_own, cot_partner),
            vecs,
            up,
            down,
            second_shared,
            rows,
        )
        if block == 1:
            first_part_far[block] = swap(second[block][3], "seq", 1)
    feed_parts = feed_forward_grads(
        scalars,
        [(forward[k][2], second[k][2], second[k][1], forward[k][4]) for k in range(2)],
        rows,
    )
    first_part_far[1], second, second_shared, feed_parts = together(
        first_part_far[1], second, second_shared, feed_parts
    )
    first_part_far[0] = swap(second[0][3], "seq", 1)
    layer_output, sums_two, sums_hidden = second_shared
    attention_grad, ctx_grad, inners, first_shared = [None, None], [None, None], [None, None], []
    logs, scaled = [log_far, log_near], [scaled_far, scaled_near]

    def finish(block):
        attention_grad[block], ctx_grad[block], inners[block], *shared = first_norm(
            scalars,
            block,
            second[block][3],
            first_part_far[block],
            second[block][0],
            forward[block][0],
            forward[block][1],
            vecs,
            out_mine,
            scaled[block],
            logs[block],
            first_shared,
            rows,
        )
        return shared

    *first_shared, halo_send = finish(1)
    halo_grad = swap(halo_send, "seq", 2)
    if direct:
        feed_sums = combine(scalars, feed_parts[0], swap(feed_parts[1], "dp", 1))
        feed_sums = spread(feed_sums)
    else:
        feed_sums = scattered(rows_of(*feed_parts).reshape(D, -1))
    own_grad, sums_one = finish(0)

    grads, input_keep, input_send, sums_projection = attend_backward(
        scalars, pair, halo, [*ctx_grad, halo_grad], logs, inners, hot, weight, rows
    )
    input_far = swap(input_send, "seq", 1)
    small = small_sums(scalars, sums_one, sums_two, sums_hidden, sums_projection)
    small_side = swap(small, "seq", 1)
    projection_parts = projection_grads(scalars, x, grads, rows)
    projection_parts, small_side, feed_sums = together(projection_parts, small_side, feed_sums)
    if direct:
        feed_keep, feed_send = total_feed(scalars, feed_sums)
        attention_grad, feed_send = together(attention_grad, feed_send)
    out_blocks = [(ctx_mine[k], ctx_partner[k], attention_grad[k]) for k in range(2)]
    if direct:
        projection_received = swap(projection_parts[1], "dp", 1)
        out_parts = output_grads(scalars, out_blocks, small, small_side)
        out_received = swap(out_parts[1], "dp", 1)
        feed_far = swap(feed_send, "seq", 2)
        sums = spread(
            combine_both(scalars, projection_parts[0], projection_received, out_parts[0], out_received)
        )
    else:
        out_parts = rows_of(*output_grads(scalars, out_blocks, small, small_side))
        sums = scattered(
            jnp.concatenate(
                [rows_of(*projection_parts).reshape(D, -1), out_parts[:, :, :HALF].reshape(D, -1)], axis=1
            )
        )
        feed_keep, feed_send = total_feed(scalars, feed_sums)
        feed_far = swap(feed_send, "seq", 2)
    if direct:
        sums, feed_far, input_far = together(sums, feed_far, input_far)
    keep, send = total_projection(scalars, sums)
    received = swap(send, "seq", 2)
    up_grad, down_grad = finish_feed(scalars, feed_keep, feed_far)
    input_grad = own_grad + input_keep + input_far.astype(F32)
    if direct:
        received, up_grad, input_grad = together(received, up_grad, input_grad)
    projections = list(finish_projection(scalars, keep, received))
    if direct:
        projections, vec, tall_lines = projections[:4], projections[4:-1], projections[-1]
    else:
        tile = out_parts[:, :LABELS, HALF:] + out_parts[:, LABELS : 2 * LABELS, HALF:]
        tile = tile + swap(tile, "seq", 2)
        wide_lines = tile[:, :VECS, :BLOCK].transpose(1, 0, 2).reshape(VECS, D)
        wide_lines = lax.psum_scatter(wide_lines, "dp", scatter_dimension=1, tiled=True)
        tall_lines = lax.psum_scatter(tile[:, VECS : VECS + 3].reshape(-1), "dp", tiled=True)
        vec = [wide_lines[k] for k in range(VECS)]
    return (
        layer_output[None],
        input_grad[None],
        *projections,
        vec[0],
        vec[1],
        vec[2],
        vec[3],
        vec[4],
        up_grad,
        tall_lines,
        down_grad.T,
        vec[5],
        vec[6],
        vec[7],
    )


def solution(mesh):
    placed = (
        P("dp", "seq", None),
        P("dp", "seq"),
        P("dp", "seq"),
        P("dp", "seq"),
        P("dp", "seq"),
        P("dp", "seq"),
        P("dp"),
        P("dp"),
        P("dp"),
        P("dp"),
        P("dp"),
        P("dp", "seq"),
        P("dp"),
        P("seq", "dp"),
        P("dp"),
        P("dp"),
        P("dp"),
        P("dp", "seq", None),
    )
    return jax.shard_map(
        per_device,
        mesh=mesh,
        in_specs=placed,
        out_specs=(
            P("dp", "seq", None),
            P("dp", "seq", None),
            P("dp", "seq"),
            P("dp", "seq"),
            P("dp", "seq"),
            P("dp", "seq"),
            P("dp"),
            P("dp"),
            P("dp"),
            P("dp"),
            P("dp"),
            P("dp", "seq"),
            P("dp"),
            P("seq", "dp"),
            P("dp"),
            P("dp"),
            P("dp"),
        ),
        check_vma=False,
    )
```
